32 devices in a mesh: dp: 8 (over y, x, core), expert: 4 (over z).
Axes of the slice: x: 2, y: 2, z: 4, core: 2. Of those that a mesh axis runs over, the one named last changes fastest.
Arguments:
- tokens: bfloat16 [2, 8192, 512], P(None, ('dp', 'expert')), may hold values from -6 to 6
- image_ids: int32 [2, 8192], P(None, ('dp', 'expert')), may hold values from 0 to 41, never falling along the last dimension, each value on 1 to 197 neighbouring positions
- routes: int32 [2, 8192, 2], P(None, ('dp', 'expert')), may hold values from 0 to 7, all different within a row; in each aligned block of 256 rows (0 to 255, 256 to 511, ..., all dimensions but the last counted through in order) at most 128 rows name the same one
- qkv_weight: bfloat16 [3, 512, 512], P(None, ('dp', 'expert')), may hold values from -0.375 to 0.375
- out_weight: bfloat16 [512, 512], P(('dp', 'expert')), may hold values from -0.375 to 0.375
- router_weight: bfloat16 [512, 8], P(('dp', 'expert')), may hold values from -0.1875 to 0.1875
- norm_gains: bfloat16 [2, 512], P(None, ('dp', 'expert')), may hold values from 0.5 to 1.5
- norm_biases: bfloat16 [2, 512], P(None, ('dp', 'expert')), may hold values from -2 to 2
- expert_in: bfloat16 [8, 512, 2048], P('expert', 'dp'), may hold values from -0.25 to 0.25
- expert_out: bfloat16 [8, 2048, 512], P('expert', 'dp'), may hold values from -1 to 1
- cotangent: bfloat16 [2, 8192, 512], P(None, ('dp', 'expert')), may hold values from -6 to 6
Outputs:
- block_out: bfloat16 [2, 8192, 512], P(None, ('dp', 'expert'))
- input_grad: bfloat16 [2, 8192, 512], P(None, ('dp', 'expert'))
- qkv_grad: float32 [3, 512, 512], P(None, ('dp', 'expert'))
- out_grad: float32 [512, 512], P(('dp', 'expert'))
- router_grad: float32 [512, 8], P(('dp', 'expert'))
- gains_grad: float32 [2, 512], P(None, ('dp', 'expert'))
- biases_grad: float32 [2, 512], P(None, ('dp', 'expert'))
- expert_in_grad: float32 [8, 512, 2048], P('expert', 'dp')
- expert_out_grad: float32 [8, 2048, 512], P('expert', 'dp')
The draws below stay inside these ranges and needn't reach their ends.
Inputs may be any that keep to these rules, and one draw needn't show every extreme that they name: `image_ids`: along each micro-batch's rows the numbers never fall and start at 0; each image has 1 to 197 rows, some image exactly 197. `routes`: A row names two different experts. Within one micro-batch, the 256 rows held by one device name any one expert at most 128 times, counting both choices; this most is reached.
All inputs are finite; a program needn't handle non-finite values.
Results may differ from the reference program's by a relative error of at most 0.015.
The reference program's roundings to bfloat16 on the way count: a program that leaves them out, or rounds other values in their place, can miss the bound.
Values may be sent and summed in bfloat16 or wider, within the bound.
A program may use at most 192 MiB of HBM per device.

```python
import math
import jax
import jax.numpy as jnp
import numpy as np
from jax import lax

D = 512
HEADS = 8
HEAD_DIM = 64
FF = 2048
TOP = 2
IMG = 197
MICRO = 2
MB_DEV = 256
EXPERTS = 8
TOKENS_MB = 8192
SLOT = 128
CAP = 2560
SEGS = 42


def level_of(stream_key, shape, cuts, least, top_value):
    factor_of, own = 1.0, jax.random.fold_in(stream_key, 6)
    for position, shards_of in cuts:
        steps = jnp.exp(jax.random.uniform(jax.random.fold_in(own, position), (shards_of,), jnp.float32, least / len(cuts), top_value / len(cuts)))
        factor_of = factor_of * jnp.repeat(steps, shape[position] // shards_of).reshape([-1 if axis == position else 1 for axis in range(len(shape))])
    return factor_of


def split_up(number_of, total, limit, skew):
    weights = [(1 << 20) // math.isqrt(rank ** skew) + 1 for rank in range(2, number_of + 1)]
    rest, counts = total - limit - (number_of - 1), [1] * (number_of - 1)
    while rest > 0:
        free = [i for i in range(number_of - 1) if counts[i] < limit]
        pool, remaining = sum([weights[i] for i in free]), rest
        for i in free:
            more = min(limit - counts[i], max(1, remaining * weights[i] // pool), rest)
            counts[i] = counts[i] + more
            rest = rest - more
    return np.array([limit] + counts)


def uneven(key, number_of, total, most, lean):
    if number_of == 2:
        one = jax.random.randint(key, (), max(1, total - most), min(most, total - 1) + 1)
        return jnp.stack([one, total - one])
    lengths = jnp.asarray(split_up(number_of, total, most, lean), jnp.int32)
    couples = (number_of - 1) // 2
    source_of, receiver = lengths[1:1 + 2 * couples:2], lengths[2:2 + 2 * couples:2]
    room = jnp.minimum(source_of - 1, most - receiver)
    passed = jax.random.randint(jax.random.fold_in(key, 1), (couples,), 0, 1 << 20) % (room + 1)
    lengths = lengths.at[1:1 + 2 * couples:2].set(source_of - passed).at[2:2 + 2 * couples:2].set(receiver + passed)
    return lengths[jax.random.permutation(jax.random.fold_in(key, 2), number_of)]


def assign_block(rng, own, number, rows, amount, top, bound, slope):
    ranking = jax.random.permutation(rng, amount)
    heavy_load, usual = shares(amount, rows * top, bound, slope, True), shares(amount, rows * top, bound, slope, False)
    places = jnp.arange(amount)

    def named(sizes, turn):
        used = int((sizes > 0).sum())
        fixed = max(1, used // 4)
        passed = fixed + (places - fixed + turn * (used - fixed)) % max(1, amount - fixed)
        return jnp.zeros((amount,), jnp.int32).at[ranking[jnp.where(places < fixed, places, passed)]].set(jnp.asarray(sizes, jnp.int32))

    sizes = jnp.where(number % 4 == 0, named(heavy_load, number // 4), named(usual, number - number // 4 - 1))
    mixed = jax.random.permutation(jax.random.fold_in(own, 3), amount)
    source_of, receiver = mixed[0:amount // 2 * 2:2], mixed[1:amount // 2 * 2:2]
    margin = jnp.minimum(sizes[source_of] - 1, bound - sizes[receiver]) // 2
    margin = jnp.where((source_of == ranking[0]) | (receiver == ranking[0]) | (sizes[receiver] == 0), 0, jnp.maximum(margin, 0))
    passed = jax.random.randint(jax.random.fold_in(own, 4), (amount // 2,), 0, 1 << 20) % (margin + 1)
    sizes = sizes.at[source_of].add(-passed).at[receiver].add(passed)
    items = jnp.searchsorted(jnp.cumsum(sizes), jnp.arange(rows * top), side="right").astype(jnp.int32)
    table = items.reshape(top, rows).T
    table = table[jax.random.permutation(jax.random.fold_in(own, 1), rows)]
    turn = jax.random.randint(jax.random.fold_in(own, 2), (rows, 1), 0, top)
    return jnp.take_along_axis(table, (jnp.arange(top)[None, :] + turn) % top, axis=1)


def shares(count, total, reach, lean, full):
    portions = [(1 << 20) // math.isqrt(grade ** lean) + 1 for grade in range(1, count + 1)]
    largest = reach if full else min(reach, max(-(-total // count), total * portions[0] // sum(portions)))
    least = 1 if total - largest >= count - 1 else 0
    counts, surplus = [largest] + [least] * (count - 1), total - largest - least * (count - 1)
    while surplus > 0:
        free = [i for i in range(1, count) if counts[i] < largest] or [i for i in range(1, count) if counts[i] < reach]
        mass, remaining = sum([portions[i] for i in free]), surplus
        for i in free:
            extra = min(reach - counts[i], max(1, remaining * portions[i] // mass), surplus)
            counts[i] = counts[i] + extra
            surplus = surplus - extra
    return np.array(counts)


def centred(stream_key, extent, scale, most, pieces=(), kind=jnp.bfloat16):
    array = scale * jax.random.normal(stream_key, extent, jnp.float32)
    if pieces:
        array = array * level_of(stream_key, extent, pieces, -0.22, 0.18)
    return jnp.clip(array, -most, most).astype(kind)


def setup_inputs(seed: int = 0) -> dict:
    arg_keys = jax.random.split(jax.random.key(seed), 12)
    tokens = centred(arg_keys[0], (MICRO, TOKENS_MB, D), 1.0, 6.0, ((1, 32),))
    image_ids = jax.vmap(lambda own: jnp.searchsorted(jnp.cumsum(uneven(own, SEGS, TOKENS_MB, IMG, 0)), jnp.arange(TOKENS_MB), side="right"))(jax.random.split(arg_keys[1], MICRO)).reshape((MICRO, TOKENS_MB)).astype(jnp.int32)
    routes_keys = jax.random.split(jax.random.fold_in(arg_keys[2], 1), MICRO * TOKENS_MB // MB_DEV)
    routes_turns = jax.random.permutation(jax.random.fold_in(arg_keys[2], 3), MICRO * TOKENS_MB // MB_DEV)
    routes = jax.vmap(lambda own, number: assign_block(jax.random.fold_in(arg_keys[2], 2), own, number, MB_DEV, EXPERTS, TOP, SLOT, 1))(routes_keys, routes_turns).reshape((MICRO, TOKENS_MB, TOP))
    qkv_weight = centred(arg_keys[3], (3, D, D), (D // 2) ** -0.5, 0.375, ((1, 32),))
    out_weight = centred(arg_keys[4], (D, D), (D // 2) ** -0.5, 0.375, ((0, 32),))
    router_weight = centred(arg_keys[5], (D, EXPERTS), (2 * D) ** -0.5, 0.1875, ((0, 32),))
    norm_gains = jnp.clip(1.0 + 0.1 * jax.random.normal(arg_keys[6], (2, D), jnp.float32), 0.5, 1.5).astype(jnp.bfloat16)
    norm_biases = centred(arg_keys[7], (2, D), 0.3, 2.0, ((1, 32),))
    expert_in = centred(arg_keys[8], (EXPERTS, D, FF), D ** -0.5, 0.25, ((0, 4), (1, 8)))
    expert_out = centred(arg_keys[9], (EXPERTS, FF, D), (max(1, FF // (EXPERTS * EXPERTS))) ** -0.5, 1.0, ((0, 4), (1, 8)))
    cotangent = centred(arg_keys[10], (MICRO, TOKENS_MB, D), 1.0, 6.0, ((1, 32),))
    return dict(tokens=tokens, image_ids=image_ids, routes=routes, qkv_weight=qkv_weight, out_weight=out_weight, router_weight=router_weight, norm_gains=norm_gains, norm_biases=norm_biases, expert_in=expert_in, expert_out=expert_out, cotangent=cotangent)


neg_big = -1e+30
norm_eps = 1e-06
highest = lax.Precision.HIGHEST

@jax.custom_vjp
def low(v):
    return lax.optimization_barrier(v.astype(jnp.bfloat16)).astype(jnp.float32)

@jax.custom_vjp
def low_back(v):
    return v

def low_keep(v):
    return (low(v), None)

def low_pass(kept, grad):
    return (grad,)

def back_keep(v):
    return (v, None)

def back_low(kept, grad):
    return (low(grad),)
low.defvjp(low_keep, low_pass)
low_back.defvjp(back_keep, back_low)

def layer_norm(values, gain_row, bias_row):
    centre = lax.optimization_barrier(jnp.mean(values, axis=-1, keepdims=True))
    offset = values - centre
    spread = lax.optimization_barrier(jnp.mean(offset * offset, axis=-1, keepdims=True))
    return offset * lax.rsqrt(spread + norm_eps) * gain_row + bias_row

def tanh_gelu(values):
    return jax.nn.gelu(values, approximate=True)

def routing(route_ids):
    labels = jnp.arange(EXPERTS, dtype=jnp.int32)[None, :]
    first_hot = (route_ids[:, 0:1] == labels).astype(jnp.int32)
    second_hot = (route_ids[:, 1:2] == labels).astype(jnp.int32)
    total_first = lax.optimization_barrier(jnp.sum(first_hot, axis=0))
    place_first = lax.optimization_barrier(jnp.sum((jnp.cumsum(first_hot, axis=0) - first_hot) * first_hot, axis=1))
    place_second = lax.optimization_barrier(jnp.sum((jnp.cumsum(second_hot, axis=0) - second_hot + total_first[None, :]) * second_hot, axis=1))
    places = jnp.stack([place_first, place_second], axis=1)
    kept_mask = places < CAP
    flat_index = jnp.where(kept_mask, route_ids * CAP + places, EXPERTS * CAP).astype(jnp.int32)
    token_index = jnp.repeat(jnp.arange(TOKENS_MB, dtype=jnp.int32), TOP)
    source = jnp.full((EXPERTS * CAP + 1,), TOKENS_MB, jnp.int32).at[flat_index.reshape(-1)].set(token_index)
    return (first_hot, second_hot, flat_index, kept_mask, source[:EXPERTS * CAP])

def one_micro(tokens_f, ids_row, route_plan, qkv_full, out_full, router_full, gain_pair, bias_pair, expert_up_weight, expert_down_weight):
    first_hot, second_hot, flat_index, kept_mask, source = route_plan
    rim_rows = IMG - 1
    score_scale = 1.0 / math.sqrt(HEAD_DIM)
    normed_one = low(layer_norm(tokens_f, gain_pair[0], bias_pair[0]))
    projected = low(low_back(jnp.einsum('rd,cde->cre', normed_one, qkv_full, precision=highest)))
    query_all = projected[0]
    padded = jnp.pad(projected[1:], ((0, 0), (rim_rows, rim_rows), (0, 0)))
    padded_ids = jnp.pad(ids_row, (rim_rows, rim_rows), constant_values=-1)

    def attend_block(block_start):
        query_heads = lax.dynamic_slice_in_dim(query_all, block_start, MB_DEV, 0).reshape(MB_DEV, HEADS, HEAD_DIM)
        key_rows = lax.dynamic_slice_in_dim(padded, block_start, MB_DEV + 2 * rim_rows, 1)
        ids_query = lax.dynamic_slice_in_dim(ids_row, block_start, MB_DEV, 0)
        ids_key = lax.dynamic_slice_in_dim(padded_ids, block_start, MB_DEV + 2 * rim_rows, 0)
        key_heads = key_rows[0].reshape(-1, HEADS, HEAD_DIM)
        value_heads = key_rows[1].reshape(-1, HEADS, HEAD_DIM)
        scores = low_back(jnp.einsum('qhd,khd->hqk', query_heads, key_heads, precision=highest) * score_scale)
        scores = jnp.where((ids_query[:, None] == ids_key[None, :])[None], scores, neg_big)
        att_low = low(jax.nn.softmax(scores, axis=-1))
        return jnp.einsum('hqk,khd->qhd', att_low, value_heads, precision=highest).reshape(MB_DEV, D)
    starts = jnp.arange(TOKENS_MB // MB_DEV, dtype=jnp.int32) * MB_DEV
    mixed_rows = lax.map(jax.checkpoint(attend_block), starts).reshape(TOKENS_MB, D)
    mixed_rows = low(low_back(mixed_rows))
    residual = tokens_f + low_back(jnp.dot(mixed_rows, out_full, precision=highest))
    normed_two = low(layer_norm(residual, gain_pair[1], bias_pair[1]))
    router_probs = jax.nn.softmax(jnp.dot(normed_two, router_full, precision=highest), axis=-1)
    picked = jnp.stack([lax.optimization_barrier(jnp.sum(first_hot * router_probs, axis=1)), lax.optimization_barrier(jnp.sum(second_hot * router_probs, axis=1))], axis=1)
    gate_values = kept_mask.astype(router_probs.dtype) * picked
    flat_table = jnp.concatenate([normed_two, jnp.zeros((1, D), normed_two.dtype)], axis=0)
    expert_inputs = low_back(flat_table[source].reshape(EXPERTS, CAP, D))

    def expert_block(operands):
        rows_in, weight_a, weight_b = operands
        hidden_pre = low_back(jnp.dot(rows_in, weight_a, precision=highest))
        hidden_activation = low(tanh_gelu(hidden_pre))
        return low(low_back(jnp.dot(hidden_activation, weight_b, precision=highest)))
    produced = lax.map(jax.checkpoint(expert_block), (expert_inputs, expert_up_weight, expert_down_weight))
    flat_out = jnp.concatenate([produced.reshape(EXPERTS * CAP, D), jnp.zeros((1, D), produced.dtype)], axis=0)
    expert_rows = flat_out[flat_index]
    return residual + lax.optimization_barrier(jnp.sum(gate_values[:, :, None] * expert_rows, axis=1))

def reference(tokens, image_ids, routes, qkv_weight, out_weight, router_weight, norm_gains, norm_biases, expert_in, expert_out, cotangent):
    plans = [routing(routes[batch_index]) for batch_index in range(MICRO)]

    def whole_block(tokens_f, qkv_full, out_full, router_full, gain_pair, bias_pair, expert_up_weight, expert_down_weight):
        return jnp.stack([one_micro(tokens_f[batch_index], image_ids[batch_index], plans[batch_index], qkv_full, out_full, router_full, gain_pair, bias_pair, expert_up_weight, expert_down_weight) for batch_index in range(MICRO)])
    block_value, pullback = jax.vjp(whole_block, tokens.astype(jnp.float32), qkv_weight.astype(jnp.float32), out_weight.astype(jnp.float32), router_weight.astype(jnp.float32), norm_gains.astype(jnp.float32), norm_biases.astype(jnp.float32), expert_in.astype(jnp.float32), expert_out.astype(jnp.float32))
    gradients = pullback(cotangent.astype(jnp.float32))
    return (block_value.astype(jnp.bfloat16), gradients[0].astype(jnp.bfloat16), gradients[1], gradients[2], gradients[3], gradients[4], gradients[5], gradients[6], gradients[7])
```

```python
import math

import jax
import jax.numpy as jnp
from jax import lax
from jax.sharding import PartitionSpec as P

D = 512
HEADS = 8
HEAD_DIM = 64
FF = 2048
TOP = 2
IMG = 197
MICRO = 2


neg_big = -1e30
norm_eps = 1e-06
highest = lax.Precision.HIGHEST


def padded(cells, sides, width):
    for axis, dim in sides:
        count = lax.axis_size(axis)
        ends = count - 1
        head = lax.slice_in_dim(cells, 0, width, axis=dim)
        tail = lax.slice_in_dim(cells, cells.shape[dim] - width, cells.shape[dim], axis=dim)
        cells = jnp.concatenate(
            [
                lax.ppermute(tail, axis, [(i, (i + 1) % count) for i in range(ends)]),
                cells,
                lax.ppermute(head, axis, [((i + 1) % count, i) for i in range(ends)]),
            ],
            axis=dim,
        )
    return cells


def layer_norm(values, gain_row, bias_row):
    centre = jnp.mean(values, axis=-1, keepdims=True)
    offset = values - centre
    spread = jnp.mean(offset * offset, axis=-1, keepdims=True)
    return offset * lax.rsqrt(spread + norm_eps) * gain_row + bias_row


def tanh_gelu(values):
    return jax.nn.gelu(values, approximate=True)


def fetch_dense(qkv_weight, out_weight, router_weight, norm_gains, norm_biases):
    rows, experts = router_weight.shape
    small = jnp.concatenate([router_weight, norm_gains.T, norm_biases.T], axis=1)
    small = jnp.pad(small, ((0, 0), (0, D - experts - 4)))
    packed = jnp.concatenate([qkv_weight, out_weight[None], small[None]], axis=0)
    full = lax.all_gather(packed, ("dp", "expert"), axis=1, tiled=True)
    return (
        full[:3],
        full[3],
        full[4][:, :experts],
        full[4][:, experts : experts + 2].T,
        full[4][:, experts + 2 : experts + 4].T,
    )


def fetch_experts(expert_in, expert_out):
    return (
        lax.all_gather(expert_in, "dp", axis=1, tiled=True),
        lax.all_gather(expert_out, "dp", axis=1, tiled=True),
    )


def plan_routes(route_ids, shard_experts):
    row_count = route_ids.shape[0]
    experts = shard_experts * lax.axis_size("expert")
    devices = lax.axis_size(("dp", "expert"))
    slot_count = 2 * TOP * row_count // experts
    capacity = 5 * TOP * row_count * devices // (4 * experts)
    labels = lax.broadcasted_iota(jnp.int32, (1, experts), 1)
    first_hot = (route_ids[:, 0:1] == labels).astype(jnp.int32)
    second_hot = (route_ids[:, 1:2] == labels).astype(jnp.int32)
    counts = jnp.stack([jnp.sum(first_hot, axis=0), jnp.sum(second_hot, axis=0)])
    all_counts = lax.all_gather(counts[None], ("dp", "expert"), axis=0, tiled=True)
    earlier = (
        lax.broadcasted_iota(jnp.int32, (devices, 1, 1), 0) < lax.axis_index(("dp", "expert"))
    ).astype(jnp.int32)
    before = jnp.sum(all_counts * earlier, axis=0)
    total_first = jnp.sum(all_counts[:, 0, :], axis=0)
    row_before = (
        lax.broadcasted_iota(jnp.int32, (row_count, row_count), 0)
        > lax.broadcasted_iota(jnp.int32, (row_count, row_count), 1)
    ).astype(jnp.bfloat16)

    def rank_of(hot):
        ahead = jnp.dot(row_before, hot.astype(jnp.bfloat16), preferred_element_type=jnp.float32)
        return jnp.sum(ahead.astype(jnp.int32) * hot, axis=1)

    rank_first = rank_of(first_hot)
    rank_second = rank_of(second_hot)
    place_first = jnp.sum(first_hot * before[0][None, :], axis=1) + rank_first
    place_second = jnp.sum(second_hot * (total_first + before[1])[None, :], axis=1) + rank_second
    kept_mask = jnp.stack([place_first < capacity, place_second < capacity], axis=1)
    slot_second = jnp.sum(second_hot * counts[0][None, :], axis=1) + rank_second
    flat_index = jnp.stack(
        [route_ids[:, 0] * slot_count + rank_first, route_ids[:, 1] * slot_count + slot_second],
        axis=1,
    )
    target = jnp.where(kept_mask, flat_index, experts * slot_count)
    return (first_hot, second_hot, target, kept_mask.astype(jnp.float32))


def fill_slots(row_pairs, target, experts, slot_count):
    feature_count = row_pairs.shape[-1]
    buffer = jnp.zeros((experts * slot_count + 1, feature_count), row_pairs.dtype)
    buffer = buffer.at[target.reshape(-1)].set(row_pairs.reshape(-1, feature_count))
    return buffer[:-1].reshape(experts, 1, slot_count, feature_count)


def read_slots(returned, target):
    feature_count = returned.shape[-1]
    flat_table = jnp.concatenate(
        [returned.reshape(-1, feature_count), jnp.zeros((1, feature_count), returned.dtype)], axis=0
    )
    return flat_table[target]


def run_forward(tokens_f, ids_ext, route_plan, dense_set, expert_set):
    qkv_full, out_full, router_full, gain_pair, bias_pair = dense_set
    expert_up_weight, expert_down_weight = expert_set
    first_hot, second_hot, target, kept_mask = route_plan
    row_count = tokens_f.shape[0]
    rim_rows = IMG - 1
    score_scale = 1.0 / math.sqrt(HEAD_DIM)
    experts = router_full.shape[1]
    slot_count = 2 * TOP * row_count // experts
    normed_one = layer_norm(
        tokens_f, gain_pair[0].astype(jnp.float32), bias_pair[0].astype(jnp.float32)
    ).astype(jnp.bfloat16)
    projected = jnp.einsum(
        "rd,cde->cre", normed_one, qkv_full, preferred_element_type=jnp.float32
    ).astype(jnp.bfloat16)
    key_value = padded(projected[1:], ((("dp", "expert"), 1),), rim_rows)
    query_heads = projected[0].reshape(row_count, HEADS, HEAD_DIM)
    key_heads = key_value[0].reshape(-1, HEADS, HEAD_DIM)
    value_heads = key_value[1].reshape(-1, HEADS, HEAD_DIM)
    same_image = ids_ext[rim_rows : rim_rows + row_count][:, None] == ids_ext[None, :]
    scores = (
        jnp.einsum("qhd,khd->hqk", query_heads, key_heads, preferred_element_type=jnp.float32)
        * score_scale
    )
    scores = jnp.where(same_image[None], scores, neg_big)
    top_score = jnp.max(scores, axis=-1, keepdims=True)
    log_total = top_score + jnp.log(jnp.sum(jnp.exp(scores - top_score), axis=-1, keepdims=True))
    att_probs = jnp.exp(scores - log_total)
    att_low = att_probs.astype(jnp.bfloat16)
    mixed_rows = (
        jnp.einsum("hqk,khd->qhd", att_low, value_heads, preferred_element_type=jnp.float32)
        .reshape(row_count, D)
        .astype(jnp.bfloat16)
    )
    residual = tokens_f + jnp.dot(mixed_rows, out_full, preferred_element_type=jnp.float32)
    normed_two = layer_norm(
        residual, gain_pair[1].astype(jnp.float32), bias_pair[1].astype(jnp.float32)
    ).astype(jnp.bfloat16)
    router_probs = jax.nn.softmax(
        jnp.dot(normed_two, router_full, preferred_element_type=jnp.float32), axis=-1
    )
    picked = jnp.stack(
        [jnp.sum(first_hot * router_probs, axis=1), jnp.sum(second_hot * router_probs, axis=1)],
        axis=1,
    )
    gate_values = kept_mask * picked
    outgoing = fill_slots(
        jnp.broadcast_to(normed_two[:, None, :], (row_count, TOP, D)), target, experts, slot_count
    )
    arrived = lax.all_to_all(outgoing, "expert", split_axis=0, concat_axis=1, tiled=True)
    shard_experts = arrived.shape[0]
    collected_token_rows = arrived.reshape(shard_experts, -1, D)
    hidden_pre = jnp.einsum(
        "ycq,yqt->yct", collected_token_rows, expert_up_weight, preferred_element_type=jnp.float32
    )
    hidden_activation = tanh_gelu(hidden_pre).astype(jnp.bfloat16)
    produced = jnp.einsum(
        "nso,nop->nsp", hidden_activation, expert_down_weight, preferred_element_type=jnp.float32
    ).astype(jnp.bfloat16)
    returned = lax.all_to_all(
        produced.reshape(arrived.shape), "expert", split_axis=1, concat_axis=0, tiled=True
    )
    expert_rows = read_slots(returned, target)
    block_value = residual + jnp.sum(
        gate_values[:, :, None] * expert_rows.astype(jnp.float32), axis=1
    )
    return (
        normed_one,
        query_heads,
        key_heads,
        value_heads,
        att_probs,
        att_low,
        mixed_rows,
        residual,
        normed_two,
        router_probs,
        gate_values,
        collected_token_rows,
        hidden_pre,
        hidden_activation,
        expert_rows,
        block_value,
    )


def run_backward(tokens_f, ids_ext, route_plan, dense_set, expert_set, upstream, gradients):
    qkv_full, out_full, router_full, gain_pair, bias_pair = dense_set
    expert_up_weight, expert_down_weight = expert_set
    first_hot, second_hot, target, kept_mask = route_plan
    grad_qkv, grad_out, grad_router, grad_gains, grad_biases, grad_in, grad_expert_out = gradients
    (
        normed_one,
        query_heads,
        key_heads,
        value_heads,
        att_probs,
        att_low,
        mixed_rows,
        residual,
        normed_two,
        router_probs,
        gate_values,
        collected_token_rows,
        hidden_pre,
        hidden_activation,
        expert_rows,
        block_value,
    ) = run_forward(tokens_f, ids_ext, route_plan, dense_set, expert_set)
    row_count = tokens_f.shape[0]
    rim_rows = IMG - 1
    score_scale = 1.0 / math.sqrt(HEAD_DIM)
    experts = router_full.shape[1]
    slot_count = 2 * TOP * row_count // experts
    shard_experts = expert_up_weight.shape[0]
    d_gate = kept_mask * jnp.sum(upstream[:, None, :] * expert_rows.astype(jnp.float32), axis=-1)
    d_sent = (gate_values[:, :, None] * upstream[:, None, :]).astype(jnp.bfloat16)
    d_arrived = lax.all_to_all(
        fill_slots(d_sent, target, experts, slot_count),
        "expert",
        split_axis=0,
        concat_axis=1,
        tiled=True,
    )
    produced_rows_grad = d_arrived.reshape(shard_experts, -1, D)
    activation_grad = jnp.einsum(
        "tkw,tew->tke", produced_rows_grad, expert_down_weight, preferred_element_type=jnp.float32
    )
    grad_expert_out = grad_expert_out + jnp.einsum(
        "meq,mek->mqk", hidden_activation, produced_rows_grad, preferred_element_type=jnp.float32
    )
    gelu_value, gelu_back = jax.vjp(tanh_gelu, hidden_pre)
    preactivation_grad = gelu_back(activation_grad)[0].astype(jnp.bfloat16)
    grad_in = grad_in + jnp.einsum(
        "zjo,zjm->zom", collected_token_rows, preactivation_grad, preferred_element_type=jnp.float32
    )
    d_rows = jnp.einsum(
        "iht,imt->ihm", preactivation_grad, expert_up_weight, preferred_element_type=jnp.float32
    ).astype(jnp.bfloat16)
    d_back = lax.all_to_all(
        d_rows.reshape(d_arrived.shape), "expert", split_axis=1, concat_axis=0, tiled=True
    )
    d_normed_two = jnp.sum(
        kept_mask[:, :, None] * read_slots(d_back, target).astype(jnp.float32), axis=1
    )
    d_probs = first_hot * d_gate[:, 0:1] + second_hot * d_gate[:, 1:2]
    d_logits = router_probs * (d_probs - jnp.sum(router_probs * d_probs, axis=-1, keepdims=True))
    router_wide = router_full.astype(jnp.float32)
    d_normed_two = d_normed_two + jnp.dot(d_logits, router_wide.T, precision=highest)
    grad_router = grad_router + jnp.dot(
        normed_two.astype(jnp.float32).T, d_logits, precision=highest
    )
    norm_value, second_back = jax.vjp(
        layer_norm, residual, gain_pair[1].astype(jnp.float32), bias_pair[1].astype(jnp.float32)
    )
    d_resid_part, d_gain_two, d_bias_two = second_back(d_normed_two)
    d_resid = upstream + d_resid_part
    d_attn = d_resid.astype(jnp.bfloat16)
    grad_out = grad_out + jnp.einsum(
        "rd,re->de", mixed_rows, d_attn, preferred_element_type=jnp.float32
    )
    d_mixed = (
        jnp.einsum("re,de->rd", d_attn, out_full, preferred_element_type=jnp.float32)
        .astype(jnp.bfloat16)
        .reshape(row_count, HEADS, HEAD_DIM)
    )
    d_att = jnp.einsum("qhd,khd->hqk", d_mixed, value_heads, preferred_element_type=jnp.float32)
    d_scores = (att_probs * (d_att - jnp.sum(att_probs * d_att, axis=-1, keepdims=True))).astype(
        jnp.bfloat16
    )
    d_query = (
        (
            jnp.einsum("hqk,khd->qhd", d_scores, key_heads, preferred_element_type=jnp.float32)
            * score_scale
        )
        .astype(jnp.bfloat16)
        .reshape(row_count, D)
    )
    d_key = (
        jnp.einsum("hqk,qhd->khd", d_scores, query_heads, preferred_element_type=jnp.float32)
        * score_scale
    )
    d_value = jnp.einsum("hqk,qhd->khd", att_low, d_mixed, preferred_element_type=jnp.float32)
    d_pair = jnp.stack([d_key.reshape(-1, D), d_value.reshape(-1, D)])
    rim_grads = jnp.concatenate([d_pair[:, :rim_rows], d_pair[:, rim_rows + row_count :]], axis=1)
    beside_all = padded(rim_grads.astype(jnp.bfloat16), ((("dp", "expert"), 1),), rim_rows).astype(
        rim_grads.dtype
    )
    own_part = d_pair[:, rim_rows : rim_rows + row_count]
    from_below = jnp.pad(beside_all[:, :rim_rows], ((0, 0), (0, row_count - rim_rows), (0, 0)))
    from_above = jnp.pad(beside_all[:, 3 * rim_rows :], ((0, 0), (row_count - rim_rows, 0), (0, 0)))
    d_kv = (own_part + from_below + from_above).astype(jnp.bfloat16)
    d_projected = jnp.concatenate([d_query[None], d_kv], axis=0)
    grad_qkv = grad_qkv + jnp.einsum(
        "rd,cre->cde", normed_one, d_projected, preferred_element_type=jnp.float32
    )
    d_normed_one = jnp.einsum(
        "cre,cde->rd", d_projected, qkv_full, preferred_element_type=jnp.float32
    )
    first_value, first_back = jax.vjp(
        layer_norm, tokens_f, gain_pair[0].astype(jnp.float32), bias_pair[0].astype(jnp.float32)
    )
    d_tokens_part, d_gain_one, d_bias_one = first_back(d_normed_one)
    grad_gains = grad_gains + jnp.stack([d_gain_one, d_gain_two])
    grad_biases = grad_biases + jnp.stack([d_bias_one, d_bias_two])
    input_rows = (d_resid + d_tokens_part).astype(jnp.bfloat16)
    return (
        input_rows,
        (grad_qkv, grad_out, grad_router, grad_gains, grad_biases, grad_in, grad_expert_out),
    )


def body(
    tokens,
    image_ids,
    routes,
    qkv_weight,
    out_weight,
    router_weight,
    norm_gains,
    norm_biases,
    expert_in,
    expert_out,
    cotangent,
):
    shard_experts = expert_in.shape[0]
    rim_rows = IMG - 1
    experts = shard_experts * lax.axis_size("expert")
    outputs = []
    saved_state = []
    for batch_index in range(MICRO):
        dense_set = fetch_dense(qkv_weight, out_weight, router_weight, norm_gains, norm_biases)
        expert_set = fetch_experts(expert_in, expert_out)
        ids_ext = padded(image_ids[batch_index] + 1, ((("dp", "expert"), 0),), rim_rows)
        route_plan = plan_routes(routes[batch_index], shard_experts)
        forward_state = run_forward(
            tokens[batch_index].astype(jnp.float32), ids_ext, route_plan, dense_set, expert_set
        )
        outputs.append(forward_state[-1].astype(jnp.bfloat16))
        saved_state.append((ids_ext, route_plan))
    gradients = (
        jnp.zeros((3, D, D), jnp.float32),
        jnp.zeros((D, D), jnp.float32),
        jnp.zeros((D, experts), jnp.float32),
        jnp.zeros((2, D), jnp.float32),
        jnp.zeros((2, D), jnp.float32),
        jnp.zeros((shard_experts, D, FF), jnp.float32),
        jnp.zeros((shard_experts, FF, D), jnp.float32),
    )
    input_grads = []
    for batch_index in range(MICRO):
        dense_set = fetch_dense(qkv_weight, out_weight, router_weight, norm_gains, norm_biases)
        expert_set = fetch_experts(expert_in, expert_out)
        ids_ext, route_plan = saved_state[batch_index]
        input_rows, gradients = run_backward(
            tokens[batch_index].astype(jnp.float32),
            ids_ext,
            route_plan,
            dense_set,
            expert_set,
            cotangent[batch_index].astype(jnp.float32),
            gradients,
        )
        input_grads.append(input_rows)
    grad_qkv, grad_out, grad_router, grad_gains, grad_biases, grad_in, grad_expert_out = gradients
    small = jnp.concatenate([grad_router, grad_gains.T, grad_biases.T], axis=1)
    small = jnp.pad(small, ((0, 0), (0, D - experts - 4)))
    packed = jnp.concatenate([grad_qkv, grad_out[None], small[None]], axis=0)
    packed = lax.psum_scatter(packed, ("dp", "expert"), scatter_dimension=1, tiled=True)
    dense_grads = (
        packed[:3],
        packed[3],
        packed[4][:, :experts],
        packed[4][:, experts : experts + 2].T,
        packed[4][:, experts + 2 : experts + 4].T,
    )
    expert_grads = (
        lax.psum_scatter(
            grad_in.astype(jnp.bfloat16), "dp", scatter_dimension=1, tiled=True
        ).astype(jnp.float32),
        lax.psum_scatter(
            grad_expert_out.astype(jnp.bfloat16), "dp", scatter_dimension=1, tiled=True
        ).astype(jnp.float32),
    )
    return (
        jnp.stack(outputs),
        jnp.stack(input_grads),
        dense_grads[0],
        dense_grads[1],
        dense_grads[2],
        dense_grads[3],
        dense_grads[4],
        expert_grads[0],
        expert_grads[1],
    )


def solution(mesh):
    return jax.shard_map(
        body,
        mesh=mesh,
        in_specs=(
            P(None, ("dp", "expert"), None),
            P(None, ("dp", "expert")),
            P(None, ("dp", "expert"), None),
            P(None, ("dp", "expert"), None),
            P(("dp", "expert"), None),
            P(("dp", "expert"), None),
            P(None, ("dp", "expert")),
            P(None, ("dp", "expert")),
            P("expert", "dp", None),
            P("expert", "dp", None),
            P(None, ("dp", "expert"), None),
        ),
        out_specs=(
            P(None, ("dp", "expert"), None),
            P(None, ("dp", "expert"), None),
            P(None, ("dp", "expert"), None),
            P(("dp", "expert"), None),
            P(("dp", "expert"), None),
            P(None, ("dp", "expert")),
            P(None, ("dp", "expert")),
            P("expert", "dp", None),
            P("expert", "dp", None),
        ),
        check_vma=False,
    )
```

```python
import functools
import math

import jax
import jax.numpy as jnp
from jax import lax
from jax.experimental import pallas as pl
from jax.experimental.pallas import tpu as pltpu
from jax.sharding import PartitionSpec as P

D = 512
HEADS = 8
HEAD_DIM = 64
FF = 2048
TOP = 2
IMG = 197
MICRO = 2


neg_big = -1e30
norm_eps = 1e-06
highest = lax.Precision.HIGHEST


def padded(cells, sides, width):
    for axis, dim in sides:
        count = lax.axis_size(axis)
        ends = count - 1
        head = lax.slice_in_dim(cells, 0, width, axis=dim)
        tail = lax.slice_in_dim(cells, cells.shape[dim] - width, cells.shape[dim], axis=dim)
        cells = jnp.concatenate(
            [
                lax.ppermute(tail, axis, [(i, (i + 1) % count) for i in range(ends)]),
                cells,
                lax.ppermute(head, axis, [((i + 1) % count, i) for i in range(ends)]),
            ],
            axis=dim,
        )
    return cells


def layer_norm(values, gain_row, bias_row):
    centre = jnp.mean(values, axis=-1, keepdims=True)
    offset = values - centre
    spread = jnp.mean(offset * offset, axis=-1, keepdims=True)
    return offset * lax.rsqrt(spread + norm_eps) * gain_row + bias_row


def tanh_gelu(values):
    return jax.nn.gelu(values, approximate=True)


def fetch_dense(qkv_weight, out_weight, router_weight, norm_gains, norm_biases):
    rows, experts = router_weight.shape
    small = jnp.concatenate([router_weight, norm_gains.T, norm_biases.T], axis=1)
    small = jnp.pad(small, ((0, 0), (0, D - experts - 4)))
    packed = jnp.concatenate([qkv_weight, out_weight[None], small[None]], axis=0)
    full = lax.all_gather(packed, ("dp", "expert"), axis=1, tiled=True)
    return (
        full[:3],
        full[3],
        full[4][:, :experts],
        full[4][:, experts : experts + 2].T,
        full[4][:, experts + 2 : experts + 4].T,
    )


def fetch_experts(expert_in, expert_out):
    return (
        lax.all_gather(expert_in, "dp", axis=1, tiled=True),
        lax.all_gather(expert_out, "dp", axis=1, tiled=True),
    )


def plan_routes(route_ids, shard_experts):
    row_count = route_ids.shape[0]
    experts = shard_experts * lax.axis_size("expert")
    devices = lax.axis_size(("dp", "expert"))
    slot_count = 2 * TOP * row_count // experts
    capacity = 5 * TOP * row_count * devices // (4 * experts)
    labels = lax.broadcasted_iota(jnp.int32, (1, experts), 1)
    first_hot = (route_ids[:, 0:1] == labels).astype(jnp.int32)
    second_hot = (route_ids[:, 1:2] == labels).astype(jnp.int32)
    counts = jnp.stack([jnp.sum(first_hot, axis=0), jnp.sum(second_hot, axis=0)])
    all_counts = lax.all_gather(counts[None], ("dp", "expert"), axis=0, tiled=True)
    earlier = (
        lax.broadcasted_iota(jnp.int32, (devices, 1, 1), 0) < lax.axis_index(("dp", "expert"))
    ).astype(jnp.int32)
    before = jnp.sum(all_counts * earlier, axis=0)
    total_first = jnp.sum(all_counts[:, 0, :], axis=0)
    row_before = (
        lax.broadcasted_iota(jnp.int32, (row_count, row_count), 0)
        > lax.broadcasted_iota(jnp.int32, (row_count, row_count), 1)
    ).astype(jnp.bfloat16)

    def rank_of(hot):
        ahead = jnp.dot(row_before, hot.astype(jnp.bfloat16), preferred_element_type=jnp.float32)
        return jnp.sum(ahead.astype(jnp.int32) * hot, axis=1)

    rank_first = rank_of(first_hot)
    rank_second = rank_of(second_hot)
    place_first = jnp.sum(first_hot * before[0][None, :], axis=1) + rank_first
    place_second = jnp.sum(second_hot * (total_first + before[1])[None, :], axis=1) + rank_second
    kept_mask = jnp.stack([place_first < capacity, place_second < capacity], axis=1)
    slot_second = jnp.sum(second_hot * counts[0][None, :], axis=1) + rank_second
    flat_index = jnp.stack(
        [route_ids[:, 0] * slot_count + rank_first, route_ids[:, 1] * slot_count + slot_second],
        axis=1,
    )
    target = jnp.where(kept_mask, flat_index, experts * slot_count)
    return (first_hot, second_hot, target, kept_mask.astype(jnp.float32))


def fill_slots(row_pairs, target, experts, slot_count):
    feature_count = row_pairs.shape[-1]
    buffer = jnp.zeros((experts * slot_count + 1, feature_count), row_pairs.dtype)
    buffer = buffer.at[target.reshape(-1)].set(row_pairs.reshape(-1, feature_count))
    return buffer[:-1].reshape(experts, 1, slot_count, feature_count)


def read_slots(returned, target):
    feature_count = returned.shape[-1]
    flat_table = jnp.concatenate(
        [returned.reshape(-1, feature_count), jnp.zeros((1, feature_count), returned.dtype)], axis=0
    )
    return flat_table[target]


def run_forward(tokens_f, ids_ext, route_plan, dense_set, expert_set):
    qkv_full, out_full, router_full, gain_pair, bias_pair = dense_set
    expert_up_weight, expert_down_weight = expert_set
    first_hot, second_hot, target, kept_mask = route_plan
    row_count = tokens_f.shape[0]
    rim_rows = IMG - 1
    score_scale = 1.0 / math.sqrt(HEAD_DIM)
    experts = router_full.shape[1]
    slot_count = 2 * TOP * row_count // experts
    normed_one = layer_norm(
        tokens_f, gain_pair[0].astype(jnp.float32), bias_pair[0].astype(jnp.float32)
    ).astype(jnp.bfloat16)
    projected = jnp.einsum(
        "rd,cde->cre", normed_one, qkv_full, preferred_element_type=jnp.float32
    ).astype(jnp.bfloat16)
    key_value = padded(projected[1:], ((("dp", "expert"), 1),), rim_rows)
    query_heads = projected[0].reshape(row_count, HEADS, HEAD_DIM)
    key_heads = key_value[0].reshape(-1, HEADS, HEAD_DIM)
    value_heads = key_value[1].reshape(-1, HEADS, HEAD_DIM)
    same_image = ids_ext[rim_rows : rim_rows + row_count][:, None] == ids_ext[None, :]
    scores = (
        jnp.einsum("qhd,khd->hqk", query_heads, key_heads, preferred_element_type=jnp.float32)
        * score_scale
    )
    scores = jnp.where(same_image[None], scores, neg_big)
    top_score = jnp.max(scores, axis=-1, keepdims=True)
    log_total = top_score + jnp.log(jnp.sum(jnp.exp(scores - top_score), axis=-1, keepdims=True))
    att_probs = jnp.exp(scores - log_total)
    att_low = att_probs.astype(jnp.bfloat16)
    mixed_rows = (
        jnp.einsum("hqk,khd->qhd", att_low, value_heads, preferred_element_type=jnp.float32)
        .reshape(row_count, D)
        .astype(jnp.bfloat16)
    )
    residual = tokens_f + jnp.dot(mixed_rows, out_full, preferred_element_type=jnp.float32)
    normed_two = layer_norm(
        residual, gain_pair[1].astype(jnp.float32), bias_pair[1].astype(jnp.float32)
    ).astype(jnp.bfloat16)
    router_probs = jax.nn.softmax(
        jnp.dot(normed_two, router_full, preferred_element_type=jnp.float32), axis=-1
    )
    picked = jnp.stack(
        [jnp.sum(first_hot * router_probs, axis=1), jnp.sum(second_hot * router_probs, axis=1)],
        axis=1,
    )
    gate_values = kept_mask * picked
    outgoing = fill_slots(
        jnp.broadcast_to(normed_two[:, None, :], (row_count, TOP, D)), target, experts, slot_count
    )
    arrived = lax.all_to_all(outgoing, "expert", split_axis=0, concat_axis=1, tiled=True)
    shard_experts = arrived.shape[0]
    collected_token_rows = arrived.reshape(shard_experts, -1, D)
    hidden_pre = jnp.einsum(
        "ycq,yqt->yct", collected_token_rows, expert_up_weight, preferred_element_type=jnp.float32
    )
    hidden_activation = tanh_gelu(hidden_pre).astype(jnp.bfloat16)
    produced = jnp.einsum(
        "nso,nop->nsp", hidden_activation, expert_down_weight, preferred_element_type=jnp.float32
    ).astype(jnp.bfloat16)
    returned = lax.all_to_all(
        produced.reshape(arrived.shape), "expert", split_axis=1, concat_axis=0, tiled=True
    )
    expert_rows = read_slots(returned, target)
    block_value = residual + jnp.sum(
        gate_values[:, :, None] * expert_rows.astype(jnp.float32), axis=1
    )
    return (
        normed_one,
        query_heads,
        key_heads,
        value_heads,
        att_probs,
        att_low,
        mixed_rows,
        residual,
        normed_two,
        router_probs,
        gate_values,
        collected_token_rows,
        hidden_pre,
        hidden_activation,
        expert_rows,
        block_value,
    )


def run_backward(tokens_f, ids_ext, route_plan, dense_set, expert_set, upstream, gradients):
    qkv_full, out_full, router_full, gain_pair, bias_pair = dense_set
    expert_up_weight, expert_down_weight = expert_set
    first_hot, second_hot, target, kept_mask = route_plan
    grad_qkv, grad_out, grad_router, grad_gains, grad_biases, grad_in, grad_expert_out = gradients
    (
        normed_one,
        query_heads,
        key_heads,
        value_heads,
        att_probs,
        att_low,
        mixed_rows,
        residual,
        normed_two,
        router_probs,
        gate_values,
        collected_token_rows,
        hidden_pre,
        hidden_activation,
        expert_rows,
        block_value,
    ) = run_forward(tokens_f, ids_ext, route_plan, dense_set, expert_set)
    row_count = tokens_f.shape[0]
    rim_rows = IMG - 1
    score_scale = 1.0 / math.sqrt(HEAD_DIM)
    experts = router_full.shape[1]
    slot_count = 2 * TOP * row_count // experts
    shard_experts = expert_up_weight.shape[0]
    d_gate = kept_mask * jnp.sum(upstream[:, None, :] * expert_rows.astype(jnp.float32), axis=-1)
    d_sent = (gate_values[:, :, None] * upstream[:, None, :]).astype(jnp.bfloat16)
    d_arrived = lax.all_to_all(
        fill_slots(d_sent, target, experts, slot_count),
        "expert",
        split_axis=0,
        concat_axis=1,
        tiled=True,
    )
    produced_rows_grad = d_arrived.reshape(shard_experts, -1, D)
    activation_grad = jnp.einsum(
        "tkw,tew->tke", produced_rows_grad, expert_down_weight, preferred_element_type=jnp.float32
    )
    grad_expert_out = grad_expert_out + jnp.einsum(
        "meq,mek->mqk", hidden_activation, produced_rows_grad, preferred_element_type=jnp.float32
    )
    gelu_value, gelu_back = jax.vjp(tanh_gelu, hidden_pre)
    preactivation_grad = gelu_back(activation_grad)[0].astype(jnp.bfloat16)
    grad_in = grad_in + jnp.einsum(
        "zjo,zjm->zom", collected_token_rows, preactivation_grad, preferred_element_type=jnp.float32
    )
    d_rows = jnp.einsum(
        "iht,imt->ihm", preactivation_grad, expert_up_weight, preferred_element_type=jnp.float32
    ).astype(jnp.bfloat16)
    d_back = lax.all_to_all(
        d_rows.reshape(d_arrived.shape), "expert", split_axis=1, concat_axis=0, tiled=True
    )
    d_normed_two = jnp.sum(
        kept_mask[:, :, None] * read_slots(d_back, target).astype(jnp.float32), axis=1
    )
    d_probs = first_hot * d_gate[:, 0:1] + second_hot * d_gate[:, 1:2]
    d_logits = router_probs * (d_probs - jnp.sum(router_probs * d_probs, axis=-1, keepdims=True))
    router_wide = router_full.astype(jnp.float32)
    d_normed_two = d_normed_two + jnp.dot(d_logits, router_wide.T, precision=highest)
    grad_router = grad_router + jnp.dot(
        normed_two.astype(jnp.float32).T, d_logits, precision=highest
    )
    norm_value, second_back = jax.vjp(
        layer_norm, residual, gain_pair[1].astype(jnp.float32), bias_pair[1].astype(jnp.float32)
    )
    d_resid_part, d_gain_two, d_bias_two = second_back(d_normed_two)
    d_resid = upstream + d_resid_part
    d_attn = d_resid.astype(jnp.bfloat16)
    grad_out = grad_out + jnp.einsum(
        "rd,re->de", mixed_rows, d_attn, preferred_element_type=jnp.float32
    )
    d_mixed = (
        jnp.einsum("re,de->rd", d_attn, out_full, preferred_element_type=jnp.float32)
        .astype(jnp.bfloat16)
        .reshape(row_count, HEADS, HEAD_DIM)
    )
    d_att = jnp.einsum("qhd,khd->hqk", d_mixed, value_heads, preferred_element_type=jnp.float32)
    d_scores = (att_probs * (d_att - jnp.sum(att_probs * d_att, axis=-1, keepdims=True))).astype(
        jnp.bfloat16
    )
    d_query = (
        (
            jnp.einsum("hqk,khd->qhd", d_scores, key_heads, preferred_element_type=jnp.float32)
            * score_scale
        )
        .astype(jnp.bfloat16)
        .reshape(row_count, D)
    )
    d_key = (
        jnp.einsum("hqk,qhd->khd", d_scores, query_heads, preferred_element_type=jnp.float32)
        * score_scale
    )
    d_value = jnp.einsum("hqk,qhd->khd", att_low, d_mixed, preferred_element_type=jnp.float32)
    d_pair = jnp.stack([d_key.reshape(-1, D), d_value.reshape(-1, D)])
    rim_grads = jnp.concatenate([d_pair[:, :rim_rows], d_pair[:, rim_rows + row_count :]], axis=1)
    beside_all = padded(rim_grads.astype(jnp.bfloat16), ((("dp", "expert"), 1),), rim_rows).astype(
        rim_grads.dtype
    )
    own_part = d_pair[:, rim_rows : rim_rows + row_count]
    from_below = jnp.pad(beside_all[:, :rim_rows], ((0, 0), (0, row_count - rim_rows), (0, 0)))
    from_above = jnp.pad(beside_all[:, 3 * rim_rows :], ((0, 0), (row_count - rim_rows, 0), (0, 0)))
    d_kv = (own_part + from_below + from_above).astype(jnp.bfloat16)
    d_projected = jnp.concatenate([d_query[None], d_kv], axis=0)
    grad_qkv = grad_qkv + jnp.einsum(
        "rd,cre->cde", normed_one, d_projected, preferred_element_type=jnp.float32
    )
    d_normed_one = jnp.einsum(
        "cre,cde->rd", d_projected, qkv_full, preferred_element_type=jnp.float32
    )
    first_value, first_back = jax.vjp(
        layer_norm, tokens_f, gain_pair[0].astype(jnp.float32), bias_pair[0].astype(jnp.float32)
    )
    d_tokens_part, d_gain_one, d_bias_one = first_back(d_normed_one)
    grad_gains = grad_gains + jnp.stack([d_gain_one, d_gain_two])
    grad_biases = grad_biases + jnp.stack([d_bias_one, d_bias_two])
    input_rows = (d_resid + d_tokens_part).astype(jnp.bfloat16)
    return (
        input_rows,
        (grad_qkv, grad_out, grad_router, grad_gains, grad_biases, grad_in, grad_expert_out),
    )


def body(
    tokens,
    image_ids,
    routes,
    qkv_weight,
    out_weight,
    router_weight,
    norm_gains,
    norm_biases,
    expert_in,
    expert_out,
    cotangent,
):
    shard_experts = expert_in.shape[0]
    rim_rows = IMG - 1
    experts = shard_experts * lax.axis_size("expert")
    outputs = []
    saved_state = []
    for batch_index in range(MICRO):
        dense_set = fetch_dense(qkv_weight, out_weight, router_weight, norm_gains, norm_biases)
        expert_set = fetch_experts(expert_in, expert_out)
        ids_ext = padded(image_ids[batch_index] + 1, ((("dp", "expert"), 0),), rim_rows)
        route_plan = plan_routes(routes[batch_index], shard_experts)
        forward_state = run_forward(
            tokens[batch_index].astype(jnp.float32), ids_ext, route_plan, dense_set, expert_set
        )
        outputs.append(forward_state[-1].astype(jnp.bfloat16))
        saved_state.append((ids_ext, route_plan))
    gradients = (
        jnp.zeros((3, D, D), jnp.float32),
        jnp.zeros((D, D), jnp.float32),
        jnp.zeros((D, experts), jnp.float32),
        jnp.zeros((2, D), jnp.float32),
        jnp.zeros((2, D), jnp.float32),
        jnp.zeros((shard_experts, D, FF), jnp.float32),
        jnp.zeros((shard_experts, FF, D), jnp.float32),
    )
    input_grads = []
    for batch_index in range(MICRO):
        dense_set = fetch_dense(qkv_weight, out_weight, router_weight, norm_gains, norm_biases)
        expert_set = fetch_experts(expert_in, expert_out)
        ids_ext, route_plan = saved_state[batch_index]
        input_rows, gradients = run_backward(
            tokens[batch_index].astype(jnp.float32),
            ids_ext,
            route_plan,
            dense_set,
            expert_set,
            cotangent[batch_index].astype(jnp.float32),
            gradients,
        )
        input_grads.append(input_rows)
    grad_qkv, grad_out, grad_router, grad_gains, grad_biases, grad_in, grad_expert_out = gradients
    small = jnp.concatenate([grad_router, grad_gains.T, grad_biases.T], axis=1)
    small = jnp.pad(small, ((0, 0), (0, D - experts - 4)))
    packed = jnp.concatenate([grad_qkv, grad_out[None], small[None]], axis=0)
    packed = lax.psum_scatter(packed, ("dp", "expert"), scatter_dimension=1, tiled=True)
    dense_grads = (
        packed[:3],
        packed[3],
        packed[4][:, :experts],
        packed[4][:, experts : experts + 2].T,
        packed[4][:, experts + 2 : experts + 4].T,
    )
    expert_grads = (
        lax.psum_scatter(
            grad_in.astype(jnp.bfloat16), "dp", scatter_dimension=1, tiled=True
        ).astype(jnp.float32),
        lax.psum_scatter(
            grad_expert_out.astype(jnp.bfloat16), "dp", scatter_dimension=1, tiled=True
        ).astype(jnp.float32),
    )
    return (
        jnp.stack(outputs),
        jnp.stack(input_grads),
        dense_grads[0],
        dense_grads[1],
        dense_grads[2],
        dense_grads[3],
        dense_grads[4],
        expert_grads[0],
        expert_grads[1],
    )


MESH = pl.DeviceIdType.MESH
f32, bf16 = jnp.float32, jnp.bfloat16
VMEM_BYTES = 62 << 20


def mm(a, b):
    return jnp.dot(a, b, preferred_element_type=f32)


def mm_nt(a, b):
    return lax.dot_general(a, b, (((1,), (1,)), ((), ())), preferred_element_type=f32)


def normed(values, gain_row, bias_row):
    centre = jnp.mean(values, axis=-1, keepdims=True)
    offset = values - centre
    spread = jnp.mean(offset * offset, axis=-1, keepdims=True)
    return offset * lax.rsqrt(spread + norm_eps) * gain_row + bias_row


class Wire:
    def __init__(self, send_sems, recv_sems, other):
        self.send_sems, self.recv_sems, self.other = send_sems, recv_sems, other
        self.used, self.sent = 0, {}

    def roles(self, count=1):
        self.used += count
        return self.used - count

    def copy(self, send_role, recv_role, src, dst, device):
        return pltpu.make_async_remote_copy(
            src_ref=src,
            dst_ref=dst,
            send_sem=self.send_sems.at[send_role],
            recv_sem=self.recv_sems.at[recv_role],
            device_id=device,
            device_id_type=MESH,
        )

    def send(self, role, src, dst, device, recv_role=None):
        self.copy(role, role if recv_role is None else recv_role, src, dst, device).start()

    def arrive(self, role, like):
        self.copy(role, role, like, like, self.other).wait_recv()

    def left(self, role, like):
        self.copy(role, role, like, like, self.other).wait_send()


class Place:
    def __init__(self, nd, ne):
        self.nd, self.ne = nd, ne
        self.d, self.z = lax.axis_index("dp"), lax.axis_index("expert")
        d, z = self.d, self.z
        self.c = lax.rem(d, 2)
        self.sib_d = d + 1 - 2 * self.c
        self.sib = (self.sib_d, z)
        self.idx = d * ne + z
        last = (z == ne - 1).astype(jnp.int32)
        first = (z == 0).astype(jnp.int32)
        self.next = (lax.rem(d + last, nd), lax.rem(z + 1, ne))
        self.prev = (lax.rem(d + nd - first, nd), lax.rem(z + ne - 1, ne))
        self.up = (d, jnp.minimum(z + 1, ne - 1))
        self.down = (d, jnp.maximum(z - 1, 0))

    def chip(self, k):
        return lax.rem(self.d + 2 * k, self.nd)

    def enter(self):
        bar = pltpu.get_barrier_semaphore()

        def greet(device):
            pl.semaphore_signal(bar, inc=1, device_id=device, device_id_type=MESH)

        for k in range(1, self.nd):
            greet((lax.rem(self.d + k, self.nd), self.z))
        for k in range(1, self.ne):
            zk = lax.rem(self.z + k, self.ne)
            greet((self.d, zk))
            greet((self.sib_d, zk))
        greet(self.next)
        greet(self.prev)
        pl.semaphore_wait(bar, self.nd - 1 + 2 * (self.ne - 1) + 2)


class Chain:
    def __init__(self, wire, me, full):
        self.wire, self.me, self.full = wire, me, full
        n = me.ne
        self.up, self.dn = wire.roles(n - 1), wire.roles(n - 1)
        self.su, self.sd, self.so = wire.roles(n - 1), wire.roles(n - 1), wire.roles()

    def at(self, z):
        return self.full.at[z * 2 + self.me.c]

    def own(self, src):
        m, n = self.me, self.me.ne

        @pl.when(m.z < n - 1)
        def _():
            self.wire.send(self.up, src, self.at(m.z), m.up)

        @pl.when(m.z > 0)
        def _():
            self.wire.send(self.dn, src, self.at(m.z), m.down)

        self.wire.send(self.so, src, self.at(m.z), m.sib)

    def pump(self, k):
        m, n, w = self.me, self.me.ne, self.wire

        @pl.when(m.z >= k + 1)
        def _():
            block = self.at(m.z - 1 - k)
            w.arrive(self.up + k, block)
            if k + 1 < n - 1:

                @pl.when(m.z < n - 1)
                def _():
                    w.send(self.up + k + 1, block, block, m.up)

            w.send(self.su + k, block, block, m.sib)

        @pl.when(m.z + k + 1 < n)
        def _():
            block = self.at(m.z + 1 + k)
            w.arrive(self.dn + k, block)
            if k + 1 < n - 1:

                @pl.when(m.z > 0)
                def _():
                    w.send(self.dn + k + 1, block, block, m.down)

            w.send(self.sd + k, block, block, m.sib)

    def finish(self):
        m, n, w, like = self.me, self.me.ne, self.wire, self.full.at[0]
        w.arrive(self.so, like)
        for k in range(n - 1):

            @pl.when(m.z >= k + 1)
            def _():
                w.arrive(self.su + k, like)

            @pl.when(m.z + k + 1 < n)
            def _():
                w.arrive(self.sd + k, like)

    def drain(self):
        m, n, w, like = self.me, self.me.ne, self.wire, self.full.at[0]
        w.left(self.so, like)
        for k in range(n - 1):

            @pl.when((m.z < n - 1) & (m.z >= k))
            def _():
                w.left(self.up + k, like)

            @pl.when((m.z > 0) & (m.z + k < n))
            def _():
                w.left(self.dn + k, like)

            @pl.when(m.z >= k + 1)
            def _():
                w.left(self.su + k, like)

            @pl.when(m.z + k + 1 < n)
            def _():
                w.left(self.sd + k, like)


def front_kernel(
    nd,
    ne,
    tok,
    ids,
    routes,
    qkv,
    outw,
    small,
    win,
    wout,
    cot,
    o_block,
    o_din,
    o_dprobs,
    o_up,
    o_down,
    o_n2,
    o_probs,
    o_resid,
    o_mixed,
    o_qkv,
    o_lse,
    w_all,
    o_small,
    o_idr,
    s_src,
    s_all,
    hp,
    hn,
    ip,
    inx,
    gx,
    gd,
    wu,
    wd,
    rk_src,
    rk,
    hnorm,
    bias,
    d_wu,
    d_wd,
    pm,
    xs,
    ds,
    deo,
    xt,
    dt,
    gt,
    acc_eo,
    acc_di,
    ys,
    qo,
    cs,
    cr,
    ud,
    dgs,
    dg,
    send_sems,
    recv_sems,
    local_sems,
):
    me = Place(nd, ne)
    d, z, c = me.d, me.z, me.c
    rows = tok.shape[1]
    share = qkv.shape[1]
    experts = 2 * ne
    halo = hp.shape[1]
    ext = 3 * rows
    slots = 4 * rows // experts
    capacity = 5 * TOP * rows * nd * ne // (4 * experts)
    e = 2 * z + c
    wire = Wire(send_sems, recv_sems, me.sib)
    lane = lax.broadcasted_iota(jnp.int32, (1, 128), 1)

    before_row = (
        lax.broadcasted_iota(jnp.int32, (rows, rows), 0)
        > lax.broadcasted_iota(jnp.int32, (rows, rows), 1)
    ).astype(bf16)
    hots = []
    s_src[0:share, :] = small[...]
    s_src[share : share + 16, :] = jnp.zeros((16, 128), bf16)
    row16 = lax.broadcasted_iota(jnp.int32, (16, 128), 0)
    counts = jnp.zeros((16, 128), f32)
    for mb in range(MICRO):
        pair = [(routes[mb, :, k : k + 1] == lane).astype(f32) for k in range(TOP)]
        hots.append(pair)
        for k in range(TOP):
            counts = jnp.where(row16 == mb * TOP + k, jnp.sum(pair[k], axis=0, keepdims=True), counts)
    s_src[share : share + 16, :] = counts.astype(bf16)

    me.enter()

    r_dz = wire.roles(3 * (ne - 1))
    mine = pl.ds(pl.multiple_of(me.idx * share, 16), share)
    for k in range(1, ne):
        dev = (d, lax.rem(z + k, ne))
        wire.send(r_dz + 3 * (k - 1), qkv, w_all.at[pl.ds(0, 3), mine], dev)
        wire.send(r_dz + 3 * (k - 1) + 1, outw, w_all.at[3, mine], dev)
        wire.send(r_dz + 3 * (k - 1) + 2, s_src, s_all.at[me.idx], dev)
    local = [
        pltpu.make_async_copy(qkv, w_all.at[pl.ds(0, 3), mine], local_sems.at[0]),
        pltpu.make_async_copy(outw, w_all.at[3, mine], local_sems.at[1]),
        pltpu.make_async_copy(s_src, s_all.at[me.idx], local_sems.at[2]),
    ]
    for cp in local:
        cp.start()
    r_id = wire.roles(2)
    wire.send(r_id, ids, ip, me.next)
    wire.send(r_id + 1, ids, inx, me.prev)
    r_h = wire.roles(2 * MICRO)
    for mb in range(MICRO):
        wire.send(r_h + 2 * mb, tok.at[mb, pl.ds(rows - halo, halo)], hp.at[mb], me.next)
        wire.send(r_h + 2 * mb + 1, tok.at[mb, pl.ds(0, halo)], hn.at[mb], me.prev)
    g_d = [Chain(wire, me, gd.at[mb]) for mb in range(MICRO)]
    g_x = [Chain(wire, me, gx.at[mb]) for mb in range(MICRO)]
    own_d = [
        pltpu.make_async_copy(cot.at[mb], gd.at[mb, z * 2 + c], local_sems.at[3 + mb])
        for mb in range(MICRO)
    ]
    for cp in own_d:
        cp.start()
    g_d[0].own(cot.at[0])

    for cp in local:
        cp.wait()
    for k in range(1, ne):
        wire.arrive(r_dz + 3 * (k - 1), qkv)
        wire.arrive(r_dz + 3 * (k - 1) + 1, outw)
        wire.arrive(r_dz + 3 * (k - 1) + 2, s_src)

    def column(dd):
        at = pl.ds(pl.multiple_of(dd * (ne * share), 16), ne * share)
        return w_all.at[:, at], s_all.at[pl.ds(dd * ne, ne)]

    chips = nd // 2
    r_dx = wire.roles(2 * (chips - 1))
    r_ds = wire.roles(2 * chips)
    blk, sblk = column(d)
    for k in range(1, chips):
        wire.send(r_dx + 2 * (k - 1), blk, blk, (me.chip(k), z))
        wire.send(r_dx + 2 * (k - 1) + 1, sblk, sblk, (me.chip(k), z))
    wire.send(r_ds, blk, blk, me.sib)
    wire.send(r_ds + 1, sblk, sblk, me.sib)
    up_rows, down_rows = win.shape[1], wout.shape[1]
    at_up = pl.ds(pl.multiple_of(d * up_rows, 16), up_rows)
    at_down = pl.ds(pl.multiple_of(d * down_rows, 16), down_rows)
    r_w = wire.roles(2 * (nd - 1))
    own_w = [
        pltpu.make_async_copy(win.at[c], wu.at[at_up], local_sems.at[5]),
        pltpu.make_async_copy(wout.at[c], wd.at[at_down], local_sems.at[6]),
    ]
    for cp in own_w:
        cp.start()
    for k in range(1, nd):
        dd = lax.rem(d + k, nd)
        cc = lax.rem(dd, 2)
        wire.send(r_w + 2 * (k - 1), win.at[cc], wu.at[at_up], (dd, z))
        wire.send(r_w + 2 * (k - 1) + 1, wout.at[cc], wd.at[at_down], (dd, z))
    g_d[0].pump(0)
    for k in range(1, chips):
        wire.arrive(r_dx + 2 * (k - 1), blk)
        wire.arrive(r_dx + 2 * (k - 1) + 1, sblk)
        b, sb = column(lax.rem(d + nd - 2 * k, nd))
        wire.send(r_ds + 2 * k, b, b, me.sib)
        wire.send(r_ds + 2 * k + 1, sb, sb, me.sib)
    for k in range(chips):
        wire.arrive(r_ds + 2 * k, blk)
        wire.arrive(r_ds + 2 * k + 1, sblk)

    o_small[...] = s_all[:, 0:share, :].reshape(D, 128).astype(f32)
    s_rows = o_small[...].T
    all_counts = s_all[:, share : share + 16, :].astype(f32)
    ahead = lax.broadcasted_iota(jnp.int32, all_counts.shape, 0) < me.idx
    before = jnp.sum(jnp.where(ahead, all_counts, 0.0), axis=0)
    total = jnp.sum(all_counts, axis=0)
    gains = [s_rows[experts + k : experts + k + 1, :] for k in range(2)]
    biases = [s_rows[experts + 2 + k : experts + 3 + k, :] for k in range(2)]

    for mb in range(MICRO):
        one, two = hots[mb]
        rank_one = mm(before_row, one.astype(bf16))
        rank_two = mm(before_row, two.astype(bf16))
        b1, b2 = before[2 * mb : 2 * mb + 1], before[2 * mb + 1 : 2 * mb + 2]
        t1 = total[2 * mb : 2 * mb + 1]
        place_one = jnp.sum(one * (b1 + rank_one), axis=1, keepdims=True)
        place_two = jnp.sum(two * (t1 + b2 + rank_two), axis=1, keepdims=True)
        kept = one * (place_one < capacity).astype(f32) + two * (place_two < capacity).astype(f32)
        ranks = jnp.where(kept > 0.0, rank_one + rank_two, -1.0)
        rk_src[mb] = ranks.T[0:experts, :]
    r_rk = wire.roles(2 * ne)
    s_me = z * 2 + c
    for k in range(ne):
        zk = lax.rem(z + k, ne)
        if k > 0:
            wire.send(r_rk + 2 * k, rk_src, rk.at[s_me], (d, zk))
        wire.send(r_rk + 2 * k + 1, rk_src, rk.at[s_me], (me.sib_d, zk))
    rk[s_me] = rk_src[...]
    g_d[0].pump(1)

    wire.arrive(r_id, ids)
    wire.arrive(r_id + 1, ids)
    pos = lax.broadcasted_iota(jnp.int32, (1, rows), 1)
    gap = rows - halo
    for mb in range(MICRO):
        here = ids[mb : mb + 1, :].astype(f32)
        below = jnp.where((pos >= gap) & (me.idx > 0), ip[mb : mb + 1, :].astype(f32), -1.0)
        above = jnp.where(
            (pos < halo) & (me.idx < nd * ne - 1), inx[mb : mb + 1, :].astype(f32), -1.0
        )
        o_idr[mb] = jnp.concatenate([below, here, above], axis=1)

    zero_gap = jnp.zeros((gap, D), bf16)
    hnorm[0:gap, :] = zero_gap
    hnorm[ext - gap : ext, :] = zero_gap
    scale = 1.0 / math.sqrt(HEAD_DIM)
    for mb in range(MICRO):
        wire.arrive(r_h + 2 * mb, hp.at[mb])
        wire.arrive(r_h + 2 * mb + 1, hn.at[mb])

        def put(value, start):
            hnorm[start : start + value.shape[0], :] = normed(
                value.astype(f32), gains[0], biases[0]
            ).astype(bf16)

        put(hp[mb], gap)
        put(tok[mb], rows)
        put(hn[mb], 2 * rows)
        for k in range(3):
            for r in range(3):
                part = slice(r * rows, (r + 1) * rows)
                o_qkv[mb, k, part, :] = mm(hnorm[part, :], w_all[k]).astype(bf16)
        g_d[0].pump(2) if mb == 0 else g_x[0].pump(0)
        idr = o_idr[mb]
        idc = jnp.broadcast_to(idr[:, rows : 2 * rows], (128, rows)).T[:, 0:1]
        bias[...] = jnp.where(idc == idr, 0.0, neg_big)
        o_lse[mb] = jnp.zeros((rows, 128), f32)

        @pl.loop(0, HEADS // 2)
        def _(pair):
            at = pl.ds(pl.multiple_of(pair * 128, 128), 128)
            query = o_qkv[mb, 0, rows : 2 * rows, at]
            key = o_qkv[mb, 1, :, at]
            value = o_qkv[mb, 2, :, at]
            mixed = jnp.zeros((rows, 128), f32)
            lse = o_lse[mb]
            for half in range(2):
                keep = (lane < 64) if half == 0 else (lane >= 64)
                q = jnp.where(keep, query, jnp.zeros_like(query))
                v = jnp.where(keep, value, jnp.zeros_like(value))
                s = mm_nt(q, key) * scale + bias[...]
                top = jnp.max(s, axis=-1, keepdims=True)
                p = jnp.exp(s - top)
                total_p = jnp.sum(p, axis=-1, keepdims=True)
                mixed = mixed + mm((p * (1.0 / total_p)).astype(bf16), v)
                lse = jnp.where(lane == 2 * pair + half, top + jnp.log(total_p), lse)
            o_lse[mb] = lse
            o_mixed[mb, :, at] = mixed.astype(bf16)

        if mb == 1:
            g_x[0].pump(1)
        resid = tok[mb].astype(f32) + mm(o_mixed[mb], w_all[3])
        o_resid[mb] = resid
        n2 = normed(resid, gains[1], biases[1]).astype(bf16)
        o_n2[mb] = n2
        gx[mb, s_me] = n2
        g_x[mb].own(gx.at[mb, s_me])
        if mb == 0:
            g_d[1].own(cot.at[1])
        logits = mm(n2, o_small[...].astype(bf16))
        logits = jnp.where(lane < experts, logits, neg_big)
        p = jnp.exp(logits - jnp.max(logits, axis=-1, keepdims=True))
        o_probs[mb] = p / jnp.sum(p, axis=-1, keepdims=True)
    g_x[0].pump(2)

    for cp in own_w + own_d:
        cp.wait()
    for k in range(1, nd):
        wire.arrive(r_w + 2 * (k - 1), win.at[0])
        wire.arrive(r_w + 2 * (k - 1) + 1, wout.at[0])
    for k in range(ne):
        if k > 0:
            wire.arrive(r_rk + 2 * k, rk_src)
        wire.arrive(r_rk + 2 * k + 1, rk_src)
    g_d[0].finish()
    g_x[0].finish()
    d_wu[...] = jnp.zeros_like(d_wu)
    d_wd[...] = jnp.zeros_like(d_wd)

    r_cx = wire.roles(2 * MICRO * ne)
    r_up = wire.roles(2 * MICRO * ne)
    r_dn = wire.roles(2 * MICRO * ne)
    r_dg = wire.roles(MICRO * 2 * ne)
    sub = lax.broadcasted_iota(jnp.int32, (slots, rows), 0).astype(f32)
    tile = 2 * slots
    chunk = 512

    def start_sums(mb):
        for t in range(2):
            for zp in range(ne):
                wire.arrive(r_cx + (mb * 2 + t) * ne + zp, qo.at[0, 0, 0])
                qo[mb, t, zp] = (qo[mb, t, zp].astype(f32) + cr[mb, t, zp].astype(f32)).astype(bf16)

        @pl.when(z == 0)
        def _():
            for t in range(2):
                for to in range(ne - 1, 0, -1):
                    wire.send(
                        r_up + (mb * 2 + t) * ne + to, qo.at[mb, t, to], ud.at[mb, t, to], me.up
                    )

        @pl.when(z == ne - 1)
        def _():
            for t in range(2):
                for to in range(ne - 1):
                    slot = jnp.where(z - 1 == to, ne, to)
                    wire.send(
                        r_dn + (mb * 2 + t) * ne + to, qo.at[mb, t, to], ud.at[mb, t, slot], me.down
                    )

    def pass_sums(mb):
        for t in range(2):
            for k in range(ne - 1):
                to = ne - 1 - k

                @pl.when((z > 0) & (z < to))
                def _():
                    wire.arrive(r_up + (mb * 2 + t) * ne + to, qo.at[0, 0, 0])
                    qo[mb, t, to] = (
                        qo[mb, t, to].astype(f32) + ud[mb, t, to].astype(f32)
                    ).astype(bf16)
                    wire.send(
                        r_up + (mb * 2 + t) * ne + to, qo.at[mb, t, to], ud.at[mb, t, to], me.up
                    )

                @pl.when((z < ne - 1) & (z > k))
                def _():
                    wire.arrive(r_dn + (mb * 2 + t) * ne + k, qo.at[0, 0, 0])
                    qo[mb, t, k] = (
                        qo[mb, t, k].astype(f32) + ud[mb, t, k].astype(f32)
                    ).astype(bf16)
                    slot = jnp.where(z - 1 == k, ne, k)
                    wire.send(
                        r_dn + (mb * 2 + t) * ne + k, qo.at[mb, t, k], ud.at[mb, t, slot], me.down
                    )

    def end_sums(mb, t):
        out = qo[mb, t, z].astype(f32)
        acc_eo[...] = out

        @pl.when(z > 0)
        def _():
            wire.arrive(r_up + (mb * 2 + t) * ne + z, qo.at[0, 0, 0])
            acc_eo[...] += ud[mb, t, z].astype(f32)

        @pl.when(z < ne - 1)
        def _():
            wire.arrive(r_dn + (mb * 2 + t) * ne + z, qo.at[0, 0, 0])
            acc_eo[...] += ud[mb, t, ne].astype(f32)

        return acc_eo[...]

    @pl.loop(0, MICRO * ne)
    def _(i):
        mb, zi = i // ne, lax.rem(i, ne)
        zp = lax.rem(zi * (ne - 1), ne)

        @pl.when(i == ne)
        def _():
            start_sums(0)
            for k in range(ne - 1):
                g_d[1].pump(k)
                g_x[1].pump(k)
            g_d[1].finish()
            g_x[1].finish()

        for cc in range(2):
            s = zp * 2 + cc
            at = slice(cc * slots, (cc + 1) * slots)
            pick = (sub == rk[s, mb, pl.ds(e, 1), :]).astype(bf16)
            pm[cc] = pick
            xs[at, :] = mm(pick, gx[mb, s]).astype(bf16)
            ds[at, :] = mm(pick, gd[mb, s]).astype(bf16)
        x = xs[...]
        logits = mm(x, o_small[...].astype(bf16))
        logits = jnp.where(lane < experts, logits, neg_big)
        p = jnp.exp(logits - jnp.max(logits, axis=-1, keepdims=True))
        p = p / jnp.sum(p, axis=-1, keepdims=True)
        gate = jnp.sum(jnp.where(lane == e, p, 0.0), axis=-1, keepdims=True)
        gt[...] = jnp.broadcast_to(gate, (tile, 128))
        dy = (gate * ds[...].astype(f32)).astype(bf16)
        deo[...] = dy
        xt[...] = x.T
        dt[...] = dy.T
        acc_eo[...] = jnp.zeros_like(acc_eo)
        acc_di[...] = jnp.zeros_like(acc_di)

        @pl.loop(0, FF // chunk)
        def _(f):
            at = pl.ds(pl.multiple_of(f * chunk, chunk), chunk)
            pre = mm(xs[...], wu[:, at])
            sq = pre * pre
            k0 = math.sqrt(2.0 / math.pi)
            th = jnp.tanh(pre * (k0 + (k0 * 0.044715) * sq))
            half = 0.5 + 0.5 * th
            act = (pre * half).astype(bf16)
            slope = half + (0.5 * pre) * (1.0 - th * th) * (k0 + (3.0 * k0 * 0.044715) * sq)
            acc_eo[...] += mm(act, wd[at, :])
            d_act = mm_nt(deo[...], wd[at, :])
            d_pre = (slope * d_act).astype(bf16)
            acc_di[...] += mm_nt(d_pre, wu[:, at])
            d_wu[:, at] += mm(xt[...], d_pre)
            d_wd[:, at] += mm(dt[...], act)

        eo = acc_eo[...].astype(bf16).astype(f32)
        d_gate = jnp.sum(ds[...].astype(f32) * eo, axis=-1, keepdims=True)
        ys[0] = acc_di[...].astype(bf16)
        ys[1] = (gt[:, 0:1] * eo).astype(bf16)
        for own in range(2):
            cc = c if own else 1 - c
            back = pm[cc].T
            at = pl.ds(pl.multiple_of(cc * slots, slots), slots)
            for t in range(2):
                moved = mm(back, ys[t, at, :]).astype(bf16)
                if own:
                    qo[mb, t, zp] = moved
                else:
                    cs[mb, t, zp] = moved
        for t in range(2):
            role = r_cx + (mb * 2 + t) * ne + zp
            wire.send(role, cs.at[mb, t, zp], cr.at[mb, t, zp], me.sib)
        for cc in range(2):
            at = slice(cc * slots, (cc + 1) * slots)
            line = jnp.sum(pm[cc].astype(f32) * d_gate[at], axis=0, keepdims=True)
            to = zp * 2 + cc
            dgs[mb, to] = jnp.broadcast_to(line, (8, rows))

            @pl.when(to != s_me)
            def _():
                wire.send(
                    r_dg + mb * 2 * ne + to,
                    dgs.at[mb, to],
                    dg.at[mb, e],
                    (d - c + cc, zp),
                    recv_role=r_dg + mb * 2 * ne + s_me,
                )

            @pl.when(to == s_me)
            def _():
                dg[mb, e] = jnp.broadcast_to(line, (8, rows))

    pass_sums(0)
    start_sums(1)
    g_d[0].drain()
    out_copies = []
    for h in range(2):
        for q in range(4):
            at = (slice(h * 256, (h + 1) * 256), slice(q * chunk, (q + 1) * chunk))
            wu[at] = d_wu[at].astype(bf16)
            gd[0, h * 4 + q] = d_wd[at].astype(bf16)
            to = o_down.at[pl.ds(h * 256, 256), pl.ds(q * chunk, chunk)]
            out_copies.append(pltpu.make_async_copy(gd.at[0, h * 4 + q], to, local_sems.at[h * 4 + q]))
    out_copies.append(pltpu.make_async_copy(wu, o_up, local_sems.at[8]))
    for cp in out_copies:
        cp.start()

    def outputs(mb):
        o_din[mb] = end_sums(mb, 0)
        o_block[mb] = (o_resid[mb] + end_sums(mb, 1)).astype(bf16)

    outputs(0)
    pass_sums(1)
    outputs(1)
    for mb in range(MICRO):
        for s in range(2 * ne):

            @pl.when(s != s_me)
            def _():
                wire.arrive(r_dg + mb * 2 * ne + s, dgs.at[0, 0])

        groups = []
        sub8 = lax.broadcasted_iota(jnp.int32, (8, rows), 0)
        for base in range(0, experts, 8):
            group = dg[mb, base]
            for j in range(1, 8):
                group = jnp.where(sub8 == j, dg[mb, base + j], group)
            groups.append(group)
        lines = jnp.concatenate(groups + [jnp.zeros((128 - experts, rows), f32)], axis=0)
        o_dprobs[mb] = lines.T

    for cp in out_copies:
        cp.wait()
    for k in range(1, ne):
        wire.left(r_dz + 3 * (k - 1), qkv)
        wire.left(r_dz + 3 * (k - 1) + 1, outw)
        wire.left(r_dz + 3 * (k - 1) + 2, s_src)
    wire.left(r_id, ids)
    wire.left(r_id + 1, ids)
    for k in range(2 * MICRO):
        wire.left(r_h + k, hp.at[0])
    for k in range(1, chips):
        wire.left(r_dx + 2 * (k - 1), blk)
        wire.left(r_dx + 2 * (k - 1) + 1, sblk)
    for k in range(chips):
        wire.left(r_ds + 2 * k, blk)
        wire.left(r_ds + 2 * k + 1, sblk)
    for k in range(1, nd):
        wire.left(r_w + 2 * (k - 1), win.at[0])
        wire.left(r_w + 2 * (k - 1) + 1, wout.at[0])
    for k in range(ne):
        if k > 0:
            wire.left(r_rk + 2 * k, rk_src)
        wire.left(r_rk + 2 * k + 1, rk_src)
    for g in [g_d[1]] + g_x:
        g.drain()
    for mb in range(MICRO):
        for t in range(2):
            base = (mb * 2 + t) * ne
            for zp in range(ne):
                wire.left(r_cx + base + zp, qo.at[0, 0, 0])
            for to in range(1, ne):

                @pl.when(z < to)
                def _():
                    wire.left(r_up + base + to, qo.at[0, 0, 0])

            for to in range(ne - 1):

                @pl.when(z > to)
                def _():
                    wire.left(r_dn + base + to, qo.at[0, 0, 0])

        for s in range(2 * ne):

            @pl.when(s != s_me)
            def _():
                wire.left(r_dg + mb * 2 * ne + s, dgs.at[0, 0])

    assert wire.used <= ROLES


ROLES = 240


def front(nd, ne, tokens, image_ids, routes, qkv, outw, small, win, wout, cot):
    rows, share = tokens.shape[1], qkv.shape[1]
    halo = -(-(IMG - 1) // 16) * 16
    experts = 2 * ne
    slots = 4 * rows // experts
    shape = jax.ShapeDtypeStruct
    outs = (
        shape((MICRO, rows, D), bf16),
        shape((MICRO, rows, D), f32),
        shape((MICRO, rows, 128), f32),
        shape((D, FF), bf16),
        shape((D, FF), bf16),
        shape((MICRO, rows, D), bf16),
        shape((MICRO, rows, 128), f32),
        shape((MICRO, rows, D), f32),
        shape((MICRO, rows, D), bf16),
        shape((MICRO, 3, 3 * rows, D), bf16),
        shape((MICRO, rows, 128), f32),
        shape((4, D, D), bf16),
        shape((D, 128), f32),
        shape((MICRO, 1, 3 * rows), f32),
    )
    vmem, anywhere = pl.BlockSpec(memory_space=pltpu.VMEM), pl.BlockSpec(memory_space=pl.ANY)
    v = pltpu.VMEM
    return pl.pallas_call(
        functools.partial(front_kernel, nd, ne),
        out_shape=outs,
        in_specs=[vmem, vmem, vmem, anywhere, anywhere, vmem, anywhere, anywhere, anywhere],
        out_specs=[anywhere if k in (3, 4) else vmem for k in range(len(outs))],
        scratch_shapes=[
            v((share + 16, 128), bf16),
            v((nd * ne, share + 16, 128), bf16),
            v((MICRO, halo, D), bf16),
            v((MICRO, halo, D), bf16),
            v((MICRO, rows), jnp.int32),
            v((MICRO, rows), jnp.int32),
            v((MICRO, 2 * ne, rows, D), bf16),
            v((MICRO, 2 * ne, rows, D), bf16),
            v((D, FF), bf16),
            v((FF, D), bf16),
            v((MICRO, experts, rows), f32),
            v((2 * ne, MICRO, experts, rows), f32),
            v((3 * rows, D), bf16),
            v((rows, 3 * rows), f32),
            v((D, FF), f32),
            v((D, FF), f32),
            v((2, slots, rows), bf16),
            v((2 * slots, D), bf16),
            v((2 * slots, D), bf16),
            v((2 * slots, D), bf16),
            v((D, 2 * slots), bf16),
            v((D, 2 * slots), bf16),
            v((2 * slots, 128), f32),
            v((2 * slots, D), f32),
            v((2 * slots, D), f32),
            v((2, 2 * slots, D), bf16),
            v((MICRO, 2, ne, rows, D), bf16),
            v((MICRO, 2, ne, rows, D), bf16),
            v((MICRO, 2, ne, rows, D), bf16),
            v((MICRO, 2, ne + 1, rows, D), bf16),
            v((MICRO, 2 * ne, 8, rows), f32),
            v((MICRO, experts, 8, rows), f32),
            pltpu.SemaphoreType.DMA((ROLES,)),
            pltpu.SemaphoreType.DMA((ROLES,)),
            pltpu.SemaphoreType.DMA((9,)),
        ],
        compiler_params=pltpu.CompilerParams(
            collective_id=0, has_side_effects=True, vmem_limit_bytes=VMEM_BYTES
        ),
        name="front",
    )(tokens, image_ids, routes, qkv, outw, small, win, wout, cot)


def kernel_body(
    nd,
    ne,
    tokens,
    image_ids,
    routes,
    qkv_weight,
    out_weight,
    router_weight,
    norm_gains,
    norm_biases,
    expert_in,
    expert_out,
    cotangent,
):
    rows = tokens.shape[1]
    experts = 2 * ne
    small = jnp.concatenate([router_weight, norm_gains.T, norm_biases.T], axis=1)
    small = jnp.pad(small, ((0, 0), (0, 128 - experts - 4)))
    (
        block_out,
        d_in,
        d_probs,
        grad_up,
        grad_down,
        normed_two,
        probs,
        resid,
        mixed,
        qkv_ext,
        lse,
        w_full,
        s_full,
        idr,
    ) = front(
        nd, ne, tokens, image_ids, routes, qkv_weight, out_weight, small, expert_in, expert_out, cotangent
    )
    router_wide = s_full[:, :experts]
    gains = [s_full[:, experts + k] for k in range(2)]
    biases = [s_full[:, experts + 2 + k] for k in range(2)]
    scale = 1.0 / math.sqrt(HEAD_DIM)
    core = lax.rem(lax.axis_index("dp"), 2)
    g_qkv, g_out, g_router = 0.0, 0.0, 0.0
    g_gain, g_bias = [0.0, 0.0], [0.0, 0.0]
    input_grads = []
    rim = IMG - 1
    for mb in range(MICRO):
        up = cotangent[mb].astype(f32)
        prob = probs[mb][:, :experts]
        dp = d_probs[mb][:, :experts]
        d_logits = prob * (dp - jnp.sum(prob * dp, axis=-1, keepdims=True))
        dn2 = d_in[mb] + jnp.dot(d_logits, router_wide.T, precision=highest)
        g_router += jnp.dot(normed_two[mb].astype(f32).T, d_logits, precision=highest)
        _, back = jax.vjp(layer_norm, resid[mb], gains[1], biases[1])
        dv, dg, db = back(dn2)
        g_gain[1] += dg
        g_bias[1] += db
        d_resid = up + dv
        d_attn = d_resid.astype(bf16)
        g_out += jnp.einsum("rd,re->de", mixed[mb], d_attn, preferred_element_type=f32)
        d_mixed = jnp.einsum("re,de->rd", d_attn, w_full[3], preferred_element_type=f32).astype(bf16)
        d_mixed = d_mixed.reshape(rows, HEADS, HEAD_DIM)
        query = qkv_ext[mb, 0, rows : 2 * rows].reshape(rows, HEADS, HEAD_DIM)
        key = qkv_ext[mb, 1].reshape(3 * rows, HEADS, HEAD_DIM)
        value = qkv_ext[mb, 2].reshape(3 * rows, HEADS, HEAD_DIM)
        same = idr[mb, 0, rows : 2 * rows][:, None] == idr[mb, 0][None, :]
        s = jnp.einsum("qhd,khd->hqk", query, key, preferred_element_type=f32) * scale
        s = jnp.where(same[None], s, neg_big)
        p = jnp.exp(s - lse[mb][:, :HEADS].T[:, :, None])
        p_low = p.astype(bf16)
        d_att = jnp.einsum("qhd,khd->hqk", d_mixed, value, preferred_element_type=f32)
        d_s = (p * (d_att - jnp.sum(p * d_att, axis=-1, keepdims=True))).astype(bf16)
        d_q = jnp.einsum("hqk,khd->qhd", d_s, key, preferred_element_type=f32) * scale
        d_q = d_q.astype(bf16).reshape(rows, D)
        d_k = jnp.einsum("hqk,qhd->khd", d_s, query, preferred_element_type=f32) * scale
        d_v = jnp.einsum("hqk,qhd->khd", p_low, d_mixed, preferred_element_type=f32)
        pair = jnp.stack([d_k.reshape(-1, D), d_v.reshape(-1, D)])
        rims = jnp.concatenate([pair[:, rows - rim : rows], pair[:, 2 * rows : 2 * rows + rim]], axis=1)
        beside = padded(rims.astype(bf16), ((("dp", "expert"), 1),), rim).astype(f32)
        own = pair[:, rows : 2 * rows]
        low = jnp.pad(beside[:, :rim], ((0, 0), (0, rows - rim), (0, 0)))
        high = jnp.pad(beside[:, 3 * rim :], ((0, 0), (rows - rim, 0), (0, 0)))
        d_kv = (own + low + high).astype(bf16)
        d_proj = jnp.concatenate([d_q[None], d_kv], axis=0)
        token = tokens[mb].astype(f32)
        n1 = layer_norm(token, gains[0], biases[0]).astype(bf16)
        g_qkv += jnp.einsum("rd,cre->cde", n1, d_proj, preferred_element_type=f32)
        dn1 = jnp.einsum("cre,cde->rd", d_proj, w_full[:3], preferred_element_type=f32)
        _, back = jax.vjp(layer_norm, token, gains[0], biases[0])
        dv, dg, db = back(dn1)
        g_gain[0] += dg
        g_bias[0] += db
        input_grads.append((d_resid + dv).astype(bf16))
    small = jnp.concatenate(
        [g_router, jnp.stack(g_gain, axis=1), jnp.stack(g_bias, axis=1)], axis=1
    )
    small = jnp.pad(small, ((0, 0), (0, D - experts - 4)))
    packed = jnp.concatenate([g_qkv, g_out[None], small[None]], axis=0)
    packed = lax.psum_scatter(packed, ("dp", "expert"), scatter_dimension=1, tiled=True)
    zero_up = jnp.zeros_like(grad_up)
    both_up = jnp.stack([jnp.where(core == 0, grad_up, zero_up), jnp.where(core == 1, grad_up, zero_up)])
    grad_down = grad_down.T
    zero_dn = jnp.zeros_like(grad_down)
    both_dn = jnp.stack([jnp.where(core == 0, grad_down, zero_dn), jnp.where(core == 1, grad_down, zero_dn)])
    return (
        block_out,
        jnp.stack(input_grads),
        packed[:3],
        packed[3],
        packed[4][:, :experts],
        packed[4][:, experts : experts + 2].T,
        packed[4][:, experts + 2 : experts + 4].T,
        lax.psum_scatter(both_up, "dp", scatter_dimension=1, tiled=True).astype(f32),
        lax.psum_scatter(both_dn, "dp", scatter_dimension=1, tiled=True).astype(f32),
    )


def chosen_body(nd, ne, tokens, *rest):
    rows, experts = tokens.shape[1], 2 * ne
    whole = D % (16 * nd * ne) == 0 and nd % 2 == 0 and 8 * rows == experts * rows and rows % 128 == 0
    if whole and rest[-3].shape[0] == 2:
        return kernel_body(nd, ne, tokens, *rest)
    return body(tokens, *rest)


def solution(mesh):
    return jax.shard_map(
        functools.partial(chosen_body, mesh.shape["dp"], mesh.shape["expert"]),
        mesh=mesh,
        in_specs=(
            P(None, ("dp", "expert"), None),
            P(None, ("dp", "expert")),
            P(None, ("dp", "expert"), None),
            P(None, ("dp", "expert"), None),
            P(("dp", "expert"), None),
            P(("dp", "expert"), None),
            P(None, ("dp", "expert")),
            P(None, ("dp", "expert")),
            P("expert", "dp", None),
            P("expert", "dp", None),
            P(None, ("dp", "expert"), None),
        ),
        out_specs=(
            P(None, ("dp", "expert"), None),
            P(None, ("dp", "expert"), None),
            P(None, ("dp", "expert"), None),
            P(("dp", "expert"), None),
            P(("dp", "expert"), None),
            P(None, ("dp", "expert")),
            P(None, ("dp", "expert")),
            P("expert", "dp", None),
            P("expert", "dp", None),
        ),
        check_vma=False,
    )
```

```python
import functools
import math

import jax
import jax.numpy as jnp
from jax import lax
from jax.experimental import pallas as pl
from jax.experimental.pallas import tpu as pltpu
from jax.sharding import PartitionSpec as P

D = 512
HEADS = 8
HEAD_DIM = 64
FF = 2048
TOP = 2
IMG = 197
MICRO = 2


neg_big = -1e30
norm_eps = 1e-06
highest = lax.Precision.HIGHEST


def padded(cells, sides, width):
    for axis, dim in sides:
        count = lax.axis_size(axis)
        ends = count - 1
        head = lax.slice_in_dim(cells, 0, width, axis=dim)
        tail = lax.slice_in_dim(cells, cells.shape[dim] - width, cells.shape[dim], axis=dim)
        cells = jnp.concatenate(
            [
                lax.ppermute(tail, axis, [(i, (i + 1) % count) for i in range(ends)]),
                cells,
                lax.ppermute(head, axis, [((i + 1) % count, i) for i in range(ends)]),
            ],
            axis=dim,
        )
    return cells


def layer_norm(values, gain_row, bias_row):
    centre = jnp.mean(values, axis=-1, keepdims=True)
    offset = values - centre
    spread = jnp.mean(offset * offset, axis=-1, keepdims=True)
    return offset * lax.rsqrt(spread + norm_eps) * gain_row + bias_row


def tanh_gelu(values):
    return jax.nn.gelu(values, approximate=True)


def fetch_dense(qkv_weight, out_weight, router_weight, norm_gains, norm_biases):
    rows, experts = router_weight.shape
    small = jnp.concatenate([router_weight, norm_gains.T, norm_biases.T], axis=1)
    small = jnp.pad(small, ((0, 0), (0, D - experts - 4)))
    packed = jnp.concatenate([qkv_weight, out_weight[None], small[None]], axis=0)
    full = lax.all_gather(packed, ("dp", "expert"), axis=1, tiled=True)
    return (
        full[:3],
        full[3],
        full[4][:, :experts],
        full[4][:, experts : experts + 2].T,
        full[4][:, experts + 2 : experts + 4].T,
    )


def fetch_experts(expert_in, expert_out):
    return (
        lax.all_gather(expert_in, "dp", axis=1, tiled=True),
        lax.all_gather(expert_out, "dp", axis=1, tiled=True),
    )


def plan_routes(route_ids, shard_experts):
    row_count = route_ids.shape[0]
    experts = shard_experts * lax.axis_size("expert")
    devices = lax.axis_size(("dp", "expert"))
    slot_count = 2 * TOP * row_count // experts
    capacity = 5 * TOP * row_count * devices // (4 * experts)
    labels = lax.broadcasted_iota(jnp.int32, (1, experts), 1)
    first_hot = (route_ids[:, 0:1] == labels).astype(jnp.int32)
    second_hot = (route_ids[:, 1:2] == labels).astype(jnp.int32)
    counts = jnp.stack([jnp.sum(first_hot, axis=0), jnp.sum(second_hot, axis=0)])
    all_counts = lax.all_gather(counts[None], ("dp", "expert"), axis=0, tiled=True)
    earlier = (
        lax.broadcasted_iota(jnp.int32, (devices, 1, 1), 0) < lax.axis_index(("dp", "expert"))
    ).astype(jnp.int32)
    before = jnp.sum(all_counts * earlier, axis=0)
    total_first = jnp.sum(all_counts[:, 0, :], axis=0)
    row_before = (
        lax.broadcasted_iota(jnp.int32, (row_count, row_count), 0)
        > lax.broadcasted_iota(jnp.int32, (row_count, row_count), 1)
    ).astype(jnp.bfloat16)

    def rank_of(hot):
        ahead = jnp.dot(row_before, hot.astype(jnp.bfloat16), preferred_element_type=jnp.float32)
        return jnp.sum(ahead.astype(jnp.int32) * hot, axis=1)

    rank_first = rank_of(first_hot)
    rank_second = rank_of(second_hot)
    place_first = jnp.sum(first_hot * before[0][None, :], axis=1) + rank_first
    place_second = jnp.sum(second_hot * (total_first + before[1])[None, :], axis=1) + rank_second
    kept_mask = jnp.stack([place_first < capacity, place_second < capacity], axis=1)
    slot_second = jnp.sum(second_hot * counts[0][None, :], axis=1) + rank_second
    flat_index = jnp.stack(
        [route_ids[:, 0] * slot_count + rank_first, route_ids[:, 1] * slot_count + slot_second],
        axis=1,
    )
    target = jnp.where(kept_mask, flat_index, experts * slot_count)
    return (first_hot, second_hot, target, kept_mask.astype(jnp.float32))


def fill_slots(row_pairs, target, experts, slot_count):
    feature_count = row_pairs.shape[-1]
    buffer = jnp.zeros((experts * slot_count + 1, feature_count), row_pairs.dtype)
    buffer = buffer.at[target.reshape(-1)].set(row_pairs.reshape(-1, feature_count))
    return buffer[:-1].reshape(experts, 1, slot_count, feature_count)


def read_slots(returned, target):
    feature_count = returned.shape[-1]
    flat_table = jnp.concatenate(
        [returned.reshape(-1, feature_count), jnp.zeros((1, feature_count), returned.dtype)], axis=0
    )
    return flat_table[target]


def run_forward(tokens_f, ids_ext, route_plan, dense_set, expert_set):
    qkv_full, out_full, router_full, gain_pair, bias_pair = dense_set
    expert_up_weight, expert_down_weight = expert_set
    first_hot, second_hot, target, kept_mask = route_plan
    row_count = tokens_f.shape[0]
    rim_rows = IMG - 1
    score_scale = 1.0 / math.sqrt(HEAD_DIM)
    experts = router_full.shape[1]
    slot_count = 2 * TOP * row_count // experts
    normed_one = layer_norm(
        tokens_f, gain_pair[0].astype(jnp.float32), bias_pair[0].astype(jnp.float32)
    ).astype(jnp.bfloat16)
    projected = jnp.einsum(
        "rd,cde->cre", normed_one, qkv_full, preferred_element_type=jnp.float32
    ).astype(jnp.bfloat16)
    key_value = padded(projected[1:], ((("dp", "expert"), 1),), rim_rows)
    query_heads = projected[0].reshape(row_count, HEADS, HEAD_DIM)
    key_heads = key_value[0].reshape(-1, HEADS, HEAD_DIM)
    value_heads = key_value[1].reshape(-1, HEADS, HEAD_DIM)
    same_image = ids_ext[rim_rows : rim_rows + row_count][:, None] == ids_ext[None, :]
    scores = (
        jnp.einsum("qhd,khd->hqk", query_heads, key_heads, preferred_element_type=jnp.float32)
        * score_scale
    )
    scores = jnp.where(same_image[None], scores, neg_big)
    top_score = jnp.max(scores, axis=-1, keepdims=True)
    log_total = top_score + jnp.log(jnp.sum(jnp.exp(scores - top_score), axis=-1, keepdims=True))
    att_probs = jnp.exp(scores - log_total)
    att_low = att_probs.astype(jnp.bfloat16)
    mixed_rows = (
        jnp.einsum("hqk,khd->qhd", att_low, value_heads, preferred_element_type=jnp.float32)
        .reshape(row_count, D)
        .astype(jnp.bfloat16)
    )
    residual = tokens_f + jnp.dot(mixed_rows, out_full, preferred_element_type=jnp.float32)
    normed_two = layer_norm(
        residual, gain_pair[1].astype(jnp.float32), bias_pair[1].astype(jnp.float32)
    ).astype(jnp.bfloat16)
    router_probs = jax.nn.softmax(
        jnp.dot(normed_two, router_full, preferred_element_type=jnp.float32), axis=-1
    )
    picked = jnp.stack(
        [jnp.sum(first_hot * router_probs, axis=1), jnp.sum(second_hot * router_probs, axis=1)],
        axis=1,
    )
    gate_values = kept_mask * picked
    outgoing = fill_slots(
        jnp.broadcast_to(normed_two[:, None, :], (row_count, TOP, D)), target, experts, slot_count
    )
    arrived = lax.all_to_all(outgoing, "expert", split_axis=0, concat_axis=1, tiled=True)
    shard_experts = arrived.shape[0]
    collected_token_rows = arrived.reshape(shard_experts, -1, D)
    hidden_pre = jnp.einsum(
        "ycq,yqt->yct", collected_token_rows, expert_up_weight, preferred_element_type=jnp.float32
    )
    hidden_activation = tanh_gelu(hidden_pre).astype(jnp.bfloat16)
    produced = jnp.einsum(
        "nso,nop->nsp", hidden_activation, expert_down_weight, preferred_element_type=jnp.float32
    ).astype(jnp.bfloat16)
    returned = lax.all_to_all(
        produced.reshape(arrived.shape), "expert", split_axis=1, concat_axis=0, tiled=True
    )
    expert_rows = read_slots(returned, target)
    block_value = residual + jnp.sum(
        gate_values[:, :, None] * expert_rows.astype(jnp.float32), axis=1
    )
    return (
        normed_one,
        query_heads,
        key_heads,
        value_heads,
        att_probs,
        att_low,
        mixed_rows,
        residual,
        normed_two,
        router_probs,
        gate_values,
        collected_token_rows,
        hidden_pre,
        hidden_activation,
        expert_rows,
        block_value,
    )


def run_backward(tokens_f, ids_ext, route_plan, dense_set, expert_set, upstream, gradients):
    qkv_full, out_full, router_full, gain_pair, bias_pair = dense_set
    expert_up_weight, expert_down_weight = expert_set
    first_hot, second_hot, target, kept_mask = route_plan
    grad_qkv, grad_out, grad_router, grad_gains, grad_biases, grad_in, grad_expert_out = gradients
    (
        normed_one,
        query_heads,
        key_heads,
        value_heads,
        att_probs,
        att_low,
        mixed_rows,
        residual,
        normed_two,
        router_probs,
        gate_values,
        collected_token_rows,
        hidden_pre,
        hidden_activation,
        expert_rows,
        block_value,
    ) = run_forward(tokens_f, ids_ext, route_plan, dense_set, expert_set)
    row_count = tokens_f.shape[0]
    rim_rows = IMG - 1
    score_scale = 1.0 / math.sqrt(HEAD_DIM)
    experts = router_full.shape[1]
    slot_count = 2 * TOP * row_count // experts
    shard_experts = expert_up_weight.shape[0]
    d_gate = kept_mask * jnp.sum(upstream[:, None, :] * expert_rows.astype(jnp.float32), axis=-1)
    d_sent = (gate_values[:, :, None] * upstream[:, None, :]).astype(jnp.bfloat16)
    d_arrived = lax.all_to_all(
        fill_slots(d_sent, target, experts, slot_count),
        "expert",
        split_axis=0,
        concat_axis=1,
        tiled=True,
    )
    produced_rows_grad = d_arrived.reshape(shard_experts, -1, D)
    activation_grad = jnp.einsum(
        "tkw,tew->tke", produced_rows_grad, expert_down_weight, preferred_element_type=jnp.float32
    )
    grad_expert_out = grad_expert_out + jnp.einsum(
        "meq,mek->mqk", hidden_activation, produced_rows_grad, preferred_element_type=jnp.float32
    )
    gelu_value, gelu_back = jax.vjp(tanh_gelu, hidden_pre)
    preactivation_grad = gelu_back(activation_grad)[0].astype(jnp.bfloat16)
    grad_in = grad_in + jnp.einsum(
        "zjo,zjm->zom", collected_token_rows, preactivation_grad, preferred_element_type=jnp.float32
    )
    d_rows = jnp.einsum(
        "iht,imt->ihm", preactivation_grad, expert_up_weight, preferred_element_type=jnp.float32
    ).astype(jnp.bfloat16)
    d_back = lax.all_to_all(
        d_rows.reshape(d_arrived.shape), "expert", split_axis=1, concat_axis=0, tiled=True
    )
    d_normed_two = jnp.sum(
        kept_mask[:, :, None] * read_slots(d_back, target).astype(jnp.float32), axis=1
    )
    d_probs = first_hot * d_gate[:, 0:1] + second_hot * d_gate[:, 1:2]
    d_logits = router_probs * (d_probs - jnp.sum(router_probs * d_probs, axis=-1, keepdims=True))
    router_wide = router_full.astype(jnp.float32)
    d_normed_two = d_normed_two + jnp.dot(d_logits, router_wide.T, precision=highest)
    grad_router = grad_router + jnp.dot(
        normed_two.astype(jnp.float32).T, d_logits, precision=highest
    )
    norm_value, second_back = jax.vjp(
        layer_norm, residual, gain_pair[1].astype(jnp.float32), bias_pair[1].astype(jnp.float32)
    )
    d_resid_part, d_gain_two, d_bias_two = second_back(d_normed_two)
    d_resid = upstream + d_resid_part
    d_attn = d_resid.astype(jnp.bfloat16)
    grad_out = grad_out + jnp.einsum(
        "rd,re->de", mixed_rows, d_attn, preferred_element_type=jnp.float32
    )
    d_mixed = (
        jnp.einsum("re,de->rd", d_attn, out_full, preferred_element_type=jnp.float32)
        .astype(jnp.bfloat16)
        .reshape(row_count, HEADS, HEAD_DIM)
    )
    d_att = jnp.einsum("qhd,khd->hqk", d_mixed, value_heads, preferred_element_type=jnp.float32)
    d_scores = (att_probs * (d_att - jnp.sum(att_probs * d_att, axis=-1, keepdims=True))).astype(
        jnp.bfloat16
    )
    d_query = (
        (
            jnp.einsum("hqk,khd->qhd", d_scores, key_heads, preferred_element_type=jnp.float32)
            * score_scale
        )
        .astype(jnp.bfloat16)
        .reshape(row_count, D)
    )
    d_key = (
        jnp.einsum("hqk,qhd->khd", d_scores, query_heads, preferred_element_type=jnp.float32)
        * score_scale
    )
    d_value = jnp.einsum("hqk,qhd->khd", att_low, d_mixed, preferred_element_type=jnp.float32)
    d_pair = jnp.stack([d_key.reshape(-1, D), d_value.reshape(-1, D)])
    rim_grads = jnp.concatenate([d_pair[:, :rim_rows], d_pair[:, rim_rows + row_count :]], axis=1)
    beside_all = padded(rim_grads.astype(jnp.bfloat16), ((("dp", "expert"), 1),), rim_rows).astype(
        rim_grads.dtype
    )
    own_part = d_pair[:, rim_rows : rim_rows + row_count]
    from_below = jnp.pad(beside_all[:, :rim_rows], ((0, 0), (0, row_count - rim_rows), (0, 0)))
    from_above = jnp.pad(beside_all[:, 3 * rim_rows :], ((0, 0), (row_count - rim_rows, 0), (0, 0)))
    d_kv = (own_part + from_below + from_above).astype(jnp.bfloat16)
    d_projected = jnp.concatenate([d_query[None], d_kv], axis=0)
    grad_qkv = grad_qkv + jnp.einsum(
        "rd,cre->cde", normed_one, d_projected, preferred_element_type=jnp.float32
    )
    d_normed_one = jnp.einsum(
        "cre,cde->rd", d_projected, qkv_full, preferred_element_type=jnp.float32
    )
    first_value, first_back = jax.vjp(
        layer_norm, tokens_f, gain_pair[0].astype(jnp.float32), bias_pair[0].astype(jnp.float32)
    )
    d_tokens_part, d_gain_one, d_bias_one = first_back(d_normed_one)
    grad_gains = grad_gains + jnp.stack([d_gain_one, d_gain_two])
    grad_biases = grad_biases + jnp.stack([d_bias_one, d_bias_two])
    input_rows = (d_resid + d_tokens_part).astype(jnp.bfloat16)
    return (
        input_rows,
        (grad_qkv, grad_out, grad_router, grad_gains, grad_biases, grad_in, grad_expert_out),
    )


def body(
    tokens,
    image_ids,
    routes,
    qkv_weight,
    out_weight,
    router_weight,
    norm_gains,
    norm_biases,
    expert_in,
    expert_out,
    cotangent,
):
    shard_experts = expert_in.shape[0]
    rim_rows = IMG - 1
    experts = shard_experts * lax.axis_size("expert")
    outputs = []
    saved_state = []
    for batch_index in range(MICRO):
        dense_set = fetch_dense(qkv_weight, out_weight, router_weight, norm_gains, norm_biases)
        expert_set = fetch_experts(expert_in, expert_out)
        ids_ext = padded(image_ids[batch_index] + 1, ((("dp", "expert"), 0),), rim_rows)
        route_plan = plan_routes(routes[batch_index], shard_experts)
        forward_state = run_forward(
            tokens[batch_index].astype(jnp.float32), ids_ext, route_plan, dense_set, expert_set
        )
        outputs.append(forward_state[-1].astype(jnp.bfloat16))
        saved_state.append((ids_ext, route_plan))
    gradients = (
        jnp.zeros((3, D, D), jnp.float32),
        jnp.zeros((D, D), jnp.float32),
        jnp.zeros((D, experts), jnp.float32),
        jnp.zeros((2, D), jnp.float32),
        jnp.zeros((2, D), jnp.float32),
        jnp.zeros((shard_experts, D, FF), jnp.float32),
        jnp.zeros((shard_experts, FF, D), jnp.float32),
    )
    input_grads = []
    for batch_index in range(MICRO):
        dense_set = fetch_dense(qkv_weight, out_weight, router_weight, norm_gains, norm_biases)
        expert_set = fetch_experts(expert_in, expert_out)
        ids_ext, route_plan = saved_state[batch_index]
        input_rows, gradients = run_backward(
            tokens[batch_index].astype(jnp.float32),
            ids_ext,
            route_plan,
            dense_set,
            expert_set,
            cotangent[batch_index].astype(jnp.float32),
            gradients,
        )
        input_grads.append(input_rows)
    grad_qkv, grad_out, grad_router, grad_gains, grad_biases, grad_in, grad_expert_out = gradients
    small = jnp.concatenate([grad_router, grad_gains.T, grad_biases.T], axis=1)
    small = jnp.pad(small, ((0, 0), (0, D - experts - 4)))
    packed = jnp.concatenate([grad_qkv, grad_out[None], small[None]], axis=0)
    packed = lax.psum_scatter(packed, ("dp", "expert"), scatter_dimension=1, tiled=True)
    dense_grads = (
        packed[:3],
        packed[3],
        packed[4][:, :experts],
        packed[4][:, experts : experts + 2].T,
        packed[4][:, experts + 2 : experts + 4].T,
    )
    expert_grads = (
        lax.psum_scatter(
            grad_in.astype(jnp.bfloat16), "dp", scatter_dimension=1, tiled=True
        ).astype(jnp.float32),
        lax.psum_scatter(
            grad_expert_out.astype(jnp.bfloat16), "dp", scatter_dimension=1, tiled=True
        ).astype(jnp.float32),
    )
    return (
        jnp.stack(outputs),
        jnp.stack(input_grads),
        dense_grads[0],
        dense_grads[1],
        dense_grads[2],
        dense_grads[3],
        dense_grads[4],
        expert_grads[0],
        expert_grads[1],
    )


MESH = pl.DeviceIdType.MESH
f32, bf16 = jnp.float32, jnp.bfloat16
VMEM_BYTES = 62 << 20


def mm(a, b):
    return jnp.dot(a, b, preferred_element_type=f32)


def mm_nt(a, b):
    return lax.dot_general(a, b, (((1,), (1,)), ((), ())), preferred_element_type=f32)


def normed(values, gain_row, bias_row):
    centre = jnp.mean(values, axis=-1, keepdims=True)
    offset = values - centre
    spread = jnp.mean(offset * offset, axis=-1, keepdims=True)
    return offset * lax.rsqrt(spread + norm_eps) * gain_row + bias_row


class Wire:
    def __init__(self, send_sems, recv_sems, other):
        self.send_sems, self.recv_sems, self.other = send_sems, recv_sems, other
        self.used, self.sent = 0, {}

    def roles(self, count=1):
        self.used += count
        return self.used - count

    def copy(self, send_role, recv_role, src, dst, device):
        return pltpu.make_async_remote_copy(
            src_ref=src,
            dst_ref=dst,
            send_sem=self.send_sems.at[send_role],
            recv_sem=self.recv_sems.at[recv_role],
            device_id=device,
            device_id_type=MESH,
        )

    def send(self, role, src, dst, device, recv_role=None):
        self.copy(role, role if recv_role is None else recv_role, src, dst, device).start()

    def arrive(self, role, like):
        self.copy(role, role, like, like, self.other).wait_recv()

    def left(self, role, like):
        self.copy(role, role, like, like, self.other).wait_send()


class Place:
    def __init__(self, nd, ne):
        self.nd, self.ne = nd, ne
        self.d, self.z = lax.axis_index("dp"), lax.axis_index("expert")
        d, z = self.d, self.z
        self.c = lax.rem(d, 2)
        self.sib_d = d + 1 - 2 * self.c
        self.sib = (self.sib_d, z)
        self.idx = d * ne + z
        last = (z == ne - 1).astype(jnp.int32)
        first = (z == 0).astype(jnp.int32)
        self.next = (lax.rem(d + last, nd), lax.rem(z + 1, ne))
        self.prev = (lax.rem(d + nd - first, nd), lax.rem(z + ne - 1, ne))
        self.up = (d, jnp.minimum(z + 1, ne - 1))
        self.down = (d, jnp.maximum(z - 1, 0))

    def chip(self, k):
        return lax.rem(self.d + 2 * k, self.nd)

    def enter(self):
        bar = pltpu.get_barrier_semaphore()

        def greet(device):
            pl.semaphore_signal(bar, inc=1, device_id=device, device_id_type=MESH)

        for k in range(1, self.nd):
            greet((lax.rem(self.d + k, self.nd), self.z))
        for k in range(1, self.ne):
            zk = lax.rem(self.z + k, self.ne)
            greet((self.d, zk))
            greet((self.sib_d, zk))
        greet(self.next)
        greet(self.prev)
        pl.semaphore_wait(bar, self.nd - 1 + 2 * (self.ne - 1) + 2)


class Chain:
    def __init__(self, wire, me, full):
        self.wire, self.me, self.full = wire, me, full
        n = me.ne
        self.up, self.dn = wire.roles(n - 1), wire.roles(n - 1)
        self.su, self.sd, self.so = wire.roles(n - 1), wire.roles(n - 1), wire.roles()

    def at(self, z):
        return self.full.at[z * 2 + self.me.c]

    def own(self, src):
        m, n = self.me, self.me.ne

        @pl.when(m.z < n - 1)
        def _():
            self.wire.send(self.up, src, self.at(m.z), m.up)

        @pl.when(m.z > 0)
        def _():
            self.wire.send(self.dn, src, self.at(m.z), m.down)

        self.wire.send(self.so, src, self.at(m.z), m.sib)

    def pump(self, k):
        m, n, w = self.me, self.me.ne, self.wire

        @pl.when(m.z >= k + 1)
        def _():
            block = self.at(m.z - 1 - k)
            w.arrive(self.up + k, block)
            if k + 1 < n - 1:

                @pl.when(m.z < n - 1)
                def _():
                    w.send(self.up + k + 1, block, block, m.up)

            w.send(self.su + k, block, block, m.sib)

        @pl.when(m.z + k + 1 < n)
        def _():
            block = self.at(m.z + 1 + k)
            w.arrive(self.dn + k, block)
            if k + 1 < n - 1:

                @pl.when(m.z > 0)
                def _():
                    w.send(self.dn + k + 1, block, block, m.down)

            w.send(self.sd + k, block, block, m.sib)

    def finish(self):
        m, n, w, like = self.me, self.me.ne, self.wire, self.full.at[0]
        w.arrive(self.so, like)
        for k in range(n - 1):

            @pl.when(m.z >= k + 1)
            def _():
                w.arrive(self.su + k, like)

            @pl.when(m.z + k + 1 < n)
            def _():
                w.arrive(self.sd + k, like)

    def drain(self):
        m, n, w, like = self.me, self.me.ne, self.wire, self.full.at[0]
        w.left(self.so, like)
        for k in range(n - 1):

            @pl.when((m.z < n - 1) & (m.z >= k))
            def _():
                w.left(self.up + k, like)

            @pl.when((m.z > 0) & (m.z + k < n))
            def _():
                w.left(self.dn + k, like)

            @pl.when(m.z >= k + 1)
            def _():
                w.left(self.su + k, like)

            @pl.when(m.z + k + 1 < n)
            def _():
                w.left(self.sd + k, like)


def front_kernel(
    nd,
    ne,
    tok,
    ids,
    routes,
    qkv,
    outw,
    small,
    win,
    wout,
    cot,
    o_block,
    o_din,
    o_dprobs,
    o_up,
    o_down,
    o_n2,
    o_probs,
    o_resid,
    o_mixed,
    o_qkv,
    o_lse,
    w_all,
    o_small,
    o_idr,
    s_src,
    s_all,
    hp,
    hn,
    ip,
    inx,
    gx,
    gd,
    wu,
    wd,
    rk_src,
    rk,
    hnorm,
    bias,
    d_wu,
    d_wd,
    pm,
    xs,
    ds,
    deo,
    xt,
    dt,
    gt,
    acc_eo,
    acc_di,
    ys,
    qo,
    cs,
    cr,
    ud,
    dgs,
    dg,
    send_sems,
    recv_sems,
    local_sems,
):
    me = Place(nd, ne)
    d, z, c = me.d, me.z, me.c
    rows = tok.shape[1]
    share = qkv.shape[1]
    experts = 2 * ne
    halo = hp.shape[1]
    ext = 3 * rows
    slots = 4 * rows // experts
    capacity = 5 * TOP * rows * nd * ne // (4 * experts)
    e = 2 * z + c
    wire = Wire(send_sems, recv_sems, me.sib)
    lane = lax.broadcasted_iota(jnp.int32, (1, 128), 1)

    before_row = (
        lax.broadcasted_iota(jnp.int32, (rows, rows), 0)
        > lax.broadcasted_iota(jnp.int32, (rows, rows), 1)
    ).astype(bf16)
    hots = []
    s_src[0:share, :] = small[...]
    s_src[share : share + 16, :] = jnp.zeros((16, 128), bf16)
    row16 = lax.broadcasted_iota(jnp.int32, (16, 128), 0)
    counts = jnp.zeros((16, 128), f32)
    for mb in range(MICRO):
        pair = [(routes[mb, :, k : k + 1] == lane).astype(f32) for k in range(TOP)]
        hots.append(pair)
        for k in range(TOP):
            counts = jnp.where(row16 == mb * TOP + k, jnp.sum(pair[k], axis=0, keepdims=True), counts)
    s_src[share : share + 16, :] = counts.astype(bf16)

    me.enter()

    r_dz = wire.roles(3 * (ne - 1))
    mine = pl.ds(pl.multiple_of(me.idx * share, 16), share)
    for k in range(1, ne):
        dev = (d, lax.rem(z + k, ne))
        wire.send(r_dz + 3 * (k - 1), qkv, w_all.at[pl.ds(0, 3), mine], dev)
        wire.send(r_dz + 3 * (k - 1) + 1, outw, w_all.at[3, mine], dev)
        wire.send(r_dz + 3 * (k - 1) + 2, s_src, s_all.at[me.idx], dev)
    local = [
        pltpu.make_async_copy(qkv, w_all.at[pl.ds(0, 3), mine], local_sems.at[0]),
        pltpu.make_async_copy(outw, w_all.at[3, mine], local_sems.at[1]),
        pltpu.make_async_copy(s_src, s_all.at[me.idx], local_sems.at[2]),
    ]
    for cp in local:
        cp.start()
    r_id = wire.roles(2)
    wire.send(r_id, ids, ip, me.next)
    wire.send(r_id + 1, ids, inx, me.prev)
    r_h = wire.roles(2 * MICRO)
    for mb in range(MICRO):
        wire.send(r_h + 2 * mb, tok.at[mb, pl.ds(rows - halo, halo)], hp.at[mb], me.next)
        wire.send(r_h + 2 * mb + 1, tok.at[mb, pl.ds(0, halo)], hn.at[mb], me.prev)
    g_d = [Chain(wire, me, gd.at[mb]) for mb in range(MICRO)]
    g_x = [Chain(wire, me, gx.at[mb]) for mb in range(MICRO)]
    own_d = [
        pltpu.make_async_copy(cot.at[mb], gd.at[mb, z * 2 + c], local_sems.at[3 + mb])
        for mb in range(MICRO)
    ]
    for cp in own_d:
        cp.start()
    g_d[0].own(cot.at[0])

    for cp in local:
        cp.wait()
    for k in range(1, ne):
        wire.arrive(r_dz + 3 * (k - 1), qkv)
        wire.arrive(r_dz + 3 * (k - 1) + 1, outw)
        wire.arrive(r_dz + 3 * (k - 1) + 2, s_src)

    def column(dd):
        at = pl.ds(pl.multiple_of(dd * (ne * share), 16), ne * share)
        return w_all.at[:, at], s_all.at[pl.ds(dd * ne, ne)]

    chips = nd // 2
    r_dx = wire.roles(2 * (chips - 1))
    r_ds = wire.roles(2 * chips)
    blk, sblk = column(d)
    for k in range(1, chips):
        wire.send(r_dx + 2 * (k - 1), blk, blk, (me.chip(k), z))
        wire.send(r_dx + 2 * (k - 1) + 1, sblk, sblk, (me.chip(k), z))
    wire.send(r_ds, blk, blk, me.sib)
    wire.send(r_ds + 1, sblk, sblk, me.sib)
    up_rows, down_rows = win.shape[1], wout.shape[1]
    at_up = pl.ds(pl.multiple_of(d * up_rows, 16), up_rows)
    at_down = pl.ds(pl.multiple_of(d * down_rows, 16), down_rows)
    r_w = wire.roles(2 * (nd - 1))
    own_w = [
        pltpu.make_async_copy(win.at[c], wu.at[at_up], local_sems.at[5]),
        pltpu.make_async_copy(wout.at[c], wd.at[at_down], local_sems.at[6]),
    ]
    for cp in own_w:
        cp.start()
    for k in range(1, nd):
        dd = lax.rem(d + k, nd)
        cc = lax.rem(dd, 2)
        wire.send(r_w + 2 * (k - 1), win.at[cc], wu.at[at_up], (dd, z))
        wire.send(r_w + 2 * (k - 1) + 1, wout.at[cc], wd.at[at_down], (dd, z))
    g_d[0].pump(0)
    for k in range(1, chips):
        wire.arrive(r_dx + 2 * (k - 1), blk)
        wire.arrive(r_dx + 2 * (k - 1) + 1, sblk)
        b, sb = column(lax.rem(d + nd - 2 * k, nd))
        wire.send(r_ds + 2 * k, b, b, me.sib)
        wire.send(r_ds + 2 * k + 1, sb, sb, me.sib)
    for k in range(chips):
        wire.arrive(r_ds + 2 * k, blk)
        wire.arrive(r_ds + 2 * k + 1, sblk)

    o_small[...] = s_all[:, 0:share, :].reshape(D, 128).astype(f32)
    s_rows = o_small[...].T
    all_counts = s_all[:, share : share + 16, :].astype(f32)
    ahead = lax.broadcasted_iota(jnp.int32, all_counts.shape, 0) < me.idx
    before = jnp.sum(jnp.where(ahead, all_counts, 0.0), axis=0)
    total = jnp.sum(all_counts, axis=0)
    gains = [s_rows[experts + k : experts + k + 1, :] for k in range(2)]
    biases = [s_rows[experts + 2 + k : experts + 3 + k, :] for k in range(2)]

    for mb in range(MICRO):
        one, two = hots[mb]
        rank_one = mm(before_row, one.astype(bf16))
        rank_two = mm(before_row, two.astype(bf16))
        b1, b2 = before[2 * mb : 2 * mb + 1], before[2 * mb + 1 : 2 * mb + 2]
        t1 = total[2 * mb : 2 * mb + 1]
        place_one = jnp.sum(one * (b1 + rank_one), axis=1, keepdims=True)
        place_two = jnp.sum(two * (t1 + b2 + rank_two), axis=1, keepdims=True)
        kept = one * (place_one < capacity).astype(f32) + two * (place_two < capacity).astype(f32)
        ranks = jnp.where(kept > 0.0, rank_one + rank_two, -1.0)
        rk_src[mb] = ranks.T[0:experts, :]
    r_rk = wire.roles(2 * ne)
    s_me = z * 2 + c
    for k in range(ne):
        zk = lax.rem(z + k, ne)
        if k > 0:
            wire.send(r_rk + 2 * k, rk_src, rk.at[s_me], (d, zk))
        wire.send(r_rk + 2 * k + 1, rk_src, rk.at[s_me], (me.sib_d, zk))
    rk[s_me] = rk_src[...]
    g_d[0].pump(1)

    wire.arrive(r_id, ids)
    wire.arrive(r_id + 1, ids)
    pos = lax.broadcasted_iota(jnp.int32, (1, rows), 1)
    gap = rows - halo
    for mb in range(MICRO):
        here = ids[mb : mb + 1, :].astype(f32)
        below = jnp.where((pos >= gap) & (me.idx > 0), ip[mb : mb + 1, :].astype(f32), -1.0)
        above = jnp.where(
            (pos < halo) & (me.idx < nd * ne - 1), inx[mb : mb + 1, :].astype(f32), -1.0
        )
        o_idr[mb] = jnp.concatenate([below, here, above], axis=1)

    zero_gap = jnp.zeros((gap, D), bf16)
    hnorm[0:gap, :] = zero_gap
    hnorm[ext - gap : ext, :] = zero_gap
    scale = 1.0 / math.sqrt(HEAD_DIM)
    for mb in range(MICRO):
        wire.arrive(r_h + 2 * mb, hp.at[mb])
        wire.arrive(r_h + 2 * mb + 1, hn.at[mb])

        def put(value, start):
            hnorm[start : start + value.shape[0], :] = normed(
                value.astype(f32), gains[0], biases[0]
            ).astype(bf16)

        put(hp[mb], gap)
        put(tok[mb], rows)
        put(hn[mb], 2 * rows)
        for k in range(3):
            for r in range(3):
                part = slice(r * rows, (r + 1) * rows)
                o_qkv[mb, k, part, :] = mm(hnorm[part, :], w_all[k]).astype(bf16)
        g_d[0].pump(2) if mb == 0 else g_x[0].pump(0)
        idr = o_idr[mb]
        idc = jnp.broadcast_to(idr[:, rows : 2 * rows], (128, rows)).T[:, 0:1]
        bias[...] = jnp.where(idc == idr, 0.0, neg_big)
        o_lse[mb] = jnp.zeros((rows, 128), f32)

        @pl.loop(0, HEADS // 2)
        def _(pair):
            at = pl.ds(pl.multiple_of(pair * 128, 128), 128)
            query = o_qkv[mb, 0, rows : 2 * rows, at]
            key = o_qkv[mb, 1, :, at]
            value = o_qkv[mb, 2, :, at]
            mixed = jnp.zeros((rows, 128), f32)
            lse = o_lse[mb]
            for half in range(2):
                keep = (lane < 64) if half == 0 else (lane >= 64)
                q = jnp.where(keep, query, jnp.zeros_like(query))
                v = jnp.where(keep, value, jnp.zeros_like(value))
                s = mm_nt(q, key) * scale + bias[...]
                top = jnp.max(s, axis=-1, keepdims=True)
                p = jnp.exp(s - top)
                total_p = jnp.sum(p, axis=-1, keepdims=True)
                mixed = mixed + mm((p * (1.0 / total_p)).astype(bf16), v)
                lse = jnp.where(lane == 2 * pair + half, top + jnp.log(total_p), lse)
            o_lse[mb] = lse
            o_mixed[mb, :, at] = mixed.astype(bf16)

        if mb == 1:
            g_x[0].pump(1)
        resid = tok[mb].astype(f32) + mm(o_mixed[mb], w_all[3])
        o_resid[mb] = resid
        n2 = normed(resid, gains[1], biases[1]).astype(bf16)
        o_n2[mb] = n2
        gx[mb, s_me] = n2
        g_x[mb].own(gx.at[mb, s_me])
        if mb == 0:
            g_d[1].own(cot.at[1])
        logits = mm(n2, o_small[...].astype(bf16))
        logits = jnp.where(lane < experts, logits, neg_big)
        p = jnp.exp(logits - jnp.max(logits, axis=-1, keepdims=True))
        o_probs[mb] = p / jnp.sum(p, axis=-1, keepdims=True)
    g_x[0].pump(2)

    for cp in own_w + own_d:
        cp.wait()
    for k in range(1, nd):
        wire.arrive(r_w + 2 * (k - 1), win.at[0])
        wire.arrive(r_w + 2 * (k - 1) + 1, wout.at[0])
    for k in range(ne):
        if k > 0:
            wire.arrive(r_rk + 2 * k, rk_src)
        wire.arrive(r_rk + 2 * k + 1, rk_src)
    g_d[0].finish()
    g_x[0].finish()
    d_wu[...] = jnp.zeros_like(d_wu)
    d_wd[...] = jnp.zeros_like(d_wd)

    r_cx = wire.roles(2 * MICRO * ne)
    r_up = wire.roles(2 * MICRO * ne)
    r_dn = wire.roles(2 * MICRO * ne)
    r_dg = wire.roles(MICRO * 2 * ne)
    sub = lax.broadcasted_iota(jnp.int32, (slots, rows), 0).astype(f32)
    tile = 2 * slots
    chunk = 512

    def start_sums(mb):
        for t in range(2):
            for zp in range(ne):
                wire.arrive(r_cx + (mb * 2 + t) * ne + zp, qo.at[0, 0, 0])
                qo[mb, t, zp] = (qo[mb, t, zp].astype(f32) + cr[mb, t, zp].astype(f32)).astype(bf16)

        @pl.when(z == 0)
        def _():
            for t in range(2):
                for to in range(ne - 1, 0, -1):
                    wire.send(
                        r_up + (mb * 2 + t) * ne + to, qo.at[mb, t, to], ud.at[mb, t, to], me.up
                    )

        @pl.when(z == ne - 1)
        def _():
            for t in range(2):
                for to in range(ne - 1):
                    slot = jnp.where(z - 1 == to, ne, to)
                    wire.send(
                        r_dn + (mb * 2 + t) * ne + to, qo.at[mb, t, to], ud.at[mb, t, slot], me.down
                    )

    def pass_sums(mb):
        for t in range(2):
            for k in range(ne - 1):
                to = ne - 1 - k

                @pl.when((z > 0) & (z < to))
                def _():
                    wire.arrive(r_up + (mb * 2 + t) * ne + to, qo.at[0, 0, 0])
                    qo[mb, t, to] = (
                        qo[mb, t, to].astype(f32) + ud[mb, t, to].astype(f32)
                    ).astype(bf16)
                    wire.send(
                        r_up + (mb * 2 + t) * ne + to, qo.at[mb, t, to], ud.at[mb, t, to], me.up
                    )

                @pl.when((z < ne - 1) & (z > k))
                def _():
                    wire.arrive(r_dn + (mb * 2 + t) * ne + k, qo.at[0, 0, 0])
                    qo[mb, t, k] = (
                        qo[mb, t, k].astype(f32) + ud[mb, t, k].astype(f32)
                    ).astype(bf16)
                    slot = jnp.where(z - 1 == k, ne, k)
                    wire.send(
                        r_dn + (mb * 2 + t) * ne + k, qo.at[mb, t, k], ud.at[mb, t, slot], me.down
                    )

    def end_sums(mb, t):
        out = qo[mb, t, z].astype(f32)
        acc_eo[...] = out

        @pl.when(z > 0)
        def _():
            wire.arrive(r_up + (mb * 2 + t) * ne + z, qo.at[0, 0, 0])
            acc_eo[...] += ud[mb, t, z].astype(f32)

        @pl.when(z < ne - 1)
        def _():
            wire.arrive(r_dn + (mb * 2 + t) * ne + z, qo.at[0, 0, 0])
            acc_eo[...] += ud[mb, t, ne].astype(f32)

        return acc_eo[...]

    @pl.loop(0, MICRO * ne)
    def _(i):
        mb, zi = i // ne, lax.rem(i, ne)
        zp = lax.rem(zi * (ne - 1), ne)

        @pl.when(i == ne)
        def _():
            start_sums(0)
            for k in range(ne - 1):
                g_d[1].pump(k)
                g_x[1].pump(k)
            g_d[1].finish()
            g_x[1].finish()

        for cc in range(2):
            s = zp * 2 + cc
            at = slice(cc * slots, (cc + 1) * slots)
            pick = (sub == rk[s, mb, pl.ds(e, 1), :]).astype(bf16)
            pm[cc] = pick
            xs[at, :] = mm(pick, gx[mb, s]).astype(bf16)
            ds[at, :] = mm(pick, gd[mb, s]).astype(bf16)
        x = xs[...]
        logits = mm(x, o_small[...].astype(bf16))
        logits = jnp.where(lane < experts, logits, neg_big)
        p = jnp.exp(logits - jnp.max(logits, axis=-1, keepdims=True))
        p = p / jnp.sum(p, axis=-1, keepdims=True)
        gate = jnp.sum(jnp.where(lane == e, p, 0.0), axis=-1, keepdims=True)
        gt[...] = jnp.broadcast_to(gate, (tile, 128))
        dy = (gate * ds[...].astype(f32)).astype(bf16)
        deo[...] = dy
        xt[...] = x.T
        dt[...] = dy.T
        acc_eo[...] = jnp.zeros_like(acc_eo)
        acc_di[...] = jnp.zeros_like(acc_di)

        @pl.loop(0, FF // chunk)
        def _(f):
            at = pl.ds(pl.multiple_of(f * chunk, chunk), chunk)
            pre = mm(xs[...], wu[:, at])
            sq = pre * pre
            k0 = math.sqrt(2.0 / math.pi)
            th = jnp.tanh(pre * (k0 + (k0 * 0.044715) * sq))
            half = 0.5 + 0.5 * th
            act = (pre * half).astype(bf16)
            slope = half + (0.5 * pre) * (1.0 - th * th) * (k0 + (3.0 * k0 * 0.044715) * sq)
            acc_eo[...] += mm(act, wd[at, :])
            d_act = mm_nt(deo[...], wd[at, :])
            d_pre = (slope * d_act).astype(bf16)
            acc_di[...] += mm_nt(d_pre, wu[:, at])
            d_wu[:, at] += mm(xt[...], d_pre)
            d_wd[:, at] += mm(dt[...], act)

        eo = acc_eo[...].astype(bf16).astype(f32)
        d_gate = jnp.sum(ds[...].astype(f32) * eo, axis=-1, keepdims=True)
        ys[0] = acc_di[...].astype(bf16)
        ys[1] = (gt[:, 0:1] * eo).astype(bf16)
        for own in range(2):
            cc = c if own else 1 - c
            back = pm[cc].T
            at = pl.ds(pl.multiple_of(cc * slots, slots), slots)
            for t in range(2):
                moved = mm(back, ys[t, at, :]).astype(bf16)
                if own:
                    qo[mb, t, zp] = moved
                else:
                    cs[mb, t, zp] = moved
        for t in range(2):
            role = r_cx + (mb * 2 + t) * ne + zp
            wire.send(role, cs.at[mb, t, zp], cr.at[mb, t, zp], me.sib)
        for cc in range(2):
            at = slice(cc * slots, (cc + 1) * slots)
            line = jnp.sum(pm[cc].astype(f32) * d_gate[at], axis=0, keepdims=True)
            to = zp * 2 + cc
            dgs[mb, to] = jnp.broadcast_to(line, (8, rows))

            @pl.when(to != s_me)
            def _():
                wire.send(
                    r_dg + mb * 2 * ne + to,
                    dgs.at[mb, to],
                    dg.at[mb, e],
                    (d - c + cc, zp),
                    recv_role=r_dg + mb * 2 * ne + s_me,
                )

            @pl.when(to == s_me)
            def _():
                dg[mb, e] = jnp.broadcast_to(line, (8, rows))

    pass_sums(0)
    start_sums(1)
    g_d[0].drain()
    out_copies = []
    for h in range(2):
        for q in range(4):
            at = (slice(h * 256, (h + 1) * 256), slice(q * chunk, (q + 1) * chunk))
            wu[at] = d_wu[at].astype(bf16)
            gd[0, h * 4 + q] = d_wd[at].astype(bf16)
            to = o_down.at[pl.ds(h * 256, 256), pl.ds(q * chunk, chunk)]
            out_copies.append(pltpu.make_async_copy(gd.at[0, h * 4 + q], to, local_sems.at[h * 4 + q]))
    out_copies.append(pltpu.make_async_copy(wu, o_up, local_sems.at[8]))
    for cp in out_copies:
        cp.start()

    def outputs(mb):
        o_din[mb] = end_sums(mb, 0)
        o_block[mb] = (o_resid[mb] + end_sums(mb, 1)).astype(bf16)

    outputs(0)
    pass_sums(1)
    outputs(1)
    for mb in range(MICRO):
        for s in range(2 * ne):

            @pl.when(s != s_me)
            def _():
                wire.arrive(r_dg + mb * 2 * ne + s, dgs.at[0, 0])

        groups = []
        sub8 = lax.broadcasted_iota(jnp.int32, (8, rows), 0)
        for base in range(0, experts, 8):
            group = dg[mb, base]
            for j in range(1, 8):
                group = jnp.where(sub8 == j, dg[mb, base + j], group)
            groups.append(group)
        lines = jnp.concatenate(groups + [jnp.zeros((128 - experts, rows), f32)], axis=0)
        o_dprobs[mb] = lines.T

    for cp in out_copies:
        cp.wait()
    for k in range(1, ne):
        wire.left(r_dz + 3 * (k - 1), qkv)
        wire.left(r_dz + 3 * (k - 1) + 1, outw)
        wire.left(r_dz + 3 * (k - 1) + 2, s_src)
    wire.left(r_id, ids)
    wire.left(r_id + 1, ids)
    for k in range(2 * MICRO):
        wire.left(r_h + k, hp.at[0])
    for k in range(1, chips):
        wire.left(r_dx + 2 * (k - 1), blk)
        wire.left(r_dx + 2 * (k - 1) + 1, sblk)
    for k in range(chips):
        wire.left(r_ds + 2 * k, blk)
        wire.left(r_ds + 2 * k + 1, sblk)
    for k in range(1, nd):
        wire.left(r_w + 2 * (k - 1), win.at[0])
        wire.left(r_w + 2 * (k - 1) + 1, wout.at[0])
    for k in range(ne):
        if k > 0:
            wire.left(r_rk + 2 * k, rk_src)
        wire.left(r_rk + 2 * k + 1, rk_src)
    for g in [g_d[1]] + g_x:
        g.drain()
    for mb in range(MICRO):
        for t in range(2):
            base = (mb * 2 + t) * ne
            for zp in range(ne):
                wire.left(r_cx + base + zp, qo.at[0, 0, 0])
            for to in range(1, ne):

                @pl.when(z < to)
                def _():
                    wire.left(r_up + base + to, qo.at[0, 0, 0])

            for to in range(ne - 1):

                @pl.when(z > to)
                def _():
                    wire.left(r_dn + base + to, qo.at[0, 0, 0])

        for s in range(2 * ne):

            @pl.when(s != s_me)
            def _():
                wire.left(r_dg + mb * 2 * ne + s, dgs.at[0, 0])

    assert wire.used <= ROLES


ROLES = 240


def front(nd, ne, tokens, image_ids, routes, qkv, outw, small, win, wout, cot):
    rows, share = tokens.shape[1], qkv.shape[1]
    halo = -(-(IMG - 1) // 16) * 16
    experts = 2 * ne
    slots = 4 * rows // experts
    shape = jax.ShapeDtypeStruct
    outs = (
        shape((MICRO, rows, D), bf16),
        shape((MICRO, rows, D), f32),
        shape((MICRO, rows, 128), f32),
        shape((D, FF), bf16),
        shape((D, FF), bf16),
        shape((MICRO, rows, D), bf16),
        shape((MICRO, rows, 128), f32),
        shape((MICRO, rows, D), f32),
        shape((MICRO, rows, D), bf16),
        shape((MICRO, 3, 3 * rows, D), bf16),
        shape((MICRO, rows, 128), f32),
        shape((4, D, D), bf16),
        shape((D, 128), f32),
        shape((MICRO, 1, 3 * rows), f32),
    )
    vmem, anywhere = pl.BlockSpec(memory_space=pltpu.VMEM), pl.BlockSpec(memory_space=pl.ANY)
    v = pltpu.VMEM
    return pl.pallas_call(
        functools.partial(front_kernel, nd, ne),
        out_shape=outs,
        in_specs=[vmem, vmem, vmem, anywhere, anywhere, vmem, anywhere, anywhere, anywhere],
        out_specs=[anywhere if k in (3, 4) else vmem for k in range(len(outs))],
        scratch_shapes=[
            v((share + 16, 128), bf16),
            v((nd * ne, share + 16, 128), bf16),
            v((MICRO, halo, D), bf16),
            v((MICRO, halo, D), bf16),
            v((MICRO, rows), jnp.int32),
            v((MICRO, rows), jnp.int32),
            v((MICRO, 2 * ne, rows, D), bf16),
            v((MICRO, 2 * ne, rows, D), bf16),
            v((D, FF), bf16),
            v((FF, D), bf16),
            v((MICRO, experts, rows), f32),
            v((2 * ne, MICRO, experts, rows), f32),
            v((3 * rows, D), bf16),
            v((rows, 3 * rows), f32),
            v((D, FF), f32),
            v((D, FF), f32),
            v((2, slots, rows), bf16),
            v((2 * slots, D), bf16),
            v((2 * slots, D), bf16),
            v((2 * slots, D), bf16),
            v((D, 2 * slots), bf16),
            v((D, 2 * slots), bf16),
            v((2 * slots, 128), f32),
            v((2 * slots, D), f32),
            v((2 * slots, D), f32),
            v((2, 2 * slots, D), bf16),
            v((MICRO, 2, ne, rows, D), bf16),
            v((MICRO, 2, ne, rows, D), bf16),
            v((MICRO, 2, ne, rows, D), bf16),
            v((MICRO, 2, ne + 1, rows, D), bf16),
            v((MICRO, 2 * ne, 8, rows), f32),
            v((MICRO, experts, 8, rows), f32),
            pltpu.SemaphoreType.DMA((ROLES,)),
            pltpu.SemaphoreType.DMA((ROLES,)),
            pltpu.SemaphoreType.DMA((9,)),
        ],
        compiler_params=pltpu.CompilerParams(
            collective_id=0, has_side_effects=True, vmem_limit_bytes=VMEM_BYTES
        ),
        name="front",
    )(tokens, image_ids, routes, qkv, outw, small, win, wout, cot)


def mm_exact(a, b):
    return jnp.dot(a, b, preferred_element_type=f32, precision=highest)


def back_kernel(
    nd,
    ne,
    tok,
    cot,
    d_in,
    d_probs,
    up,
    down,
    n2,
    probs,
    resid,
    mixed,
    qkv,
    lse,
    w,
    small,
    idr,
    o_input,
    o_dense,
    o_small,
    o_up,
    o_down,
    gu,
    gd,
    d_res,
    dm,
    stat_src,
    stat_p,
    stat_n,
    hp,
    hn,
    stats,
    bias,
    dp,
    gw,
    gs,
    gwb,
    gsb,
    rc,
    rcs,
    sx,
    sxs,
    rx,
    rxs,
    sz,
    szs,
    rz,
    rzs,
    send_sems,
    recv_sems,
    local_sems,
):
    me = Place(nd, ne)
    d, z, c = me.d, me.z, me.c
    rows = tok.shape[1]
    experts = 2 * ne
    halo = hp.shape[1]
    gap = rows - halo
    chips = nd // 2
    wire = Wire(send_sems, recv_sems, me.sib)
    lane = lax.broadcasted_iota(jnp.int32, (1, 128), 1)
    up_rows, down_rows = gu.shape[1], gd.shape[2]
    part = D // nd
    share = part // ne
    me.enter()

    r_g = wire.roles(2 * (nd - 1))

    def up_of(dd):
        return up.at[pl.ds(pl.multiple_of(dd * up_rows, 16), up_rows)]

    def down_of(dd):
        return down.at[:, pl.ds(pl.multiple_of(dd * down_rows, 128), down_rows)]

    own_g = [
        pltpu.make_async_copy(up_of(d), gu.at[d], local_sems.at[0]),
        pltpu.make_async_copy(down_of(d), gd.at[d], local_sems.at[1]),
    ]
    for cp in own_g:
        cp.start()
    for k in range(1, nd):
        dd = lax.rem(d + k, nd)
        wire.send(r_g + 2 * (k - 1), up_of(dd), gu.at[d], (dd, z))
        wire.send(r_g + 2 * (k - 1) + 1, down_of(dd), gd.at[d], (dd, z))

    s_rows = small[...].T
    gains = [s_rows[experts + k : experts + k + 1, :] for k in range(2)]
    router = jnp.where(lane < experts, small[...], 0.0)
    head_of = (
        lax.broadcasted_iota(jnp.int32, (D, 128), 0) // HEAD_DIM
        == lax.broadcasted_iota(jnp.int32, (D, 128), 1)
    ).astype(f32)

    def norm_back(values, dn, gain):
        offset = values - jnp.mean(values, axis=-1, keepdims=True)
        inv = lax.rsqrt(jnp.mean(offset * offset, axis=-1, keepdims=True) + norm_eps)
        hat = offset * inv
        q = dn * gain
        dv = inv * (
            q
            - jnp.mean(q, axis=-1, keepdims=True)
            - hat * jnp.mean(q * hat, axis=-1, keepdims=True)
        )
        return dv, jnp.sum(dn * hat, axis=0, keepdims=True), jnp.sum(dn, axis=0, keepdims=True)

    r_h = wire.roles(4 * MICRO)
    norm_sums = [jnp.zeros((1, D), f32) for _ in range(4)]
    zero_gap = jnp.zeros((gap, D), bf16)
    own = slice(rows, 2 * rows)
    for mb in range(MICRO):
        prob, dpr = probs[mb], d_probs[mb]
        d_logits = prob * (dpr - jnp.sum(prob * dpr, axis=-1, keepdims=True))
        dn2 = d_in[mb] + lax.dot_general(
            d_logits,
            router,
            (((1,), (1,)), ((), ())),
            preferred_element_type=f32,
            precision=highest,
        )
        dv, d_gain, d_bias = norm_back(resid[mb], dn2, gains[1])
        norm_sums[1] += d_gain
        norm_sums[3] += d_bias
        d_resid = cot[mb].astype(f32) + dv
        d_res[mb] = d_resid
        d_attn = d_resid.astype(bf16)
        d_mixed = mm_nt(d_attn, w[3]).astype(bf16)
        dm[mb, own, :] = d_mixed
        delta = mm_exact(d_mixed.astype(f32) * mixed[mb].astype(f32), head_of)
        stat_src[mb, 0] = lse[mb].T[0:HEADS, :]
        stat_src[mb, 1] = delta.T[0:HEADS, :]
        low, high = pl.ds(rows, halo), pl.ds(2 * rows - halo, halo)
        wire.send(r_h + 4 * mb, dm.at[mb, high], hp.at[mb], me.next)
        wire.send(r_h + 4 * mb + 1, stat_src.at[mb], stat_p.at[mb], me.next)
        wire.send(r_h + 4 * mb + 2, dm.at[mb, low], hn.at[mb], me.prev)
        wire.send(r_h + 4 * mb + 3, stat_src.at[mb], stat_n.at[mb], me.prev)
        g_out = mm(mixed[mb].T, d_attn)
        g_router = mm_exact(n2[mb].astype(f32).T, d_logits)
        if mb == 0:
            gw[3] = g_out
            gs[...] = g_router
        else:
            gw[3] += g_out
            gs[...] += g_router

    scale = 1.0 / math.sqrt(HEAD_DIM)
    for mb in range(MICRO):
        ids = idr[mb]
        idc = jnp.broadcast_to(ids[:, own], (128, rows)).T[:, 0:1]
        bias[...] = jnp.where(idc == ids, 0.0, neg_big)
        dst = jnp.zeros((rows, 128), f32)
        delta_cols = jnp.concatenate(
            [stat_src[mb, 1], jnp.zeros((128 - HEADS, rows), f32)], axis=0
        ).T

        @pl.loop(0, HEADS // 2)
        def _(pair):
            at = pl.ds(pl.multiple_of(pair * 128, 128), 128)
            query, grad = qkv[mb, 0, own, at], dm[mb, own, at]
            key, value = qkv[mb, 1, :, at], qkv[mb, 2, :, at]
            dq = jnp.zeros((rows, 128), f32)
            for half in range(2):
                keep = (lane < 64) if half == 0 else (lane >= 64)
                h = 2 * pair + half
                q = jnp.where(keep, query, jnp.zeros_like(query))
                g = jnp.where(keep, grad, jnp.zeros_like(grad))
                k = jnp.where(keep, key, jnp.zeros_like(key))
                lse_col = jnp.sum(jnp.where(lane == h, lse[mb], 0.0), axis=1, keepdims=True)
                delta_col = jnp.sum(jnp.where(lane == h, delta_cols, 0.0), axis=1, keepdims=True)
                p = jnp.exp(mm_nt(q, key) * scale + bias[...] - lse_col)
                ds = (p * (mm_nt(g, value) - delta_col)).astype(bf16)
                dq = dq + mm(ds, k)
            dp[0, :, at] = (dq * scale).astype(bf16)

        wire.arrive(r_h + 4 * mb, hp.at[mb])
        wire.arrive(r_h + 4 * mb + 1, stat_src.at[mb])
        wire.arrive(r_h + 4 * mb + 2, hp.at[mb])
        wire.arrive(r_h + 4 * mb + 3, stat_src.at[mb])
        dm[mb, 0:gap, :] = zero_gap
        dm[mb, gap:rows, :] = hp[mb]
        dm[mb, 2 * rows : 2 * rows + halo, :] = hn[mb]
        dm[mb, 2 * rows + halo : 3 * rows, :] = zero_gap
        for k in range(2):
            stats[k, :, 0:rows] = stat_p[mb, k]
            stats[k, :, own] = stat_src[mb, k]
            stats[k, :, 2 * rows : 3 * rows] = stat_n[mb, k]

        @pl.loop(0, HEADS // 2)
        def _(pair):
            at = pl.ds(pl.multiple_of(pair * 128, 128), 128)
            query, grad = qkv[mb, 0, :, at], dm[mb, :, at]
            key, value = qkv[mb, 1, own, at], qkv[mb, 2, own, at]
            dk = jnp.zeros((rows, 128), f32)
            dv = jnp.zeros((rows, 128), f32)
            for half in range(2):
                keep = (lane < 64) if half == 0 else (lane >= 64)
                h = 2 * pair + half
                q = jnp.where(keep, query, jnp.zeros_like(query))
                g = jnp.where(keep, grad, jnp.zeros_like(grad))
                k = jnp.where(keep, key, jnp.zeros_like(key))
                v = jnp.where(keep, value, jnp.zeros_like(value))
                p = jnp.exp(mm_nt(k, query) * scale + bias[...] - stats[0, pl.ds(h, 1), :])
                ds = (p * (mm_nt(v, grad) - stats[1, pl.ds(h, 1), :])).astype(bf16)
                dk = dk + mm(ds, q)
                dv = dv + mm(p.astype(bf16), g)
            dp[1, :, at] = (dk * scale).astype(bf16)
            dp[2, :, at] = dv.astype(bf16)

        token = tok[mb].astype(f32)
        n1t = normed(token, gains[0], s_rows[experts + 2 : experts + 3, :]).astype(bf16).T
        dn1 = jnp.zeros((rows, D), f32)
        for k in range(3):
            dn1 = dn1 + mm_nt(dp[k], w[k])
            g_part = mm(n1t, dp[k])
            if mb == 0:
                gw[k] = g_part
            else:
                gw[k] += g_part
        dv, d_gain, d_bias = norm_back(token, dn1, gains[0])
        norm_sums[0] += d_gain
        norm_sums[2] += d_bias
        o_input[mb] = (d_res[mb] + dv).astype(bf16)

    rows128 = lax.broadcasted_iota(jnp.int32, (128, D), 0)
    norm_rows = jnp.zeros((128, D), f32)
    for k in range(4):
        norm_rows = jnp.where(rows128 == experts + k, norm_sums[k], norm_rows)
    gs[...] = jnp.where(lane < experts, gs[...], norm_rows.T)

    def of(dd):
        return pl.ds(pl.multiple_of(dd * part, 16), part)

    r_c = wire.roles(2 * chips)
    r_x = wire.roles(2 * (chips - 1))
    r_z = wire.roles(2 * (ne - 1))
    for k in range(chips):
        dd = 2 * k + 1 - c
        for m in range(4):
            gwb[k, m] = gw[m, of(dd), :].astype(bf16)
        gsb[k] = gs[of(dd), :]
        wire.send(r_c + 2 * k, gwb.at[k], rc.at[k], me.sib)
        wire.send(r_c + 2 * k + 1, gsb.at[k], rcs.at[k], me.sib)
    for k in range(chips):
        wire.arrive(r_c + 2 * k, rc.at[k])
        wire.arrive(r_c + 2 * k + 1, rcs.at[k])
    my_chip = d // 2
    for k in range(1, chips):
        to = lax.rem(my_chip + k, chips)
        dd = 2 * to + c
        for m in range(4):
            sx[k, m] = (gw[m, of(dd), :] + rc[to, m].astype(f32)).astype(bf16)
        sxs[k] = gs[of(dd), :] + rcs[to]
        wire.send(r_x + 2 * (k - 1), sx.at[k], rx.at[k], (dd, z))
        wire.send(r_x + 2 * (k - 1) + 1, sxs.at[k], rxs.at[k], (dd, z))
    total = [gw[m, of(d), :] + rc[my_chip, m].astype(f32) for m in range(4)]
    total_s = gs[of(d), :] + rcs[my_chip]
    for k in range(1, chips):
        wire.arrive(r_x + 2 * (k - 1), rx.at[k])
        wire.arrive(r_x + 2 * (k - 1) + 1, rxs.at[k])
        total = [total[m] + rx[k, m].astype(f32) for m in range(4)]
        total_s = total_s + rxs[k]
    for m in range(4):
        gw[m, 0:part, :] = total[m]
    gs[0:part, :] = total_s
    for k in range(1, ne):
        to = lax.rem(z + k, ne)
        at = pl.ds(pl.multiple_of(to * share, 16), share)
        for m in range(4):
            sz[k, m] = gw[m, at, :].astype(bf16)
        szs[k] = gs[at, :]
        wire.send(r_z + 2 * (k - 1), sz.at[k], rz.at[k], (d, to))
        wire.send(r_z + 2 * (k - 1) + 1, szs.at[k], rzs.at[k], (d, to))

    for cp in own_g:
        cp.wait()
    for k in range(1, nd):
        wire.arrive(r_g + 2 * (k - 1), gu.at[0])
        wire.arrive(r_g + 2 * (k - 1) + 1, gd.at[0])
    for x in range(2):
        o_up[x] = sum(gu[2 * k + x].astype(f32) for k in range(chips))
        o_down[x] = sum(gd[2 * k + x].astype(f32) for k in range(chips)).T

    at = pl.ds(pl.multiple_of(z * share, 16), share)
    for k in range(1, ne):
        wire.arrive(r_z + 2 * (k - 1), rz.at[k])
        wire.arrive(r_z + 2 * (k - 1) + 1, rzs.at[k])
    for m in range(4):
        o_dense[m] = gw[m, at, :] + sum(rz[k, m].astype(f32) for k in range(1, ne))
    o_small[...] = gs[at, :] + sum(rzs[k] for k in range(1, ne))

    for k in range(1, nd):
        wire.left(r_g + 2 * (k - 1), gu.at[0])
        wire.left(r_g + 2 * (k - 1) + 1, gd.at[0])
    for mb in range(MICRO):
        for k in range(2):
            wire.left(r_h + 4 * mb + 2 * k, hp.at[0])
            wire.left(r_h + 4 * mb + 2 * k + 1, stat_src.at[0])
    for k in range(chips):
        wire.left(r_c + 2 * k, rc.at[0])
        wire.left(r_c + 2 * k + 1, rcs.at[0])
    for k in range(1, chips):
        wire.left(r_x + 2 * (k - 1), rx.at[0])
        wire.left(r_x + 2 * (k - 1) + 1, rxs.at[0])
    for k in range(1, ne):
        wire.left(r_z + 2 * (k - 1), rz.at[0])
        wire.left(r_z + 2 * (k - 1) + 1, rzs.at[0])
    assert wire.used <= BACK_ROLES


BACK_ROLES = 64


def back(nd, ne, *args):
    tokens = args[0]
    rows = tokens.shape[1]
    halo = -(-(IMG - 1) // 16) * 16
    chips = nd // 2
    part = D // nd
    share = part // ne
    shape = jax.ShapeDtypeStruct
    outs = (
        shape((MICRO, rows, D), bf16),
        shape((4, share, D), f32),
        shape((share, 128), f32),
        shape((2, D // nd, FF), f32),
        shape((2, FF // nd, D), f32),
    )
    vmem, anywhere = pl.BlockSpec(memory_space=pltpu.VMEM), pl.BlockSpec(memory_space=pl.ANY)
    v = pltpu.VMEM
    return pl.pallas_call(
        functools.partial(back_kernel, nd, ne),
        out_shape=outs,
        in_specs=[anywhere if k in (4, 5) else vmem for k in range(len(args))],
        out_specs=[vmem] * len(outs),
        scratch_shapes=[
            v((nd, D // nd, FF), bf16),
            v((nd, D, FF // nd), bf16),
            v((MICRO, rows, D), f32),
            v((MICRO, 3 * rows, D), bf16),
            v((MICRO, 2, HEADS, rows), f32),
            v((MICRO, 2, HEADS, rows), f32),
            v((MICRO, 2, HEADS, rows), f32),
            v((MICRO, halo, D), bf16),
            v((MICRO, halo, D), bf16),
            v((2, HEADS, 3 * rows), f32),
            v((rows, 3 * rows), f32),
            v((3, rows, D), bf16),
            v((4, D, D), f32),
            v((D, 128), f32),
            v((chips, 4, part, D), bf16),
            v((chips, part, 128), f32),
            v((chips, 4, part, D), bf16),
            v((chips, part, 128), f32),
            v((chips, 4, part, D), bf16),
            v((chips, part, 128), f32),
            v((chips, 4, part, D), bf16),
            v((chips, part, 128), f32),
            v((ne, 4, share, D), bf16),
            v((ne, share, 128), f32),
            v((ne, 4, share, D), bf16),
            v((ne, share, 128), f32),
            pltpu.SemaphoreType.DMA((BACK_ROLES,)),
            pltpu.SemaphoreType.DMA((BACK_ROLES,)),
            pltpu.SemaphoreType.DMA((2,)),
        ],
        compiler_params=pltpu.CompilerParams(
            collective_id=1, has_side_effects=True, vmem_limit_bytes=VMEM_BYTES
        ),
        name="back",
    )(*args)


def kernel_body(
    nd,
    ne,
    tokens,
    image_ids,
    routes,
    qkv_weight,
    out_weight,
    router_weight,
    norm_gains,
    norm_biases,
    expert_in,
    expert_out,
    cotangent,
):
    experts = 2 * ne
    small = jnp.concatenate([router_weight, norm_gains.T, norm_biases.T], axis=1)
    small = jnp.pad(small, ((0, 0), (0, 128 - experts - 4)))
    block_out, *saved = front(
        nd, ne, tokens, image_ids, routes, qkv_weight, out_weight, small, expert_in, expert_out, cotangent
    )
    input_grad, dense, small, grad_up, grad_down = back(nd, ne, tokens, cotangent, *saved)
    return (
        block_out,
        input_grad,
        dense[:3],
        dense[3],
        small[:, :experts],
        small[:, experts : experts + 2].T,
        small[:, experts + 2 : experts + 4].T,
        grad_up,
        grad_down,
    )


def chosen_body(nd, ne, tokens, *rest):
    rows, experts = tokens.shape[1], 2 * ne
    whole = D % (16 * nd * ne) == 0 and nd % 2 == 0 and 8 * rows == experts * rows and rows % 128 == 0
    if whole and rest[-3].shape[0] == 2:
        return kernel_body(nd, ne, tokens, *rest)
    return body(tokens, *rest)


def solution(mesh):
    return jax.shard_map(
        functools.partial(chosen_body, mesh.shape["dp"], mesh.shape["expert"]),
        mesh=mesh,
        in_specs=(
            P(None, ("dp", "expert"), None),
            P(None, ("dp", "expert")),
            P(None, ("dp", "expert"), None),
            P(None, ("dp", "expert"), None),
            P(("dp", "expert"), None),
            P(("dp", "expert"), None),
            P(None, ("dp", "expert")),
            P(None, ("dp", "expert")),
            P("expert", "dp", None),
            P("expert", "dp", None),
            P(None, ("dp", "expert"), None),
        ),
        out_specs=(
            P(None, ("dp", "expert"), None),
            P(None, ("dp", "expert"), None),
            P(None, ("dp", "expert"), None),
            P(("dp", "expert"), None),
            P(("dp", "expert"), None),
            P(None, ("dp", "expert")),
            P(None, ("dp", "expert")),
            P("expert", "dp", None),
            P("expert", "dp", None),
        ),
        check_vma=False,
    )
```

```python
import functools
import math

import jax
import jax.numpy as jnp
from jax import lax
from jax.experimental import pallas as pl
from jax.experimental.pallas import tpu as pltpu
from jax.sharding import PartitionSpec as P

D = 512
HEADS = 8
HEAD_DIM = 64
FF = 2048
TOP = 2
IMG = 197
MICRO = 2


neg_big = -1e30
norm_eps = 1e-06
highest = lax.Precision.HIGHEST


def padded(cells, sides, width):
    for axis, dim in sides:
        count = lax.axis_size(axis)
        ends = count - 1
        head = lax.slice_in_dim(cells, 0, width, axis=dim)
        tail = lax.slice_in_dim(cells, cells.shape[dim] - width, cells.shape[dim], axis=dim)
        cells = jnp.concatenate(
            [
                lax.ppermute(tail, axis, [(i, (i + 1) % count) for i in range(ends)]),
                cells,
                lax.ppermute(head, axis, [((i + 1) % count, i) for i in range(ends)]),
            ],
            axis=dim,
        )
    return cells


def layer_norm(values, gain_row, bias_row):
    centre = jnp.mean(values, axis=-1, keepdims=True)
    offset = values - centre
    spread = jnp.mean(offset * offset, axis=-1, keepdims=True)
    return offset * lax.rsqrt(spread + norm_eps) * gain_row + bias_row


def tanh_gelu(values):
    return jax.nn.gelu(values, approximate=True)


def fetch_dense(qkv_weight, out_weight, router_weight, norm_gains, norm_biases):
    rows, experts = router_weight.shape
    small = jnp.concatenate([router_weight, norm_gains.T, norm_biases.T], axis=1)
    small = jnp.pad(small, ((0, 0), (0, D - experts - 4)))
    packed = jnp.concatenate([qkv_weight, out_weight[None], small[None]], axis=0)
    full = lax.all_gather(packed, ("dp", "expert"), axis=1, tiled=True)
    return (
        full[:3],
        full[3],
        full[4][:, :experts],
        full[4][:, experts : experts + 2].T,
        full[4][:, experts + 2 : experts + 4].T,
    )


def fetch_experts(expert_in, expert_out):
    return (
        lax.all_gather(expert_in, "dp", axis=1, tiled=True),
        lax.all_gather(expert_out, "dp", axis=1, tiled=True),
    )


def plan_routes(route_ids, shard_experts):
    row_count = route_ids.shape[0]
    experts = shard_experts * lax.axis_size("expert")
    devices = lax.axis_size(("dp", "expert"))
    slot_count = 2 * TOP * row_count // experts
    capacity = 5 * TOP * row_count * devices // (4 * experts)
    labels = lax.broadcasted_iota(jnp.int32, (1, experts), 1)
    first_hot = (route_ids[:, 0:1] == labels).astype(jnp.int32)
    second_hot = (route_ids[:, 1:2] == labels).astype(jnp.int32)
    counts = jnp.stack([jnp.sum(first_hot, axis=0), jnp.sum(second_hot, axis=0)])
    all_counts = lax.all_gather(counts[None], ("dp", "expert"), axis=0, tiled=True)
    earlier = (
        lax.broadcasted_iota(jnp.int32, (devices, 1, 1), 0) < lax.axis_index(("dp", "expert"))
    ).astype(jnp.int32)
    before = jnp.sum(all_counts * earlier, axis=0)
    total_first = jnp.sum(all_counts[:, 0, :], axis=0)
    row_before = (
        lax.broadcasted_iota(jnp.int32, (row_count, row_count), 0)
        > lax.broadcasted_iota(jnp.int32, (row_count, row_count), 1)
    ).astype(jnp.bfloat16)

    def rank_of(hot):
        ahead = jnp.dot(row_before, hot.astype(jnp.bfloat16), preferred_element_type=jnp.float32)
        return jnp.sum(ahead.astype(jnp.int32) * hot, axis=1)

    rank_first = rank_of(first_hot)
    rank_second = rank_of(second_hot)
    place_first = jnp.sum(first_hot * before[0][None, :], axis=1) + rank_first
    place_second = jnp.sum(second_hot * (total_first + before[1])[None, :], axis=1) + rank_second
    kept_mask = jnp.stack([place_first < capacity, place_second < capacity], axis=1)
    slot_second = jnp.sum(second_hot * counts[0][None, :], axis=1) + rank_second
    flat_index = jnp.stack(
        [route_ids[:, 0] * slot_count + rank_first, route_ids[:, 1] * slot_count + slot_second],
        axis=1,
    )
    target = jnp.where(kept_mask, flat_index, experts * slot_count)
    return (first_hot, second_hot, target, kept_mask.astype(jnp.float32))


def fill_slots(row_pairs, target, experts, slot_count):
    feature_count = row_pairs.shape[-1]
    buffer = jnp.zeros((experts * slot_count + 1, feature_count), row_pairs.dtype)
    buffer = buffer.at[target.reshape(-1)].set(row_pairs.reshape(-1, feature_count))
    return buffer[:-1].reshape(experts, 1, slot_count, feature_count)


def read_slots(returned, target):
    feature_count = returned.shape[-1]
    flat_table = jnp.concatenate(
        [returned.reshape(-1, feature_count), jnp.zeros((1, feature_count), returned.dtype)], axis=0
    )
    return flat_table[target]


def run_forward(tokens_f, ids_ext, route_plan, dense_set, expert_set):
    qkv_full, out_full, router_full, gain_pair, bias_pair = dense_set
    expert_up_weight, expert_down_weight = expert_set
    first_hot, second_hot, target, kept_mask = route_plan
    row_count = tokens_f.shape[0]
    rim_rows = IMG - 1
    score_scale = 1.0 / math.sqrt(HEAD_DIM)
    experts = router_full.shape[1]
    slot_count = 2 * TOP * row_count // experts
    normed_one = layer_norm(
        tokens_f, gain_pair[0].astype(jnp.float32), bias_pair[0].astype(jnp.float32)
    ).astype(jnp.bfloat16)
    projected = jnp.einsum(
        "rd,cde->cre", normed_one, qkv_full, preferred_element_type=jnp.float32
    ).astype(jnp.bfloat16)
    key_value = padded(projected[1:], ((("dp", "expert"), 1),), rim_rows)
    query_heads = projected[0].reshape(row_count, HEADS, HEAD_DIM)
    key_heads = key_value[0].reshape(-1, HEADS, HEAD_DIM)
    value_heads = key_value[1].reshape(-1, HEADS, HEAD_DIM)
    same_image = ids_ext[rim_rows : rim_rows + row_count][:, None] == ids_ext[None, :]
    scores = (
        jnp.einsum("qhd,khd->hqk", query_heads, key_heads, preferred_element_type=jnp.float32)
        * score_scale
    )
    scores = jnp.where(same_image[None], scores, neg_big)
    top_score = jnp.max(scores, axis=-1, keepdims=True)
    log_total = top_score + jnp.log(jnp.sum(jnp.exp(scores - top_score), axis=-1, keepdims=True))
    att_probs = jnp.exp(scores - log_total)
    att_low = att_probs.astype(jnp.bfloat16)
    mixed_rows = (
        jnp.einsum("hqk,khd->qhd", att_low, value_heads, preferred_element_type=jnp.float32)
        .reshape(row_count, D)
        .astype(jnp.bfloat16)
    )
    residual = tokens_f + jnp.dot(mixed_rows, out_full, preferred_element_type=jnp.float32)
    normed_two = layer_norm(
        residual, gain_pair[1].astype(jnp.float32), bias_pair[1].astype(jnp.float32)
    ).astype(jnp.bfloat16)
    router_probs = jax.nn.softmax(
        jnp.dot(normed_two, router_full, preferred_element_type=jnp.float32), axis=-1
    )
    picked = jnp.stack(
        [jnp.sum(first_hot * router_probs, axis=1), jnp.sum(second_hot * router_probs, axis=1)],
        axis=1,
    )
    gate_values = kept_mask * picked
    outgoing = fill_slots(
        jnp.broadcast_to(normed_two[:, None, :], (row_count, TOP, D)), target, experts, slot_count
    )
    arrived = lax.all_to_all(outgoing, "expert", split_axis=0, concat_axis=1, tiled=True)
    shard_experts = arrived.shape[0]
    collected_token_rows = arrived.reshape(shard_experts, -1, D)
    hidden_pre = jnp.einsum(
        "ycq,yqt->yct", collected_token_rows, expert_up_weight, preferred_element_type=jnp.float32
    )
    hidden_activation = tanh_gelu(hidden_pre).astype(jnp.bfloat16)
    produced = jnp.einsum(
        "nso,nop->nsp", hidden_activation, expert_down_weight, preferred_element_type=jnp.float32
    ).astype(jnp.bfloat16)
    returned = lax.all_to_all(
        produced.reshape(arrived.shape), "expert", split_axis=1, concat_axis=0, tiled=True
    )
    expert_rows = read_slots(returned, target)
    block_value = residual + jnp.sum(
        gate_values[:, :, None] * expert_rows.astype(jnp.float32), axis=1
    )
    return (
        normed_one,
        query_heads,
        key_heads,
        value_heads,
        att_probs,
        att_low,
        mixed_rows,
        residual,
        normed_two,
        router_probs,
        gate_values,
        collected_token_rows,
        hidden_pre,
        hidden_activation,
        expert_rows,
        block_value,
    )


def run_backward(tokens_f, ids_ext, route_plan, dense_set, expert_set, upstream, gradients):
    qkv_full, out_full, router_full, gain_pair, bias_pair = dense_set
    expert_up_weight, expert_down_weight = expert_set
    first_hot, second_hot, target, kept_mask = route_plan
    grad_qkv, grad_out, grad_router, grad_gains, grad_biases, grad_in, grad_expert_out = gradients
    (
        normed_one,
        query_heads,
        key_heads,
        value_heads,
        att_probs,
        att_low,
        mixed_rows,
        residual,
        normed_two,
        router_probs,
        gate_values,
        collected_token_rows,
        hidden_pre,
        hidden_activation,
        expert_rows,
        block_value,
    ) = run_forward(tokens_f, ids_ext, route_plan, dense_set, expert_set)
    row_count = tokens_f.shape[0]
    rim_rows = IMG - 1
    score_scale = 1.0 / math.sqrt(HEAD_DIM)
    experts = router_full.shape[1]
    slot_count = 2 * TOP * row_count // experts
    shard_experts = expert_up_weight.shape[0]
    d_gate = kept_mask * jnp.sum(upstream[:, None, :] * expert_rows.astype(jnp.float32), axis=-1)
    d_sent = (gate_values[:, :, None] * upstream[:, None, :]).astype(jnp.bfloat16)
    d_arrived = lax.all_to_all(
        fill_slots(d_sent, target, experts, slot_count),
        "expert",
        split_axis=0,
        concat_axis=1,
        tiled=True,
    )
    produced_rows_grad = d_arrived.reshape(shard_experts, -1, D)
    activation_grad = jnp.einsum(
        "tkw,tew->tke", produced_rows_grad, expert_down_weight, preferred_element_type=jnp.float32
    )
    grad_expert_out = grad_expert_out + jnp.einsum(
        "meq,mek->mqk", hidden_activation, produced_rows_grad, preferred_element_type=jnp.float32
    )
    gelu_value, gelu_back = jax.vjp(tanh_gelu, hidden_pre)
    preactivation_grad = gelu_back(activation_grad)[0].astype(jnp.bfloat16)
    grad_in = grad_in + jnp.einsum(
        "zjo,zjm->zom", collected_token_rows, preactivation_grad, preferred_element_type=jnp.float32
    )
    d_rows = jnp.einsum(
        "iht,imt->ihm", preactivation_grad, expert_up_weight, preferred_element_type=jnp.float32
    ).astype(jnp.bfloat16)
    d_back = lax.all_to_all(
        d_rows.reshape(d_arrived.shape), "expert", split_axis=1, concat_axis=0, tiled=True
    )
    d_normed_two = jnp.sum(
        kept_mask[:, :, None] * read_slots(d_back, target).astype(jnp.float32), axis=1
    )
    d_probs = first_hot * d_gate[:, 0:1] + second_hot * d_gate[:, 1:2]
    d_logits = router_probs * (d_probs - jnp.sum(router_probs * d_probs, axis=-1, keepdims=True))
    router_wide = router_full.astype(jnp.float32)
    d_normed_two = d_normed_two + jnp.dot(d_logits, router_wide.T, precision=highest)
    grad_router = grad_router + jnp.dot(
        normed_two.astype(jnp.float32).T, d_logits, precision=highest
    )
    norm_value, second_back = jax.vjp(
        layer_norm, residual, gain_pair[1].astype(jnp.float32), bias_pair[1].astype(jnp.float32)
    )
    d_resid_part, d_gain_two, d_bias_two = second_back(d_normed_two)
    d_resid = upstream + d_resid_part
    d_attn = d_resid.astype(jnp.bfloat16)
    grad_out = grad_out + jnp.einsum(
        "rd,re->de", mixed_rows, d_attn, preferred_element_type=jnp.float32
    )
    d_mixed = (
        jnp.einsum("re,de->rd", d_attn, out_full, preferred_element_type=jnp.float32)
        .astype(jnp.bfloat16)
        .reshape(row_count, HEADS, HEAD_DIM)
    )
    d_att = jnp.einsum("qhd,khd->hqk", d_mixed, value_heads, preferred_element_type=jnp.float32)
    d_scores = (att_probs * (d_att - jnp.sum(att_probs * d_att, axis=-1, keepdims=True))).astype(
        jnp.bfloat16
    )
    d_query = (
        (
            jnp.einsum("hqk,khd->qhd", d_scores, key_heads, preferred_element_type=jnp.float32)
            * score_scale
        )
        .astype(jnp.bfloat16)
        .reshape(row_count, D)
    )
    d_key = (
        jnp.einsum("hqk,qhd->khd", d_scores, query_heads, preferred_element_type=jnp.float32)
        * score_scale
    )
    d_value = jnp.einsum("hqk,qhd->khd", att_low, d_mixed, preferred_element_type=jnp.float32)
    d_pair = jnp.stack([d_key.reshape(-1, D), d_value.reshape(-1, D)])
    rim_grads = jnp.concatenate([d_pair[:, :rim_rows], d_pair[:, rim_rows + row_count :]], axis=1)
    beside_all = padded(rim_grads.astype(jnp.bfloat16), ((("dp", "expert"), 1),), rim_rows).astype(
        rim_grads.dtype
    )
    own_part = d_pair[:, rim_rows : rim_rows + row_count]
    from_below = jnp.pad(beside_all[:, :rim_rows], ((0, 0), (0, row_count - rim_rows), (0, 0)))
    from_above = jnp.pad(beside_all[:, 3 * rim_rows :], ((0, 0), (row_count - rim_rows, 0), (0, 0)))
    d_kv = (own_part + from_below + from_above).astype(jnp.bfloat16)
    d_projected = jnp.concatenate([d_query[None], d_kv], axis=0)
    grad_qkv = grad_qkv + jnp.einsum(
        "rd,cre->cde", normed_one, d_projected, preferred_element_type=jnp.float32
    )
    d_normed_one = jnp.einsum(
        "cre,cde->rd", d_projected, qkv_full, preferred_element_type=jnp.float32
    )
    first_value, first_back = jax.vjp(
        layer_norm, tokens_f, gain_pair[0].astype(jnp.float32), bias_pair[0].astype(jnp.float32)
    )
    d_tokens_part, d_gain_one, d_bias_one = first_back(d_normed_one)
    grad_gains = grad_gains + jnp.stack([d_gain_one, d_gain_two])
    grad_biases = grad_biases + jnp.stack([d_bias_one, d_bias_two])
    input_rows = (d_resid + d_tokens_part).astype(jnp.bfloat16)
    return (
        input_rows,
        (grad_qkv, grad_out, grad_router, grad_gains, grad_biases, grad_in, grad_expert_out),
    )


def body(
    tokens,
    image_ids,
    routes,
    qkv_weight,
    out_weight,
    router_weight,
    norm_gains,
    norm_biases,
    expert_in,
    expert_out,
    cotangent,
):
    shard_experts = expert_in.shape[0]
    rim_rows = IMG - 1
    experts = shard_experts * lax.axis_size("expert")
    outputs = []
    saved_state = []
    for batch_index in range(MICRO):
        dense_set = fetch_dense(qkv_weight, out_weight, router_weight, norm_gains, norm_biases)
        expert_set = fetch_experts(expert_in, expert_out)
        ids_ext = padded(image_ids[batch_index] + 1, ((("dp", "expert"), 0),), rim_rows)
        route_plan = plan_routes(routes[batch_index], shard_experts)
        forward_state = run_forward(
            tokens[batch_index].astype(jnp.float32), ids_ext, route_plan, dense_set, expert_set
        )
        outputs.append(forward_state[-1].astype(jnp.bfloat16))
        saved_state.append((ids_ext, route_plan))
    gradients = (
        jnp.zeros((3, D, D), jnp.float32),
        jnp.zeros((D, D), jnp.float32),
        jnp.zeros((D, experts), jnp.float32),
        jnp.zeros((2, D), jnp.float32),
        jnp.zeros((2, D), jnp.float32),
        jnp.zeros((shard_experts, D, FF), jnp.float32),
        jnp.zeros((shard_experts, FF, D), jnp.float32),
    )
    input_grads = []
    for batch_index in range(MICRO):
        dense_set = fetch_dense(qkv_weight, out_weight, router_weight, norm_gains, norm_biases)
        expert_set = fetch_experts(expert_in, expert_out)
        ids_ext, route_plan = saved_state[batch_index]
        input_rows, gradients = run_backward(
            tokens[batch_index].astype(jnp.float32),
            ids_ext,
            route_plan,
            dense_set,
            expert_set,
            cotangent[batch_index].astype(jnp.float32),
            gradients,
        )
        input_grads.append(input_rows)
    grad_qkv, grad_out, grad_router, grad_gains, grad_biases, grad_in, grad_expert_out = gradients
    small = jnp.concatenate([grad_router, grad_gains.T, grad_biases.T], axis=1)
    small = jnp.pad(small, ((0, 0), (0, D - experts - 4)))
    packed = jnp.concatenate([grad_qkv, grad_out[None], small[None]], axis=0)
    packed = lax.psum_scatter(packed, ("dp", "expert"), scatter_dimension=1, tiled=True)
    dense_grads = (
        packed[:3],
        packed[3],
        packed[4][:, :experts],
        packed[4][:, experts : experts + 2].T,
        packed[4][:, experts + 2 : experts + 4].T,
    )
    expert_grads = (
        lax.psum_scatter(
            grad_in.astype(jnp.bfloat16), "dp", scatter_dimension=1, tiled=True
        ).astype(jnp.float32),
        lax.psum_scatter(
            grad_expert_out.astype(jnp.bfloat16), "dp", scatter_dimension=1, tiled=True
        ).astype(jnp.float32),
    )
    return (
        jnp.stack(outputs),
        jnp.stack(input_grads),
        dense_grads[0],
        dense_grads[1],
        dense_grads[2],
        dense_grads[3],
        dense_grads[4],
        expert_grads[0],
        expert_grads[1],
    )


MESH = pl.DeviceIdType.MESH
f32, bf16 = jnp.float32, jnp.bfloat16
VMEM_BYTES = 62 << 20


def mm(a, b):
    return jnp.dot(a, b, preferred_element_type=f32)


def mm_nt(a, b):
    return lax.dot_general(a, b, (((1,), (1,)), ((), ())), preferred_element_type=f32)


def normed(values, gain_row, bias_row):
    centre = jnp.mean(values, axis=-1, keepdims=True)
    offset = values - centre
    spread = jnp.mean(offset * offset, axis=-1, keepdims=True)
    return offset * lax.rsqrt(spread + norm_eps) * gain_row + bias_row


class Wire:
    def __init__(self, send_sems, recv_sems, other):
        self.send_sems, self.recv_sems, self.other = send_sems, recv_sems, other
        self.used, self.sent = 0, {}

    def roles(self, count=1):
        self.used += count
        return self.used - count

    def copy(self, send_role, recv_role, src, dst, device):
        return pltpu.make_async_remote_copy(
            src_ref=src,
            dst_ref=dst,
            send_sem=self.send_sems.at[send_role],
            recv_sem=self.recv_sems.at[recv_role],
            device_id=device,
            device_id_type=MESH,
        )

    def send(self, role, src, dst, device, recv_role=None):
        self.copy(role, role if recv_role is None else recv_role, src, dst, device).start()

    def arrive(self, role, like):
        self.copy(role, role, like, like, self.other).wait_recv()

    def left(self, role, like):
        self.copy(role, role, like, like, self.other).wait_send()


class Place:
    def __init__(self, nd, ne):
        self.nd, self.ne = nd, ne
        self.d, self.z = lax.axis_index("dp"), lax.axis_index("expert")
        d, z = self.d, self.z
        self.c = lax.rem(d, 2)
        self.sib_d = d + 1 - 2 * self.c
        self.sib = (self.sib_d, z)
        self.idx = d * ne + z
        last = (z == ne - 1).astype(jnp.int32)
        first = (z == 0).astype(jnp.int32)
        self.next = (lax.rem(d + last, nd), lax.rem(z + 1, ne))
        self.prev = (lax.rem(d + nd - first, nd), lax.rem(z + ne - 1, ne))
        self.xn = d + 2 - 4 * lax.rem(d // 2, 2)
        self.yn = d + 4 - 8 * (d // 4)
        self.up = (d, jnp.minimum(z + 1, ne - 1))
        self.down = (d, jnp.maximum(z - 1, 0))

    def chip(self, k):
        return lax.rem(self.d + 2 * k, self.nd)

    def enter(self):
        bar = pltpu.get_barrier_semaphore()

        def greet(device):
            pl.semaphore_signal(bar, inc=1, device_id=device, device_id_type=MESH)

        for k in range(1, self.nd):
            greet((lax.rem(self.d + k, self.nd), self.z))
        for k in range(1, self.ne):
            zk = lax.rem(self.z + k, self.ne)
            greet((self.d, zk))
            greet((self.sib_d, zk))
        greet(self.next)
        greet(self.prev)
        pl.semaphore_wait(bar, self.nd - 1 + 2 * (self.ne - 1) + 2)


class Chain:
    def __init__(self, wire, me, full):
        self.wire, self.me, self.full = wire, me, full
        n = me.ne
        self.up, self.dn = wire.roles(n - 1), wire.roles(n - 1)
        self.su, self.sd, self.so = wire.roles(n - 1), wire.roles(n - 1), wire.roles()

    def at(self, z):
        return self.full.at[z * 2 + self.me.c]

    def own(self, src):
        m, n = self.me, self.me.ne

        @pl.when(m.z < n - 1)
        def _():
            self.wire.send(self.up, src, self.at(m.z), m.up)

        @pl.when(m.z > 0)
        def _():
            self.wire.send(self.dn, src, self.at(m.z), m.down)

        self.wire.send(self.so, src, self.at(m.z), m.sib)

    def pump(self, k):
        m, n, w = self.me, self.me.ne, self.wire

        @pl.when(m.z >= k + 1)
        def _():
            block = self.at(m.z - 1 - k)
            w.arrive(self.up + k, block)
            if k + 1 < n - 1:

                @pl.when(m.z < n - 1)
                def _():
                    w.send(self.up + k + 1, block, block, m.up)

            w.send(self.su + k, block, block, m.sib)

        @pl.when(m.z + k + 1 < n)
        def _():
            block = self.at(m.z + 1 + k)
            w.arrive(self.dn + k, block)
            if k + 1 < n - 1:

                @pl.when(m.z > 0)
                def _():
                    w.send(self.dn + k + 1, block, block, m.down)

            w.send(self.sd + k, block, block, m.sib)

    def near(self):
        self.wire.arrive(self.so, self.full.at[0])

    def finish(self, k):
        m, n, w, like = self.me, self.me.ne, self.wire, self.full.at[0]

        @pl.when(m.z >= k + 1)
        def _():
            w.arrive(self.su + k, like)

        @pl.when(m.z + k + 1 < n)
        def _():
            w.arrive(self.sd + k, like)

    def drain(self):
        m, n, w, like = self.me, self.me.ne, self.wire, self.full.at[0]
        w.left(self.so, like)
        for k in range(n - 1):

            @pl.when((m.z < n - 1) & (m.z >= k))
            def _():
                w.left(self.up + k, like)

            @pl.when((m.z > 0) & (m.z + k < n))
            def _():
                w.left(self.dn + k, like)

            @pl.when(m.z >= k + 1)
            def _():
                w.left(self.su + k, like)

            @pl.when(m.z + k + 1 < n)
            def _():
                w.left(self.sd + k, like)


def front_kernel(
    nd,
    ne,
    tok,
    ids,
    routes,
    qkv,
    outw,
    routw,
    gainw,
    biasw,
    win,
    wout,
    cot,
    o_din,
    o_y,
    o_dprobs,
    o_up,
    o_down,
    o_n2,
    o_probs,
    o_resid,
    o_mixed,
    o_qkv,
    o_lse,
    w_all,
    o_small,
    o_idr,
    s_src,
    s_all,
    hp,
    hn,
    ip,
    inx,
    gx,
    gd,
    wu,
    wd,
    rk_src,
    rk,
    bias,
    acts,
    grads,
    pm,
    xs,
    ds,
    deo,
    xt,
    dt,
    gt,
    acc_eo,
    acc_di,
    ys,
    qo,
    cs,
    cr,
    ud,
    dgs,
    dg,
    stage,
    square,
    send_sems,
    recv_sems,
    local_sems,
):
    me = Place(nd, ne)
    d, z, c = me.d, me.z, me.c
    rows = tok.shape[1]
    share = qkv.shape[1]
    experts = 2 * ne
    halo = hp.shape[1]
    ext = 3 * rows
    slots = 4 * rows // experts
    capacity = 5 * TOP * rows * nd * ne // (4 * experts)
    e = 2 * z + c
    s_me = z * 2 + c
    wire = Wire(send_sems, recv_sems, me.sib)
    lane = lax.broadcasted_iota(jnp.int32, (1, 128), 1)

    before_row = (
        lax.broadcasted_iota(jnp.int32, (rows, rows), 0)
        > lax.broadcasted_iota(jnp.int32, (rows, rows), 1)
    ).astype(bf16)
    square[...] = jnp.zeros_like(square)
    square[0:experts, 0:share] = routw[...].astype(f32)
    square[experts : experts + 2, 0:share] = gainw[...].astype(f32)
    square[experts + 2 : experts + 4, 0:share] = biasw[...].astype(f32)
    s_src[0:share, :] = square[...].T[0:share, :].astype(bf16)
    row128 = lax.broadcasted_iota(jnp.int32, (128, rows), 0)
    row16 = lax.broadcasted_iota(jnp.int32, (16, 128), 0)
    hots = []
    counts = jnp.zeros((16, 128), f32)
    for mb in range(MICRO):
        choice = routes[mb].astype(f32)
        wide = jnp.where(row128 == 0, choice[0:1], jnp.where(row128 == 1, choice[1:2], -1.0)).T
        pair = [(wide[:, k : k + 1] == lane.astype(f32)).astype(f32) for k in range(TOP)]
        hots.append(pair)
        for k in range(TOP):
            counts = jnp.where(row16 == mb * TOP + k, jnp.sum(pair[k], axis=0, keepdims=True), counts)
    s_src[share : share + 16, :] = counts.astype(bf16)

    me.enter()

    r_dz = wire.roles(3 * (ne - 1))
    mine = pl.ds(pl.multiple_of(me.idx * share, 16), share)
    for k in range(1, ne):
        dev = (d, lax.rem(z + k, ne))
        wire.send(r_dz + 3 * (k - 1), qkv, w_all.at[pl.ds(0, 3), mine], dev)
        wire.send(r_dz + 3 * (k - 1) + 1, outw, w_all.at[3, mine], dev)
        wire.send(r_dz + 3 * (k - 1) + 2, s_src, s_all.at[me.idx], dev)
    local = [
        pltpu.make_async_copy(qkv, w_all.at[pl.ds(0, 3), mine], local_sems.at[0]),
        pltpu.make_async_copy(outw, w_all.at[3, mine], local_sems.at[1]),
        pltpu.make_async_copy(s_src, s_all.at[me.idx], local_sems.at[2]),
    ]
    for cp in local:
        cp.start()
    up_rows, down_rows = win.shape[1], wout.shape[1]

    def up_at(dd, n=1):
        return wu.at[pl.ds(pl.multiple_of(dd * up_rows, 16), n * up_rows)]

    def down_at(dd, n=1):
        return wd.at[pl.ds(pl.multiple_of(dd * down_rows, 16), n * down_rows)]

    own_w = [
        pltpu.make_async_copy(win.at[c], up_at(d), local_sems.at[5]),
        pltpu.make_async_copy(wout.at[c], down_at(d), local_sems.at[6]),
    ]
    for cp in own_w:
        cp.start()
    r_ux, r_dy, r_uy, r_dx2 = (wire.roles(2) for _ in range(4))
    r_uf, r_df, r_us, r_dsib = (wire.roles() for _ in range(4))
    for cc in range(2):
        wire.send(r_ux + cc, win.at[cc], up_at(d), (me.xn - c + cc, z), recv_role=r_ux + c)
        wire.send(r_dy + cc, wout.at[cc], down_at(d), (me.yn - c + cc, z), recv_role=r_dy + c)
    r_id = wire.roles(2)
    wire.send(r_id, ids, ip, me.next)
    wire.send(r_id + 1, ids, inx, me.prev)
    r_h = wire.roles(2 * MICRO)

    def send_halo(mb):
        wire.send(r_h + 2 * mb, tok.at[mb, pl.ds(rows - halo, halo)], hp.at[mb], me.next)
        wire.send(r_h + 2 * mb + 1, tok.at[mb, pl.ds(0, halo)], hn.at[mb], me.prev)

    send_halo(0)
    g_d = [Chain(wire, me, gd.at[mb]) for mb in range(MICRO)]
    g_x = [Chain(wire, me, gx.at[mb]) for mb in range(MICRO)]
    own_d = [
        pltpu.make_async_copy(cot.at[mb], gd.at[mb, s_me], local_sems.at[3 + mb])
        for mb in range(MICRO)
    ]
    for cp in own_d:
        cp.start()

    for cp in local:
        cp.wait()
    for k in range(1, ne):
        wire.arrive(r_dz + 3 * (k - 1), qkv)
        wire.arrive(r_dz + 3 * (k - 1) + 1, outw)
        wire.arrive(r_dz + 3 * (k - 1) + 2, s_src)

    def column(dd):
        at = pl.ds(pl.multiple_of(dd * (ne * share), 16), ne * share)
        return w_all.at[:, at], s_all.at[pl.ds(dd * ne, ne)]

    chips = nd // 2
    r_dx = wire.roles(2 * (chips - 1))
    r_ds = wire.roles(2 * chips)
    blk, sblk = column(d)
    for k in range(1, chips):
        wire.send(r_dx + 2 * (k - 1), blk, blk, (me.chip(k), z))
        wire.send(r_dx + 2 * (k - 1) + 1, sblk, sblk, (me.chip(k), z))
    wire.send(r_ds, blk, blk, me.sib)
    wire.send(r_ds + 1, sblk, sblk, me.sib)
    send_halo(1)
    g_d[0].own(cot.at[0])
    wire.send(r_us, win.at[1 - c], up_at(d), me.sib)
    wire.send(r_dsib, wout.at[1 - c], down_at(d), me.sib)
    for k in range(1, chips):
        wire.arrive(r_dx + 2 * (k - 1), blk)
        wire.arrive(r_dx + 2 * (k - 1) + 1, sblk)
        b, sb = column(lax.rem(d + nd - 2 * k, nd))
        wire.send(r_ds + 2 * k, b, b, me.sib)
        wire.send(r_ds + 2 * k + 1, sb, sb, me.sib)
    for cc in range(2):
        wire.send(r_dx2 + cc, wout.at[cc], down_at(d), (me.xn - c + cc, z), recv_role=r_dx2 + c)
        wire.send(r_uy + cc, win.at[cc], up_at(d), (me.yn - c + cc, z), recv_role=r_uy + c)
        wire.arrive(r_ux + cc, win.at[0])
        wire.arrive(r_dy + cc, wout.at[0])
    wire.send(r_uf, up_at(me.xn - c, 2), up_at(me.xn - c, 2), (me.yn, z))
    wire.send(r_df, down_at(me.yn - c, 2), down_at(me.yn - c, 2), (me.xn, z))
    for k in range(chips):
        wire.arrive(r_ds + 2 * k, blk)
        wire.arrive(r_ds + 2 * k + 1, sblk)

    o_small[...] = s_all[:, 0:share, :].reshape(D, 128).astype(f32)
    s_rows = o_small[...].T
    all_counts = s_all[:, share : share + 16, :].astype(f32)
    ahead = lax.broadcasted_iota(jnp.int32, all_counts.shape, 0) < me.idx
    before = jnp.sum(jnp.where(ahead, all_counts, 0.0), axis=0)
    total = jnp.sum(all_counts, axis=0)
    gains = [s_rows[experts + k : experts + k + 1, :] for k in range(2)]
    biases = [s_rows[experts + 2 + k : experts + 3 + k, :] for k in range(2)]

    r_rk = wire.roles(2 * ne)

    def send_ranks():
        for mb in range(MICRO):
            one, two = hots[mb]
            rank_one = mm(before_row, one.astype(bf16))
            rank_two = mm(before_row, two.astype(bf16))
            b1, b2 = before[2 * mb : 2 * mb + 1], before[2 * mb + 1 : 2 * mb + 2]
            t1 = total[2 * mb : 2 * mb + 1]
            place_one = jnp.sum(one * (b1 + rank_one), axis=1, keepdims=True)
            place_two = jnp.sum(two * (t1 + b2 + rank_two), axis=1, keepdims=True)
            kept = one * (place_one < capacity).astype(f32) + two * (place_two < capacity).astype(
                f32
            )
            ranks = jnp.where(kept > 0.0, rank_one + rank_two, -1.0)
            rk_src[mb] = ranks.T[0:experts, :]
        for k in range(ne):
            zk = lax.rem(z + k, ne)
            if k > 0:
                wire.send(r_rk + 2 * k, rk_src, rk.at[s_me], (d, zk))
            wire.send(r_rk + 2 * k + 1, rk_src, rk.at[s_me], (me.sib_d, zk))
        rk[s_me] = rk_src[...]

    wire.arrive(r_id, ids)
    wire.arrive(r_id + 1, ids)
    pos = lax.broadcasted_iota(jnp.int32, (1, rows), 1)
    gap = rows - halo
    for mb in range(MICRO):
        here = ids[mb : mb + 1, :].astype(f32)
        below = jnp.where((pos >= gap) & (me.idx > 0), ip[mb : mb + 1, :].astype(f32), -1.0)
        above = jnp.where(
            (pos < halo) & (me.idx < nd * ne - 1), inx[mb : mb + 1, :].astype(f32), -1.0
        )
        o_idr[mb] = jnp.concatenate([below, here, above], axis=1)

    zero_gap = jnp.zeros((gap, D), bf16)
    acts[0:gap, 0:D] = zero_gap
    acts[ext - gap : ext, 0:D] = zero_gap
    scale = 1.0 / math.sqrt(HEAD_DIM)
    saves = [pltpu.make_async_copy(
            acts.at[pl.ds(0, ext), pl.ds(D, 3 * D)], o_qkv.at[mb], local_sems.at[7 + mb]
        )
        for mb in range(MICRO)]

    def attend(mb, hooks):
        wire.arrive(r_h + 2 * mb, hp.at[mb])
        wire.arrive(r_h + 2 * mb + 1, hn.at[mb])

        def put(value, start):
            acts[start : start + value.shape[0], 0:D] = normed(
                value.astype(f32), gains[0], biases[0]
            ).astype(bf16)

        put(hp[mb], gap)
        put(tok[mb], rows)
        put(hn[mb], 2 * rows)
        if mb > 0:
            saves[mb - 1].wait()
        for k in range(3):
            for r in range(3):
                part = slice(r * rows, (r + 1) * rows)
                acts[part, (k + 1) * D : (k + 2) * D] = mm(acts[part, 0:D], w_all[k]).astype(bf16)
        saves[mb].start()
        idr = o_idr[mb]
        idc = jnp.broadcast_to(idr[:, rows : 2 * rows], (128, rows)).T[:, 0:1]
        bias[...] = jnp.where(idc == idr, 0.0, neg_big)
        o_lse[mb] = jnp.zeros((rows, 128), f32)

        @pl.loop(0, HEADS // 2)
        def _(pair):
            at = pl.ds(pl.multiple_of(pair * 128, 128), 128)
            query, key, value = (
                acts[part, pl.ds(pl.multiple_of((k + 1) * D + pair * 128, 128), 128)]
                for k, part in enumerate((slice(rows, 2 * rows), slice(0, ext), slice(0, ext)))
            )
            mixed = jnp.zeros((rows, 128), f32)
            lse = o_lse[mb]
            for half in range(2):
                keep = (lane < 64) if half == 0 else (lane >= 64)
                q = jnp.where(keep, query, jnp.zeros_like(query))
                v = jnp.where(keep, value, jnp.zeros_like(value))
                s = mm_nt(q, key) * scale + bias[...]
                top = jnp.max(s, axis=-1, keepdims=True)
                p = jnp.exp(s - top)
                total_p = jnp.sum(p, axis=-1, keepdims=True)
                mixed = mixed + mm((p * (1.0 / total_p)).astype(bf16), v)
                lse = jnp.where(lane == 2 * pair + half, top + jnp.log(total_p), lse)
            o_lse[mb] = lse
            o_mixed[mb, :, at] = mixed.astype(bf16)
            for when, hook in hooks.items():
                pl.when(pair == when)(hook)

        resid = tok[mb].astype(f32) + mm(o_mixed[mb], w_all[3])
        o_resid[mb] = resid
        n2 = normed(resid, gains[1], biases[1]).astype(bf16)
        o_n2[mb] = n2
        gx[mb, s_me] = n2
        g_x[mb].own(gx.at[mb, s_me])
        logits = mm(n2, o_small[...].astype(bf16))
        logits = jnp.where(lane < experts, logits, neg_big)
        p = jnp.exp(logits - jnp.max(logits, axis=-1, keepdims=True))
        o_probs[mb] = p / jnp.sum(p, axis=-1, keepdims=True)

    def later_halves():
        g_x[0].pump(0)
        g_d[1].own(cot.at[1])

    attend(0, {0: lambda: g_d[0].pump(0), 3: lambda: g_d[0].pump(1)})
    send_ranks()
    attend(1, {0: lambda: g_d[0].pump(2), 2: later_halves})
    g_x[0].pump(1)

    r_cx = wire.roles(2 * MICRO * ne)
    r_up = wire.roles(MICRO * ne)
    r_dn = wire.roles(MICRO * ne)
    r_dg = wire.roles(MICRO * 2 * ne)
    sub = lax.broadcasted_iota(jnp.int32, (slots, rows), 0).astype(f32)
    tile = 2 * slots
    chunk = 512
    like = qo.at[0, 0, 0]

    def target(i):
        swap = jnp.where(i < 2, 1 - i, i)
        return jnp.where(
            z == 0, i, jnp.where(z == 1, swap, jnp.where(z == 2, ne - 1 - swap, ne - 1 - i))
        )

    def pass_up(mb, to):
        wire.send(r_up + mb * ne + to, qo.at[mb, 0, to], ud.at[mb, to], me.up)

    def pass_down(mb, to):
        slot = jnp.where(z - 1 == to, ne, to)
        wire.send(r_dn + mb * ne + to, qo.at[mb, 0, to], ud.at[mb, slot], me.down)

    def settle(mb, zp):
        for t in range(2):
            wire.arrive(r_cx + (mb * 2 + t) * ne + zp, like)
            qo[mb, t, zp] = (qo[mb, t, zp].astype(f32) + cr[mb, t, zp].astype(f32)).astype(bf16)

        @pl.when((z == 0) & (zp > 0))
        def _():
            pass_up(mb, zp)

        @pl.when((z == ne - 1) & (zp < ne - 1))
        def _():
            pass_down(mb, zp)

    def relay(mb, hop, to):
        @pl.when(z == hop)
        def _():
            wire.arrive(r_up + mb * ne + to, like)
            qo[mb, 0, to] = (qo[mb, 0, to].astype(f32) + ud[mb, to].astype(f32)).astype(bf16)
            pass_up(mb, to)

        @pl.when(z == ne - 1 - hop)
        def _():
            low = ne - 1 - to
            wire.arrive(r_dn + mb * ne + low, like)
            qo[mb, 0, low] = (qo[mb, 0, low].astype(f32) + ud[mb, low].astype(f32)).astype(bf16)
            pass_down(mb, low)

    def end_sums(mb):
        acc_eo[...] = qo[mb, 0, z].astype(f32)

        @pl.when(z > 0)
        def _():
            wire.arrive(r_up + mb * ne + z, like)
            acc_eo[...] += ud[mb, z].astype(f32)

        @pl.when(z < ne - 1)
        def _():
            wire.arrive(r_dn + mb * ne + z, like)
            acc_eo[...] += ud[mb, ne].astype(f32)

        o_din[mb] = acc_eo[...]

    def first_tile():
        for cp in own_w + own_d + saves[1:]:
            cp.wait()
        for cc in range(2):
            wire.arrive(r_uy + cc, win.at[0])
            wire.arrive(r_dx2 + cc, wout.at[0])
        wire.arrive(r_us, win.at[0])
        wire.arrive(r_dsib, wout.at[0])
        wire.arrive(r_uf, up_at(0, 2))
        wire.arrive(r_df, down_at(0, 2))
        for k in range(ne):
            if k > 0:
                wire.arrive(r_rk + 2 * k, rk_src)
            wire.arrive(r_rk + 2 * k + 1, rk_src)
        g_d[0].near()
        g_x[0].near()

    def both(mb, what, k):
        for g in (g_d[mb], g_x[mb]):
            getattr(g, what)(k)

    def tile_1():
        both(0, "finish", 0)
        g_x[0].pump(2)

    def tile_2():
        both(0, "finish", 1)

    def tile_3():
        both(0, "finish", 2)
        both(1, "pump", 0)

    def tile_4():
        g_d[1].near()
        g_x[1].near()

    def tile_5():
        both(1, "finish", 0)
        both(1, "pump", 1)
        relay(0, 1, 2)

    def tile_6():
        both(1, "finish", 1)
        both(1, "pump", 2)
        relay(0, 1, 3)

    def tile_7():
        both(1, "finish", 2)
        relay(0, 2, 3)

    before_tile = [first_tile, tile_1, tile_2, tile_3, tile_4, tile_5, tile_6, tile_7]

    @pl.loop(0, MICRO * ne)
    def _(i):
        mb = i // ne
        zp = target(lax.rem(i, ne))

        @pl.when(i > 0)
        def _():
            settle((i - 1) // ne, target(lax.rem(i - 1 + ne, ne)))

        for when, hook in enumerate(before_tile):
            pl.when(i == when)(hook)

        for cc in range(2):
            s = zp * 2 + cc
            at = slice(cc * slots, (cc + 1) * slots)
            pick = (sub == rk[s, mb, pl.ds(e, 1), :]).astype(bf16)
            pm[cc] = pick
            xs[at, :] = mm(pick, gx[mb, s]).astype(bf16)
            ds[at, :] = mm(pick, gd[mb, s]).astype(bf16)
        x = xs[...]
        logits = mm(x, o_small[...].astype(bf16))
        logits = jnp.where(lane < experts, logits, neg_big)
        p = jnp.exp(logits - jnp.max(logits, axis=-1, keepdims=True))
        p = p / jnp.sum(p, axis=-1, keepdims=True)
        gate = jnp.sum(jnp.where(lane == e, p, 0.0), axis=-1, keepdims=True)
        gt[...] = jnp.broadcast_to(gate, (tile, 128))
        dy = (gate * ds[...].astype(f32)).astype(bf16)
        deo[...] = dy
        across = pl.ds(pl.multiple_of(i * tile, tile), tile)
        xt[:, across] = x.T
        dt[:, across] = dy.T
        acc_eo[...] = jnp.zeros_like(acc_eo)
        acc_di[...] = jnp.zeros_like(acc_di)

        @pl.loop(0, FF // chunk)
        def _(f):
            at = pl.ds(pl.multiple_of(f * chunk, chunk), chunk)
            pre = mm(xs[...], wu[:, at])
            d_act = mm_nt(deo[...], wd[at, :])
            sq = pre * pre
            k0 = math.sqrt(2.0 / math.pi)
            th = jnp.tanh(pre * (k0 + (k0 * 0.044715) * sq))
            half = 0.5 + 0.5 * th
            act = (pre * half).astype(bf16)
            slope = half + (0.5 * pre) * (1.0 - th * th) * (k0 + (3.0 * k0 * 0.044715) * sq)
            d_pre = (slope * d_act).astype(bf16)
            acts[across, at] = act
            grads[across, at] = d_pre
            acc_eo[...] += mm(act, wd[at, :])
            acc_di[...] += mm_nt(d_pre, wu[:, at])

        eo = acc_eo[...].astype(bf16).astype(f32)
        d_gate = jnp.sum(ds[...].astype(f32) * eo, axis=-1, keepdims=True)
        ys[0] = acc_di[...].astype(bf16)
        ys[1] = (gt[:, 0:1] * eo).astype(bf16)
        box = lax.rem(i, 2)

        @pl.when(i > 1)
        def _():
            old = i - 2
            for t in range(2):
                wire.left(r_cx + ((old // ne) * 2 + t) * ne + target(lax.rem(old, ne)), like)

        for own in range(2):
            cc = c if own else 1 - c
            back = pm[cc].T
            at = pl.ds(pl.multiple_of(cc * slots, slots), slots)
            for t in range(2):
                moved = mm(back, ys[t, at, :]).astype(bf16)
                if own:
                    qo[mb, t, zp] = moved
                else:
                    cs[box, t] = moved
        for t in range(2):
            role = r_cx + (mb * 2 + t) * ne + zp
            wire.send(role, cs.at[box, t], cr.at[mb, t, zp], me.sib)
        for cc in range(2):
            at = slice(cc * slots, (cc + 1) * slots)
            line = jnp.sum(pm[cc].astype(f32) * d_gate[at], axis=0, keepdims=True)
            to = zp * 2 + cc
            dgs[mb, to] = jnp.broadcast_to(line, (8, rows))

            @pl.when(to != s_me)
            def _():
                wire.send(
                    r_dg + mb * 2 * ne + to,
                    dgs.at[mb, to],
                    dg.at[mb, e],
                    (d - c + cc, zp),
                    recv_role=r_dg + mb * 2 * ne + s_me,
                )

            @pl.when(to == s_me)
            def _():
                dg[mb, e] = jnp.broadcast_to(line, (8, rows))

    settle(1, target(ne - 1))

    wide_at = [pl.ds(k * chunk, chunk) for k in range(FF // chunk)]
    outs = []
    hooks = {0: lambda: relay(1, 1, 2), 1: lambda: relay(1, 1, 3), 3: lambda: relay(1, 2, 3)}
    for f, at in enumerate(wide_at):
        for k, (left, right, to) in enumerate(((xt, grads, o_up), (dt, acts, o_down))):
            if f > 1:
                outs[2 * (f - 2) + k].wait()
            stage[f % 2, k] = mm(left[...], right[:, at]).astype(bf16)
            cp = pltpu.make_async_copy(stage.at[f % 2, k], to.at[:, at], local_sems.at[9 + 2 * f + k])
            cp.start()
            outs.append(cp)
        if f in hooks:
            hooks[f]()
    end_sums(0)
    give_y = [pltpu.make_async_copy(qo.at[mb, 1], o_y.at[mb], local_sems.at[mb]) for mb in range(MICRO)]
    for cp in give_y:
        cp.start()
    for mb in range(MICRO):
        for s in range(2 * ne):

            @pl.when(s != s_me)
            def _():
                wire.arrive(r_dg + mb * 2 * ne + s, dgs.at[0, 0])

        groups = []
        sub8 = lax.broadcasted_iota(jnp.int32, (8, rows), 0)
        for base in range(0, experts, 8):
            group = dg[mb, base]
            for j in range(1, 8):
                group = jnp.where(sub8 == j, dg[mb, base + j], group)
            groups.append(group)
        lines = jnp.concatenate(groups + [jnp.zeros((128 - experts, rows), f32)], axis=0)
        o_dprobs[mb] = lines.T
    end_sums(1)
    for cp in outs[-4:] + give_y:
        cp.wait()

    for k in range(1, ne):
        wire.left(r_dz + 3 * (k - 1), qkv)
        wire.left(r_dz + 3 * (k - 1) + 1, outw)
        wire.left(r_dz + 3 * (k - 1) + 2, s_src)
    wire.left(r_id, ids)
    wire.left(r_id + 1, ids)
    for k in range(2 * MICRO):
        wire.left(r_h + k, hp.at[0])
    for k in range(1, chips):
        wire.left(r_dx + 2 * (k - 1), blk)
        wire.left(r_dx + 2 * (k - 1) + 1, sblk)
    for k in range(chips):
        wire.left(r_ds + 2 * k, blk)
        wire.left(r_ds + 2 * k + 1, sblk)
    for cc in range(2):
        wire.left(r_ux + cc, win.at[0])
        wire.left(r_uy + cc, win.at[0])
        wire.left(r_dy + cc, wout.at[0])
        wire.left(r_dx2 + cc, wout.at[0])
    wire.left(r_us, win.at[0])
    wire.left(r_dsib, wout.at[0])
    wire.left(r_uf, up_at(0, 2))
    wire.left(r_df, down_at(0, 2))
    for k in range(ne):
        if k > 0:
            wire.left(r_rk + 2 * k, rk_src)
        wire.left(r_rk + 2 * k + 1, rk_src)
    for g in g_d + g_x:
        g.drain()
    for old in (MICRO * ne - 2, MICRO * ne - 1):
        for t in range(2):
            wire.left(r_cx + ((old // ne) * 2 + t) * ne + target(old % ne), like)
    for mb in range(MICRO):
        for to in range(1, ne):

            @pl.when(z < to)
            def _():
                wire.left(r_up + mb * ne + to, like)

        for to in range(ne - 1):

            @pl.when(z > to)
            def _():
                wire.left(r_dn + mb * ne + to, like)

        for s in range(2 * ne):

            @pl.when(s != s_me)
            def _():
                wire.left(r_dg + mb * 2 * ne + s, dgs.at[0, 0])

    assert wire.used <= ROLES


ROLES = 192


def front(nd, ne, *args):
    tokens, qkv = args[0], args[3]
    rows, share = tokens.shape[1], qkv.shape[1]
    halo = -(-(IMG - 1) // 16) * 16
    experts = 2 * ne
    slots = 4 * rows // experts
    tile = 2 * slots
    every = MICRO * ne * tile
    shape = jax.ShapeDtypeStruct
    vmem, anywhere = pl.BlockSpec(memory_space=pltpu.VMEM), pl.BlockSpec(memory_space=pl.ANY)
    outs = (
        (vmem, (MICRO, rows, D), f32),
        (anywhere, (MICRO, ne, rows, D), bf16),
        (vmem, (MICRO, rows, 128), f32),
        (anywhere, (D, FF), bf16),
        (anywhere, (D, FF), bf16),
        (vmem, (MICRO, rows, D), bf16),
        (vmem, (MICRO, rows, 128), f32),
        (vmem, (MICRO, rows, D), f32),
        (vmem, (MICRO, rows, D), bf16),
        (anywhere, (MICRO, 3 * rows, 3 * D), bf16),
        (vmem, (MICRO, rows, 128), f32),
        (vmem, (4, D, D), bf16),
        (vmem, (D, 128), f32),
        (vmem, (MICRO, 1, 3 * rows), f32),
    )
    v = pltpu.VMEM
    return pl.pallas_call(
        functools.partial(front_kernel, nd, ne),
        out_shape=[shape(*o[1:]) for o in outs],
        in_specs=[vmem, vmem, vmem, anywhere, anywhere, vmem, vmem, vmem] + [anywhere] * 3,
        out_specs=[o[0] for o in outs],
        scratch_shapes=[
            v((share + 16, 128), bf16),
            v((nd * ne, share + 16, 128), bf16),
            v((MICRO, halo, D), bf16),
            v((MICRO, halo, D), bf16),
            v((MICRO, rows), jnp.int32),
            v((MICRO, rows), jnp.int32),
            v((MICRO, 2 * ne, rows, D), bf16),
            v((MICRO, 2 * ne, rows, D), bf16),
            v((D, FF), bf16),
            v((FF, D), bf16),
            v((MICRO, experts, rows), f32),
            v((2 * ne, MICRO, experts, rows), f32),
            v((rows, 3 * rows), f32),
            v((every, FF), bf16),
            v((every, FF), bf16),
            v((2, slots, rows), bf16),
            v((tile, D), bf16),
            v((tile, D), bf16),
            v((tile, D), bf16),
            v((D, every), bf16),
            v((D, every), bf16),
            v((tile, 128), f32),
            v((tile, D), f32),
            v((tile, D), f32),
            v((2, tile, D), bf16),
            v((MICRO, 2, ne, rows, D), bf16),
            v((2, 2, rows, D), bf16),
            v((MICRO, 2, ne, rows, D), bf16),
            v((MICRO, ne + 1, rows, D), bf16),
            v((MICRO, 2 * ne, 8, rows), f32),
            v((MICRO, experts, 8, rows), f32),
            v((2, 2, D, 512), bf16),
            v((128, 128), f32),
            pltpu.SemaphoreType.DMA((ROLES,)),
            pltpu.SemaphoreType.DMA((ROLES,)),
            pltpu.SemaphoreType.DMA((17,)),
        ],
        compiler_params=pltpu.CompilerParams(
            collective_id=0, has_side_effects=True, vmem_limit_bytes=VMEM_BYTES
        ),
        name="front",
    )(*args)


def mm_exact(a, b):
    return jnp.dot(a, b, preferred_element_type=f32, precision=highest)


def back_kernel(
    nd,
    ne,
    tok,
    cot,
    d_in,
    y,
    d_probs,
    up,
    down,
    n2,
    probs,
    resid,
    mixed,
    qkv,
    lse,
    w,
    small,
    idr,
    o_block,
    o_input,
    o_dense,
    o_small,
    o_up,
    o_down,
    yq,
    yu,
    gu,
    gd,
    d_res,
    dm,
    stat_src,
    stat_p,
    stat_n,
    hp,
    hn,
    stats,
    bias,
    dp,
    gw,
    gs,
    gwb,
    gsb,
    rc,
    rcs,
    sx,
    sxs,
    rx,
    rxs,
    sz,
    szs,
    rz,
    rzs,
    block,
    send_sems,
    recv_sems,
    local_sems,
):
    me = Place(nd, ne)
    d, z, c = me.d, me.z, me.c
    rows = tok.shape[1]
    experts = 2 * ne
    halo = hp.shape[1]
    gap = rows - halo
    chips = nd // 2
    wire = Wire(send_sems, recv_sems, me.sib)
    lane = lax.broadcasted_iota(jnp.int32, (1, 128), 1)
    up_rows, down_rows = gu.shape[1], gd.shape[2]
    part = D // nd
    share = part // ne
    me.enter()

    r_g = wire.roles(2 * (nd - 1))

    def up_of(dd):
        return up.at[pl.ds(pl.multiple_of(dd * up_rows, 16), up_rows)]

    def down_of(dd):
        return down.at[:, pl.ds(pl.multiple_of(dd * down_rows, 128), down_rows)]

    own_g = [
        pltpu.make_async_copy(up_of(d), gu.at[d], local_sems.at[0]),
        pltpu.make_async_copy(down_of(d), gd.at[d], local_sems.at[1]),
    ]
    for cp in own_g:
        cp.start()
    for k in range(1, nd):
        dd = lax.rem(d + k, nd)
        wire.send(r_g + 2 * (k - 1), up_of(dd), gu.at[d], (dd, z))
        wire.send(r_g + 2 * (k - 1) + 1, down_of(dd), gd.at[d], (dd, z))

    fetch = pltpu.make_async_copy(y, yq, local_sems.at[2])
    fetch.start()
    r_up = wire.roles(MICRO * ne)
    r_dn = wire.roles(MICRO * ne)
    like = yq.at[0, 0]

    def pass_up(mb, to):
        wire.send(r_up + mb * ne + to, yq.at[mb, to], yu.at[mb, to], me.up)

    def pass_down(mb, to):
        slot = jnp.where(z - 1 == to, ne, to)
        wire.send(r_dn + mb * ne + to, yq.at[mb, to], yu.at[mb, slot], me.down)

    def start_sums(mb):
        @pl.when(z == 0)
        def _():
            for to in range(ne - 1, 0, -1):
                pass_up(mb, to)

        @pl.when(z == ne - 1)
        def _():
            for to in range(ne - 1):
                pass_down(mb, to)

    def relay(mb, hop, to):
        @pl.when(z == hop)
        def _():
            wire.arrive(r_up + mb * ne + to, like)
            yq[mb, to] = (yq[mb, to].astype(f32) + yu[mb, to].astype(f32)).astype(bf16)
            pass_up(mb, to)

        @pl.when(z == ne - 1 - hop)
        def _():
            low = ne - 1 - to
            wire.arrive(r_dn + mb * ne + low, like)
            yq[mb, low] = (yq[mb, low].astype(f32) + yu[mb, low].astype(f32)).astype(bf16)
            pass_down(mb, low)

    def end_sums(mb):
        block[...] = resid[mb] + yq[mb, z].astype(f32)

        @pl.when(z > 0)
        def _():
            wire.arrive(r_up + mb * ne + z, like)
            block[...] += yu[mb, z].astype(f32)

        @pl.when(z < ne - 1)
        def _():
            wire.arrive(r_dn + mb * ne + z, like)
            block[...] += yu[mb, ne].astype(f32)

        o_block[mb] = block[...].astype(bf16)

    s_rows = small[...].T
    gains = [s_rows[experts + k : experts + k + 1, :] for k in range(2)]
    router = jnp.where(lane < experts, small[...], 0.0)
    head_of = (
        lax.broadcasted_iota(jnp.int32, (D, 128), 0) // HEAD_DIM
        == lax.broadcasted_iota(jnp.int32, (D, 128), 1)
    ).astype(f32)

    def norm_back(values, dn, gain):
        offset = values - jnp.mean(values, axis=-1, keepdims=True)
        inv = lax.rsqrt(jnp.mean(offset * offset, axis=-1, keepdims=True) + norm_eps)
        hat = offset * inv
        q = dn * gain
        dv = inv * (
            q
            - jnp.mean(q, axis=-1, keepdims=True)
            - hat * jnp.mean(q * hat, axis=-1, keepdims=True)
        )
        return dv, jnp.sum(dn * hat, axis=0, keepdims=True), jnp.sum(dn, axis=0, keepdims=True)

    r_h = wire.roles(4 * MICRO)
    norm_sums = [jnp.zeros((1, D), f32) for _ in range(4)]
    zero_gap = jnp.zeros((gap, D), bf16)
    own = slice(rows, 2 * rows)
    for mb in range(MICRO):
        prob, dpr = probs[mb], d_probs[mb]
        d_logits = prob * (dpr - jnp.sum(prob * dpr, axis=-1, keepdims=True))
        dn2 = d_in[mb] + lax.dot_general(
            d_logits,
            router,
            (((1,), (1,)), ((), ())),
            preferred_element_type=f32,
            precision=highest,
        )
        dv, d_gain, d_bias = norm_back(resid[mb], dn2, gains[1])
        norm_sums[1] += d_gain
        norm_sums[3] += d_bias
        d_resid = cot[mb].astype(f32) + dv
        d_res[mb] = d_resid
        d_attn = d_resid.astype(bf16)
        d_mixed = mm_nt(d_attn, w[3]).astype(bf16)
        dm[mb, own, :] = d_mixed
        delta = mm_exact(d_mixed.astype(f32) * mixed[mb].astype(f32), head_of)
        stat_src[mb, 0] = lse[mb].T[0:HEADS, :]
        stat_src[mb, 1] = delta.T[0:HEADS, :]
        low, high = pl.ds(rows, halo), pl.ds(2 * rows - halo, halo)
        wire.send(r_h + 4 * mb, dm.at[mb, high], hp.at[mb], me.next)
        wire.send(r_h + 4 * mb + 1, stat_src.at[mb], stat_p.at[mb], me.next)
        wire.send(r_h + 4 * mb + 2, dm.at[mb, low], hn.at[mb], me.prev)
        wire.send(r_h + 4 * mb + 3, stat_src.at[mb], stat_n.at[mb], me.prev)
        g_out = mm(mixed[mb].T, d_attn)
        g_router = mm_exact(n2[mb].astype(f32).T, d_logits)
        if mb == 0:
            gw[3] = g_out
            gs[...] = g_router
        else:
            gw[3] += g_out
            gs[...] += g_router

    fetch.wait()
    for mb in range(MICRO):
        start_sums(mb)
    scale = 1.0 / math.sqrt(HEAD_DIM)
    for mb in range(MICRO):
        ids = idr[mb]
        idc = jnp.broadcast_to(ids[:, own], (128, rows)).T[:, 0:1]
        bias[...] = jnp.where(idc == ids, 0.0, neg_big)
        dst = jnp.zeros((rows, 128), f32)
        delta_cols = jnp.concatenate(
            [stat_src[mb, 1], jnp.zeros((128 - HEADS, rows), f32)], axis=0
        ).T

        @pl.loop(0, HEADS // 2)
        def _(pair):
            at = pl.ds(pl.multiple_of(pair * 128, 128), 128)
            query, key, value = (
                qkv[mb, part, pl.ds(pl.multiple_of(k * D + pair * 128, 128), 128)]
                for k, part in enumerate((own, slice(None), slice(None)))
            )
            grad = dm[mb, own, at]
            dq = jnp.zeros((rows, 128), f32)
            for half in range(2):
                keep = (lane < 64) if half == 0 else (lane >= 64)
                h = 2 * pair + half
                q = jnp.where(keep, query, jnp.zeros_like(query))
                g = jnp.where(keep, grad, jnp.zeros_like(grad))
                k = jnp.where(keep, key, jnp.zeros_like(key))
                lse_col = jnp.sum(jnp.where(lane == h, lse[mb], 0.0), axis=1, keepdims=True)
                delta_col = jnp.sum(jnp.where(lane == h, delta_cols, 0.0), axis=1, keepdims=True)
                p = jnp.exp(mm_nt(q, key) * scale + bias[...] - lse_col)
                ds = (p * (mm_nt(g, value) - delta_col)).astype(bf16)
                dq = dq + mm(ds, k)
            dp[0, :, at] = (dq * scale).astype(bf16)

        relay(mb, 1, 3)
        wire.arrive(r_h + 4 * mb, hp.at[mb])
        wire.arrive(r_h + 4 * mb + 1, stat_src.at[mb])
        wire.arrive(r_h + 4 * mb + 2, hp.at[mb])
        wire.arrive(r_h + 4 * mb + 3, stat_src.at[mb])
        dm[mb, 0:gap, :] = zero_gap
        dm[mb, gap:rows, :] = hp[mb]
        dm[mb, 2 * rows : 2 * rows + halo, :] = hn[mb]
        dm[mb, 2 * rows + halo : 3 * rows, :] = zero_gap
        for k in range(2):
            stats[k, :, 0:rows] = stat_p[mb, k]
            stats[k, :, own] = stat_src[mb, k]
            stats[k, :, 2 * rows : 3 * rows] = stat_n[mb, k]

        @pl.loop(0, HEADS // 2)
        def _(pair):
            at = pl.ds(pl.multiple_of(pair * 128, 128), 128)
            query, key, value = (
                qkv[mb, part, pl.ds(pl.multiple_of(k * D + pair * 128, 128), 128)]
                for k, part in enumerate((slice(None), own, own))
            )
            grad = dm[mb, :, at]
            dk = jnp.zeros((rows, 128), f32)
            dv = jnp.zeros((rows, 128), f32)
            for half in range(2):
                keep = (lane < 64) if half == 0 else (lane >= 64)
                h = 2 * pair + half
                q = jnp.where(keep, query, jnp.zeros_like(query))
                g = jnp.where(keep, grad, jnp.zeros_like(grad))
                k = jnp.where(keep, key, jnp.zeros_like(key))
                v = jnp.where(keep, value, jnp.zeros_like(value))
                p = jnp.exp(mm_nt(k, query) * scale + bias[...] - stats[0, pl.ds(h, 1), :])
                ds = (p * (mm_nt(v, grad) - stats[1, pl.ds(h, 1), :])).astype(bf16)
                dk = dk + mm(ds, q)
                dv = dv + mm(p.astype(bf16), g)
            dp[1, :, at] = (dk * scale).astype(bf16)
            dp[2, :, at] = dv.astype(bf16)

        relay(mb, 2, 3)
        relay(mb, 1, 2)
        token = tok[mb].astype(f32)
        n1t = normed(token, gains[0], s_rows[experts + 2 : experts + 3, :]).astype(bf16).T
        dn1 = jnp.zeros((rows, D), f32)
        for k in range(3):
            dn1 = dn1 + mm_nt(dp[k], w[k])
            g_part = mm(n1t, dp[k])
            if mb == 0:
                gw[k] = g_part
            else:
                gw[k] += g_part
        dv, d_gain, d_bias = norm_back(token, dn1, gains[0])
        norm_sums[0] += d_gain
        norm_sums[2] += d_bias
        o_input[mb] = (d_res[mb] + dv).astype(bf16)

    rows128 = lax.broadcasted_iota(jnp.int32, (128, D), 0)
    norm_rows = jnp.zeros((128, D), f32)
    for k in range(4):
        norm_rows = jnp.where(rows128 == experts + k, norm_sums[k], norm_rows)
    gs[...] = jnp.where(lane < experts, gs[...], norm_rows.T)

    def of(dd):
        return pl.ds(pl.multiple_of(dd * part, 16), part)

    r_c = wire.roles(2 * chips)
    r_x = wire.roles(2 * (chips - 1))
    r_z = wire.roles(2 * (ne - 1))
    for k in range(chips):
        dd = 2 * k + 1 - c
        for m in range(4):
            gwb[k, m] = gw[m, of(dd), :].astype(bf16)
        gsb[k] = gs[of(dd), :]
        wire.send(r_c + 2 * k, gwb.at[k], rc.at[k], me.sib)
        wire.send(r_c + 2 * k + 1, gsb.at[k], rcs.at[k], me.sib)
    for k in range(chips):
        wire.arrive(r_c + 2 * k, rc.at[k])
        wire.arrive(r_c + 2 * k + 1, rcs.at[k])
    my_chip = d // 2
    for k in range(1, chips):
        to = lax.rem(my_chip + k, chips)
        dd = 2 * to + c
        for m in range(4):
            sx[k, m] = (gw[m, of(dd), :] + rc[to, m].astype(f32)).astype(bf16)
        sxs[k] = gs[of(dd), :] + rcs[to]
        wire.send(r_x + 2 * (k - 1), sx.at[k], rx.at[k], (dd, z))
        wire.send(r_x + 2 * (k - 1) + 1, sxs.at[k], rxs.at[k], (dd, z))
    total = [gw[m, of(d), :] + rc[my_chip, m].astype(f32) for m in range(4)]
    total_s = gs[of(d), :] + rcs[my_chip]
    for k in range(1, chips):
        wire.arrive(r_x + 2 * (k - 1), rx.at[k])
        wire.arrive(r_x + 2 * (k - 1) + 1, rxs.at[k])
        total = [total[m] + rx[k, m].astype(f32) for m in range(4)]
        total_s = total_s + rxs[k]
    for m in range(4):
        gw[m, 0:part, :] = total[m]
    gs[0:part, :] = total_s
    for k in range(1, ne):
        to = lax.rem(z + k, ne)
        at = pl.ds(pl.multiple_of(to * share, 16), share)
        for m in range(4):
            sz[k, m] = gw[m, at, :].astype(bf16)
        szs[k] = gs[at, :]
        wire.send(r_z + 2 * (k - 1), sz.at[k], rz.at[k], (d, to))
        wire.send(r_z + 2 * (k - 1) + 1, szs.at[k], rzs.at[k], (d, to))

    for cp in own_g:
        cp.wait()
    for k in range(1, nd):
        wire.arrive(r_g + 2 * (k - 1), gu.at[0])
        wire.arrive(r_g + 2 * (k - 1) + 1, gd.at[0])
    for x in range(2):
        o_up[x] = sum(gu[2 * k + x].astype(f32) for k in range(chips))
        o_down[x] = sum(gd[2 * k + x].astype(f32) for k in range(chips)).T

    for mb in range(MICRO):
        end_sums(mb)
    at = pl.ds(pl.multiple_of(z * share, 16), share)
    for k in range(1, ne):
        wire.arrive(r_z + 2 * (k - 1), rz.at[k])
        wire.arrive(r_z + 2 * (k - 1) + 1, rzs.at[k])
    for m in range(4):
        o_dense[m] = gw[m, at, :] + sum(rz[k, m].astype(f32) for k in range(1, ne))
    o_small[...] = gs[at, :] + sum(rzs[k] for k in range(1, ne))

    for k in range(1, nd):
        wire.left(r_g + 2 * (k - 1), gu.at[0])
        wire.left(r_g + 2 * (k - 1) + 1, gd.at[0])
    for mb in range(MICRO):
        for to in range(1, ne):

            @pl.when(z < to)
            def _():
                wire.left(r_up + mb * ne + to, like)

        for to in range(ne - 1):

            @pl.when(z > to)
            def _():
                wire.left(r_dn + mb * ne + to, like)

        for k in range(2):
            wire.left(r_h + 4 * mb + 2 * k, hp.at[0])
            wire.left(r_h + 4 * mb + 2 * k + 1, stat_src.at[0])
    for k in range(chips):
        wire.left(r_c + 2 * k, rc.at[0])
        wire.left(r_c + 2 * k + 1, rcs.at[0])
    for k in range(1, chips):
        wire.left(r_x + 2 * (k - 1), rx.at[0])
        wire.left(r_x + 2 * (k - 1) + 1, rxs.at[0])
    for k in range(1, ne):
        wire.left(r_z + 2 * (k - 1), rz.at[0])
        wire.left(r_z + 2 * (k - 1) + 1, rzs.at[0])
    assert wire.used <= BACK_ROLES


BACK_ROLES = 80


def back(nd, ne, *args):
    tokens = args[0]
    rows = tokens.shape[1]
    halo = -(-(IMG - 1) // 16) * 16
    chips = nd // 2
    part = D // nd
    share = part // ne
    shape = jax.ShapeDtypeStruct
    outs = (
        shape((MICRO, rows, D), bf16),
        shape((MICRO, rows, D), bf16),
        shape((4, share, D), f32),
        shape((share, 128), f32),
        shape((2, D // nd, FF), f32),
        shape((2, FF // nd, D), f32),
    )
    vmem, anywhere = pl.BlockSpec(memory_space=pltpu.VMEM), pl.BlockSpec(memory_space=pl.ANY)
    v = pltpu.VMEM
    return pl.pallas_call(
        functools.partial(back_kernel, nd, ne),
        out_shape=outs,
        in_specs=[anywhere if k in (3, 5, 6) else vmem for k in range(len(args))],
        out_specs=[vmem] * len(outs),
        scratch_shapes=[
            v((MICRO, ne, rows, D), bf16),
            v((MICRO, ne + 1, rows, D), bf16),
            v((nd, D // nd, FF), bf16),
            v((nd, D, FF // nd), bf16),
            v((MICRO, rows, D), f32),
            v((MICRO, 3 * rows, D), bf16),
            v((MICRO, 2, HEADS, rows), f32),
            v((MICRO, 2, HEADS, rows), f32),
            v((MICRO, 2, HEADS, rows), f32),
            v((MICRO, halo, D), bf16),
            v((MICRO, halo, D), bf16),
            v((2, HEADS, 3 * rows), f32),
            v((rows, 3 * rows), f32),
            v((3, rows, D), bf16),
            v((4, D, D), f32),
            v((D, 128), f32),
            v((chips, 4, part, D), bf16),
            v((chips, part, 128), f32),
            v((chips, 4, part, D), bf16),
            v((chips, part, 128), f32),
            v((chips, 4, part, D), bf16),
            v((chips, part, 128), f32),
            v((chips, 4, part, D), bf16),
            v((chips, part, 128), f32),
            v((ne, 4, share, D), bf16),
            v((ne, share, 128), f32),
            v((ne, 4, share, D), bf16),
            v((ne, share, 128), f32),
            v((rows, D), f32),
            pltpu.SemaphoreType.DMA((BACK_ROLES,)),
            pltpu.SemaphoreType.DMA((BACK_ROLES,)),
            pltpu.SemaphoreType.DMA((3,)),
        ],
        compiler_params=pltpu.CompilerParams(
            collective_id=1, has_side_effects=True, vmem_limit_bytes=VMEM_BYTES
        ),
        name="back",
    )(*args)


def kernel_body(
    nd,
    ne,
    tokens,
    image_ids,
    routes,
    qkv_weight,
    out_weight,
    router_weight,
    norm_gains,
    norm_biases,
    expert_in,
    expert_out,
    cotangent,
):
    experts = 2 * ne
    saved = front(
        nd,
        ne,
        tokens,
        image_ids,
        routes.transpose(0, 2, 1),
        qkv_weight,
        out_weight,
        router_weight.T,
        norm_gains,
        norm_biases,
        expert_in,
        expert_out,
        cotangent,
    )
    block_out, input_grad, dense, small, grad_up, grad_down = back(nd, ne, tokens, cotangent, *saved)
    return (
        block_out,
        input_grad,
        dense[:3],
        dense[3],
        small[:, :experts],
        small[:, experts : experts + 2].T,
        small[:, experts + 2 : experts + 4].T,
        grad_up,
        grad_down,
    )


def chosen_body(nd, ne, tokens, *rest):
    rows, experts = tokens.shape[1], 2 * ne
    whole = D % (16 * nd * ne) == 0 and nd % 2 == 0 and 8 * rows == experts * rows and rows % 128 == 0
    whole = whole and nd == 8 and ne == 4
    if whole and rest[-3].shape[0] == 2:
        return kernel_body(nd, ne, tokens, *rest)
    return body(tokens, *rest)


def solution(mesh):
    return jax.shard_map(
        functools.partial(chosen_body, mesh.shape["dp"], mesh.shape["expert"]),
        mesh=mesh,
        in_specs=(
            P(None, ("dp", "expert"), None),
            P(None, ("dp", "expert")),
            P(None, ("dp", "expert"), None),
            P(None, ("dp", "expert"), None),
            P(("dp", "expert"), None),
            P(("dp", "expert"), None),
            P(None, ("dp", "expert")),
            P(None, ("dp", "expert")),
            P("expert", "dp", None),
            P("expert", "dp", None),
            P(None, ("dp", "expert"), None),
        ),
        out_specs=(
            P(None, ("dp", "expert"), None),
            P(None, ("dp", "expert"), None),
            P(None, ("dp", "expert"), None),
            P(("dp", "expert"), None),
            P(("dp", "expert"), None),
            P(None, ("dp", "expert")),
            P(None, ("dp", "expert")),
            P("expert", "dp", None),
            P("expert", "dp", None),
        ),
        check_vma=False,
    )
```

```python
import functools
import math

import jax
import jax.numpy as jnp
from jax import lax
from jax.experimental import pallas as pl
from jax.experimental.pallas import tpu as pltpu
from jax.sharding import PartitionSpec as P

D = 512
HEADS = 8
HEAD_DIM = 64
FF = 2048
TOP = 2
IMG = 197
MICRO = 2


neg_big = -1e30
norm_eps = 1e-06
highest = lax.Precision.HIGHEST


def padded(cells, sides, width):
    for axis, dim in sides:
        count = lax.axis_size(axis)
        ends = count - 1
        head = lax.slice_in_dim(cells, 0, width, axis=dim)
        tail = lax.slice_in_dim(cells, cells.shape[dim] - width, cells.shape[dim], axis=dim)
        cells = jnp.concatenate(
            [
                lax.ppermute(tail, axis, [(i, (i + 1) % count) for i in range(ends)]),
                cells,
                lax.ppermute(head, axis, [((i + 1) % count, i) for i in range(ends)]),
            ],
            axis=dim,
        )
    return cells


def layer_norm(values, gain_row, bias_row):
    centre = jnp.mean(values, axis=-1, keepdims=True)
    offset = values - centre
    spread = jnp.mean(offset * offset, axis=-1, keepdims=True)
    return offset * lax.rsqrt(spread + norm_eps) * gain_row + bias_row


def tanh_gelu(values):
    return jax.nn.gelu(values, approximate=True)


def fetch_dense(qkv_weight, out_weight, router_weight, norm_gains, norm_biases):
    rows, experts = router_weight.shape
    small = jnp.concatenate([router_weight, norm_gains.T, norm_biases.T], axis=1)
    small = jnp.pad(small, ((0, 0), (0, D - experts - 4)))
    packed = jnp.concatenate([qkv_weight, out_weight[None], small[None]], axis=0)
    full = lax.all_gather(packed, ("dp", "expert"), axis=1, tiled=True)
    return (
        full[:3],
        full[3],
        full[4][:, :experts],
        full[4][:, experts : experts + 2].T,
        full[4][:, experts + 2 : experts + 4].T,
    )


def fetch_experts(expert_in, expert_out):
    return (
        lax.all_gather(expert_in, "dp", axis=1, tiled=True),
        lax.all_gather(expert_out, "dp", axis=1, tiled=True),
    )


def plan_routes(route_ids, shard_experts):
    row_count = route_ids.shape[0]
    experts = shard_experts * lax.axis_size("expert")
    devices = lax.axis_size(("dp", "expert"))
    slot_count = 2 * TOP * row_count // experts
    capacity = 5 * TOP * row_count * devices // (4 * experts)
    labels = lax.broadcasted_iota(jnp.int32, (1, experts), 1)
    first_hot = (route_ids[:, 0:1] == labels).astype(jnp.int32)
    second_hot = (route_ids[:, 1:2] == labels).astype(jnp.int32)
    counts = jnp.stack([jnp.sum(first_hot, axis=0), jnp.sum(second_hot, axis=0)])
    all_counts = lax.all_gather(counts[None], ("dp", "expert"), axis=0, tiled=True)
    earlier = (
        lax.broadcasted_iota(jnp.int32, (devices, 1, 1), 0) < lax.axis_index(("dp", "expert"))
    ).astype(jnp.int32)
    before = jnp.sum(all_counts * earlier, axis=0)
    total_first = jnp.sum(all_counts[:, 0, :], axis=0)
    row_before = (
        lax.broadcasted_iota(jnp.int32, (row_count, row_count), 0)
        > lax.broadcasted_iota(jnp.int32, (row_count, row_count), 1)
    ).astype(jnp.bfloat16)

    def rank_of(hot):
        ahead = jnp.dot(row_before, hot.astype(jnp.bfloat16), preferred_element_type=jnp.float32)
        return jnp.sum(ahead.astype(jnp.int32) * hot, axis=1)

    rank_first = rank_of(first_hot)
    rank_second = rank_of(second_hot)
    place_first = jnp.sum(first_hot * before[0][None, :], axis=1) + rank_first
    place_second = jnp.sum(second_hot * (total_first + before[1])[None, :], axis=1) + rank_second
    kept_mask = jnp.stack([place_first < capacity, place_second < capacity], axis=1)
    slot_second = jnp.sum(second_hot * counts[0][None, :], axis=1) + rank_second
    flat_index = jnp.stack(
        [route_ids[:, 0] * slot_count + rank_first, route_ids[:, 1] * slot_count + slot_second],
        axis=1,
    )
    target = jnp.where(kept_mask, flat_index, experts * slot_count)
    return (first_hot, second_hot, target, kept_mask.astype(jnp.float32))


def fill_slots(row_pairs, target, experts, slot_count):
    feature_count = row_pairs.shape[-1]
    buffer = jnp.zeros((experts * slot_count + 1, feature_count), row_pairs.dtype)
    buffer = buffer.at[target.reshape(-1)].set(row_pairs.reshape(-1, feature_count))
    return buffer[:-1].reshape(experts, 1, slot_count, feature_count)


def read_slots(returned, target):
    feature_count = returned.shape[-1]
    flat_table = jnp.concatenate(
        [returned.reshape(-1, feature_count), jnp.zeros((1, feature_count), returned.dtype)], axis=0
    )
    return flat_table[target]


def run_forward(tokens_f, ids_ext, route_plan, dense_set, expert_set):
    qkv_full, out_full, router_full, gain_pair, bias_pair = dense_set
    expert_up_weight, expert_down_weight = expert_set
    first_hot, second_hot, target, kept_mask = route_plan
    row_count = tokens_f.shape[0]
    rim_rows = IMG - 1
    score_scale = 1.0 / math.sqrt(HEAD_DIM)
    experts = router_full.shape[1]
    slot_count = 2 * TOP * row_count // experts
    normed_one = layer_norm(
        tokens_f, gain_pair[0].astype(jnp.float32), bias_pair[0].astype(jnp.float32)
    ).astype(jnp.bfloat16)
    projected = jnp.einsum(
        "rd,cde->cre", normed_one, qkv_full, preferred_element_type=jnp.float32
    ).astype(jnp.bfloat16)
    key_value = padded(projected[1:], ((("dp", "expert"), 1),), rim_rows)
    query_heads = projected[0].reshape(row_count, HEADS, HEAD_DIM)
    key_heads = key_value[0].reshape(-1, HEADS, HEAD_DIM)
    value_heads = key_value[1].reshape(-1, HEADS, HEAD_DIM)
    same_image = ids_ext[rim_rows : rim_rows + row_count][:, None] == ids_ext[None, :]
    scores = (
        jnp.einsum("qhd,khd->hqk", query_heads, key_heads, preferred_element_type=jnp.float32)
        * score_scale
    )
    scores = jnp.where(same_image[None], scores, neg_big)
    top_score = jnp.max(scores, axis=-1, keepdims=True)
    log_total = top_score + jnp.log(jnp.sum(jnp.exp(scores - top_score), axis=-1, keepdims=True))
    att_probs = jnp.exp(scores - log_total)
    att_low = att_probs.astype(jnp.bfloat16)
    mixed_rows = (
        jnp.einsum("hqk,khd->qhd", att_low, value_heads, preferred_element_type=jnp.float32)
        .reshape(row_count, D)
        .astype(jnp.bfloat16)
    )
    residual = tokens_f + jnp.dot(mixed_rows, out_full, preferred_element_type=jnp.float32)
    normed_two = layer_norm(
        residual, gain_pair[1].astype(jnp.float32), bias_pair[1].astype(jnp.float32)
    ).astype(jnp.bfloat16)
    router_probs = jax.nn.softmax(
        jnp.dot(normed_two, router_full, preferred_element_type=jnp.float32), axis=-1
    )
    picked = jnp.stack(
        [jnp.sum(first_hot * router_probs, axis=1), jnp.sum(second_hot * router_probs, axis=1)],
        axis=1,
    )
    gate_values = kept_mask * picked
    outgoing = fill_slots(
        jnp.broadcast_to(normed_two[:, None, :], (row_count, TOP, D)), target, experts, slot_count
    )
    arrived = lax.all_to_all(outgoing, "expert", split_axis=0, concat_axis=1, tiled=True)
    shard_experts = arrived.shape[0]
    collected_token_rows = arrived.reshape(shard_experts, -1, D)
    hidden_pre = jnp.einsum(
        "ycq,yqt->yct", collected_token_rows, expert_up_weight, preferred_element_type=jnp.float32
    )
    hidden_activation = tanh_gelu(hidden_pre).astype(jnp.bfloat16)
    produced = jnp.einsum(
        "nso,nop->nsp", hidden_activation, expert_down_weight, preferred_element_type=jnp.float32
    ).astype(jnp.bfloat16)
    returned = lax.all_to_all(
        produced.reshape(arrived.shape), "expert", split_axis=1, concat_axis=0, tiled=True
    )
    expert_rows = read_slots(returned, target)
    block_value = residual + jnp.sum(
        gate_values[:, :, None] * expert_rows.astype(jnp.float32), axis=1
    )
    return (
        normed_one,
        query_heads,
        key_heads,
        value_heads,
        att_probs,
        att_low,
        mixed_rows,
        residual,
        normed_two,
        router_probs,
        gate_values,
        collected_token_rows,
        hidden_pre,
        hidden_activation,
        expert_rows,
        block_value,
    )


def run_backward(tokens_f, ids_ext, route_plan, dense_set, expert_set, upstream, gradients):
    qkv_full, out_full, router_full, gain_pair, bias_pair = dense_set
    expert_up_weight, expert_down_weight = expert_set
    first_hot, second_hot, target, kept_mask = route_plan
    grad_qkv, grad_out, grad_router, grad_gains, grad_biases, grad_in, grad_expert_out = gradients
    (
        normed_one,
        query_heads,
        key_heads,
        value_heads,
        att_probs,
        att_low,
        mixed_rows,
        residual,
        normed_two,
        router_probs,
        gate_values,
        collected_token_rows,
        hidden_pre,
        hidden_activation,
        expert_rows,
        block_value,
    ) = run_forward(tokens_f, ids_ext, route_plan, dense_set, expert_set)
    row_count = tokens_f.shape[0]
    rim_rows = IMG - 1
    score_scale = 1.0 / math.sqrt(HEAD_DIM)
    experts = router_full.shape[1]
    slot_count = 2 * TOP * row_count // experts
    shard_experts = expert_up_weight.shape[0]
    d_gate = kept_mask * jnp.sum(upstream[:, None, :] * expert_rows.astype(jnp.float32), axis=-1)
    d_sent = (gate_values[:, :, None] * upstream[:, None, :]).astype(jnp.bfloat16)
    d_arrived = lax.all_to_all(
        fill_slots(d_sent, target, experts, slot_count),
        "expert",
        split_axis=0,
        concat_axis=1,
        tiled=True,
    )
    produced_rows_grad = d_arrived.reshape(shard_experts, -1, D)
    activation_grad = jnp.einsum(
        "tkw,tew->tke", produced_rows_grad, expert_down_weight, preferred_element_type=jnp.float32
    )
    grad_expert_out = grad_expert_out + jnp.einsum(
        "meq,mek->mqk", hidden_activation, produced_rows_grad, preferred_element_type=jnp.float32
    )
    gelu_value, gelu_back = jax.vjp(tanh_gelu, hidden_pre)
    preactivation_grad = gelu_back(activation_grad)[0].astype(jnp.bfloat16)
    grad_in = grad_in + jnp.einsum(
        "zjo,zjm->zom", collected_token_rows, preactivation_grad, preferred_element_type=jnp.float32
    )
    d_rows = jnp.einsum(
        "iht,imt->ihm", preactivation_grad, expert_up_weight, preferred_element_type=jnp.float32
    ).astype(jnp.bfloat16)
    d_back = lax.all_to_all(
        d_rows.reshape(d_arrived.shape), "expert", split_axis=1, concat_axis=0, tiled=True
    )
    d_normed_two = jnp.sum(
        kept_mask[:, :, None] * read_slots(d_back, target).astype(jnp.float32), axis=1
    )
    d_probs = first_hot * d_gate[:, 0:1] + second_hot * d_gate[:, 1:2]
    d_logits = router_probs * (d_probs - jnp.sum(router_probs * d_probs, axis=-1, keepdims=True))
    router_wide = router_full.astype(jnp.float32)
    d_normed_two = d_normed_two + jnp.dot(d_logits, router_wide.T, precision=highest)
    grad_router = grad_router + jnp.dot(
        normed_two.astype(jnp.float32).T, d_logits, precision=highest
    )
    norm_value, second_back = jax.vjp(
        layer_norm, residual, gain_pair[1].astype(jnp.float32), bias_pair[1].astype(jnp.float32)
    )
    d_resid_part, d_gain_two, d_bias_two = second_back(d_normed_two)
    d_resid = upstream + d_resid_part
    d_attn = d_resid.astype(jnp.bfloat16)
    grad_out = grad_out + jnp.einsum(
        "rd,re->de", mixed_rows, d_attn, preferred_element_type=jnp.float32
    )
    d_mixed = (
        jnp.einsum("re,de->rd", d_attn, out_full, preferred_element_type=jnp.float32)
        .astype(jnp.bfloat16)
        .reshape(row_count, HEADS, HEAD_DIM)
    )
    d_att = jnp.einsum("qhd,khd->hqk", d_mixed, value_heads, preferred_element_type=jnp.float32)
    d_scores = (att_probs * (d_att - jnp.sum(att_probs * d_att, axis=-1, keepdims=True))).astype(
        jnp.bfloat16
    )
    d_query = (
        (
            jnp.einsum("hqk,khd->qhd", d_scores, key_heads, preferred_element_type=jnp.float32)
            * score_scale
        )
        .astype(jnp.bfloat16)
        .reshape(row_count, D)
    )
    d_key = (
        jnp.einsum("hqk,qhd->khd", d_scores, query_heads, preferred_element_type=jnp.float32)
        * score_scale
    )
    d_value = jnp.einsum("hqk,qhd->khd", att_low, d_mixed, preferred_element_type=jnp.float32)
    d_pair = jnp.stack([d_key.reshape(-1, D), d_value.reshape(-1, D)])
    rim_grads = jnp.concatenate([d_pair[:, :rim_rows], d_pair[:, rim_rows + row_count :]], axis=1)
    beside_all = padded(rim_grads.astype(jnp.bfloat16), ((("dp", "expert"), 1),), rim_rows).astype(
        rim_grads.dtype
    )
    own_part = d_pair[:, rim_rows : rim_rows + row_count]
    from_below = jnp.pad(beside_all[:, :rim_rows], ((0, 0), (0, row_count - rim_rows), (0, 0)))
    from_above = jnp.pad(beside_all[:, 3 * rim_rows :], ((0, 0), (row_count - rim_rows, 0), (0, 0)))
    d_kv = (own_part + from_below + from_above).astype(jnp.bfloat16)
    d_projected = jnp.concatenate([d_query[None], d_kv], axis=0)
    grad_qkv = grad_qkv + jnp.einsum(
        "rd,cre->cde", normed_one, d_projected, preferred_element_type=jnp.float32
    )
    d_normed_one = jnp.einsum(
        "cre,cde->rd", d_projected, qkv_full, preferred_element_type=jnp.float32
    )
    first_value, first_back = jax.vjp(
        layer_norm, tokens_f, gain_pair[0].astype(jnp.float32), bias_pair[0].astype(jnp.float32)
    )
    d_tokens_part, d_gain_one, d_bias_one = first_back(d_normed_one)
    grad_gains = grad_gains + jnp.stack([d_gain_one, d_gain_two])
    grad_biases = grad_biases + jnp.stack([d_bias_one, d_bias_two])
    input_rows = (d_resid + d_tokens_part).astype(jnp.bfloat16)
    return (
        input_rows,
        (grad_qkv, grad_out, grad_router, grad_gains, grad_biases, grad_in, grad_expert_out),
    )


def body(
    tokens,
    image_ids,
    routes,
    qkv_weight,
    out_weight,
    router_weight,
    norm_gains,
    norm_biases,
    expert_in,
    expert_out,
    cotangent,
):
    shard_experts = expert_in.shape[0]
    rim_rows = IMG - 1
    experts = shard_experts * lax.axis_size("expert")
    outputs = []
    saved_state = []
    for batch_index in range(MICRO):
        dense_set = fetch_dense(qkv_weight, out_weight, router_weight, norm_gains, norm_biases)
        expert_set = fetch_experts(expert_in, expert_out)
        ids_ext = padded(image_ids[batch_index] + 1, ((("dp", "expert"), 0),), rim_rows)
        route_plan = plan_routes(routes[batch_index], shard_experts)
        forward_state = run_forward(
            tokens[batch_index].astype(jnp.float32), ids_ext, route_plan, dense_set, expert_set
        )
        outputs.append(forward_state[-1].astype(jnp.bfloat16))
        saved_state.append((ids_ext, route_plan))
    gradients = (
        jnp.zeros((3, D, D), jnp.float32),
        jnp.zeros((D, D), jnp.float32),
        jnp.zeros((D, experts), jnp.float32),
        jnp.zeros((2, D), jnp.float32),
        jnp.zeros((2, D), jnp.float32),
        jnp.zeros((shard_experts, D, FF), jnp.float32),
        jnp.zeros((shard_experts, FF, D), jnp.float32),
    )
    input_grads = []
    for batch_index in range(MICRO):
        dense_set = fetch_dense(qkv_weight, out_weight, router_weight, norm_gains, norm_biases)
        expert_set = fetch_experts(expert_in, expert_out)
        ids_ext, route_plan = saved_state[batch_index]
        input_rows, gradients = run_backward(
            tokens[batch_index].astype(jnp.float32),
            ids_ext,
            route_plan,
            dense_set,
            expert_set,
            cotangent[batch_index].astype(jnp.float32),
            gradients,
        )
        input_grads.append(input_rows)
    grad_qkv, grad_out, grad_router, grad_gains, grad_biases, grad_in, grad_expert_out = gradients
    small = jnp.concatenate([grad_router, grad_gains.T, grad_biases.T], axis=1)
    small = jnp.pad(small, ((0, 0), (0, D - experts - 4)))
    packed = jnp.concatenate([grad_qkv, grad_out[None], small[None]], axis=0)
    packed = lax.psum_scatter(packed, ("dp", "expert"), scatter_dimension=1, tiled=True)
    dense_grads = (
        packed[:3],
        packed[3],
        packed[4][:, :experts],
        packed[4][:, experts : experts + 2].T,
        packed[4][:, experts + 2 : experts + 4].T,
    )
    expert_grads = (
        lax.psum_scatter(
            grad_in.astype(jnp.bfloat16), "dp", scatter_dimension=1, tiled=True
        ).astype(jnp.float32),
        lax.psum_scatter(
            grad_expert_out.astype(jnp.bfloat16), "dp", scatter_dimension=1, tiled=True
        ).astype(jnp.float32),
    )
    return (
        jnp.stack(outputs),
        jnp.stack(input_grads),
        dense_grads[0],
        dense_grads[1],
        dense_grads[2],
        dense_grads[3],
        dense_grads[4],
        expert_grads[0],
        expert_grads[1],
    )


MESH = pl.DeviceIdType.MESH
f32, bf16 = jnp.float32, jnp.bfloat16
VMEM_BYTES = 62 << 20


def mm(a, b):
    return jnp.dot(a, b, preferred_element_type=f32)


def mm_nt(a, b):
    return lax.dot_general(a, b, (((1,), (1,)), ((), ())), preferred_element_type=f32)


def normed(values, gain_row, bias_row):
    centre = jnp.mean(values, axis=-1, keepdims=True)
    offset = values - centre
    spread = jnp.mean(offset * offset, axis=-1, keepdims=True)
    return offset * lax.rsqrt(spread + norm_eps) * gain_row + bias_row


class Wire:
    def __init__(self, send_sems, recv_sems, other):
        self.send_sems, self.recv_sems, self.other = send_sems, recv_sems, other
        self.used, self.sent = 0, {}

    def roles(self, count=1):
        self.used += count
        return self.used - count

    def copy(self, send_role, recv_role, src, dst, device):
        return pltpu.make_async_remote_copy(
            src_ref=src,
            dst_ref=dst,
            send_sem=self.send_sems.at[send_role],
            recv_sem=self.recv_sems.at[recv_role],
            device_id=device,
            device_id_type=MESH,
        )

    def send(self, role, src, dst, device, recv_role=None):
        self.copy(role, role if recv_role is None else recv_role, src, dst, device).start()

    def arrive(self, role, like):
        self.copy(role, role, like, like, self.other).wait_recv()

    def left(self, role, like):
        self.copy(role, role, like, like, self.other).wait_send()


class Place:
    def __init__(self, nd, ne):
        self.nd, self.ne = nd, ne
        self.d, self.z = lax.axis_index("dp"), lax.axis_index("expert")
        d, z = self.d, self.z
        self.c = lax.rem(d, 2)
        self.sib_d = d + 1 - 2 * self.c
        self.sib = (self.sib_d, z)
        self.idx = d * ne + z
        last = (z == ne - 1).astype(jnp.int32)
        first = (z == 0).astype(jnp.int32)
        self.next = (lax.rem(d + last, nd), lax.rem(z + 1, ne))
        self.prev = (lax.rem(d + nd - first, nd), lax.rem(z + ne - 1, ne))
        self.xn = d + 2 - 4 * lax.rem(d // 2, 2)
        self.yn = d + 4 - 8 * (d // 4)
        self.up = (d, jnp.minimum(z + 1, ne - 1))
        self.down = (d, jnp.maximum(z - 1, 0))

    def chip(self, k):
        return lax.rem(self.d + 2 * k, self.nd)

    def enter(self):
        bar = pltpu.get_barrier_semaphore()

        def greet(device):
            pl.semaphore_signal(bar, inc=1, device_id=device, device_id_type=MESH)

        for k in range(1, self.nd):
            greet((lax.rem(self.d + k, self.nd), self.z))
        for k in range(1, self.ne):
            zk = lax.rem(self.z + k, self.ne)
            greet((self.d, zk))
            greet((self.sib_d, zk))
        greet(self.next)
        greet(self.prev)
        pl.semaphore_wait(bar, self.nd - 1 + 2 * (self.ne - 1) + 2)


class Chain:
    def __init__(self, wire, me, full):
        self.wire, self.me, self.full = wire, me, full
        n = me.ne
        self.up, self.dn = wire.roles(n - 1), wire.roles(n - 1)
        self.su, self.sd, self.so = wire.roles(n - 1), wire.roles(n - 1), wire.roles()

    def at(self, z):
        return self.full.at[z * 2 + self.me.c]

    def own(self, src):
        m, n = self.me, self.me.ne

        @pl.when(m.z < n - 1)
        def _():
            self.wire.send(self.up, src, self.at(m.z), m.up)

        @pl.when(m.z > 0)
        def _():
            self.wire.send(self.dn, src, self.at(m.z), m.down)

        self.wire.send(self.so, src, self.at(m.z), m.sib)

    def pump(self, k):
        m, n, w = self.me, self.me.ne, self.wire

        @pl.when(m.z >= k + 1)
        def _():
            block = self.at(m.z - 1 - k)
            w.arrive(self.up + k, block)
            if k + 1 < n - 1:

                @pl.when(m.z < n - 1)
                def _():
                    w.send(self.up + k + 1, block, block, m.up)

            w.send(self.su + k, block, block, m.sib)

        @pl.when(m.z + k + 1 < n)
        def _():
            block = self.at(m.z + 1 + k)
            w.arrive(self.dn + k, block)
            if k + 1 < n - 1:

                @pl.when(m.z > 0)
                def _():
                    w.send(self.dn + k + 1, block, block, m.down)

            w.send(self.sd + k, block, block, m.sib)

    def near(self):
        self.wire.arrive(self.so, self.full.at[0])

    def finish(self, k):
        m, n, w, like = self.me, self.me.ne, self.wire, self.full.at[0]

        @pl.when(m.z >= k + 1)
        def _():
            w.arrive(self.su + k, like)

        @pl.when(m.z + k + 1 < n)
        def _():
            w.arrive(self.sd + k, like)

    def drain(self):
        m, n, w, like = self.me, self.me.ne, self.wire, self.full.at[0]
        w.left(self.so, like)
        for k in range(n - 1):

            @pl.when((m.z < n - 1) & (m.z >= k))
            def _():
                w.left(self.up + k, like)

            @pl.when((m.z > 0) & (m.z + k < n))
            def _():
                w.left(self.dn + k, like)

            @pl.when(m.z >= k + 1)
            def _():
                w.left(self.su + k, like)

            @pl.when(m.z + k + 1 < n)
            def _():
                w.left(self.sd + k, like)


def front_kernel(
    nd,
    ne,
    tok,
    ids,
    routes,
    qkv,
    outw,
    routw,
    gainw,
    biasw,
    win,
    wout,
    cot,
    o_din,
    o_y,
    o_dprobs,
    o_up,
    o_down,
    g_n2,
    g_probs,
    g_resid,
    g_mixed,
    o_qkv,
    g_lse,
    g_w,
    o_small,
    o_idr,
    s_src,
    s_all,
    hp,
    hn,
    ip,
    inx,
    gx,
    gd,
    wu,
    wd,
    rk_src,
    rk,
    bias,
    acts,
    grads,
    pm,
    xs,
    ds,
    deo,
    xt,
    dt,
    gt,
    acc_eo,
    ys,
    qo,
    cs,
    cr,
    ud,
    dgs,
    dg,
    stage,
    square,
    o_probs,
    o_resid,
    o_mixed,
    o_lse,
    w_all,
    give_sems,
    send_sems,
    recv_sems,
    local_sems,
):
    me = Place(nd, ne)
    d, z, c = me.d, me.z, me.c
    rows = tok.shape[1]
    share = qkv.shape[1]
    experts = 2 * ne
    halo = hp.shape[1]
    ext = 3 * rows
    slots = 4 * rows // experts
    capacity = 5 * TOP * rows * nd * ne // (4 * experts)
    e = 2 * z + c
    s_me = z * 2 + c
    wire = Wire(send_sems, recv_sems, me.sib)
    lane = lax.broadcasted_iota(jnp.int32, (1, 128), 1)

    me.enter()

    r_dz = wire.roles(3 * (ne - 1))
    mine = pl.ds(pl.multiple_of(me.idx * share, 16), share)
    for k in range(1, ne):
        dev = (d, lax.rem(z + k, ne))
        wire.send(r_dz + 3 * (k - 1), qkv, w_all.at[pl.ds(0, 3), mine], dev)
        wire.send(r_dz + 3 * (k - 1) + 1, outw, w_all.at[3, mine], dev)
    local = [
        pltpu.make_async_copy(qkv, w_all.at[pl.ds(0, 3), mine], local_sems.at[0]),
        pltpu.make_async_copy(outw, w_all.at[3, mine], local_sems.at[1]),
    ]
    for cp in local:
        cp.start()
    up_rows, down_rows = win.shape[1], wout.shape[1]

    def up_at(dd, n=1):
        return wu.at[pl.ds(pl.multiple_of(dd * up_rows, 16), n * up_rows)]

    def down_at(dd, n=1):
        return wd.at[pl.ds(pl.multiple_of(dd * down_rows, 16), n * down_rows)]

    own_w = [
        pltpu.make_async_copy(win.at[c], up_at(d), local_sems.at[5]),
        pltpu.make_async_copy(wout.at[c], down_at(d), local_sems.at[6]),
    ]
    for cp in own_w:
        cp.start()
    r_ux, r_dy, r_uy, r_dx2 = (wire.roles(2) for _ in range(4))
    r_uf, r_df, r_us, r_dsib = (wire.roles() for _ in range(4))
    for cc in range(2):
        wire.send(r_ux + cc, win.at[cc], up_at(d), (me.xn - c + cc, z), recv_role=r_ux + c)
        wire.send(r_dy + cc, wout.at[cc], down_at(d), (me.yn - c + cc, z), recv_role=r_dy + c)
    r_id = wire.roles(2)
    wire.send(r_id, ids, ip, me.next)
    wire.send(r_id + 1, ids, inx, me.prev)
    r_h = wire.roles(2 * MICRO)

    def send_halo(mb):
        wire.send(r_h + 2 * mb, tok.at[mb, pl.ds(rows - halo, halo)], hp.at[mb], me.next)
        wire.send(r_h + 2 * mb + 1, tok.at[mb, pl.ds(0, halo)], hn.at[mb], me.prev)

    send_halo(0)
    before_row = (
        lax.broadcasted_iota(jnp.int32, (rows, rows), 0)
        > lax.broadcasted_iota(jnp.int32, (rows, rows), 1)
    ).astype(bf16)
    square[...] = jnp.zeros_like(square)
    square[0:experts, 0:share] = routw[...].astype(f32)
    square[experts : experts + 2, 0:share] = gainw[...].astype(f32)
    square[experts + 2 : experts + 4, 0:share] = biasw[...].astype(f32)
    s_src[0:share, :] = square[...].T[0:share, :].astype(bf16)
    row128 = lax.broadcasted_iota(jnp.int32, (128, rows), 0)
    row16 = lax.broadcasted_iota(jnp.int32, (16, 128), 0)
    hots = []
    counts = jnp.zeros((16, 128), f32)
    for mb in range(MICRO):
        choice = routes[mb].astype(f32)
        wide = jnp.where(row128 == 0, choice[0:1], jnp.where(row128 == 1, choice[1:2], -1.0)).T
        pair = [(wide[:, k : k + 1] == lane.astype(f32)).astype(f32) for k in range(TOP)]
        hots.append(pair)
        for k in range(TOP):
            counts = jnp.where(row16 == mb * TOP + k, jnp.sum(pair[k], axis=0, keepdims=True), counts)
    s_src[share : share + 16, :] = counts.astype(bf16)

    for k in range(1, ne):
        wire.send(r_dz + 3 * (k - 1) + 2, s_src, s_all.at[me.idx], (d, lax.rem(z + k, ne)))
    s_all[me.idx] = s_src[...]
    g_d = [Chain(wire, me, gd.at[mb]) for mb in range(MICRO)]
    g_x = [Chain(wire, me, gx.at[mb]) for mb in range(MICRO)]
    own_d = [
        pltpu.make_async_copy(cot.at[mb], gd.at[mb, s_me], local_sems.at[3 + mb])
        for mb in range(MICRO)
    ]
    for cp in own_d:
        cp.start()

    for cp in local:
        cp.wait()
    for k in range(1, ne):
        wire.arrive(r_dz + 3 * (k - 1), qkv)
        wire.arrive(r_dz + 3 * (k - 1) + 1, outw)
        wire.arrive(r_dz + 3 * (k - 1) + 2, s_src)

    def column(dd):
        at = pl.ds(pl.multiple_of(dd * (ne * share), 16), ne * share)
        return w_all.at[:, at], s_all.at[pl.ds(dd * ne, ne)]

    chips = nd // 2
    r_dx = wire.roles(2 * (chips - 1))
    r_ds = wire.roles(2 * chips)
    blk, sblk = column(d)
    for k in range(1, chips):
        wire.send(r_dx + 2 * (k - 1), blk, blk, (me.chip(k), z))
        wire.send(r_dx + 2 * (k - 1) + 1, sblk, sblk, (me.chip(k), z))
    wire.send(r_ds, blk, blk, me.sib)
    wire.send(r_ds + 1, sblk, sblk, me.sib)
    send_halo(1)
    g_d[0].own(cot.at[0])
    wire.send(r_us, win.at[1 - c], up_at(d), me.sib)
    wire.send(r_dsib, wout.at[1 - c], down_at(d), me.sib)
    for k in range(1, chips):
        wire.arrive(r_dx + 2 * (k - 1), blk)
        wire.arrive(r_dx + 2 * (k - 1) + 1, sblk)
        b, sb = column(lax.rem(d + nd - 2 * k, nd))
        wire.send(r_ds + 2 * k, b, b, me.sib)
        wire.send(r_ds + 2 * k + 1, sb, sb, me.sib)
    for cc in range(2):
        wire.send(r_dx2 + cc, wout.at[cc], down_at(d), (me.xn - c + cc, z), recv_role=r_dx2 + c)
        wire.send(r_uy + cc, win.at[cc], up_at(d), (me.yn - c + cc, z), recv_role=r_uy + c)
        wire.arrive(r_ux + cc, win.at[0])
        wire.arrive(r_dy + cc, wout.at[0])
    wire.send(r_uf, up_at(me.xn - c, 2), up_at(me.xn - c, 2), (me.yn, z))
    wire.send(r_df, down_at(me.yn - c, 2), down_at(me.yn - c, 2), (me.xn, z))
    for k in range(chips):
        wire.arrive(r_ds + 2 * k, blk)
        wire.arrive(r_ds + 2 * k + 1, sblk)

    o_small[...] = s_all[:, 0:share, :].reshape(D, 128).astype(f32)
    s_rows = o_small[...].T
    all_counts = s_all[:, share : share + 16, :].astype(f32)
    ahead = lax.broadcasted_iota(jnp.int32, all_counts.shape, 0) < me.idx
    before = jnp.sum(jnp.where(ahead, all_counts, 0.0), axis=0)
    total = jnp.sum(all_counts, axis=0)
    gains = [s_rows[experts + k : experts + k + 1, :] for k in range(2)]
    biases = [s_rows[experts + 2 + k : experts + 3 + k, :] for k in range(2)]

    r_rk = wire.roles(2 * ne)

    def send_ranks():
        for mb in range(MICRO):
            one, two = hots[mb]
            rank_one = mm(before_row, one.astype(bf16))
            rank_two = mm(before_row, two.astype(bf16))
            b1, b2 = before[2 * mb : 2 * mb + 1], before[2 * mb + 1 : 2 * mb + 2]
            t1 = total[2 * mb : 2 * mb + 1]
            place_one = jnp.sum(one * (b1 + rank_one), axis=1, keepdims=True)
            place_two = jnp.sum(two * (t1 + b2 + rank_two), axis=1, keepdims=True)
            kept = one * (place_one < capacity).astype(f32) + two * (place_two < capacity).astype(
                f32
            )
            ranks = jnp.where(kept > 0.0, rank_one + rank_two, -1.0)
            rk_src[mb] = ranks.T[0:experts, :]
        for k in range(ne):
            zk = lax.rem(z + k, ne)
            if k > 0:
                wire.send(r_rk + 2 * k, rk_src, rk.at[s_me], (d, zk))
            wire.send(r_rk + 2 * k + 1, rk_src, rk.at[s_me], (me.sib_d, zk))
        rk[s_me] = rk_src[...]

    wire.arrive(r_id, ids)
    wire.arrive(r_id + 1, ids)
    pos = lax.broadcasted_iota(jnp.int32, (1, rows), 1)
    gap = rows - halo
    for mb in range(MICRO):
        here = ids[mb : mb + 1, :].astype(f32)
        below = jnp.where((pos >= gap) & (me.idx > 0), ip[mb : mb + 1, :].astype(f32), -1.0)
        above = jnp.where(
            (pos < halo) & (me.idx < nd * ne - 1), inx[mb : mb + 1, :].astype(f32), -1.0
        )
        o_idr[mb] = jnp.concatenate([below, here, above], axis=1)

    zero_gap = jnp.zeros((gap, D), bf16)
    acts[0:gap, 0:D] = zero_gap
    acts[ext - gap : ext, 0:D] = zero_gap
    scale = 1.0 / math.sqrt(HEAD_DIM)
    given = []

    def give(src, dst):
        given.append(pltpu.make_async_copy(src, dst, give_sems.at[len(given)]))
        given[-1].start()

    give(w_all, g_w)
    saves = [pltpu.make_async_copy(
            acts.at[pl.ds(0, ext), pl.ds(D, 3 * D)], o_qkv.at[mb], local_sems.at[7 + mb]
        )
        for mb in range(MICRO)]

    def attend(mb, hooks):
        wire.arrive(r_h + 2 * mb, hp.at[mb])
        wire.arrive(r_h + 2 * mb + 1, hn.at[mb])

        def put(value, start):
            acts[start : start + value.shape[0], 0:D] = normed(
                value.astype(f32), gains[0], biases[0]
            ).astype(bf16)

        put(hp[mb], gap)
        put(tok[mb], rows)
        put(hn[mb], 2 * rows)
        if mb > 0:
            saves[mb - 1].wait()
        for k in range(3):
            for r in range(3):
                part = slice(r * rows, (r + 1) * rows)
                acts[part, (k + 1) * D : (k + 2) * D] = mm(acts[part, 0:D], w_all[k]).astype(bf16)
        saves[mb].start()
        idr = o_idr[mb]
        idc = jnp.broadcast_to(idr[:, rows : 2 * rows], (128, rows)).T[:, 0:1]
        bias[...] = jnp.where(idc == idr, 0.0, neg_big)
        o_lse[mb] = jnp.zeros((rows, 128), f32)

        @pl.loop(0, HEADS // 2, unroll=True)
        def _(pair):
            at = pl.ds(pl.multiple_of(pair * 128, 128), 128)
            query, key, value = (
                acts[part, pl.ds(pl.multiple_of((k + 1) * D + pair * 128, 128), 128)]
                for k, part in enumerate((slice(rows, 2 * rows), slice(0, ext), slice(0, ext)))
            )
            mixed = jnp.zeros((rows, 128), f32)
            lse = o_lse[mb]
            for half in range(2):
                keep = (lane < 64) if half == 0 else (lane >= 64)
                q = jnp.where(keep, query, jnp.zeros_like(query))
                v = jnp.where(keep, value, jnp.zeros_like(value))
                s = mm_nt(q, key) * scale + bias[...]
                top = jnp.max(s, axis=-1, keepdims=True)
                p = jnp.exp(s - top)
                total_p = jnp.sum(p, axis=-1, keepdims=True)
                mixed = mixed + mm((p * (1.0 / total_p)).astype(bf16), v)
                lse = jnp.where(lane == 2 * pair + half, top + jnp.log(total_p), lse)
            o_lse[mb] = lse
            o_mixed[mb, :, at] = mixed.astype(bf16)
            for when, hook in hooks.items():
                pl.when(pair == when)(hook)

        resid = tok[mb].astype(f32) + mm(o_mixed[mb], w_all[3])
        o_resid[mb] = resid
        n2 = normed(resid, gains[1], biases[1]).astype(bf16)
        gx[mb, s_me] = n2
        g_x[mb].own(gx.at[mb, s_me])
        logits = mm(n2, o_small[...].astype(bf16))
        logits = jnp.where(lane < experts, logits, neg_big)
        p = jnp.exp(logits - jnp.max(logits, axis=-1, keepdims=True))
        o_probs[mb] = p / jnp.sum(p, axis=-1, keepdims=True)
        give(gx.at[mb, s_me], g_n2.at[mb])
        give(o_probs.at[mb], g_probs.at[mb])
        give(o_resid.at[mb], g_resid.at[mb])
        give(o_mixed.at[mb], g_mixed.at[mb])
        give(o_lse.at[mb], g_lse.at[mb])

    def later_halves():
        g_x[0].pump(0)
        g_d[1].own(cot.at[1])

    attend(0, {0: lambda: g_d[0].pump(0), 3: lambda: g_d[0].pump(1)})
    send_ranks()
    attend(1, {0: lambda: g_d[0].pump(2), 2: later_halves})
    g_x[0].pump(1)

    r_cx = wire.roles(2 * MICRO * ne)
    r_up = wire.roles(MICRO * ne)
    r_dn = wire.roles(MICRO * ne)
    r_dg = wire.roles(MICRO * 2 * ne)
    sub = lax.broadcasted_iota(jnp.int32, (slots, rows), 0).astype(f32)
    tile = 2 * slots
    chunk = 512
    like = qo.at[0, 0, 0]

    def target(i):
        swap = jnp.where(i < 2, 1 - i, i)
        return jnp.where(
            z == 0, i, jnp.where(z == 1, swap, jnp.where(z == 2, ne - 1 - swap, ne - 1 - i))
        )

    def pass_up(mb, to):
        wire.send(r_up + mb * ne + to, qo.at[mb, 0, to], ud.at[mb, to], me.up)

    def pass_down(mb, to):
        slot = jnp.where(z - 1 == to, ne, to)
        wire.send(r_dn + mb * ne + to, qo.at[mb, 0, to], ud.at[mb, slot], me.down)

    def settle(mb, zp):
        for t in range(2):
            wire.arrive(r_cx + (mb * 2 + t) * ne + zp, like)
            qo[mb, t, zp] = (qo[mb, t, zp].astype(f32) + cr[mb, t, zp].astype(f32)).astype(bf16)

        @pl.when((z == 0) & (zp > 0))
        def _():
            pass_up(mb, zp)

        @pl.when((z == ne - 1) & (zp < ne - 1))
        def _():
            pass_down(mb, zp)

    def relay(mb, hop, to):
        @pl.when(z == hop)
        def _():
            wire.arrive(r_up + mb * ne + to, like)
            qo[mb, 0, to] = (qo[mb, 0, to].astype(f32) + ud[mb, to].astype(f32)).astype(bf16)
            pass_up(mb, to)

        @pl.when(z == ne - 1 - hop)
        def _():
            low = ne - 1 - to
            wire.arrive(r_dn + mb * ne + low, like)
            qo[mb, 0, low] = (qo[mb, 0, low].astype(f32) + ud[mb, low].astype(f32)).astype(bf16)
            pass_down(mb, low)

    def end_sums(mb):
        acc_eo[...] = qo[mb, 0, z].astype(f32)

        @pl.when(z > 0)
        def _():
            wire.arrive(r_up + mb * ne + z, like)
            acc_eo[...] += ud[mb, z].astype(f32)

        @pl.when(z < ne - 1)
        def _():
            wire.arrive(r_dn + mb * ne + z, like)
            acc_eo[...] += ud[mb, ne].astype(f32)

        o_din[mb] = acc_eo[...]

    def first_tile():
        for cp in own_w + own_d + saves[1:]:
            cp.wait()
        for cc in range(2):
            wire.arrive(r_uy + cc, win.at[0])
            wire.arrive(r_dx2 + cc, wout.at[0])
        wire.arrive(r_us, win.at[0])
        wire.arrive(r_dsib, wout.at[0])
        wire.arrive(r_uf, up_at(0, 2))
        wire.arrive(r_df, down_at(0, 2))
        for k in range(ne):
            if k > 0:
                wire.arrive(r_rk + 2 * k, rk_src)
            wire.arrive(r_rk + 2 * k + 1, rk_src)
        g_d[0].near()
        g_x[0].near()

    def both(mb, what, k):
        for g in (g_d[mb], g_x[mb]):
            getattr(g, what)(k)

    def tile_1():
        both(0, "finish", 0)
        g_x[0].pump(2)

    def tile_2():
        both(0, "finish", 1)

    def tile_3():
        both(0, "finish", 2)
        both(1, "pump", 0)

    def tile_4():
        g_d[1].near()
        g_x[1].near()

    def tile_5():
        both(1, "finish", 0)
        both(1, "pump", 1)
        relay(0, 1, 2)

    def tile_6():
        both(1, "finish", 1)
        both(1, "pump", 2)
        relay(0, 1, 3)

    def tile_7():
        both(1, "finish", 2)
        relay(0, 2, 3)

    before_tile = [first_tile, tile_1, tile_2, tile_3, tile_4, tile_5, tile_6, tile_7]

    @pl.loop(0, MICRO * ne)
    def _(i):
        mb = i // ne
        zp = target(lax.rem(i, ne))

        for when, hook in enumerate(before_tile):
            pl.when(i == when)(hook)

        for cc in range(2):
            s = zp * 2 + cc
            at = slice(cc * slots, (cc + 1) * slots)
            pick = (sub == rk[s, mb, pl.ds(e, 1), :]).astype(bf16)
            pm[cc] = pick
            xs[at, :] = mm(pick, gx[mb, s]).astype(bf16)
            ds[at, :] = mm(pick, gd[mb, s]).astype(bf16)
        x = xs[...]
        logits = mm(x, o_small[...].astype(bf16))
        logits = jnp.where(lane < experts, logits, neg_big)
        p = jnp.exp(logits - jnp.max(logits, axis=-1, keepdims=True))
        p = p / jnp.sum(p, axis=-1, keepdims=True)
        gate = jnp.sum(jnp.where(lane == e, p, 0.0), axis=-1, keepdims=True)
        gt[...] = jnp.broadcast_to(gate, (tile, 128))
        dy = (gate * ds[...].astype(f32)).astype(bf16)
        deo[...] = dy
        across = pl.ds(pl.multiple_of(i * tile, tile), tile)
        xt[:, across] = x.T
        dt[:, across] = dy.T

        @pl.loop(0, FF // 256, unroll=True)
        def _(f):
            at = pl.ds(pl.multiple_of(f * 256, 256), 256)
            pre = mm(xs[...], wu[:, at])
            d_act = mm_nt(deo[...], wd[at, :])
            sq = pre * pre
            k0 = math.sqrt(2.0 / math.pi)
            th = jnp.tanh(pre * (k0 + (k0 * 0.044715) * sq))
            half = 0.5 + 0.5 * th
            slope = half + (0.5 * pre) * (1.0 - th * th) * (k0 + (3.0 * k0 * 0.044715) * sq)
            acts[across, at] = (pre * half).astype(bf16)
            grads[across, at] = (slope * d_act).astype(bf16)

        @pl.when(i > 0)
        def _():
            settle((i - 1) // ne, target(lax.rem(i - 1 + ne, ne)))

        eo = mm(acts[across, :], wd[...]).astype(bf16).astype(f32)
        d_gate = jnp.sum(ds[...].astype(f32) * eo, axis=-1, keepdims=True)
        ys[0] = mm_nt(grads[across, :], wu[...]).astype(bf16)
        ys[1] = (gt[:, 0:1] * eo).astype(bf16)
        box = lax.rem(i, 2)

        @pl.when(i > 1)
        def _():
            old = i - 2
            for t in range(2):
                wire.left(r_cx + ((old // ne) * 2 + t) * ne + target(lax.rem(old, ne)), like)

        for own in range(2):
            cc = c if own else 1 - c
            back = pm[cc].T
            at = pl.ds(pl.multiple_of(cc * slots, slots), slots)
            for t in range(2):
                moved = mm(back, ys[t, at, :]).astype(bf16)
                if own:
                    qo[mb, t, zp] = moved
                else:
                    cs[box, t] = moved
        for t in range(2):
            role = r_cx + (mb * 2 + t) * ne + zp
            wire.send(role, cs.at[box, t], cr.at[mb, t, zp], me.sib)
        for cc in range(2):
            at = slice(cc * slots, (cc + 1) * slots)
            line = jnp.sum(pm[cc].astype(f32) * d_gate[at], axis=0, keepdims=True)
            to = zp * 2 + cc
            dgs[mb, to] = jnp.broadcast_to(line, (8, rows))

            @pl.when(to != s_me)
            def _():
                wire.send(
                    r_dg + mb * 2 * ne + to,
                    dgs.at[mb, to],
                    dg.at[mb, e],
                    (d - c + cc, zp),
                    recv_role=r_dg + mb * 2 * ne + s_me,
                )

            @pl.when(to == s_me)
            def _():
                dg[mb, e] = jnp.broadcast_to(line, (8, rows))

    settle(1, target(ne - 1))

    wide_at = [pl.ds(k * chunk, chunk) for k in range(FF // chunk)]
    outs = []
    hooks = {0: lambda: relay(1, 1, 2), 1: lambda: relay(1, 1, 3), 3: lambda: relay(1, 2, 3)}
    for f, at in enumerate(wide_at):
        for k, (left, right, to) in enumerate(((xt, grads, o_up), (dt, acts, o_down))):
            if f > 1:
                outs[2 * (f - 2) + k].wait()
            stage[f % 2, k] = mm(left[...], right[:, at]).astype(bf16)
            cp = pltpu.make_async_copy(stage.at[f % 2, k], to.at[:, at], local_sems.at[9 + 2 * f + k])
            cp.start()
            outs.append(cp)
        if f in hooks:
            hooks[f]()
    end_sums(0)
    give_y = [pltpu.make_async_copy(qo.at[mb, 1], o_y.at[mb], local_sems.at[mb]) for mb in range(MICRO)]
    for cp in give_y:
        cp.start()
    for mb in range(MICRO):
        for s in range(2 * ne):

            @pl.when(s != s_me)
            def _():
                wire.arrive(r_dg + mb * 2 * ne + s, dgs.at[0, 0])

        groups = []
        sub8 = lax.broadcasted_iota(jnp.int32, (8, rows), 0)
        for base in range(0, experts, 8):
            group = dg[mb, base]
            for j in range(1, 8):
                group = jnp.where(sub8 == j, dg[mb, base + j], group)
            groups.append(group)
        lines = jnp.concatenate(groups + [jnp.zeros((128 - experts, rows), f32)], axis=0)
        o_dprobs[mb] = lines.T
    end_sums(1)
    for cp in outs[-4:] + give_y + given:
        cp.wait()

    for k in range(1, ne):
        wire.left(r_dz + 3 * (k - 1), qkv)
        wire.left(r_dz + 3 * (k - 1) + 1, outw)
        wire.left(r_dz + 3 * (k - 1) + 2, s_src)
    wire.left(r_id, ids)
    wire.left(r_id + 1, ids)
    for k in range(2 * MICRO):
        wire.left(r_h + k, hp.at[0])
    for k in range(1, chips):
        wire.left(r_dx + 2 * (k - 1), blk)
        wire.left(r_dx + 2 * (k - 1) + 1, sblk)
    for k in range(chips):
        wire.left(r_ds + 2 * k, blk)
        wire.left(r_ds + 2 * k + 1, sblk)
    for cc in range(2):
        wire.left(r_ux + cc, win.at[0])
        wire.left(r_uy + cc, win.at[0])
        wire.left(r_dy + cc, wout.at[0])
        wire.left(r_dx2 + cc, wout.at[0])
    wire.left(r_us, win.at[0])
    wire.left(r_dsib, wout.at[0])
    wire.left(r_uf, up_at(0, 2))
    wire.left(r_df, down_at(0, 2))
    for k in range(ne):
        if k > 0:
            wire.left(r_rk + 2 * k, rk_src)
        wire.left(r_rk + 2 * k + 1, rk_src)
    for g in g_d + g_x:
        g.drain()
    for old in (MICRO * ne - 2, MICRO * ne - 1):
        for t in range(2):
            wire.left(r_cx + ((old // ne) * 2 + t) * ne + target(old % ne), like)
    for mb in range(MICRO):
        for to in range(1, ne):

            @pl.when(z < to)
            def _():
                wire.left(r_up + mb * ne + to, like)

        for to in range(ne - 1):

            @pl.when(z > to)
            def _():
                wire.left(r_dn + mb * ne + to, like)

        for s in range(2 * ne):

            @pl.when(s != s_me)
            def _():
                wire.left(r_dg + mb * 2 * ne + s, dgs.at[0, 0])

    assert wire.used <= ROLES


ROLES = 192


def front(nd, ne, *args):
    tokens, qkv = args[0], args[3]
    rows, share = tokens.shape[1], qkv.shape[1]
    halo = -(-(IMG - 1) // 16) * 16
    experts = 2 * ne
    slots = 4 * rows // experts
    tile = 2 * slots
    every = MICRO * ne * tile
    shape = jax.ShapeDtypeStruct
    vmem, anywhere = pl.BlockSpec(memory_space=pltpu.VMEM), pl.BlockSpec(memory_space=pl.ANY)
    outs = (
        (vmem, (MICRO, rows, D), f32),
        (anywhere, (MICRO, ne, rows, D), bf16),
        (vmem, (MICRO, rows, 128), f32),
        (anywhere, (D, FF), bf16),
        (anywhere, (D, FF), bf16),
        (anywhere, (MICRO, rows, D), bf16),
        (anywhere, (MICRO, rows, 128), f32),
        (anywhere, (MICRO, rows, D), f32),
        (anywhere, (MICRO, rows, D), bf16),
        (anywhere, (MICRO, 3 * rows, 3 * D), bf16),
        (anywhere, (MICRO, rows, 128), f32),
        (anywhere, (4, D, D), bf16),
        (vmem, (D, 128), f32),
        (vmem, (MICRO, 1, 3 * rows), f32),
    )
    v = pltpu.VMEM
    return pl.pallas_call(
        functools.partial(front_kernel, nd, ne),
        out_shape=[shape(*o[1:]) for o in outs],
        in_specs=[vmem, vmem, vmem, anywhere, anywhere, vmem, vmem, vmem] + [anywhere] * 3,
        out_specs=[o[0] for o in outs],
        scratch_shapes=[
            v((share + 16, 128), bf16),
            v((nd * ne, share + 16, 128), bf16),
            v((MICRO, halo, D), bf16),
            v((MICRO, halo, D), bf16),
            v((MICRO, rows), jnp.int32),
            v((MICRO, rows), jnp.int32),
            v((MICRO, 2 * ne, rows, D), bf16),
            v((MICRO, 2 * ne, rows, D), bf16),
            v((D, FF), bf16),
            v((FF, D), bf16),
            v((MICRO, experts, rows), f32),
            v((2 * ne, MICRO, experts, rows), f32),
            v((rows, 3 * rows), f32),
            v((every, FF), bf16),
            v((every, FF), bf16),
            v((2, slots, rows), bf16),
            v((tile, D), bf16),
            v((tile, D), bf16),
            v((tile, D), bf16),
            v((D, every), bf16),
            v((D, every), bf16),
            v((tile, 128), f32),
            v((rows, D), f32),
            v((2, tile, D), bf16),
            v((MICRO, 2, ne, rows, D), bf16),
            v((2, 2, rows, D), bf16),
            v((MICRO, 2, ne, rows, D), bf16),
            v((MICRO, ne + 1, rows, D), bf16),
            v((MICRO, 2 * ne, 8, rows), f32),
            v((MICRO, experts, 8, rows), f32),
            v((2, 2, D, 512), bf16),
            v((128, 128), f32),
            v((MICRO, rows, 128), f32),
            v((MICRO, rows, D), f32),
            v((MICRO, rows, D), bf16),
            v((MICRO, rows, 128), f32),
            v((4, D, D), bf16),
            pltpu.SemaphoreType.DMA((16,)),
            pltpu.SemaphoreType.DMA((ROLES,)),
            pltpu.SemaphoreType.DMA((ROLES,)),
            pltpu.SemaphoreType.DMA((17,)),
        ],
        compiler_params=pltpu.CompilerParams(
            collective_id=0, has_side_effects=True, vmem_limit_bytes=VMEM_BYTES
        ),
        name="front",
    )(*args)


def mm_exact(a, b):
    return jnp.dot(a, b, preferred_element_type=f32, precision=highest)


def back_kernel(
    nd,
    ne,
    tok,
    cot,
    d_in,
    y,
    d_probs,
    up,
    down,
    n2,
    probs,
    resid,
    mixed,
    qkv_in,
    lse,
    w_in,
    small,
    idr,
    o_block,
    o_input,
    o_dense,
    o_small,
    o_up,
    o_down,
    yq,
    yu,
    gu,
    gd,
    d_res,
    dm,
    stat_src,
    stat_p,
    stat_n,
    hp,
    hn,
    stats,
    bias,
    dp,
    gw,
    gs,
    gwb,
    gsb,
    rc,
    rcs,
    sx,
    sxs,
    rx,
    rxs,
    sz,
    szs,
    rz,
    rzs,
    block,
    qkv,
    w,
    send_sems,
    recv_sems,
    local_sems,
):
    me = Place(nd, ne)
    d, z, c = me.d, me.z, me.c
    rows = tok.shape[1]
    experts = 2 * ne
    halo = hp.shape[1]
    gap = rows - halo
    chips = nd // 2
    wire = Wire(send_sems, recv_sems, me.sib)
    lane = lax.broadcasted_iota(jnp.int32, (1, 128), 1)
    up_rows, down_rows = gu.shape[1], gd.shape[2]
    part = D // nd
    share = part // ne
    me.enter()

    r_g = wire.roles(2 * (nd - 1))

    def up_of(dd):
        return up.at[pl.ds(pl.multiple_of(dd * up_rows, 16), up_rows)]

    def down_of(dd):
        return down.at[:, pl.ds(pl.multiple_of(dd * down_rows, 128), down_rows)]

    own_g = [
        pltpu.make_async_copy(up_of(d), gu.at[d], local_sems.at[0]),
        pltpu.make_async_copy(down_of(d), gd.at[d], local_sems.at[1]),
    ]
    for cp in own_g:
        cp.start()
    for k in range(1, nd):
        dd = lax.rem(d + k, nd)
        wire.send(r_g + 2 * (k - 1), up_of(dd), gu.at[d], (dd, z))
        wire.send(r_g + 2 * (k - 1) + 1, down_of(dd), gd.at[d], (dd, z))

    fetches = [
        pltpu.make_async_copy(w_in.at[3], w.at[3], local_sems.at[2]),
        pltpu.make_async_copy(qkv_in.at[0], qkv.at[0], local_sems.at[3]),
        pltpu.make_async_copy(qkv_in.at[1], qkv.at[1], local_sems.at[4]),
        pltpu.make_async_copy(w_in.at[pl.ds(0, 3)], w.at[pl.ds(0, 3)], local_sems.at[5]),
        pltpu.make_async_copy(y.at[0, z], yq.at[0], local_sems.at[6]),
        pltpu.make_async_copy(y.at[1, z], yq.at[1], local_sems.at[7]),
    ]
    for cp in fetches:
        cp.start()
    r_y = wire.roles(MICRO * ne)
    like = yq.at[0]

    def send_y(mb):
        for k in range(1, ne):
            to = lax.rem(z + k, ne)
            wire.send(r_y + mb * ne + k, y.at[mb, to], yu.at[mb, k], (d, to))

    def end_sums(mb):
        block[...] = resid[mb] + yq[mb].astype(f32)
        for k in range(1, ne):
            wire.arrive(r_y + mb * ne + k, like)
            block[...] += yu[mb, k].astype(f32)
        o_block[mb] = block[...].astype(bf16)

    s_rows = small[...].T
    gains = [s_rows[experts + k : experts + k + 1, :] for k in range(2)]
    router = jnp.where(lane < experts, small[...], 0.0)
    head_of = (
        lax.broadcasted_iota(jnp.int32, (D, 128), 0) // HEAD_DIM
        == lax.broadcasted_iota(jnp.int32, (D, 128), 1)
    ).astype(f32)

    def norm_back(values, dn, gain):
        offset = values - jnp.mean(values, axis=-1, keepdims=True)
        inv = lax.rsqrt(jnp.mean(offset * offset, axis=-1, keepdims=True) + norm_eps)
        hat = offset * inv
        q = dn * gain
        dv = inv * (
            q
            - jnp.mean(q, axis=-1, keepdims=True)
            - hat * jnp.mean(q * hat, axis=-1, keepdims=True)
        )
        return dv, jnp.sum(dn * hat, axis=0, keepdims=True), jnp.sum(dn, axis=0, keepdims=True)

    r_h = wire.roles(4 * MICRO)
    norm_sums = [jnp.zeros((1, D), f32) for _ in range(4)]
    zero_gap = jnp.zeros((gap, D), bf16)
    own = slice(rows, 2 * rows)
    for mb in range(MICRO):
        prob, dpr = probs[mb], d_probs[mb]
        d_logits = prob * (dpr - jnp.sum(prob * dpr, axis=-1, keepdims=True))
        dn2 = d_in[mb] + lax.dot_general(
            d_logits,
            router,
            (((1,), (1,)), ((), ())),
            preferred_element_type=f32,
            precision=highest,
        )
        dv, d_gain, d_bias = norm_back(resid[mb], dn2, gains[1])
        norm_sums[1] += d_gain
        norm_sums[3] += d_bias
        d_resid = cot[mb].astype(f32) + dv
        d_res[mb] = d_resid
        d_attn = d_resid.astype(bf16)
        if mb == 0:
            fetches[0].wait()
        d_mixed = mm_nt(d_attn, w[3]).astype(bf16)
        dm[mb, own, :] = d_mixed
        delta = mm_exact(d_mixed.astype(f32) * mixed[mb].astype(f32), head_of)
        stat_src[mb, 0] = lse[mb].T[0:HEADS, :]
        stat_src[mb, 1] = delta.T[0:HEADS, :]
        low, high = pl.ds(rows, halo), pl.ds(2 * rows - halo, halo)
        wire.send(r_h + 4 * mb, dm.at[mb, high], hp.at[mb], me.next)
        wire.send(r_h + 4 * mb + 1, stat_src.at[mb], stat_p.at[mb], me.next)
        wire.send(r_h + 4 * mb + 2, dm.at[mb, low], hn.at[mb], me.prev)
        wire.send(r_h + 4 * mb + 3, stat_src.at[mb], stat_n.at[mb], me.prev)
        g_out = mm(mixed[mb].T, d_attn)
        g_router = mm_exact(n2[mb].astype(f32).T, d_logits)
        if mb == 0:
            gw[3] = g_out
            gs[...] = g_router
        else:
            gw[3] += g_out
            gs[...] += g_router

    scale = 1.0 / math.sqrt(HEAD_DIM)
    for mb in range(MICRO):
        ids = idr[mb]
        fetches[1 + mb].wait()
        if mb == 0:
            fetches[3].wait()
        idc = jnp.broadcast_to(ids[:, own], (128, rows)).T[:, 0:1]
        bias[...] = jnp.where(idc == ids, 0.0, neg_big)
        dst = jnp.zeros((rows, 128), f32)
        delta_cols = jnp.concatenate(
            [stat_src[mb, 1], jnp.zeros((128 - HEADS, rows), f32)], axis=0
        ).T

        @pl.loop(0, HEADS // 2, unroll=True)
        def _(pair):
            at = pl.ds(pl.multiple_of(pair * 128, 128), 128)
            query, key, value = (
                qkv[mb, part, pl.ds(pl.multiple_of(k * D + pair * 128, 128), 128)]
                for k, part in enumerate((own, slice(None), slice(None)))
            )
            grad = dm[mb, own, at]
            dq = jnp.zeros((rows, 128), f32)
            for half in range(2):
                keep = (lane < 64) if half == 0 else (lane >= 64)
                h = 2 * pair + half
                q = jnp.where(keep, query, jnp.zeros_like(query))
                g = jnp.where(keep, grad, jnp.zeros_like(grad))
                k = jnp.where(keep, key, jnp.zeros_like(key))
                lse_col = jnp.sum(jnp.where(lane == h, lse[mb], 0.0), axis=1, keepdims=True)
                delta_col = jnp.sum(jnp.where(lane == h, delta_cols, 0.0), axis=1, keepdims=True)
                p = jnp.exp(mm_nt(q, key) * scale + bias[...] - lse_col)
                ds = (p * (mm_nt(g, value) - delta_col)).astype(bf16)
                dq = dq + mm(ds, k)
            dp[0, :, at] = (dq * scale).astype(bf16)

        wire.arrive(r_h + 4 * mb, hp.at[mb])
        wire.arrive(r_h + 4 * mb + 1, stat_src.at[mb])
        wire.arrive(r_h + 4 * mb + 2, hp.at[mb])
        wire.arrive(r_h + 4 * mb + 3, stat_src.at[mb])
        send_y(mb)
        dm[mb, 0:gap, :] = zero_gap
        dm[mb, gap:rows, :] = hp[mb]
        dm[mb, 2 * rows : 2 * rows + halo, :] = hn[mb]
        dm[mb, 2 * rows + halo : 3 * rows, :] = zero_gap
        for k in range(2):
            stats[k, :, 0:rows] = stat_p[mb, k]
            stats[k, :, own] = stat_src[mb, k]
            stats[k, :, 2 * rows : 3 * rows] = stat_n[mb, k]

        @pl.loop(0, HEADS // 2, unroll=True)
        def _(pair):
            at = pl.ds(pl.multiple_of(pair * 128, 128), 128)
            query, key, value = (
                qkv[mb, part, pl.ds(pl.multiple_of(k * D + pair * 128, 128), 128)]
                for k, part in enumerate((slice(None), own, own))
            )
            grad = dm[mb, :, at]
            dk = jnp.zeros((rows, 128), f32)
            dv = jnp.zeros((rows, 128), f32)
            for half in range(2):
                keep = (lane < 64) if half == 0 else (lane >= 64)
                h = 2 * pair + half
                q = jnp.where(keep, query, jnp.zeros_like(query))
                g = jnp.where(keep, grad, jnp.zeros_like(grad))
                k = jnp.where(keep, key, jnp.zeros_like(key))
                v = jnp.where(keep, value, jnp.zeros_like(value))
                p = jnp.exp(mm_nt(k, query) * scale + bias[...] - stats[0, pl.ds(h, 1), :])
                ds = (p * (mm_nt(v, grad) - stats[1, pl.ds(h, 1), :])).astype(bf16)
                dk = dk + mm(ds, q)
                dv = dv + mm(p.astype(bf16), g)
            dp[1, :, at] = (dk * scale).astype(bf16)
            dp[2, :, at] = dv.astype(bf16)

        token = tok[mb].astype(f32)
        n1t = normed(token, gains[0], s_rows[experts + 2 : experts + 3, :]).astype(bf16).T
        dn1 = jnp.zeros((rows, D), f32)
        for k in range(3):
            dn1 = dn1 + mm_nt(dp[k], w[k])
            g_part = mm(n1t, dp[k])
            if mb == 0:
                gw[k] = g_part
            else:
                gw[k] += g_part
        dv, d_gain, d_bias = norm_back(token, dn1, gains[0])
        norm_sums[0] += d_gain
        norm_sums[2] += d_bias
        o_input[mb] = (d_res[mb] + dv).astype(bf16)

    rows128 = lax.broadcasted_iota(jnp.int32, (128, D), 0)
    norm_rows = jnp.zeros((128, D), f32)
    for k in range(4):
        norm_rows = jnp.where(rows128 == experts + k, norm_sums[k], norm_rows)
    gs[...] = jnp.where(lane < experts, gs[...], norm_rows.T)

    def of(dd):
        return pl.ds(pl.multiple_of(dd * part, 16), part)

    r_c = wire.roles(2 * chips)
    r_x = wire.roles(2 * (chips - 1))
    r_z = wire.roles(2 * (ne - 1))
    for k in range(chips):
        dd = 2 * k + 1 - c
        for m in range(4):
            gwb[k, m] = gw[m, of(dd), :].astype(bf16)
        gsb[k] = gs[of(dd), :]
        wire.send(r_c + 2 * k, gwb.at[k], rc.at[k], me.sib)
        wire.send(r_c + 2 * k + 1, gsb.at[k], rcs.at[k], me.sib)
    for k in range(chips):
        wire.arrive(r_c + 2 * k, rc.at[k])
        wire.arrive(r_c + 2 * k + 1, rcs.at[k])
    my_chip = d // 2
    for k in range(1, chips):
        to = lax.rem(my_chip + k, chips)
        dd = 2 * to + c
        for m in range(4):
            sx[k, m] = (gw[m, of(dd), :] + rc[to, m].astype(f32)).astype(bf16)
        sxs[k] = gs[of(dd), :] + rcs[to]
        wire.send(r_x + 2 * (k - 1), sx.at[k], rx.at[k], (dd, z))
        wire.send(r_x + 2 * (k - 1) + 1, sxs.at[k], rxs.at[k], (dd, z))
    total = [gw[m, of(d), :] + rc[my_chip, m].astype(f32) for m in range(4)]
    total_s = gs[of(d), :] + rcs[my_chip]
    for k in range(1, chips):
        wire.arrive(r_x + 2 * (k - 1), rx.at[k])
        wire.arrive(r_x + 2 * (k - 1) + 1, rxs.at[k])
        total = [total[m] + rx[k, m].astype(f32) for m in range(4)]
        total_s = total_s + rxs[k]
    for m in range(4):
        gw[m, 0:part, :] = total[m]
    gs[0:part, :] = total_s
    for k in range(1, ne):
        to = lax.rem(z + k, ne)
        at = pl.ds(pl.multiple_of(to * share, 16), share)
        for m in range(4):
            sz[k, m] = gw[m, at, :].astype(bf16)
        szs[k] = gs[at, :]
        wire.send(r_z + 2 * (k - 1), sz.at[k], rz.at[k], (d, to))
        wire.send(r_z + 2 * (k - 1) + 1, szs.at[k], rzs.at[k], (d, to))

    for cp in own_g:
        cp.wait()
    for k in range(1, nd):
        wire.arrive(r_g + 2 * (k - 1), gu.at[0])
        wire.arrive(r_g + 2 * (k - 1) + 1, gd.at[0])
    for x in range(2):
        o_up[x] = sum(gu[2 * k + x].astype(f32) for k in range(chips))
        o_down[x] = sum(gd[2 * k + x].astype(f32) for k in range(chips)).T

    for cp in fetches[4:]:
        cp.wait()
    for mb in range(MICRO):
        end_sums(mb)
    at = pl.ds(pl.multiple_of(z * share, 16), share)
    for k in range(1, ne):
        wire.arrive(r_z + 2 * (k - 1), rz.at[k])
        wire.arrive(r_z + 2 * (k - 1) + 1, rzs.at[k])
    for m in range(4):
        o_dense[m] = gw[m, at, :] + sum(rz[k, m].astype(f32) for k in range(1, ne))
    o_small[...] = gs[at, :] + sum(rzs[k] for k in range(1, ne))

    for k in range(1, nd):
        wire.left(r_g + 2 * (k - 1), gu.at[0])
        wire.left(r_g + 2 * (k - 1) + 1, gd.at[0])
    for mb in range(MICRO):
        for k in range(1, ne):
            wire.left(r_y + mb * ne + k, like)
        for k in range(2):
            wire.left(r_h + 4 * mb + 2 * k, hp.at[0])
            wire.left(r_h + 4 * mb + 2 * k + 1, stat_src.at[0])
    for k in range(chips):
        wire.left(r_c + 2 * k, rc.at[0])
        wire.left(r_c + 2 * k + 1, rcs.at[0])
    for k in range(1, chips):
        wire.left(r_x + 2 * (k - 1), rx.at[0])
        wire.left(r_x + 2 * (k - 1) + 1, rxs.at[0])
    for k in range(1, ne):
        wire.left(r_z + 2 * (k - 1), rz.at[0])
        wire.left(r_z + 2 * (k - 1) + 1, rzs.at[0])
    assert wire.used <= BACK_ROLES


BACK_ROLES = 80


def back(nd, ne, *args):
    tokens = args[0]
    rows = tokens.shape[1]
    halo = -(-(IMG - 1) // 16) * 16
    chips = nd // 2
    part = D // nd
    share = part // ne
    shape = jax.ShapeDtypeStruct
    outs = (
        shape((MICRO, rows, D), bf16),
        shape((MICRO, rows, D), bf16),
        shape((4, share, D), f32),
        shape((share, 128), f32),
        shape((2, D // nd, FF), f32),
        shape((2, FF // nd, D), f32),
    )
    vmem, anywhere = pl.BlockSpec(memory_space=pltpu.VMEM), pl.BlockSpec(memory_space=pl.ANY)
    v = pltpu.VMEM
    return pl.pallas_call(
        functools.partial(back_kernel, nd, ne),
        out_shape=outs,
        in_specs=[anywhere if k in (3, 5, 6, 11, 13) else vmem for k in range(len(args))],
        out_specs=[vmem] * len(outs),
        scratch_shapes=[
            v((MICRO, rows, D), bf16),
            v((MICRO, ne, rows, D), bf16),
            v((nd, D // nd, FF), bf16),
            v((nd, D, FF // nd), bf16),
            v((MICRO, rows, D), f32),
            v((MICRO, 3 * rows, D), bf16),
            v((MICRO, 2, HEADS, rows), f32),
            v((MICRO, 2, HEADS, rows), f32),
            v((MICRO, 2, HEADS, rows), f32),
            v((MICRO, halo, D), bf16),
            v((MICRO, halo, D), bf16),
            v((2, HEADS, 3 * rows), f32),
            v((rows, 3 * rows), f32),
            v((3, rows, D), bf16),
            v((4, D, D), f32),
            v((D, 128), f32),
            v((chips, 4, part, D), bf16),
            v((chips, part, 128), f32),
            v((chips, 4, part, D), bf16),
            v((chips, part, 128), f32),
            v((chips, 4, part, D), bf16),
            v((chips, part, 128), f32),
            v((chips, 4, part, D), bf16),
            v((chips, part, 128), f32),
            v((ne, 4, share, D), bf16),
            v((ne, share, 128), f32),
            v((ne, 4, share, D), bf16),
            v((ne, share, 128), f32),
            v((rows, D), f32),
            v((MICRO, 3 * rows, 3 * D), bf16),
            v((4, D, D), bf16),
            pltpu.SemaphoreType.DMA((BACK_ROLES,)),
            pltpu.SemaphoreType.DMA((BACK_ROLES,)),
            pltpu.SemaphoreType.DMA((8,)),
        ],
        compiler_params=pltpu.CompilerParams(
            collective_id=1, has_side_effects=True, vmem_limit_bytes=VMEM_BYTES
        ),
        name="back",
    )(*args)


def finish_kernel(block, inputs, dense, small, up, down, *rest):
    o_block, o_input, o_qkv, o_out, o_router, o_gain, o_bias, o_up, o_down = rest[:9]
    bufs, in_sems, out_sems = rest[9:-2], rest[-2], rest[-1]
    moves = (
        (up, o_up),
        (down, o_down),
        (inputs, o_input),
        (block, o_block),
        (dense.at[pl.ds(0, 3)], o_qkv),
        (dense.at[3], o_out),
    )
    ins = [pltpu.make_async_copy(m[0], b, in_sems.at[k]) for k, (m, b) in enumerate(zip(moves, bufs))]
    outs = [pltpu.make_async_copy(b, m[1], out_sems.at[k]) for k, (m, b) in enumerate(zip(moves, bufs))]
    for cp in ins:
        cp.start()
    experts, share = o_router.shape
    turned = jnp.concatenate([small[...], jnp.zeros((128 - share, 128), f32)], axis=0).T
    o_router[...] = turned[0:experts, 0:share]
    o_gain[...] = turned[experts : experts + 2, 0:share]
    o_bias[...] = turned[experts + 2 : experts + 4, 0:share]
    for there, back_again in zip(ins, outs):
        there.wait()
        back_again.start()
    for cp in outs:
        cp.wait()


def finish(experts, *args):
    block, inputs, dense, small, up, down = args
    share = small.shape[0]
    vmem, anywhere = pl.BlockSpec(memory_space=pltpu.VMEM), pl.BlockSpec(memory_space=pl.ANY)
    shape = jax.ShapeDtypeStruct
    outs = (
        (anywhere, block),
        (anywhere, inputs),
        (anywhere, shape((3, share, D), f32)),
        (anywhere, shape((share, D), f32)),
        (vmem, shape((experts, share), f32)),
        (vmem, shape((2, share), f32)),
        (vmem, shape((2, share), f32)),
        (anywhere, up),
        (anywhere, down),
    )
    bufs = (up, down, inputs, block, outs[2][1], outs[3][1])
    return pl.pallas_call(
        finish_kernel,
        out_shape=[shape(o[1].shape, o[1].dtype) for o in outs],
        in_specs=[vmem if k == 3 else anywhere for k in range(len(args))],
        out_specs=[o[0] for o in outs],
        scratch_shapes=[
            *(pltpu.VMEM(b.shape, b.dtype) for b in bufs),
            pltpu.SemaphoreType.DMA((7,)),
            pltpu.SemaphoreType.DMA((7,)),
        ],
        name="finish",
    )(*args)


def kernel_body(
    nd,
    ne,
    tokens,
    image_ids,
    routes,
    qkv_weight,
    out_weight,
    router_weight,
    norm_gains,
    norm_biases,
    expert_in,
    expert_out,
    cotangent,
):
    experts = 2 * ne
    saved = front(
        nd,
        ne,
        tokens,
        image_ids,
        routes.transpose(0, 2, 1),
        qkv_weight,
        out_weight,
        router_weight.T,
        norm_gains,
        norm_biases,
        expert_in,
        expert_out,
        cotangent,
    )
    outs = finish(experts, *back(nd, ne, tokens, cotangent, *saved))
    return (*outs[:4], outs[4].T, *outs[5:])


def chosen_body(nd, ne, tokens, *rest):
    rows, experts = tokens.shape[1], 2 * ne
    whole = D % (16 * nd * ne) == 0 and nd % 2 == 0 and 8 * rows == experts * rows and rows % 128 == 0
    whole = whole and nd == 8 and ne == 4
    if whole and rest[-3].shape[0] == 2:
        return kernel_body(nd, ne, tokens, *rest)
    return body(tokens, *rest)


def solution(mesh):
    return jax.shard_map(
        functools.partial(chosen_body, mesh.shape["dp"], mesh.shape["expert"]),
        mesh=mesh,
        in_specs=(
            P(None, ("dp", "expert"), None),
            P(None, ("dp", "expert")),
            P(None, ("dp", "expert"), None),
            P(None, ("dp", "expert"), None),
            P(("dp", "expert"), None),
            P(("dp", "expert"), None),
            P(None, ("dp", "expert")),
            P(None, ("dp", "expert")),
            P("expert", "dp", None),
            P("expert", "dp", None),
            P(None, ("dp", "expert"), None),
        ),
        out_specs=(
            P(None, ("dp", "expert"), None),
            P(None, ("dp", "expert"), None),
            P(None, ("dp", "expert"), None),
            P(("dp", "expert"), None),
            P(("dp", "expert"), None),
            P(None, ("dp", "expert")),
            P(None, ("dp", "expert")),
            P("expert", "dp", None),
            P("expert", "dp", None),
        ),
        check_vma=False,
    )
```

```python
import functools
import math

import jax
import jax.numpy as jnp
from jax import lax
from jax.experimental import pallas as pl
from jax.experimental.pallas import tpu as pltpu
from jax.sharding import PartitionSpec as P

D = 512
HEADS = 8
HEAD_DIM = 64
FF = 2048
TOP = 2
IMG = 197
MICRO = 2


neg_big = -1e30
norm_eps = 1e-06
highest = lax.Precision.HIGHEST


def padded(cells, sides, width):
    for axis, dim in sides:
        count = lax.axis_size(axis)
        ends = count - 1
        head = lax.slice_in_dim(cells, 0, width, axis=dim)
        tail = lax.slice_in_dim(cells, cells.shape[dim] - width, cells.shape[dim], axis=dim)
        cells = jnp.concatenate(
            [
                lax.ppermute(tail, axis, [(i, (i + 1) % count) for i in range(ends)]),
                cells,
                lax.ppermute(head, axis, [((i + 1) % count, i) for i in range(ends)]),
            ],
            axis=dim,
        )
    return cells


def layer_norm(values, gain_row, bias_row):
    centre = jnp.mean(values, axis=-1, keepdims=True)
    offset = values - centre
    spread = jnp.mean(offset * offset, axis=-1, keepdims=True)
    return offset * lax.rsqrt(spread + norm_eps) * gain_row + bias_row


def tanh_gelu(values):
    return jax.nn.gelu(values, approximate=True)


def fetch_dense(qkv_weight, out_weight, router_weight, norm_gains, norm_biases):
    rows, experts = router_weight.shape
    small = jnp.concatenate([router_weight, norm_gains.T, norm_biases.T], axis=1)
    small = jnp.pad(small, ((0, 0), (0, D - experts - 4)))
    packed = jnp.concatenate([qkv_weight, out_weight[None], small[None]], axis=0)
    full = lax.all_gather(packed, ("dp", "expert"), axis=1, tiled=True)
    return (
        full[:3],
        full[3],
        full[4][:, :experts],
        full[4][:, experts : experts + 2].T,
        full[4][:, experts + 2 : experts + 4].T,
    )


def fetch_experts(expert_in, expert_out):
    return (
        lax.all_gather(expert_in, "dp", axis=1, tiled=True),
        lax.all_gather(expert_out, "dp", axis=1, tiled=True),
    )


def plan_routes(route_ids, shard_experts):
    row_count = route_ids.shape[0]
    experts = shard_experts * lax.axis_size("expert")
    devices = lax.axis_size(("dp", "expert"))
    slot_count = 2 * TOP * row_count // experts
    capacity = 5 * TOP * row_count * devices // (4 * experts)
    labels = lax.broadcasted_iota(jnp.int32, (1, experts), 1)
    first_hot = (route_ids[:, 0:1] == labels).astype(jnp.int32)
    second_hot = (route_ids[:, 1:2] == labels).astype(jnp.int32)
    counts = jnp.stack([jnp.sum(first_hot, axis=0), jnp.sum(second_hot, axis=0)])
    all_counts = lax.all_gather(counts[None], ("dp", "expert"), axis=0, tiled=True)
    earlier = (
        lax.broadcasted_iota(jnp.int32, (devices, 1, 1), 0) < lax.axis_index(("dp", "expert"))
    ).astype(jnp.int32)
    before = jnp.sum(all_counts * earlier, axis=0)
    total_first = jnp.sum(all_counts[:, 0, :], axis=0)
    row_before = (
        lax.broadcasted_iota(jnp.int32, (row_count, row_count), 0)
        > lax.broadcasted_iota(jnp.int32, (row_count, row_count), 1)
    ).astype(jnp.bfloat16)

    def rank_of(hot):
        ahead = jnp.dot(row_before, hot.astype(jnp.bfloat16), preferred_element_type=jnp.float32)
        return jnp.sum(ahead.astype(jnp.int32) * hot, axis=1)

    rank_first = rank_of(first_hot)
    rank_second = rank_of(second_hot)
    place_first = jnp.sum(first_hot * before[0][None, :], axis=1) + rank_first
    place_second = jnp.sum(second_hot * (total_first + before[1])[None, :], axis=1) + rank_second
    kept_mask = jnp.stack([place_first < capacity, place_second < capacity], axis=1)
    slot_second = jnp.sum(second_hot * counts[0][None, :], axis=1) + rank_second
    flat_index = jnp.stack(
        [route_ids[:, 0] * slot_count + rank_first, route_ids[:, 1] * slot_count + slot_second],
        axis=1,
    )
    target = jnp.where(kept_mask, flat_index, experts * slot_count)
    return (first_hot, second_hot, target, kept_mask.astype(jnp.float32))


def fill_slots(row_pairs, target, experts, slot_count):
    feature_count = row_pairs.shape[-1]
    buffer = jnp.zeros((experts * slot_count + 1, feature_count), row_pairs.dtype)
    buffer = buffer.at[target.reshape(-1)].set(row_pairs.reshape(-1, feature_count))
    return buffer[:-1].reshape(experts, 1, slot_count, feature_count)


def read_slots(returned, target):
    feature_count = returned.shape[-1]
    flat_table = jnp.concatenate(
        [returned.reshape(-1, feature_count), jnp.zeros((1, feature_count), returned.dtype)], axis=0
    )
    return flat_table[target]


def run_forward(tokens_f, ids_ext, route_plan, dense_set, expert_set):
    qkv_full, out_full, router_full, gain_pair, bias_pair = dense_set
    expert_up_weight, expert_down_weight = expert_set
    first_hot, second_hot, target, kept_mask = route_plan
    row_count = tokens_f.shape[0]
    rim_rows = IMG - 1
    score_scale = 1.0 / math.sqrt(HEAD_DIM)
    experts = router_full.shape[1]
    slot_count = 2 * TOP * row_count // experts
    normed_one = layer_norm(
        tokens_f, gain_pair[0].astype(jnp.float32), bias_pair[0].astype(jnp.float32)
    ).astype(jnp.bfloat16)
    projected = jnp.einsum(
        "rd,cde->cre", normed_one, qkv_full, preferred_element_type=jnp.float32
    ).astype(jnp.bfloat16)
    key_value = padded(projected[1:], ((("dp", "expert"), 1),), rim_rows)
    query_heads = projected[0].reshape(row_count, HEADS, HEAD_DIM)
    key_heads = key_value[0].reshape(-1, HEADS, HEAD_DIM)
    value_heads = key_value[1].reshape(-1, HEADS, HEAD_DIM)
    same_image = ids_ext[rim_rows : rim_rows + row_count][:, None] == ids_ext[None, :]
    scores = (
        jnp.einsum("qhd,khd->hqk", query_heads, key_heads, preferred_element_type=jnp.float32)
        * score_scale
    )
    scores = jnp.where(same_image[None], scores, neg_big)
    top_score = jnp.max(scores, axis=-1, keepdims=True)
    log_total = top_score + jnp.log(jnp.sum(jnp.exp(scores - top_score), axis=-1, keepdims=True))
    att_probs = jnp.exp(scores - log_total)
    att_low = att_probs.astype(jnp.bfloat16)
    mixed_rows = (
        jnp.einsum("hqk,khd->qhd", att_low, value_heads, preferred_element_type=jnp.float32)
        .reshape(row_count, D)
        .astype(jnp.bfloat16)
    )
    residual = tokens_f + jnp.dot(mixed_rows, out_full, preferred_element_type=jnp.float32)
    normed_two = layer_norm(
        residual, gain_pair[1].astype(jnp.float32), bias_pair[1].astype(jnp.float32)
    ).astype(jnp.bfloat16)
    router_probs = jax.nn.softmax(
        jnp.dot(normed_two, router_full, preferred_element_type=jnp.float32), axis=-1
    )
    picked = jnp.stack(
        [jnp.sum(first_hot * router_probs, axis=1), jnp.sum(second_hot * router_probs, axis=1)],
        axis=1,
    )
    gate_values = kept_mask * picked
    outgoing = fill_slots(
        jnp.broadcast_to(normed_two[:, None, :], (row_count, TOP, D)), target, experts, slot_count
    )
    arrived = lax.all_to_all(outgoing, "expert", split_axis=0, concat_axis=1, tiled=True)
    shard_experts = arrived.shape[0]
    collected_token_rows = arrived.reshape(shard_experts, -1, D)
    hidden_pre = jnp.einsum(
        "ycq,yqt->yct", collected_token_rows, expert_up_weight, preferred_element_type=jnp.float32
    )
    hidden_activation = tanh_gelu(hidden_pre).astype(jnp.bfloat16)
    produced = jnp.einsum(
        "nso,nop->nsp", hidden_activation, expert_down_weight, preferred_element_type=jnp.float32
    ).astype(jnp.bfloat16)
    returned = lax.all_to_all(
        produced.reshape(arrived.shape), "expert", split_axis=1, concat_axis=0, tiled=True
    )
    expert_rows = read_slots(returned, target)
    block_value = residual + jnp.sum(
        gate_values[:, :, None] * expert_rows.astype(jnp.float32), axis=1
    )
    return (
        normed_one,
        query_heads,
        key_heads,
        value_heads,
        att_probs,
        att_low,
        mixed_rows,
        residual,
        normed_two,
        router_probs,
        gate_values,
        collected_token_rows,
        hidden_pre,
        hidden_activation,
        expert_rows,
        block_value,
    )


def run_backward(tokens_f, ids_ext, route_plan, dense_set, expert_set, upstream, gradients):
    qkv_full, out_full, router_full, gain_pair, bias_pair = dense_set
    expert_up_weight, expert_down_weight = expert_set
    first_hot, second_hot, target, kept_mask = route_plan
    grad_qkv, grad_out, grad_router, grad_gains, grad_biases, grad_in, grad_expert_out = gradients
    (
        normed_one,
        query_heads,
        key_heads,
        value_heads,
        att_probs,
        att_low,
        mixed_rows,
        residual,
        normed_two,
        router_probs,
        gate_values,
        collected_token_rows,
        hidden_pre,
        hidden_activation,
        expert_rows,
        block_value,
    ) = run_forward(tokens_f, ids_ext, route_plan, dense_set, expert_set)
    row_count = tokens_f.shape[0]
    rim_rows = IMG - 1
    score_scale = 1.0 / math.sqrt(HEAD_DIM)
    experts = router_full.shape[1]
    slot_count = 2 * TOP * row_count // experts
    shard_experts = expert_up_weight.shape[0]
    d_gate = kept_mask * jnp.sum(upstream[:, None, :] * expert_rows.astype(jnp.float32), axis=-1)
    d_sent = (gate_values[:, :, None] * upstream[:, None, :]).astype(jnp.bfloat16)
    d_arrived = lax.all_to_all(
        fill_slots(d_sent, target, experts, slot_count),
        "expert",
        split_axis=0,
        concat_axis=1,
        tiled=True,
    )
    produced_rows_grad = d_arrived.reshape(shard_experts, -1, D)
    activation_grad = jnp.einsum(
        "tkw,tew->tke", produced_rows_grad, expert_down_weight, preferred_element_type=jnp.float32
    )
    grad_expert_out = grad_expert_out + jnp.einsum(
        "meq,mek->mqk", hidden_activation, produced_rows_grad, preferred_element_type=jnp.float32
    )
    gelu_value, gelu_back = jax.vjp(tanh_gelu, hidden_pre)
    preactivation_grad = gelu_back(activation_grad)[0].astype(jnp.bfloat16)
    grad_in = grad_in + jnp.einsum(
        "zjo,zjm->zom", collected_token_rows, preactivation_grad, preferred_element_type=jnp.float32
    )
    d_rows = jnp.einsum(
        "iht,imt->ihm", preactivation_grad, expert_up_weight, preferred_element_type=jnp.float32
    ).astype(jnp.bfloat16)
    d_back = lax.all_to_all(
        d_rows.reshape(d_arrived.shape), "expert", split_axis=1, concat_axis=0, tiled=True
    )
    d_normed_two = jnp.sum(
        kept_mask[:, :, None] * read_slots(d_back, target).astype(jnp.float32), axis=1
    )
    d_probs = first_hot * d_gate[:, 0:1] + second_hot * d_gate[:, 1:2]
    d_logits = router_probs * (d_probs - jnp.sum(router_probs * d_probs, axis=-1, keepdims=True))
    router_wide = router_full.astype(jnp.float32)
    d_normed_two = d_normed_two + jnp.dot(d_logits, router_wide.T, precision=highest)
    grad_router = grad_router + jnp.dot(
        normed_two.astype(jnp.float32).T, d_logits, precision=highest
    )
    norm_value, second_back = jax.vjp(
        layer_norm, residual, gain_pair[1].astype(jnp.float32), bias_pair[1].astype(jnp.float32)
    )
    d_resid_part, d_gain_two, d_bias_two = second_back(d_normed_two)
    d_resid = upstream + d_resid_part
    d_attn = d_resid.astype(jnp.bfloat16)
    grad_out = grad_out + jnp.einsum(
        "rd,re->de", mixed_rows, d_attn, preferred_element_type=jnp.float32
    )
    d_mixed = (
        jnp.einsum("re,de->rd", d_attn, out_full, preferred_element_type=jnp.float32)
        .astype(jnp.bfloat16)
        .reshape(row_count, HEADS, HEAD_DIM)
    )
    d_att = jnp.einsum("qhd,khd->hqk", d_mixed, value_heads, preferred_element_type=jnp.float32)
    d_scores = (att_probs * (d_att - jnp.sum(att_probs * d_att, axis=-1, keepdims=True))).astype(
        jnp.bfloat16
    )
    d_query = (
        (
            jnp.einsum("hqk,khd->qhd", d_scores, key_heads, preferred_element_type=jnp.float32)
            * score_scale
        )
        .astype(jnp.bfloat16)
        .reshape(row_count, D)
    )
    d_key = (
        jnp.einsum("hqk,qhd->khd", d_scores, query_heads, preferred_element_type=jnp.float32)
        * score_scale
    )
    d_value = jnp.einsum("hqk,qhd->khd", att_low, d_mixed, preferred_element_type=jnp.float32)
    d_pair = jnp.stack([d_key.reshape(-1, D), d_value.reshape(-1, D)])
    rim_grads = jnp.concatenate([d_pair[:, :rim_rows], d_pair[:, rim_rows + row_count :]], axis=1)
    beside_all = padded(rim_grads.astype(jnp.bfloat16), ((("dp", "expert"), 1),), rim_rows).astype(
        rim_grads.dtype
    )
    own_part = d_pair[:, rim_rows : rim_rows + row_count]
    from_below = jnp.pad(beside_all[:, :rim_rows], ((0, 0), (0, row_count - rim_rows), (0, 0)))
    from_above = jnp.pad(beside_all[:, 3 * rim_rows :], ((0, 0), (row_count - rim_rows, 0), (0, 0)))
    d_kv = (own_part + from_below + from_above).astype(jnp.bfloat16)
    d_projected = jnp.concatenate([d_query[None], d_kv], axis=0)
    grad_qkv = grad_qkv + jnp.einsum(
        "rd,cre->cde", normed_one, d_projected, preferred_element_type=jnp.float32
    )
    d_normed_one = jnp.einsum(
        "cre,cde->rd", d_projected, qkv_full, preferred_element_type=jnp.float32
    )
    first_value, first_back = jax.vjp(
        layer_norm, tokens_f, gain_pair[0].astype(jnp.float32), bias_pair[0].astype(jnp.float32)
    )
    d_tokens_part, d_gain_one, d_bias_one = first_back(d_normed_one)
    grad_gains = grad_gains + jnp.stack([d_gain_one, d_gain_two])
    grad_biases = grad_biases + jnp.stack([d_bias_one, d_bias_two])
    input_rows = (d_resid + d_tokens_part).astype(jnp.bfloat16)
    return (
        input_rows,
        (grad_qkv, grad_out, grad_router, grad_gains, grad_biases, grad_in, grad_expert_out),
    )


def body(
    tokens,
    image_ids,
    routes,
    qkv_weight,
    out_weight,
    router_weight,
    norm_gains,
    norm_biases,
    expert_in,
    expert_out,
    cotangent,
):
    shard_experts = expert_in.shape[0]
    rim_rows = IMG - 1
    experts = shard_experts * lax.axis_size("expert")
    outputs = []
    saved_state = []
    for batch_index in range(MICRO):
        dense_set = fetch_dense(qkv_weight, out_weight, router_weight, norm_gains, norm_biases)
        expert_set = fetch_experts(expert_in, expert_out)
        ids_ext = padded(image_ids[batch_index] + 1, ((("dp", "expert"), 0),), rim_rows)
        route_plan = plan_routes(routes[batch_index], shard_experts)
        forward_state = run_forward(
            tokens[batch_index].astype(jnp.float32), ids_ext, route_plan, dense_set, expert_set
        )
        outputs.append(forward_state[-1].astype(jnp.bfloat16))
        saved_state.append((ids_ext, route_plan))
    gradients = (
        jnp.zeros((3, D, D), jnp.float32),
        jnp.zeros((D, D), jnp.float32),
        jnp.zeros((D, experts), jnp.float32),
        jnp.zeros((2, D), jnp.float32),
        jnp.zeros((2, D), jnp.float32),
        jnp.zeros((shard_experts, D, FF), jnp.float32),
        jnp.zeros((shard_experts, FF, D), jnp.float32),
    )
    input_grads = []
    for batch_index in range(MICRO):
        dense_set = fetch_dense(qkv_weight, out_weight, router_weight, norm_gains, norm_biases)
        expert_set = fetch_experts(expert_in, expert_out)
        ids_ext, route_plan = saved_state[batch_index]
        input_rows, gradients = run_backward(
            tokens[batch_index].astype(jnp.float32),
            ids_ext,
            route_plan,
            dense_set,
            expert_set,
            cotangent[batch_index].astype(jnp.float32),
            gradients,
        )
        input_grads.append(input_rows)
    grad_qkv, grad_out, grad_router, grad_gains, grad_biases, grad_in, grad_expert_out = gradients
    small = jnp.concatenate([grad_router, grad_gains.T, grad_biases.T], axis=1)
    small = jnp.pad(small, ((0, 0), (0, D - experts - 4)))
    packed = jnp.concatenate([grad_qkv, grad_out[None], small[None]], axis=0)
    packed = lax.psum_scatter(packed, ("dp", "expert"), scatter_dimension=1, tiled=True)
    dense_grads = (
        packed[:3],
        packed[3],
        packed[4][:, :experts],
        packed[4][:, experts : experts + 2].T,
        packed[4][:, experts + 2 : experts + 4].T,
    )
    expert_grads = (
        lax.psum_scatter(
            grad_in.astype(jnp.bfloat16), "dp", scatter_dimension=1, tiled=True
        ).astype(jnp.float32),
        lax.psum_scatter(
            grad_expert_out.astype(jnp.bfloat16), "dp", scatter_dimension=1, tiled=True
        ).astype(jnp.float32),
    )
    return (
        jnp.stack(outputs),
        jnp.stack(input_grads),
        dense_grads[0],
        dense_grads[1],
        dense_grads[2],
        dense_grads[3],
        dense_grads[4],
        expert_grads[0],
        expert_grads[1],
    )


MESH = pl.DeviceIdType.MESH
f32, bf16 = jnp.float32, jnp.bfloat16
VMEM_BYTES = 62 << 20


def mm(a, b):
    return jnp.dot(a, b, preferred_element_type=f32)


def mm_nt(a, b):
    return lax.dot_general(a, b, (((1,), (1,)), ((), ())), preferred_element_type=f32)


def normed(values, gain_row, bias_row):
    centre = jnp.mean(values, axis=-1, keepdims=True)
    offset = values - centre
    spread = jnp.mean(offset * offset, axis=-1, keepdims=True)
    return offset * lax.rsqrt(spread + norm_eps) * gain_row + bias_row


class Wire:
    def __init__(self, send_sems, recv_sems, other):
        self.send_sems, self.recv_sems, self.other = send_sems, recv_sems, other
        self.used, self.sent = 0, {}

    def roles(self, count=1):
        self.used += count
        return self.used - count

    def copy(self, send_role, recv_role, src, dst, device):
        return pltpu.make_async_remote_copy(
            src_ref=src,
            dst_ref=dst,
            send_sem=self.send_sems.at[send_role],
            recv_sem=self.recv_sems.at[recv_role],
            device_id=device,
            device_id_type=MESH,
        )

    def send(self, role, src, dst, device, recv_role=None):
        self.copy(role, role if recv_role is None else recv_role, src, dst, device).start()

    def arrive(self, role, like):
        self.copy(role, role, like, like, self.other).wait_recv()

    def left(self, role, like):
        self.copy(role, role, like, like, self.other).wait_send()


class Place:
    def __init__(self, nd, ne):
        self.nd, self.ne = nd, ne
        self.d, self.z = lax.axis_index("dp"), lax.axis_index("expert")
        d, z = self.d, self.z
        self.c = lax.rem(d, 2)
        self.sib_d = d + 1 - 2 * self.c
        self.sib = (self.sib_d, z)
        self.idx = d * ne + z
        last = (z == ne - 1).astype(jnp.int32)
        first = (z == 0).astype(jnp.int32)
        self.next = (lax.rem(d + last, nd), lax.rem(z + 1, ne))
        self.prev = (lax.rem(d + nd - first, nd), lax.rem(z + ne - 1, ne))
        self.xn = d + 2 - 4 * lax.rem(d // 2, 2)
        self.yn = d + 4 - 8 * (d // 4)
        self.up = (d, jnp.minimum(z + 1, ne - 1))
        self.down = (d, jnp.maximum(z - 1, 0))

    def chip(self, k):
        return lax.rem(self.d + 2 * k, self.nd)

    def enter(self):
        bar = pltpu.get_barrier_semaphore()

        def greet(device):
            pl.semaphore_signal(bar, inc=1, device_id=device, device_id_type=MESH)

        for k in range(1, self.nd):
            greet((lax.rem(self.d + k, self.nd), self.z))
        for k in range(1, self.ne):
            zk = lax.rem(self.z + k, self.ne)
            greet((self.d, zk))
            greet((self.sib_d, zk))
        greet(self.next)
        greet(self.prev)
        pl.semaphore_wait(bar, self.nd - 1 + 2 * (self.ne - 1) + 2)


class Chain:
    def __init__(self, wire, me, full):
        self.wire, self.me, self.full = wire, me, full
        n = me.ne
        self.up, self.dn = wire.roles(n - 1), wire.roles(n - 1)
        self.su, self.sd, self.so = wire.roles(n - 1), wire.roles(n - 1), wire.roles()

    def at(self, z):
        return self.full.at[z * 2 + self.me.c]

    def own(self, src):
        m, n = self.me, self.me.ne

        @pl.when(m.z < n - 1)
        def _():
            self.wire.send(self.up, src, self.at(m.z), m.up)

        @pl.when(m.z > 0)
        def _():
            self.wire.send(self.dn, src, self.at(m.z), m.down)

        self.wire.send(self.so, src, self.at(m.z), m.sib)

    def pump(self, k):
        m, n, w = self.me, self.me.ne, self.wire

        @pl.when(m.z >= k + 1)
        def _():
            block = self.at(m.z - 1 - k)
            w.arrive(self.up + k, block)
            if k + 1 < n - 1:

                @pl.when(m.z < n - 1)
                def _():
                    w.send(self.up + k + 1, block, block, m.up)

            w.send(self.su + k, block, block, m.sib)

        @pl.when(m.z + k + 1 < n)
        def _():
            block = self.at(m.z + 1 + k)
            w.arrive(self.dn + k, block)
            if k + 1 < n - 1:

                @pl.when(m.z > 0)
                def _():
                    w.send(self.dn + k + 1, block, block, m.down)

            w.send(self.sd + k, block, block, m.sib)

    def near(self):
        self.wire.arrive(self.so, self.full.at[0])

    def finish(self, k):
        m, n, w, like = self.me, self.me.ne, self.wire, self.full.at[0]

        @pl.when(m.z >= k + 1)
        def _():
            w.arrive(self.su + k, like)

        @pl.when(m.z + k + 1 < n)
        def _():
            w.arrive(self.sd + k, like)

    def drain(self):
        m, n, w, like = self.me, self.me.ne, self.wire, self.full.at[0]
        w.left(self.so, like)
        for k in range(n - 1):

            @pl.when((m.z < n - 1) & (m.z >= k))
            def _():
                w.left(self.up + k, like)

            @pl.when((m.z > 0) & (m.z + k < n))
            def _():
                w.left(self.dn + k, like)

            @pl.when(m.z >= k + 1)
            def _():
                w.left(self.su + k, like)

            @pl.when(m.z + k + 1 < n)
            def _():
                w.left(self.sd + k, like)


def front_kernel(
    nd,
    ne,
    tok,
    ids,
    routes,
    qkv,
    outw,
    routw,
    gainw,
    biasw,
    win,
    wout,
    cot,
    o_din,
    o_y,
    o_dprobs,
    o_up,
    o_down,
    g_n2,
    g_probs,
    g_resid,
    g_mixed,
    o_qkv,
    g_lse,
    g_w,
    o_small,
    o_idr,
    s_src,
    s_all,
    hp,
    hn,
    ip,
    inx,
    gx,
    gd,
    wu,
    wd,
    rk_src,
    rk,
    bias,
    acts,
    grads,
    pm,
    xs,
    ds,
    deo,
    xt,
    dt,
    gt,
    acc_eo,
    ys,
    qo,
    cs,
    cr,
    ud,
    dgs,
    dg,
    stage,
    square,
    o_probs,
    o_resid,
    o_mixed,
    o_lse,
    w_all,
    give_sems,
    send_sems,
    recv_sems,
    local_sems,
):
    me = Place(nd, ne)
    d, z, c = me.d, me.z, me.c
    rows = tok.shape[1]
    share = qkv.shape[1]
    experts = 2 * ne
    halo = hp.shape[1]
    ext = 3 * rows
    slots = 4 * rows // experts
    capacity = 5 * TOP * rows * nd * ne // (4 * experts)
    e = 2 * z + c
    s_me = z * 2 + c
    wire = Wire(send_sems, recv_sems, me.sib)
    lane = lax.broadcasted_iota(jnp.int32, (1, 128), 1)

    me.enter()

    r_dz = wire.roles(3 * (ne - 1))
    mine = pl.ds(pl.multiple_of(me.idx * share, 16), share)
    for k in range(1, ne):
        dev = (d, lax.rem(z + k, ne))
        wire.send(r_dz + 3 * (k - 1), qkv, w_all.at[pl.ds(0, 3), mine], dev)
        wire.send(r_dz + 3 * (k - 1) + 1, outw, w_all.at[3, mine], dev)
    local = [
        pltpu.make_async_copy(qkv, w_all.at[pl.ds(0, 3), mine], local_sems.at[0]),
        pltpu.make_async_copy(outw, w_all.at[3, mine], local_sems.at[1]),
    ]
    for cp in local:
        cp.start()
    up_rows, down_rows = win.shape[1], wout.shape[1]

    def up_at(dd, n=1):
        return wu.at[pl.ds(pl.multiple_of(dd * up_rows, 16), n * up_rows)]

    def down_at(dd, n=1):
        return wd.at[pl.ds(pl.multiple_of(dd * down_rows, 16), n * down_rows)]

    own_w = [
        pltpu.make_async_copy(win.at[c], up_at(d), local_sems.at[5]),
        pltpu.make_async_copy(wout.at[c], down_at(d), local_sems.at[6]),
    ]
    for cp in own_w:
        cp.start()
    r_ux, r_dy, r_uy, r_dx2 = (wire.roles(2) for _ in range(4))
    r_uf, r_df, r_us, r_dsib = (wire.roles() for _ in range(4))
    for cc in range(2):
        wire.send(r_ux + cc, win.at[cc], up_at(d), (me.xn - c + cc, z), recv_role=r_ux + c)
        wire.send(r_dy + cc, wout.at[cc], down_at(d), (me.yn - c + cc, z), recv_role=r_dy + c)
    r_id = wire.roles(2)
    wire.send(r_id, ids, ip, me.next)
    wire.send(r_id + 1, ids, inx, me.prev)
    r_h = wire.roles(2 * MICRO)

    def send_halo(mb):
        wire.send(r_h + 2 * mb, tok.at[mb, pl.ds(rows - halo, halo)], hp.at[mb], me.next)
        wire.send(r_h + 2 * mb + 1, tok.at[mb, pl.ds(0, halo)], hn.at[mb], me.prev)

    send_halo(0)
    before_row = (
        lax.broadcasted_iota(jnp.int32, (rows, rows), 0)
        > lax.broadcasted_iota(jnp.int32, (rows, rows), 1)
    ).astype(bf16)
    square[...] = jnp.zeros_like(square)
    square[0:experts, 0:share] = routw[...].astype(f32)
    square[experts : experts + 2, 0:share] = gainw[...].astype(f32)
    square[experts + 2 : experts + 4, 0:share] = biasw[...].astype(f32)
    s_src[0:share, :] = square[...].T[0:share, :].astype(bf16)
    row128 = lax.broadcasted_iota(jnp.int32, (128, rows), 0)
    row16 = lax.broadcasted_iota(jnp.int32, (16, 128), 0)
    hots = []
    counts = jnp.zeros((16, 128), f32)
    for mb in range(MICRO):
        choice = routes[mb].astype(f32)
        wide = jnp.where(row128 == 0, choice[0:1], jnp.where(row128 == 1, choice[1:2], -1.0)).T
        pair = [(wide[:, k : k + 1] == lane.astype(f32)).astype(f32) for k in range(TOP)]
        hots.append(pair)
        for k in range(TOP):
            counts = jnp.where(row16 == mb * TOP + k, jnp.sum(pair[k], axis=0, keepdims=True), counts)
    s_src[share : share + 16, :] = counts.astype(bf16)

    for k in range(1, ne):
        wire.send(r_dz + 3 * (k - 1) + 2, s_src, s_all.at[me.idx], (d, lax.rem(z + k, ne)))
    s_all[me.idx] = s_src[...]
    g_d = [Chain(wire, me, gd.at[mb]) for mb in range(MICRO)]
    g_x = [Chain(wire, me, gx.at[mb]) for mb in range(MICRO)]
    own_d = [
        pltpu.make_async_copy(cot.at[mb], gd.at[mb, s_me], local_sems.at[3 + mb])
        for mb in range(MICRO)
    ]
    for cp in own_d:
        cp.start()

    for cp in local:
        cp.wait()
    for k in range(1, ne):
        wire.arrive(r_dz + 3 * (k - 1), qkv)
        wire.arrive(r_dz + 3 * (k - 1) + 1, outw)
        wire.arrive(r_dz + 3 * (k - 1) + 2, s_src)

    def column(dd):
        at = pl.ds(pl.multiple_of(dd * (ne * share), 16), ne * share)
        return w_all.at[:, at], s_all.at[pl.ds(dd * ne, ne)]

    chips = nd // 2
    r_dx = wire.roles(2 * (chips - 1))
    r_ds = wire.roles(2 * chips)
    blk, sblk = column(d)
    for k in range(1, chips):
        wire.send(r_dx + 2 * (k - 1), blk, blk, (me.chip(k), z))
        wire.send(r_dx + 2 * (k - 1) + 1, sblk, sblk, (me.chip(k), z))
    wire.send(r_ds, blk, blk, me.sib)
    wire.send(r_ds + 1, sblk, sblk, me.sib)
    send_halo(1)
    g_d[0].own(cot.at[0])
    wire.send(r_us, win.at[1 - c], up_at(d), me.sib)
    wire.send(r_dsib, wout.at[1 - c], down_at(d), me.sib)
    for k in range(1, chips):
        wire.arrive(r_dx + 2 * (k - 1), blk)
        wire.arrive(r_dx + 2 * (k - 1) + 1, sblk)
        b, sb = column(lax.rem(d + nd - 2 * k, nd))
        wire.send(r_ds + 2 * k, b, b, me.sib)
        wire.send(r_ds + 2 * k + 1, sb, sb, me.sib)
    for cc in range(2):
        wire.send(r_dx2 + cc, wout.at[cc], down_at(d), (me.xn - c + cc, z), recv_role=r_dx2 + c)
        wire.send(r_uy + cc, win.at[cc], up_at(d), (me.yn - c + cc, z), recv_role=r_uy + c)
        wire.arrive(r_ux + cc, win.at[0])
        wire.arrive(r_dy + cc, wout.at[0])
    wire.send(r_uf, up_at(me.xn - c, 2), up_at(me.xn - c, 2), (me.yn, z))
    wire.send(r_df, down_at(me.yn - c, 2), down_at(me.yn - c, 2), (me.xn, z))
    for k in range(chips):
        wire.arrive(r_ds + 2 * k, blk)
        wire.arrive(r_ds + 2 * k + 1, sblk)

    o_small[...] = s_all[:, 0:share, :].reshape(D, 128).astype(f32)
    s_rows = o_small[...].T
    all_counts = s_all[:, share : share + 16, :].astype(f32)
    ahead = lax.broadcasted_iota(jnp.int32, all_counts.shape, 0) < me.idx
    before = jnp.sum(jnp.where(ahead, all_counts, 0.0), axis=0)
    total = jnp.sum(all_counts, axis=0)
    gains = [s_rows[experts + k : experts + k + 1, :] for k in range(2)]
    biases = [s_rows[experts + 2 + k : experts + 3 + k, :] for k in range(2)]

    r_rk = wire.roles(2 * ne)

    def send_ranks():
        for mb in range(MICRO):
            one, two = hots[mb]
            rank_one = mm(before_row, one.astype(bf16))
            rank_two = mm(before_row, two.astype(bf16))
            b1, b2 = before[2 * mb : 2 * mb + 1], before[2 * mb + 1 : 2 * mb + 2]
            t1 = total[2 * mb : 2 * mb + 1]
            place_one = jnp.sum(one * (b1 + rank_one), axis=1, keepdims=True)
            place_two = jnp.sum(two * (t1 + b2 + rank_two), axis=1, keepdims=True)
            kept = one * (place_one < capacity).astype(f32) + two * (place_two < capacity).astype(
                f32
            )
            ranks = jnp.where(kept > 0.0, rank_one + rank_two, -1.0)
            rk_src[mb] = ranks.T[0:experts, :]
        for k in range(ne):
            zk = lax.rem(z + k, ne)
            if k > 0:
                wire.send(r_rk + 2 * k, rk_src, rk.at[s_me], (d, zk))
            wire.send(r_rk + 2 * k + 1, rk_src, rk.at[s_me], (me.sib_d, zk))
        rk[s_me] = rk_src[...]

    wire.arrive(r_id, ids)
    wire.arrive(r_id + 1, ids)
    pos = lax.broadcasted_iota(jnp.int32, (1, rows), 1)
    gap = rows - halo
    for mb in range(MICRO):
        here = ids[mb : mb + 1, :].astype(f32)
        below = jnp.where((pos >= gap) & (me.idx > 0), ip[mb : mb + 1, :].astype(f32), -1.0)
        above = jnp.where(
            (pos < halo) & (me.idx < nd * ne - 1), inx[mb : mb + 1, :].astype(f32), -1.0
        )
        o_idr[mb] = jnp.concatenate([below, here, above], axis=1)

    zero_gap = jnp.zeros((gap, D), bf16)
    acts[0:gap, 0:D] = zero_gap
    acts[ext - gap : ext, 0:D] = zero_gap
    scale = 1.0 / math.sqrt(HEAD_DIM)
    given = []

    def give(src, dst):
        given.append(pltpu.make_async_copy(src, dst, give_sems.at[len(given)]))
        given[-1].start()

    give(w_all, g_w)
    saves = [pltpu.make_async_copy(
            acts.at[pl.ds(0, ext), pl.ds(D, 3 * D)], o_qkv.at[mb], local_sems.at[7 + mb]
        )
        for mb in range(MICRO)]

    def attend(mb, hooks):
        wire.arrive(r_h + 2 * mb, hp.at[mb])
        wire.arrive(r_h + 2 * mb + 1, hn.at[mb])

        def put(value, start):
            acts[start : start + value.shape[0], 0:D] = normed(
                value.astype(f32), gains[0], biases[0]
            ).astype(bf16)

        put(hp[mb], gap)
        put(tok[mb], rows)
        put(hn[mb], 2 * rows)
        if mb > 0:
            saves[mb - 1].wait()
        for k in range(3):
            for r in range(3):
                part = slice(r * rows, (r + 1) * rows)
                acts[part, (k + 1) * D : (k + 2) * D] = mm(acts[part, 0:D], w_all[k]).astype(bf16)
        saves[mb].start()
        idr = o_idr[mb]
        idc = jnp.broadcast_to(idr[:, rows : 2 * rows], (128, rows)).T[:, 0:1]
        bias[...] = jnp.where(idc == idr, 0.0, neg_big)
        o_lse[mb] = jnp.zeros((rows, 128), f32)

        @pl.loop(0, HEADS // 2, unroll=True)
        def _(pair):
            at = pl.ds(pl.multiple_of(pair * 128, 128), 128)
            query, key, value = (
                acts[part, pl.ds(pl.multiple_of((k + 1) * D + pair * 128, 128), 128)]
                for k, part in enumerate((slice(rows, 2 * rows), slice(0, ext), slice(0, ext)))
            )
            mixed = jnp.zeros((rows, 128), f32)
            lse = o_lse[mb]
            for half in range(2):
                keep = (lane < 64) if half == 0 else (lane >= 64)
                q = jnp.where(keep, query, jnp.zeros_like(query))
                v = jnp.where(keep, value, jnp.zeros_like(value))
                s = mm_nt(q, key) * scale + bias[...]
                top = jnp.max(s, axis=-1, keepdims=True)
                p = jnp.exp(s - top)
                total_p = jnp.sum(p, axis=-1, keepdims=True)
                mixed = mixed + mm((p * (1.0 / total_p)).astype(bf16), v)
                lse = jnp.where(lane == 2 * pair + half, top + jnp.log(total_p), lse)
            o_lse[mb] = lse
            o_mixed[mb, :, at] = mixed.astype(bf16)
            for when, hook in hooks.items():
                pl.when(pair == when)(hook)

        resid = tok[mb].astype(f32) + mm(o_mixed[mb], w_all[3])
        o_resid[mb] = resid
        n2 = normed(resid, gains[1], biases[1]).astype(bf16)
        gx[mb, s_me] = n2
        g_x[mb].own(gx.at[mb, s_me])
        logits = mm(n2, o_small[...].astype(bf16))
        logits = jnp.where(lane < experts, logits, neg_big)
        p = jnp.exp(logits - jnp.max(logits, axis=-1, keepdims=True))
        o_probs[mb] = p / jnp.sum(p, axis=-1, keepdims=True)
        give(gx.at[mb, s_me], g_n2.at[mb])
        give(o_probs.at[mb], g_probs.at[mb])
        give(o_resid.at[mb], g_resid.at[mb])
        give(o_mixed.at[mb], g_mixed.at[mb])
        give(o_lse.at[mb], g_lse.at[mb])

    def later_halves():
        g_x[0].pump(0)
        g_d[1].own(cot.at[1])

    attend(0, {0: lambda: g_d[0].pump(0), 3: lambda: g_d[0].pump(1)})
    send_ranks()
    attend(1, {0: lambda: g_d[0].pump(2), 2: later_halves})
    g_x[0].pump(1)

    r_cx = wire.roles(2 * MICRO * ne)
    r_up = wire.roles(MICRO * ne)
    r_dn = wire.roles(MICRO * ne)
    r_dg = wire.roles(MICRO * 2 * ne)
    r_far = wire.roles()
    sub = lax.broadcasted_iota(jnp.int32, (slots, rows), 0).astype(f32)
    tile = 2 * slots
    chunk = 512
    like = qo.at[0, 0, 0]

    def target(i):
        swap = jnp.where(i < 2, 1 - i, i)
        return jnp.where(
            z == 0, i, jnp.where(z == 1, swap, jnp.where(z == 2, ne - 1 - swap, ne - 1 - i))
        )

    def pass_up(mb, to):
        wire.send(r_up + mb * ne + to, qo.at[mb, 0, to], ud.at[mb, to], me.up)

    def pass_down(mb, to):
        slot = jnp.where(z - 1 == to, ne, to)
        wire.send(r_dn + mb * ne + to, qo.at[mb, 0, to], ud.at[mb, slot], me.down)

    def settle(mb, zp):
        for t in range(2):
            wire.arrive(r_cx + (mb * 2 + t) * ne + zp, like)
            qo[mb, t, zp] = (qo[mb, t, zp].astype(f32) + cr[mb, t, zp].astype(f32)).astype(bf16)

        straight = (mb > 0) & (z + zp == ne - 1) & ((z == 0) | (zp == 0))

        @pl.when((z == 0) & (zp > 0) & jnp.logical_not(straight))
        def _():
            pass_up(mb, zp)

        @pl.when((z == ne - 1) & (zp < ne - 1) & jnp.logical_not(straight))
        def _():
            pass_down(mb, zp)

        @pl.when(straight)
        def _():
            wire.send(r_far, qo.at[1, 0, zp], ud.at[1, 1], (d, zp))

    def relay(mb, hop, to):
        @pl.when(z == hop)
        def _():
            wire.arrive(r_up + mb * ne + to, like)
            qo[mb, 0, to] = (qo[mb, 0, to].astype(f32) + ud[mb, to].astype(f32)).astype(bf16)
            pass_up(mb, to)

        @pl.when(z == ne - 1 - hop)
        def _():
            low = ne - 1 - to
            wire.arrive(r_dn + mb * ne + low, like)
            qo[mb, 0, low] = (qo[mb, 0, low].astype(f32) + ud[mb, low].astype(f32)).astype(bf16)
            pass_down(mb, low)

    def end_sums(mb):
        acc_eo[...] = qo[mb, 0, z].astype(f32)

        @pl.when(z > 0)
        def _():
            wire.arrive(r_up + mb * ne + z, like)
            acc_eo[...] += ud[mb, z].astype(f32)

        @pl.when(z < ne - 1)
        def _():
            wire.arrive(r_dn + mb * ne + z, like)
            acc_eo[...] += ud[mb, ne].astype(f32)

        if mb > 0:

            @pl.when((z == 0) | (z == ne - 1))
            def _():
                wire.arrive(r_far, like)
                acc_eo[...] += ud[mb, 1].astype(f32)

        o_din[mb] = acc_eo[...]

    def first_tile():
        for cp in own_w + own_d + saves[1:]:
            cp.wait()
        for cc in range(2):
            wire.arrive(r_uy + cc, win.at[0])
            wire.arrive(r_dx2 + cc, wout.at[0])
        wire.arrive(r_us, win.at[0])
        wire.arrive(r_dsib, wout.at[0])
        wire.arrive(r_uf, up_at(0, 2))
        wire.arrive(r_df, down_at(0, 2))
        for k in range(ne):
            if k > 0:
                wire.arrive(r_rk + 2 * k, rk_src)
            wire.arrive(r_rk + 2 * k + 1, rk_src)
        g_d[0].near()
        g_x[0].near()

    def both(mb, what, k):
        for g in (g_d[mb], g_x[mb]):
            getattr(g, what)(k)

    def tile_1():
        both(0, "finish", 0)
        g_x[0].pump(2)

    def tile_2():
        both(0, "finish", 1)

    def tile_3():
        both(0, "finish", 2)
        both(1, "pump", 0)

    def tile_4():
        g_d[1].near()
        g_x[1].near()

    def tile_5():
        both(1, "finish", 0)
        both(1, "pump", 1)
        relay(0, 1, 2)

    def tile_6():
        both(1, "finish", 1)
        both(1, "pump", 2)
        relay(0, 1, 3)

    def tile_7():
        both(1, "finish", 2)
        relay(0, 2, 3)

    before_tile = [first_tile, tile_1, tile_2, tile_3, tile_4, tile_5, tile_6, tile_7]

    @pl.loop(0, MICRO * ne)
    def _(i):
        mb = i // ne
        zp = target(lax.rem(i, ne))

        for when, hook in enumerate(before_tile):
            pl.when(i == when)(hook)

        for cc in range(2):
            s = zp * 2 + cc
            at = slice(cc * slots, (cc + 1) * slots)
            pick = (sub == rk[s, mb, pl.ds(e, 1), :]).astype(bf16)
            pm[cc] = pick
            xs[at, :] = mm(pick, gx[mb, s]).astype(bf16)
            ds[at, :] = mm(pick, gd[mb, s]).astype(bf16)
        x = xs[...]
        logits = mm(x, o_small[...].astype(bf16))
        logits = jnp.where(lane < experts, logits, neg_big)
        p = jnp.exp(logits - jnp.max(logits, axis=-1, keepdims=True))
        p = p / jnp.sum(p, axis=-1, keepdims=True)
        gate = jnp.sum(jnp.where(lane == e, p, 0.0), axis=-1, keepdims=True)
        gt[...] = jnp.broadcast_to(gate, (tile, 128))
        dy = (gate * ds[...].astype(f32)).astype(bf16)
        deo[...] = dy
        across = pl.ds(pl.multiple_of(i * tile, tile), tile)
        xt[:, across] = x.T
        dt[:, across] = dy.T

        @pl.loop(0, FF // 256, unroll=True)
        def _(f):
            at = pl.ds(pl.multiple_of(f * 256, 256), 256)
            pre = mm(xs[...], wu[:, at])
            d_act = mm_nt(deo[...], wd[at, :])
            sq = pre * pre
            k0 = math.sqrt(2.0 / math.pi)
            th = jnp.tanh(pre * (k0 + (k0 * 0.044715) * sq))
            half = 0.5 + 0.5 * th
            slope = half + (0.5 * pre) * (1.0 - th * th) * (k0 + (3.0 * k0 * 0.044715) * sq)
            acts[across, at] = (pre * half).astype(bf16)
            grads[across, at] = (slope * d_act).astype(bf16)

        @pl.when(i > 0)
        def _():
            settle((i - 1) // ne, target(lax.rem(i - 1 + ne, ne)))

        eo = mm(acts[across, :], wd[...]).astype(bf16).astype(f32)
        d_gate = jnp.sum(ds[...].astype(f32) * eo, axis=-1, keepdims=True)
        ys[0] = mm_nt(grads[across, :], wu[...]).astype(bf16)
        ys[1] = (gt[:, 0:1] * eo).astype(bf16)
        box = lax.rem(i, 2)

        @pl.when(i > 1)
        def _():
            old = i - 2
            for t in range(2):
                wire.left(r_cx + ((old // ne) * 2 + t) * ne + target(lax.rem(old, ne)), like)

        for own in range(2):
            cc = c if own else 1 - c
            back = pm[cc].T
            at = pl.ds(pl.multiple_of(cc * slots, slots), slots)
            for t in range(2):
                moved = mm(back, ys[t, at, :]).astype(bf16)
                if own:
                    qo[mb, t, zp] = moved
                else:
                    cs[box, t] = moved
        for t in range(2):
            role = r_cx + (mb * 2 + t) * ne + zp
            wire.send(role, cs.at[box, t], cr.at[mb, t, zp], me.sib)
        for cc in range(2):
            at = slice(cc * slots, (cc + 1) * slots)
            line = jnp.sum(pm[cc].astype(f32) * d_gate[at], axis=0, keepdims=True)
            to = zp * 2 + cc
            dgs[mb, to] = jnp.broadcast_to(line, (8, rows))

            @pl.when(to != s_me)
            def _():
                wire.send(
                    r_dg + mb * 2 * ne + to,
                    dgs.at[mb, to],
                    dg.at[mb, e],
                    (d - c + cc, zp),
                    recv_role=r_dg + mb * 2 * ne + s_me,
                )

            @pl.when(to == s_me)
            def _():
                dg[mb, e] = jnp.broadcast_to(line, (8, rows))

    settle(1, target(ne - 1))

    @pl.when(z == 1)
    def _():
        pass_up(1, ne - 1)

    @pl.when(z == ne - 2)
    def _():
        pass_down(1, 0)


    wide_at = [pl.ds(k * chunk, chunk) for k in range(FF // chunk)]
    outs = []
    hooks = {0: lambda: relay(1, 1, 2), 2: lambda: relay(1, 2, 3)}
    for f, at in enumerate(wide_at):
        for k, (left, right, to) in enumerate(((xt, grads, o_up), (dt, acts, o_down))):
            if f > 1:
                outs[2 * (f - 2) + k].wait()
            stage[f % 2, k] = mm(left[...], right[:, at]).astype(bf16)
            cp = pltpu.make_async_copy(stage.at[f % 2, k], to.at[:, at], local_sems.at[9 + 2 * f + k])
            cp.start()
            outs.append(cp)
        if f in hooks:
            hooks[f]()
    end_sums(0)
    give_y = [pltpu.make_async_copy(qo.at[mb, 1], o_y.at[mb], local_sems.at[mb]) for mb in range(MICRO)]
    for cp in give_y:
        cp.start()
    for mb in range(MICRO):
        for s in range(2 * ne):

            @pl.when(s != s_me)
            def _():
                wire.arrive(r_dg + mb * 2 * ne + s, dgs.at[0, 0])

        groups = []
        sub8 = lax.broadcasted_iota(jnp.int32, (8, rows), 0)
        for base in range(0, experts, 8):
            group = dg[mb, base]
            for j in range(1, 8):
                group = jnp.where(sub8 == j, dg[mb, base + j], group)
            groups.append(group)
        lines = jnp.concatenate(groups + [jnp.zeros((128 - experts, rows), f32)], axis=0)
        o_dprobs[mb] = lines.T
    end_sums(1)
    for cp in outs[-4:] + give_y + given:
        cp.wait()

    for k in range(1, ne):
        wire.left(r_dz + 3 * (k - 1), qkv)
        wire.left(r_dz + 3 * (k - 1) + 1, outw)
        wire.left(r_dz + 3 * (k - 1) + 2, s_src)
    wire.left(r_id, ids)
    wire.left(r_id + 1, ids)
    for k in range(2 * MICRO):
        wire.left(r_h + k, hp.at[0])
    for k in range(1, chips):
        wire.left(r_dx + 2 * (k - 1), blk)
        wire.left(r_dx + 2 * (k - 1) + 1, sblk)
    for k in range(chips):
        wire.left(r_ds + 2 * k, blk)
        wire.left(r_ds + 2 * k + 1, sblk)
    for cc in range(2):
        wire.left(r_ux + cc, win.at[0])
        wire.left(r_uy + cc, win.at[0])
        wire.left(r_dy + cc, wout.at[0])
        wire.left(r_dx2 + cc, wout.at[0])
    wire.left(r_us, win.at[0])
    wire.left(r_dsib, wout.at[0])
    wire.left(r_uf, up_at(0, 2))
    wire.left(r_df, down_at(0, 2))
    for k in range(ne):
        if k > 0:
            wire.left(r_rk + 2 * k, rk_src)
        wire.left(r_rk + 2 * k + 1, rk_src)
    for g in g_d + g_x:
        g.drain()
    for old in (MICRO * ne - 2, MICRO * ne - 1):
        for t in range(2):
            wire.left(r_cx + ((old // ne) * 2 + t) * ne + target(old % ne), like)
    @pl.when((z == 0) | (z == ne - 1))
    def _():
        wire.left(r_far, like)

    for mb in range(MICRO):
        for to in range(ne):
            lowest = 1 if mb > 0 and to == ne - 1 else 0
            highest = ne - 2 if mb > 0 and to == 0 else ne - 1

            @pl.when((z < to) & (z >= lowest))
            def _():
                wire.left(r_up + mb * ne + to, like)

            @pl.when((z > to) & (z <= highest))
            def _():
                wire.left(r_dn + mb * ne + to, like)

        for s in range(2 * ne):

            @pl.when(s != s_me)
            def _():
                wire.left(r_dg + mb * 2 * ne + s, dgs.at[0, 0])

    assert wire.used <= ROLES


ROLES = 192


def front(nd, ne, *args):
    tokens, qkv = args[0], args[3]
    rows, share = tokens.shape[1], qkv.shape[1]
    halo = -(-(IMG - 1) // 16) * 16
    experts = 2 * ne
    slots = 4 * rows // experts
    tile = 2 * slots
    every = MICRO * ne * tile
    shape = jax.ShapeDtypeStruct
    vmem, anywhere = pl.BlockSpec(memory_space=pltpu.VMEM), pl.BlockSpec(memory_space=pl.ANY)
    outs = (
        (vmem, (MICRO, rows, D), f32),
        (anywhere, (MICRO, ne, rows, D), bf16),
        (vmem, (MICRO, rows, 128), f32),
        (anywhere, (D, FF), bf16),
        (anywhere, (D, FF), bf16),
        (anywhere, (MICRO, rows, D), bf16),
        (anywhere, (MICRO, rows, 128), f32),
        (anywhere, (MICRO, rows, D), f32),
        (anywhere, (MICRO, rows, D), bf16),
        (anywhere, (MICRO, 3 * rows, 3 * D), bf16),
        (anywhere, (MICRO, rows, 128), f32),
        (anywhere, (4, D, D), bf16),
        (vmem, (D, 128), f32),
        (vmem, (MICRO, 1, 3 * rows), f32),
    )
    v = pltpu.VMEM
    return pl.pallas_call(
        functools.partial(front_kernel, nd, ne),
        out_shape=[shape(*o[1:]) for o in outs],
        in_specs=[vmem, vmem, vmem, anywhere, anywhere, vmem, vmem, vmem] + [anywhere] * 3,
        out_specs=[o[0] for o in outs],
        scratch_shapes=[
            v((share + 16, 128), bf16),
            v((nd * ne, share + 16, 128), bf16),
            v((MICRO, halo, D), bf16),
            v((MICRO, halo, D), bf16),
            v((MICRO, rows), jnp.int32),
            v((MICRO, rows), jnp.int32),
            v((MICRO, 2 * ne, rows, D), bf16),
            v((MICRO, 2 * ne, rows, D), bf16),
            v((D, FF), bf16),
            v((FF, D), bf16),
            v((MICRO, experts, rows), f32),
            v((2 * ne, MICRO, experts, rows), f32),
            v((rows, 3 * rows), f32),
            v((every, FF), bf16),
            v((every, FF), bf16),
            v((2, slots, rows), bf16),
            v((tile, D), bf16),
            v((tile, D), bf16),
            v((tile, D), bf16),
            v((D, every), bf16),
            v((D, every), bf16),
            v((tile, 128), f32),
            v((rows, D), f32),
            v((2, tile, D), bf16),
            v((MICRO, 2, ne, rows, D), bf16),
            v((2, 2, rows, D), bf16),
            v((MICRO, 2, ne, rows, D), bf16),
            v((MICRO, ne + 1, rows, D), bf16),
            v((MICRO, 2 * ne, 8, rows), f32),
            v((MICRO, experts, 8, rows), f32),
            v((2, 2, D, 512), bf16),
            v((128, 128), f32),
            v((MICRO, rows, 128), f32),
            v((MICRO, rows, D), f32),
            v((MICRO, rows, D), bf16),
            v((MICRO, rows, 128), f32),
            v((4, D, D), bf16),
            pltpu.SemaphoreType.DMA((16,)),
            pltpu.SemaphoreType.DMA((ROLES,)),
            pltpu.SemaphoreType.DMA((ROLES,)),
            pltpu.SemaphoreType.DMA((17,)),
        ],
        compiler_params=pltpu.CompilerParams(
            collective_id=0, has_side_effects=True, vmem_limit_bytes=VMEM_BYTES
        ),
        name="front",
    )(*args)


def mm_exact(a, b):
    return jnp.dot(a, b, preferred_element_type=f32, precision=highest)


def back_kernel(
    nd,
    ne,
    tok,
    cot,
    d_in,
    y,
    d_probs,
    up,
    down,
    n2,
    probs,
    resid,
    mixed,
    qkv_in,
    lse,
    w_in,
    small,
    idr,
    o_block,
    o_input,
    o_dense,
    o_small,
    o_up,
    o_down,
    yq,
    yu,
    gu,
    gd,
    d_res,
    dm,
    stat_src,
    stat_p,
    stat_n,
    hp,
    hn,
    stats,
    bias,
    dp,
    gw,
    gs,
    gwb,
    gsb,
    rc,
    rcs,
    sx,
    sxs,
    rx,
    rxs,
    sz,
    szs,
    rz,
    rzs,
    block,
    qkv,
    w,
    send_sems,
    recv_sems,
    local_sems,
):
    me = Place(nd, ne)
    d, z, c = me.d, me.z, me.c
    rows = tok.shape[1]
    experts = 2 * ne
    halo = hp.shape[1]
    gap = rows - halo
    chips = nd // 2
    wire = Wire(send_sems, recv_sems, me.sib)
    lane = lax.broadcasted_iota(jnp.int32, (1, 128), 1)
    up_rows, down_rows = gu.shape[1], gd.shape[2]
    part = D // nd
    share = part // ne
    me.enter()

    r_g = wire.roles(2 * (nd - 1))

    def up_of(dd):
        return up.at[pl.ds(pl.multiple_of(dd * up_rows, 16), up_rows)]

    def down_of(dd):
        return down.at[:, pl.ds(pl.multiple_of(dd * down_rows, 128), down_rows)]

    own_g = [
        pltpu.make_async_copy(up_of(d), gu.at[d], local_sems.at[0]),
        pltpu.make_async_copy(down_of(d), gd.at[d], local_sems.at[1]),
    ]
    for cp in own_g:
        cp.start()
    for k in range(1, nd):
        dd = lax.rem(d + k, nd)
        wire.send(r_g + 2 * (k - 1), up_of(dd), gu.at[d], (dd, z))
        wire.send(r_g + 2 * (k - 1) + 1, down_of(dd), gd.at[d], (dd, z))

    fetches = [
        pltpu.make_async_copy(w_in.at[3], w.at[3], local_sems.at[2]),
        pltpu.make_async_copy(qkv_in.at[0], qkv.at[0], local_sems.at[3]),
        pltpu.make_async_copy(qkv_in.at[1], qkv.at[1], local_sems.at[4]),
        pltpu.make_async_copy(w_in.at[pl.ds(0, 3)], w.at[pl.ds(0, 3)], local_sems.at[5]),
        pltpu.make_async_copy(y.at[0, z], yq.at[0], local_sems.at[6]),
        pltpu.make_async_copy(y.at[1, z], yq.at[1], local_sems.at[7]),
    ]
    for cp in fetches:
        cp.start()
    r_y = wire.roles(MICRO * ne)
    like = yq.at[0]

    def send_y(mb):
        for k in range(1, ne):
            to = lax.rem(z + k, ne)
            wire.send(r_y + mb * ne + k, y.at[mb, to], yu.at[mb, k], (d, to))

    def end_sums(mb):
        block[...] = resid[mb] + yq[mb].astype(f32)
        for k in range(1, ne):
            wire.arrive(r_y + mb * ne + k, like)
            block[...] += yu[mb, k].astype(f32)
        o_block[mb] = block[...].astype(bf16)

    s_rows = small[...].T
    gains = [s_rows[experts + k : experts + k + 1, :] for k in range(2)]
    router = jnp.where(lane < experts, small[...], 0.0)
    head_of = (
        lax.broadcasted_iota(jnp.int32, (D, 128), 0) // HEAD_DIM
        == lax.broadcasted_iota(jnp.int32, (D, 128), 1)
    ).astype(f32)

    def norm_back(values, dn, gain):
        offset = values - jnp.mean(values, axis=-1, keepdims=True)
        inv = lax.rsqrt(jnp.mean(offset * offset, axis=-1, keepdims=True) + norm_eps)
        hat = offset * inv
        q = dn * gain
        dv = inv * (
            q
            - jnp.mean(q, axis=-1, keepdims=True)
            - hat * jnp.mean(q * hat, axis=-1, keepdims=True)
        )
        return dv, jnp.sum(dn * hat, axis=0, keepdims=True), jnp.sum(dn, axis=0, keepdims=True)

    r_h = wire.roles(4 * MICRO)
    norm_sums = [jnp.zeros((1, D), f32) for _ in range(4)]
    zero_gap = jnp.zeros((gap, D), bf16)
    own = slice(rows, 2 * rows)
    for mb in range(MICRO):
        prob, dpr = probs[mb], d_probs[mb]
        d_logits = prob * (dpr - jnp.sum(prob * dpr, axis=-1, keepdims=True))
        dn2 = d_in[mb] + lax.dot_general(
            d_logits,
            router,
            (((1,), (1,)), ((), ())),
            preferred_element_type=f32,
            precision=highest,
        )
        dv, d_gain, d_bias = norm_back(resid[mb], dn2, gains[1])
        norm_sums[1] += d_gain
        norm_sums[3] += d_bias
        d_resid = cot[mb].astype(f32) + dv
        d_res[mb] = d_resid
        d_attn = d_resid.astype(bf16)
        if mb == 0:
            fetches[0].wait()
        d_mixed = mm_nt(d_attn, w[3]).astype(bf16)
        dm[mb, own, :] = d_mixed
        delta = mm_exact(d_mixed.astype(f32) * mixed[mb].astype(f32), head_of)
        stat_src[mb, 0] = lse[mb].T[0:HEADS, :]
        stat_src[mb, 1] = delta.T[0:HEADS, :]
        low, high = pl.ds(rows, halo), pl.ds(2 * rows - halo, halo)
        wire.send(r_h + 4 * mb, dm.at[mb, high], hp.at[mb], me.next)
        wire.send(r_h + 4 * mb + 1, stat_src.at[mb], stat_p.at[mb], me.next)
        wire.send(r_h + 4 * mb + 2, dm.at[mb, low], hn.at[mb], me.prev)
        wire.send(r_h + 4 * mb + 3, stat_src.at[mb], stat_n.at[mb], me.prev)
        g_out = mm(mixed[mb].T, d_attn)
        g_router = mm_exact(n2[mb].astype(f32).T, d_logits)
        if mb == 0:
            gw[3] = g_out
            gs[...] = g_router
        else:
            gw[3] += g_out
            gs[...] += g_router

    scale = 1.0 / math.sqrt(HEAD_DIM)
    for mb in range(MICRO):
        ids = idr[mb]
        fetches[1 + mb].wait()
        if mb == 0:
            fetches[3].wait()
        idc = jnp.broadcast_to(ids[:, own], (128, rows)).T[:, 0:1]
        bias[...] = jnp.where(idc == ids, 0.0, neg_big)
        dst = jnp.zeros((rows, 128), f32)
        delta_cols = jnp.concatenate(
            [stat_src[mb, 1], jnp.zeros((128 - HEADS, rows), f32)], axis=0
        ).T

        @pl.loop(0, HEADS // 2, unroll=True)
        def _(pair):
            at = pl.ds(pl.multiple_of(pair * 128, 128), 128)
            query, key, value = (
                qkv[mb, part, pl.ds(pl.multiple_of(k * D + pair * 128, 128), 128)]
                for k, part in enumerate((own, slice(None), slice(None)))
            )
            grad = dm[mb, own, at]
            dq = jnp.zeros((rows, 128), f32)
            for half in range(2):
                keep = (lane < 64) if half == 0 else (lane >= 64)
                h = 2 * pair + half
                q = jnp.where(keep, query, jnp.zeros_like(query))
                g = jnp.where(keep, grad, jnp.zeros_like(grad))
                k = jnp.where(keep, key, jnp.zeros_like(key))
                lse_col = jnp.sum(jnp.where(lane == h, lse[mb], 0.0), axis=1, keepdims=True)
                delta_col = jnp.sum(jnp.where(lane == h, delta_cols, 0.0), axis=1, keepdims=True)
                p = jnp.exp(mm_nt(q, key) * scale + bias[...] - lse_col)
                ds = (p * (mm_nt(g, value) - delta_col)).astype(bf16)
                dq = dq + mm(ds, k)
            dp[0, :, at] = (dq * scale).astype(bf16)

        wire.arrive(r_h + 4 * mb, hp.at[mb])
        wire.arrive(r_h + 4 * mb + 1, stat_src.at[mb])
        wire.arrive(r_h + 4 * mb + 2, hp.at[mb])
        wire.arrive(r_h + 4 * mb + 3, stat_src.at[mb])
        send_y(mb)
        dm[mb, 0:gap, :] = zero_gap
        dm[mb, gap:rows, :] = hp[mb]
        dm[mb, 2 * rows : 2 * rows + halo, :] = hn[mb]
        dm[mb, 2 * rows + halo : 3 * rows, :] = zero_gap
        for k in range(2):
            stats[k, :, 0:rows] = stat_p[mb, k]
            stats[k, :, own] = stat_src[mb, k]
            stats[k, :, 2 * rows : 3 * rows] = stat_n[mb, k]

        @pl.loop(0, HEADS // 2, unroll=True)
        def _(pair):
            at = pl.ds(pl.multiple_of(pair * 128, 128), 128)
            query, key, value = (
                qkv[mb, part, pl.ds(pl.multiple_of(k * D + pair * 128, 128), 128)]
                for k, part in enumerate((slice(None), own, own))
            )
            grad = dm[mb, :, at]
            dk = jnp.zeros((rows, 128), f32)
            dv = jnp.zeros((rows, 128), f32)
            for half in range(2):
                keep = (lane < 64) if half == 0 else (lane >= 64)
                h = 2 * pair + half
                q = jnp.where(keep, query, jnp.zeros_like(query))
                g = jnp.where(keep, grad, jnp.zeros_like(grad))
                k = jnp.where(keep, key, jnp.zeros_like(key))
                v = jnp.where(keep, value, jnp.zeros_like(value))
                p = jnp.exp(mm_nt(k, query) * scale + bias[...] - stats[0, pl.ds(h, 1), :])
                ds = (p * (mm_nt(v, grad) - stats[1, pl.ds(h, 1), :])).astype(bf16)
                dk = dk + mm(ds, q)
                dv = dv + mm(p.astype(bf16), g)
            dp[1, :, at] = (dk * scale).astype(bf16)
            dp[2, :, at] = dv.astype(bf16)

        token = tok[mb].astype(f32)
        n1t = normed(token, gains[0], s_rows[experts + 2 : experts + 3, :]).astype(bf16).T
        dn1 = jnp.zeros((rows, D), f32)
        for k in range(3):
            dn1 = dn1 + mm_nt(dp[k], w[k])
            g_part = mm(n1t, dp[k])
            if mb == 0:
                gw[k] = g_part
            else:
                gw[k] += g_part
        dv, d_gain, d_bias = norm_back(token, dn1, gains[0])
        norm_sums[0] += d_gain
        norm_sums[2] += d_bias
        o_input[mb] = (d_res[mb] + dv).astype(bf16)

    rows128 = lax.broadcasted_iota(jnp.int32, (128, D), 0)
    norm_rows = jnp.zeros((128, D), f32)
    for k in range(4):
        norm_rows = jnp.where(rows128 == experts + k, norm_sums[k], norm_rows)
    gs[...] = jnp.where(lane < experts, gs[...], norm_rows.T)

    def of(dd):
        return pl.ds(pl.multiple_of(dd * part, 16), part)

    r_c = wire.roles(2 * chips)
    r_x = wire.roles(2 * (chips - 1))
    r_z = wire.roles(2 * (ne - 1))
    for k in range(chips):
        dd = 2 * k + 1 - c
        for m in range(4):
            gwb[k, m] = gw[m, of(dd), :].astype(bf16)
        gsb[k] = gs[of(dd), :]
        wire.send(r_c + 2 * k, gwb.at[k], rc.at[k], me.sib)
        wire.send(r_c + 2 * k + 1, gsb.at[k], rcs.at[k], me.sib)
    for k in range(chips):
        wire.arrive(r_c + 2 * k, rc.at[k])
        wire.arrive(r_c + 2 * k + 1, rcs.at[k])
    my_chip = d // 2
    for k in range(1, chips):
        to = lax.rem(my_chip + k, chips)
        dd = 2 * to + c
        for m in range(4):
            sx[k, m] = (gw[m, of(dd), :] + rc[to, m].astype(f32)).astype(bf16)
        sxs[k] = gs[of(dd), :] + rcs[to]
        wire.send(r_x + 2 * (k - 1), sx.at[k], rx.at[k], (dd, z))
        wire.send(r_x + 2 * (k - 1) + 1, sxs.at[k], rxs.at[k], (dd, z))
    total = [gw[m, of(d), :] + rc[my_chip, m].astype(f32) for m in range(4)]
    total_s = gs[of(d), :] + rcs[my_chip]
    for k in range(1, chips):
        wire.arrive(r_x + 2 * (k - 1), rx.at[k])
        wire.arrive(r_x + 2 * (k - 1) + 1, rxs.at[k])
        total = [total[m] + rx[k, m].astype(f32) for m in range(4)]
        total_s = total_s + rxs[k]
    for m in range(4):
        gw[m, 0:part, :] = total[m]
    gs[0:part, :] = total_s
    for k in range(1, ne):
        to = lax.rem(z + k, ne)
        at = pl.ds(pl.multiple_of(to * share, 16), share)
        for m in range(4):
            sz[k, m] = gw[m, at, :].astype(bf16)
        szs[k] = gs[at, :]
        wire.send(r_z + 2 * (k - 1), sz.at[k], rz.at[k], (d, to))
        wire.send(r_z + 2 * (k - 1) + 1, szs.at[k], rzs.at[k], (d, to))

    for cp in own_g:
        cp.wait()
    for k in range(1, nd):
        wire.arrive(r_g + 2 * (k - 1), gu.at[0])
        wire.arrive(r_g + 2 * (k - 1) + 1, gd.at[0])
    for x in range(2):
        o_up[x] = sum(gu[2 * k + x].astype(f32) for k in range(chips))
        o_down[x] = sum(gd[2 * k + x].astype(f32) for k in range(chips)).T

    for cp in fetches[4:]:
        cp.wait()
    for mb in range(MICRO):
        end_sums(mb)
    at = pl.ds(pl.multiple_of(z * share, 16), share)
    for k in range(1, ne):
        wire.arrive(r_z + 2 * (k - 1), rz.at[k])
        wire.arrive(r_z + 2 * (k - 1) + 1, rzs.at[k])
    for m in range(4):
        o_dense[m] = gw[m, at, :] + sum(rz[k, m].astype(f32) for k in range(1, ne))
    o_small[...] = gs[at, :] + sum(rzs[k] for k in range(1, ne))

    for k in range(1, nd):
        wire.left(r_g + 2 * (k - 1), gu.at[0])
        wire.left(r_g + 2 * (k - 1) + 1, gd.at[0])
    for mb in range(MICRO):
        for k in range(1, ne):
            wire.left(r_y + mb * ne + k, like)
        for k in range(2):
            wire.left(r_h + 4 * mb + 2 * k, hp.at[0])
            wire.left(r_h + 4 * mb + 2 * k + 1, stat_src.at[0])
    for k in range(chips):
        wire.left(r_c + 2 * k, rc.at[0])
        wire.left(r_c + 2 * k + 1, rcs.at[0])
    for k in range(1, chips):
        wire.left(r_x + 2 * (k - 1), rx.at[0])
        wire.left(r_x + 2 * (k - 1) + 1, rxs.at[0])
    for k in range(1, ne):
        wire.left(r_z + 2 * (k - 1), rz.at[0])
        wire.left(r_z + 2 * (k - 1) + 1, rzs.at[0])
    assert wire.used <= BACK_ROLES


BACK_ROLES = 80


def back(nd, ne, *args):
    tokens = args[0]
    rows = tokens.shape[1]
    halo = -(-(IMG - 1) // 16) * 16
    chips = nd // 2
    part = D // nd
    share = part // ne
    shape = jax.ShapeDtypeStruct
    outs = (
        shape((MICRO, rows, D), bf16),
        shape((MICRO, rows, D), bf16),
        shape((4, share, D), f32),
        shape((share, 128), f32),
        shape((2, D // nd, FF), f32),
        shape((2, FF // nd, D), f32),
    )
    vmem, anywhere = pl.BlockSpec(memory_space=pltpu.VMEM), pl.BlockSpec(memory_space=pl.ANY)
    v = pltpu.VMEM
    return pl.pallas_call(
        functools.partial(back_kernel, nd, ne),
        out_shape=outs,
        in_specs=[anywhere if k in (3, 5, 6, 11, 13) else vmem for k in range(len(args))],
        out_specs=[vmem] * len(outs),
        scratch_shapes=[
            v((MICRO, rows, D), bf16),
            v((MICRO, ne, rows, D), bf16),
            v((nd, D // nd, FF), bf16),
            v((nd, D, FF // nd), bf16),
            v((MICRO, rows, D), f32),
            v((MICRO, 3 * rows, D), bf16),
            v((MICRO, 2, HEADS, rows), f32),
            v((MICRO, 2, HEADS, rows), f32),
            v((MICRO, 2, HEADS, rows), f32),
            v((MICRO, halo, D), bf16),
            v((MICRO, halo, D), bf16),
            v((2, HEADS, 3 * rows), f32),
            v((rows, 3 * rows), f32),
            v((3, rows, D), bf16),
            v((4, D, D), f32),
            v((D, 128), f32),
            v((chips, 4, part, D), bf16),
            v((chips, part, 128), f32),
            v((chips, 4, part, D), bf16),
            v((chips, part, 128), f32),
            v((chips, 4, part, D), bf16),
            v((chips, part, 128), f32),
            v((chips, 4, part, D), bf16),
            v((chips, part, 128), f32),
            v((ne, 4, share, D), bf16),
            v((ne, share, 128), f32),
            v((ne, 4, share, D), bf16),
            v((ne, share, 128), f32),
            v((rows, D), f32),
            v((MICRO, 3 * rows, 3 * D), bf16),
            v((4, D, D), bf16),
            pltpu.SemaphoreType.DMA((BACK_ROLES,)),
            pltpu.SemaphoreType.DMA((BACK_ROLES,)),
            pltpu.SemaphoreType.DMA((8,)),
        ],
        compiler_params=pltpu.CompilerParams(
            collective_id=1, has_side_effects=True, vmem_limit_bytes=VMEM_BYTES
        ),
        name="back",
    )(*args)


def finish_kernel(block, inputs, dense, small, up, down, *rest):
    o_block, o_input, o_qkv, o_out, o_router, o_gain, o_bias, o_up, o_down = rest[:9]
    bufs, in_sems, out_sems = rest[9:-2], rest[-2], rest[-1]
    moves = (
        (up, o_up),
        (down, o_down),
        (inputs, o_input),
        (block, o_block),
        (dense.at[pl.ds(0, 3)], o_qkv),
        (dense.at[3], o_out),
    )
    ins = [pltpu.make_async_copy(m[0], b, in_sems.at[k]) for k, (m, b) in enumerate(zip(moves, bufs))]
    outs = [pltpu.make_async_copy(b, m[1], out_sems.at[k]) for k, (m, b) in enumerate(zip(moves, bufs))]
    for cp in ins:
        cp.start()
    experts, share = o_router.shape
    turned = jnp.concatenate([small[...], jnp.zeros((128 - share, 128), f32)], axis=0).T
    o_router[...] = turned[0:experts, 0:share]
    o_gain[...] = turned[experts : experts + 2, 0:share]
    o_bias[...] = turned[experts + 2 : experts + 4, 0:share]
    for there, back_again in zip(ins, outs):
        there.wait()
        back_again.start()
    for cp in outs:
        cp.wait()


def finish(experts, *args):
    block, inputs, dense, small, up, down = args
    share = small.shape[0]
    vmem, anywhere = pl.BlockSpec(memory_space=pltpu.VMEM), pl.BlockSpec(memory_space=pl.ANY)
    shape = jax.ShapeDtypeStruct
    outs = (
        (anywhere, block),
        (anywhere, inputs),
        (anywhere, shape((3, share, D), f32)),
        (anywhere, shape((share, D), f32)),
        (vmem, shape((experts, share), f32)),
        (vmem, shape((2, share), f32)),
        (vmem, shape((2, share), f32)),
        (anywhere, up),
        (anywhere, down),
    )
    bufs = (up, down, inputs, block, outs[2][1], outs[3][1])
    return pl.pallas_call(
        finish_kernel,
        out_shape=[shape(o[1].shape, o[1].dtype) for o in outs],
        in_specs=[vmem if k == 3 else anywhere for k in range(len(args))],
        out_specs=[o[0] for o in outs],
        scratch_shapes=[
            *(pltpu.VMEM(b.shape, b.dtype) for b in bufs),
            pltpu.SemaphoreType.DMA((7,)),
            pltpu.SemaphoreType.DMA((7,)),
        ],
        name="finish",
    )(*args)


def kernel_body(
    nd,
    ne,
    tokens,
    image_ids,
    routes,
    qkv_weight,
    out_weight,
    router_weight,
    norm_gains,
    norm_biases,
    expert_in,
    expert_out,
    cotangent,
):
    experts = 2 * ne
    saved = front(
        nd,
        ne,
        tokens,
        image_ids,
        routes.transpose(0, 2, 1),
        qkv_weight,
        out_weight,
        router_weight.T,
        norm_gains,
        norm_biases,
        expert_in,
        expert_out,
        cotangent,
    )
    outs = finish(experts, *back(nd, ne, tokens, cotangent, *saved))
    return (*outs[:4], outs[4].T, *outs[5:])


def chosen_body(nd, ne, tokens, *rest):
    rows, experts = tokens.shape[1], 2 * ne
    whole = D % (16 * nd * ne) == 0 and nd % 2 == 0 and 8 * rows == experts * rows and rows % 128 == 0
    whole = whole and nd == 8 and ne == 4
    if whole and rest[-3].shape[0] == 2:
        return kernel_body(nd, ne, tokens, *rest)
    return body(tokens, *rest)


def solution(mesh):
    return jax.shard_map(
        functools.partial(chosen_body, mesh.shape["dp"], mesh.shape["expert"]),
        mesh=mesh,
        in_specs=(
            P(None, ("dp", "expert"), None),
            P(None, ("dp", "expert")),
            P(None, ("dp", "expert"), None),
            P(None, ("dp", "expert"), None),
            P(("dp", "expert"), None),
            P(("dp", "expert"), None),
            P(None, ("dp", "expert")),
            P(None, ("dp", "expert")),
            P("expert", "dp", None),
            P("expert", "dp", None),
            P(None, ("dp", "expert"), None),
        ),
        out_specs=(
            P(None, ("dp", "expert"), None),
            P(None, ("dp", "expert"), None),
            P(None, ("dp", "expert"), None),
            P(("dp", "expert"), None),
            P(("dp", "expert"), None),
            P(None, ("dp", "expert")),
            P(None, ("dp", "expert")),
            P("expert", "dp", None),
            P("expert", "dp", None),
        ),
        check_vma=False,
    )
```

```python
import functools
import math

import jax
import jax.numpy as jnp
from jax import lax
from jax.experimental import pallas as pl
from jax.experimental.pallas import tpu as pltpu
from jax.sharding import PartitionSpec as P

D = 512
HEADS = 8
HEAD_DIM = 64
FF = 2048
TOP = 2
IMG = 197
MICRO = 2


neg_big = -1e30
norm_eps = 1e-06
highest = lax.Precision.HIGHEST


def padded(cells, sides, width):
    for axis, dim in sides:
        count = lax.axis_size(axis)
        ends = count - 1
        head = lax.slice_in_dim(cells, 0, width, axis=dim)
        tail = lax.slice_in_dim(cells, cells.shape[dim] - width, cells.shape[dim], axis=dim)
        cells = jnp.concatenate(
            [
                lax.ppermute(tail, axis, [(i, (i + 1) % count) for i in range(ends)]),
                cells,
                lax.ppermute(head, axis, [((i + 1) % count, i) for i in range(ends)]),
            ],
            axis=dim,
        )
    return cells


def layer_norm(values, gain_row, bias_row):
    centre = jnp.mean(values, axis=-1, keepdims=True)
    offset = values - centre
    spread = jnp.mean(offset * offset, axis=-1, keepdims=True)
    return offset * lax.rsqrt(spread + norm_eps) * gain_row + bias_row


def tanh_gelu(values):
    return jax.nn.gelu(values, approximate=True)


def fetch_dense(qkv_weight, out_weight, router_weight, norm_gains, norm_biases):
    rows, experts = router_weight.shape
    small = jnp.concatenate([router_weight, norm_gains.T, norm_biases.T], axis=1)
    small = jnp.pad(small, ((0, 0), (0, D - experts - 4)))
    packed = jnp.concatenate([qkv_weight, out_weight[None], small[None]], axis=0)
    full = lax.all_gather(packed, ("dp", "expert"), axis=1, tiled=True)
    return (
        full[:3],
        full[3],
        full[4][:, :experts],
        full[4][:, experts : experts + 2].T,
        full[4][:, experts + 2 : experts + 4].T,
    )


def fetch_experts(expert_in, expert_out):
    return (
        lax.all_gather(expert_in, "dp", axis=1, tiled=True),
        lax.all_gather(expert_out, "dp", axis=1, tiled=True),
    )


def plan_routes(route_ids, shard_experts):
    row_count = route_ids.shape[0]
    experts = shard_experts * lax.axis_size("expert")
    devices = lax.axis_size(("dp", "expert"))
    slot_count = 2 * TOP * row_count // experts
    capacity = 5 * TOP * row_count * devices // (4 * experts)
    labels = lax.broadcasted_iota(jnp.int32, (1, experts), 1)
    first_hot = (route_ids[:, 0:1] == labels).astype(jnp.int32)
    second_hot = (route_ids[:, 1:2] == labels).astype(jnp.int32)
    counts = jnp.stack([jnp.sum(first_hot, axis=0), jnp.sum(second_hot, axis=0)])
    all_counts = lax.all_gather(counts[None], ("dp", "expert"), axis=0, tiled=True)
    earlier = (
        lax.broadcasted_iota(jnp.int32, (devices, 1, 1), 0) < lax.axis_index(("dp", "expert"))
    ).astype(jnp.int32)
    before = jnp.sum(all_counts * earlier, axis=0)
    total_first = jnp.sum(all_counts[:, 0, :], axis=0)
    row_before = (
        lax.broadcasted_iota(jnp.int32, (row_count, row_count), 0)
        > lax.broadcasted_iota(jnp.int32, (row_count, row_count), 1)
    ).astype(jnp.bfloat16)

    def rank_of(hot):
        ahead = jnp.dot(row_before, hot.astype(jnp.bfloat16), preferred_element_type=jnp.float32)
        return jnp.sum(ahead.astype(jnp.int32) * hot, axis=1)

    rank_first = rank_of(first_hot)
    rank_second = rank_of(second_hot)
    place_first = jnp.sum(first_hot * before[0][None, :], axis=1) + rank_first
    place_second = jnp.sum(second_hot * (total_first + before[1])[None, :], axis=1) + rank_second
    kept_mask = jnp.stack([place_first < capacity, place_second < capacity], axis=1)
    slot_second = jnp.sum(second_hot * counts[0][None, :], axis=1) + rank_second
    flat_index = jnp.stack(
        [route_ids[:, 0] * slot_count + rank_first, route_ids[:, 1] * slot_count + slot_second],
        axis=1,
    )
    target = jnp.where(kept_mask, flat_index, experts * slot_count)
    return (first_hot, second_hot, target, kept_mask.astype(jnp.float32))


def fill_slots(row_pairs, target, experts, slot_count):
    feature_count = row_pairs.shape[-1]
    buffer = jnp.zeros((experts * slot_count + 1, feature_count), row_pairs.dtype)
    buffer = buffer.at[target.reshape(-1)].set(row_pairs.reshape(-1, feature_count))
    return buffer[:-1].reshape(experts, 1, slot_count, feature_count)


def read_slots(returned, target):
    feature_count = returned.shape[-1]
    flat_table = jnp.concatenate(
        [returned.reshape(-1, feature_count), jnp.zeros((1, feature_count), returned.dtype)], axis=0
    )
    return flat_table[target]


def run_forward(tokens_f, ids_ext, route_plan, dense_set, expert_set):
    qkv_full, out_full, router_full, gain_pair, bias_pair = dense_set
    expert_up_weight, expert_down_weight = expert_set
    first_hot, second_hot, target, kept_mask = route_plan
    row_count = tokens_f.shape[0]
    rim_rows = IMG - 1
    score_scale = 1.0 / math.sqrt(HEAD_DIM)
    experts = router_full.shape[1]
    slot_count = 2 * TOP * row_count // experts
    normed_one = layer_norm(
        tokens_f, gain_pair[0].astype(jnp.float32), bias_pair[0].astype(jnp.float32)
    ).astype(jnp.bfloat16)
    projected = jnp.einsum(
        "rd,cde->cre", normed_one, qkv_full, preferred_element_type=jnp.float32
    ).astype(jnp.bfloat16)
    key_value = padded(projected[1:], ((("dp", "expert"), 1),), rim_rows)
    query_heads = projected[0].reshape(row_count, HEADS, HEAD_DIM)
    key_heads = key_value[0].reshape(-1, HEADS, HEAD_DIM)
    value_heads = key_value[1].reshape(-1, HEADS, HEAD_DIM)
    same_image = ids_ext[rim_rows : rim_rows + row_count][:, None] == ids_ext[None, :]
    scores = (
        jnp.einsum("qhd,khd->hqk", query_heads, key_heads, preferred_element_type=jnp.float32)
        * score_scale
    )
    scores = jnp.where(same_image[None], scores, neg_big)
    top_score = jnp.max(scores, axis=-1, keepdims=True)
    log_total = top_score + jnp.log(jnp.sum(jnp.exp(scores - top_score), axis=-1, keepdims=True))
    att_probs = jnp.exp(scores - log_total)
    att_low = att_probs.astype(jnp.bfloat16)
    mixed_rows = (
        jnp.einsum("hqk,khd->qhd", att_low, value_heads, preferred_element_type=jnp.float32)
        .reshape(row_count, D)
        .astype(jnp.bfloat16)
    )
    residual = tokens_f + jnp.dot(mixed_rows, out_full, preferred_element_type=jnp.float32)
    normed_two = layer_norm(
        residual, gain_pair[1].astype(jnp.float32), bias_pair[1].astype(jnp.float32)
    ).astype(jnp.bfloat16)
    router_probs = jax.nn.softmax(
        jnp.dot(normed_two, router_full, preferred_element_type=jnp.float32), axis=-1
    )
    picked = jnp.stack(
        [jnp.sum(first_hot * router_probs, axis=1), jnp.sum(second_hot * router_probs, axis=1)],
        axis=1,
    )
    gate_values = kept_mask * picked
    outgoing = fill_slots(
        jnp.broadcast_to(normed_two[:, None, :], (row_count, TOP, D)), target, experts, slot_count
    )
    arrived = lax.all_to_all(outgoing, "expert", split_axis=0, concat_axis=1, tiled=True)
    shard_experts = arrived.shape[0]
    collected_token_rows = arrived.reshape(shard_experts, -1, D)
    hidden_pre = jnp.einsum(
        "ycq,yqt->yct", collected_token_rows, expert_up_weight, preferred_element_type=jnp.float32
    )
    hidden_activation = tanh_gelu(hidden_pre).astype(jnp.bfloat16)
    produced = jnp.einsum(
        "nso,nop->nsp", hidden_activation, expert_down_weight, preferred_element_type=jnp.float32
    ).astype(jnp.bfloat16)
    returned = lax.all_to_all(
        produced.reshape(arrived.shape), "expert", split_axis=1, concat_axis=0, tiled=True
    )
    expert_rows = read_slots(returned, target)
    block_value = residual + jnp.sum(
        gate_values[:, :, None] * expert_rows.astype(jnp.float32), axis=1
    )
    return (
        normed_one,
        query_heads,
        key_heads,
        value_heads,
        att_probs,
        att_low,
        mixed_rows,
        residual,
        normed_two,
        router_probs,
        gate_values,
        collected_token_rows,
        hidden_pre,
        hidden_activation,
        expert_rows,
        block_value,
    )


def run_backward(tokens_f, ids_ext, route_plan, dense_set, expert_set, upstream, gradients):
    qkv_full, out_full, router_full, gain_pair, bias_pair = dense_set
    expert_up_weight, expert_down_weight = expert_set
    first_hot, second_hot, target, kept_mask = route_plan
    grad_qkv, grad_out, grad_router, grad_gains, grad_biases, grad_in, grad_expert_out = gradients
    (
        normed_one,
        query_heads,
        key_heads,
        value_heads,
        att_probs,
        att_low,
        mixed_rows,
        residual,
        normed_two,
        router_probs,
        gate_values,
        collected_token_rows,
        hidden_pre,
        hidden_activation,
        expert_rows,
        block_value,
    ) = run_forward(tokens_f, ids_ext, route_plan, dense_set, expert_set)
    row_count = tokens_f.shape[0]
    rim_rows = IMG - 1
    score_scale = 1.0 / math.sqrt(HEAD_DIM)
    experts = router_full.shape[1]
    slot_count = 2 * TOP * row_count // experts
    shard_experts = expert_up_weight.shape[0]
    d_gate = kept_mask * jnp.sum(upstream[:, None, :] * expert_rows.astype(jnp.float32), axis=-1)
    d_sent = (gate_values[:, :, None] * upstream[:, None, :]).astype(jnp.bfloat16)
    d_arrived = lax.all_to_all(
        fill_slots(d_sent, target, experts, slot_count),
        "expert",
        split_axis=0,
        concat_axis=1,
        tiled=True,
    )
    produced_rows_grad = d_arrived.reshape(shard_experts, -1, D)
    activation_grad = jnp.einsum(
        "tkw,tew->tke", produced_rows_grad, expert_down_weight, preferred_element_type=jnp.float32
    )
    grad_expert_out = grad_expert_out + jnp.einsum(
        "meq,mek->mqk", hidden_activation, produced_rows_grad, preferred_element_type=jnp.float32
    )
    gelu_value, gelu_back = jax.vjp(tanh_gelu, hidden_pre)
    preactivation_grad = gelu_back(activation_grad)[0].astype(jnp.bfloat16)
    grad_in = grad_in + jnp.einsum(
        "zjo,zjm->zom", collected_token_rows, preactivation_grad, preferred_element_type=jnp.float32
    )
    d_rows = jnp.einsum(
        "iht,imt->ihm", preactivation_grad, expert_up_weight, preferred_element_type=jnp.float32
    ).astype(jnp.bfloat16)
    d_back = lax.all_to_all(
        d_rows.reshape(d_arrived.shape), "expert", split_axis=1, concat_axis=0, tiled=True
    )
    d_normed_two = jnp.sum(
        kept_mask[:, :, None] * read_slots(d_back, target).astype(jnp.float32), axis=1
    )
    d_probs = first_hot * d_gate[:, 0:1] + second_hot * d_gate[:, 1:2]
    d_logits = router_probs * (d_probs - jnp.sum(router_probs * d_probs, axis=-1, keepdims=True))
    router_wide = router_full.astype(jnp.float32)
    d_normed_two = d_normed_two + jnp.dot(d_logits, router_wide.T, precision=highest)
    grad_router = grad_router + jnp.dot(
        normed_two.astype(jnp.float32).T, d_logits, precision=highest
    )
    norm_value, second_back = jax.vjp(
        layer_norm, residual, gain_pair[1].astype(jnp.float32), bias_pair[1].astype(jnp.float32)
    )
    d_resid_part, d_gain_two, d_bias_two = second_back(d_normed_two)
    d_resid = upstream + d_resid_part
    d_attn = d_resid.astype(jnp.bfloat16)
    grad_out = grad_out + jnp.einsum(
        "rd,re->de", mixed_rows, d_attn, preferred_element_type=jnp.float32
    )
    d_mixed = (
        jnp.einsum("re,de->rd", d_attn, out_full, preferred_element_type=jnp.float32)
        .astype(jnp.bfloat16)
        .reshape(row_count, HEADS, HEAD_DIM)
    )
    d_att = jnp.einsum("qhd,khd->hqk", d_mixed, value_heads, preferred_element_type=jnp.float32)
    d_scores = (att_probs * (d_att - jnp.sum(att_probs * d_att, axis=-1, keepdims=True))).astype(
        jnp.bfloat16
    )
    d_query = (
        (
            jnp.einsum("hqk,khd->qhd", d_scores, key_heads, preferred_element_type=jnp.float32)
            * score_scale
        )
        .astype(jnp.bfloat16)
        .reshape(row_count, D)
    )
    d_key = (
        jnp.einsum("hqk,qhd->khd", d_scores, query_heads, preferred_element_type=jnp.float32)
        * score_scale
    )
    d_value = jnp.einsum("hqk,qhd->khd", att_low, d_mixed, preferred_element_type=jnp.float32)
    d_pair = jnp.stack([d_key.reshape(-1, D), d_value.reshape(-1, D)])
    rim_grads = jnp.concatenate([d_pair[:, :rim_rows], d_pair[:, rim_rows + row_count :]], axis=1)
    beside_all = padded(rim_grads.astype(jnp.bfloat16), ((("dp", "expert"), 1),), rim_rows).astype(
        rim_grads.dtype
    )
    own_part = d_pair[:, rim_rows : rim_rows + row_count]
    from_below = jnp.pad(beside_all[:, :rim_rows], ((0, 0), (0, row_count - rim_rows), (0, 0)))
    from_above = jnp.pad(beside_all[:, 3 * rim_rows :], ((0, 0), (row_count - rim_rows, 0), (0, 0)))
    d_kv = (own_part + from_below + from_above).astype(jnp.bfloat16)
    d_projected = jnp.concatenate([d_query[None], d_kv], axis=0)
    grad_qkv = grad_qkv + jnp.einsum(
        "rd,cre->cde", normed_one, d_projected, preferred_element_type=jnp.float32
    )
    d_normed_one = jnp.einsum(
        "cre,cde->rd", d_projected, qkv_full, preferred_element_type=jnp.float32
    )
    first_value, first_back = jax.vjp(
        layer_norm, tokens_f, gain_pair[0].astype(jnp.float32), bias_pair[0].astype(jnp.float32)
    )
    d_tokens_part, d_gain_one, d_bias_one = first_back(d_normed_one)
    grad_gains = grad_gains + jnp.stack([d_gain_one, d_gain_two])
    grad_biases = grad_biases + jnp.stack([d_bias_one, d_bias_two])
    input_rows = (d_resid + d_tokens_part).astype(jnp.bfloat16)
    return (
        input_rows,
        (grad_qkv, grad_out, grad_router, grad_gains, grad_biases, grad_in, grad_expert_out),
    )


def body(
    tokens,
    image_ids,
    routes,
    qkv_weight,
    out_weight,
    router_weight,
    norm_gains,
    norm_biases,
    expert_in,
    expert_out,
    cotangent,
):
    shard_experts = expert_in.shape[0]
    rim_rows = IMG - 1
    experts = shard_experts * lax.axis_size("expert")
    outputs = []
    saved_state = []
    for batch_index in range(MICRO):
        dense_set = fetch_dense(qkv_weight, out_weight, router_weight, norm_gains, norm_biases)
        expert_set = fetch_experts(expert_in, expert_out)
        ids_ext = padded(image_ids[batch_index] + 1, ((("dp", "expert"), 0),), rim_rows)
        route_plan = plan_routes(routes[batch_index], shard_experts)
        forward_state = run_forward(
            tokens[batch_index].astype(jnp.float32), ids_ext, route_plan, dense_set, expert_set
        )
        outputs.append(forward_state[-1].astype(jnp.bfloat16))
        saved_state.append((ids_ext, route_plan))
    gradients = (
        jnp.zeros((3, D, D), jnp.float32),
        jnp.zeros((D, D), jnp.float32),
        jnp.zeros((D, experts), jnp.float32),
        jnp.zeros((2, D), jnp.float32),
        jnp.zeros((2, D), jnp.float32),
        jnp.zeros((shard_experts, D, FF), jnp.float32),
        jnp.zeros((shard_experts, FF, D), jnp.float32),
    )
    input_grads = []
    for batch_index in range(MICRO):
        dense_set = fetch_dense(qkv_weight, out_weight, router_weight, norm_gains, norm_biases)
        expert_set = fetch_experts(expert_in, expert_out)
        ids_ext, route_plan = saved_state[batch_index]
        input_rows, gradients = run_backward(
            tokens[batch_index].astype(jnp.float32),
            ids_ext,
            route_plan,
            dense_set,
            expert_set,
            cotangent[batch_index].astype(jnp.float32),
            gradients,
        )
        input_grads.append(input_rows)
    grad_qkv, grad_out, grad_router, grad_gains, grad_biases, grad_in, grad_expert_out = gradients
    small = jnp.concatenate([grad_router, grad_gains.T, grad_biases.T], axis=1)
    small = jnp.pad(small, ((0, 0), (0, D - experts - 4)))
    packed = jnp.concatenate([grad_qkv, grad_out[None], small[None]], axis=0)
    packed = lax.psum_scatter(packed, ("dp", "expert"), scatter_dimension=1, tiled=True)
    dense_grads = (
        packed[:3],
        packed[3],
        packed[4][:, :experts],
        packed[4][:, experts : experts + 2].T,
        packed[4][:, experts + 2 : experts + 4].T,
    )
    expert_grads = (
        lax.psum_scatter(
            grad_in.astype(jnp.bfloat16), "dp", scatter_dimension=1, tiled=True
        ).astype(jnp.float32),
        lax.psum_scatter(
            grad_expert_out.astype(jnp.bfloat16), "dp", scatter_dimension=1, tiled=True
        ).astype(jnp.float32),
    )
    return (
        jnp.stack(outputs),
        jnp.stack(input_grads),
        dense_grads[0],
        dense_grads[1],
        dense_grads[2],
        dense_grads[3],
        dense_grads[4],
        expert_grads[0],
        expert_grads[1],
    )


MESH = pl.DeviceIdType.MESH
f32, bf16 = jnp.float32, jnp.bfloat16
VMEM_BYTES = 62 << 20


def mm(a, b):
    return jnp.dot(a, b, preferred_element_type=f32)


def mm_nt(a, b):
    return lax.dot_general(a, b, (((1,), (1,)), ((), ())), preferred_element_type=f32)


def normed(values, gain_row, bias_row):
    centre = jnp.mean(values, axis=-1, keepdims=True)
    offset = values - centre
    spread = jnp.mean(offset * offset, axis=-1, keepdims=True)
    return offset * lax.rsqrt(spread + norm_eps) * gain_row + bias_row


class Wire:
    def __init__(self, send_sems, recv_sems, other):
        self.send_sems, self.recv_sems, self.other = send_sems, recv_sems, other
        self.used, self.sent = 0, {}

    def roles(self, count=1):
        self.used += count
        return self.used - count

    def copy(self, send_role, recv_role, src, dst, device):
        return pltpu.make_async_remote_copy(
            src_ref=src,
            dst_ref=dst,
            send_sem=self.send_sems.at[send_role],
            recv_sem=self.recv_sems.at[recv_role],
            device_id=device,
            device_id_type=MESH,
        )

    def send(self, role, src, dst, device, recv_role=None):
        self.copy(role, role if recv_role is None else recv_role, src, dst, device).start()

    def arrive(self, role, like):
        self.copy(role, role, like, like, self.other).wait_recv()

    def left(self, role, like):
        self.copy(role, role, like, like, self.other).wait_send()


class Place:
    def __init__(self, nd, ne):
        self.nd, self.ne = nd, ne
        self.d, self.z = lax.axis_index("dp"), lax.axis_index("expert")
        d, z = self.d, self.z
        self.c = lax.rem(d, 2)
        self.sib_d = d + 1 - 2 * self.c
        self.sib = (self.sib_d, z)
        self.idx = d * ne + z
        last = (z == ne - 1).astype(jnp.int32)
        first = (z == 0).astype(jnp.int32)
        self.next = (lax.rem(d + last, nd), lax.rem(z + 1, ne))
        self.prev = (lax.rem(d + nd - first, nd), lax.rem(z + ne - 1, ne))
        self.xn = d + 2 - 4 * lax.rem(d // 2, 2)
        self.yn = d + 4 - 8 * (d // 4)
        self.up = (d, jnp.minimum(z + 1, ne - 1))
        self.down = (d, jnp.maximum(z - 1, 0))

    def chip(self, k):
        return lax.rem(self.d + 2 * k, self.nd)

    def enter(self):
        bar = pltpu.get_barrier_semaphore()

        def greet(device):
            pl.semaphore_signal(bar, inc=1, device_id=device, device_id_type=MESH)

        for k in range(1, self.nd):
            greet((lax.rem(self.d + k, self.nd), self.z))
        for k in range(1, self.ne):
            zk = lax.rem(self.z + k, self.ne)
            greet((self.d, zk))
            greet((self.sib_d, zk))
        greet(self.next)
        greet(self.prev)
        pl.semaphore_wait(bar, self.nd - 1 + 2 * (self.ne - 1) + 2)


class Chain:
    def __init__(self, wire, me, full):
        self.wire, self.me, self.full = wire, me, full
        n = me.ne
        self.up, self.dn = wire.roles(n - 1), wire.roles(n - 1)
        self.su, self.sd, self.so = wire.roles(n - 1), wire.roles(n - 1), wire.roles()

    def at(self, z):
        return self.full.at[z * 2 + self.me.c]

    def own(self, src):
        m, n = self.me, self.me.ne

        @pl.when(m.z < n - 1)
        def _():
            self.wire.send(self.up, src, self.at(m.z), m.up)

        @pl.when(m.z > 0)
        def _():
            self.wire.send(self.dn, src, self.at(m.z), m.down)

        self.wire.send(self.so, src, self.at(m.z), m.sib)

    def pump(self, k):
        m, n, w = self.me, self.me.ne, self.wire

        @pl.when(m.z >= k + 1)
        def _():
            block = self.at(m.z - 1 - k)
            w.arrive(self.up + k, block)
            if k + 1 < n - 1:

                @pl.when(m.z < n - 1)
                def _():
                    w.send(self.up + k + 1, block, block, m.up)

            w.send(self.su + k, block, block, m.sib)

        @pl.when(m.z + k + 1 < n)
        def _():
            block = self.at(m.z + 1 + k)
            w.arrive(self.dn + k, block)
            if k + 1 < n - 1:

                @pl.when(m.z > 0)
                def _():
                    w.send(self.dn + k + 1, block, block, m.down)

            w.send(self.sd + k, block, block, m.sib)

    def near(self):
        self.wire.arrive(self.so, self.full.at[0])

    def finish(self, k):
        m, n, w, like = self.me, self.me.ne, self.wire, self.full.at[0]

        @pl.when(m.z >= k + 1)
        def _():
            w.arrive(self.su + k, like)

        @pl.when(m.z + k + 1 < n)
        def _():
            w.arrive(self.sd + k, like)

    def drain(self):
        m, n, w, like = self.me, self.me.ne, self.wire, self.full.at[0]
        w.left(self.so, like)
        for k in range(n - 1):

            @pl.when((m.z < n - 1) & (m.z >= k))
            def _():
                w.left(self.up + k, like)

            @pl.when((m.z > 0) & (m.z + k < n))
            def _():
                w.left(self.dn + k, like)

            @pl.when(m.z >= k + 1)
            def _():
                w.left(self.su + k, like)

            @pl.when(m.z + k + 1 < n)
            def _():
                w.left(self.sd + k, like)


def front_kernel(
    nd,
    ne,
    tok,
    ids,
    routes,
    qkv,
    outw,
    routw,
    gainw,
    biasw,
    win,
    wout,
    cot,
    o_din,
    o_y,
    o_dprobs,
    o_up,
    o_down,
    g_n2,
    g_probs,
    g_resid,
    g_mixed,
    o_qkv,
    g_lse,
    g_w,
    o_small,
    o_idr,
    s_src,
    s_all,
    hp,
    hn,
    ip,
    inx,
    gx,
    gd,
    wu,
    wd,
    rk_src,
    rk,
    bias,
    acts,
    grads,
    pm,
    xs,
    ds,
    deo,
    xt,
    dt,
    gt,
    acc_eo,
    ys,
    qo,
    cs,
    cr,
    ud,
    dgs,
    dg,
    stage,
    square,
    o_probs,
    o_resid,
    o_mixed,
    o_lse,
    w_all,
    give_sems,
    send_sems,
    recv_sems,
    local_sems,
):
    me = Place(nd, ne)
    d, z, c = me.d, me.z, me.c
    rows = tok.shape[1]
    share = qkv.shape[1]
    experts = 2 * ne
    halo = hp.shape[1]
    ext = 3 * rows
    slots = 4 * rows // experts
    capacity = 5 * TOP * rows * nd * ne // (4 * experts)
    e = 2 * z + c
    s_me = z * 2 + c
    wire = Wire(send_sems, recv_sems, me.sib)
    lane = lax.broadcasted_iota(jnp.int32, (1, 128), 1)

    me.enter()

    r_dz = wire.roles(3 * (ne - 1))
    mine = pl.ds(pl.multiple_of(me.idx * share, 16), share)
    for k in range(1, ne):
        dev = (d, lax.rem(z + k, ne))
        wire.send(r_dz + 3 * (k - 1), qkv, w_all.at[pl.ds(0, 3), mine], dev)
        wire.send(r_dz + 3 * (k - 1) + 1, outw, w_all.at[3, mine], dev)
    local = [
        pltpu.make_async_copy(qkv, w_all.at[pl.ds(0, 3), mine], local_sems.at[0]),
        pltpu.make_async_copy(outw, w_all.at[3, mine], local_sems.at[1]),
    ]
    for cp in local:
        cp.start()
    up_rows, down_rows = win.shape[1], wout.shape[1]

    def up_at(dd, n=1):
        return wu.at[pl.ds(pl.multiple_of(dd * up_rows, 16), n * up_rows)]

    def down_at(dd, n=1):
        return wd.at[pl.ds(pl.multiple_of(dd * down_rows, 16), n * down_rows)]

    own_w = [
        pltpu.make_async_copy(win.at[c], up_at(d), local_sems.at[5]),
        pltpu.make_async_copy(wout.at[c], down_at(d), local_sems.at[6]),
    ]
    for cp in own_w:
        cp.start()
    r_ux, r_dy, r_uy, r_dx2 = (wire.roles(2) for _ in range(4))
    r_uf, r_df, r_us, r_dsib = (wire.roles() for _ in range(4))
    for cc in range(2):
        wire.send(r_ux + cc, win.at[cc], up_at(d), (me.xn - c + cc, z), recv_role=r_ux + c)
        wire.send(r_dy + cc, wout.at[cc], down_at(d), (me.yn - c + cc, z), recv_role=r_dy + c)
    r_id = wire.roles(2)
    wire.send(r_id, ids, ip, me.next)
    wire.send(r_id + 1, ids, inx, me.prev)
    r_h = wire.roles(2 * MICRO)

    def send_halo(mb):
        wire.send(r_h + 2 * mb, tok.at[mb, pl.ds(rows - halo, halo)], hp.at[mb], me.next)
        wire.send(r_h + 2 * mb + 1, tok.at[mb, pl.ds(0, halo)], hn.at[mb], me.prev)

    send_halo(0)
    before_row = (
        lax.broadcasted_iota(jnp.int32, (rows, rows), 0)
        > lax.broadcasted_iota(jnp.int32, (rows, rows), 1)
    ).astype(bf16)
    square[...] = jnp.zeros_like(square)
    square[0:experts, 0:share] = routw[...].astype(f32)
    square[experts : experts + 2, 0:share] = gainw[...].astype(f32)
    square[experts + 2 : experts + 4, 0:share] = biasw[...].astype(f32)
    s_src[0:share, :] = square[...].T[0:share, :].astype(bf16)
    row128 = lax.broadcasted_iota(jnp.int32, (128, rows), 0)
    row16 = lax.broadcasted_iota(jnp.int32, (16, 128), 0)
    hots = []
    counts = jnp.zeros((16, 128), f32)
    for mb in range(MICRO):
        choice = routes[mb].astype(f32)
        wide = jnp.where(row128 == 0, choice[0:1], jnp.where(row128 == 1, choice[1:2], -1.0)).T
        pair = [(wide[:, k : k + 1] == lane.astype(f32)).astype(f32) for k in range(TOP)]
        hots.append(pair)
        for k in range(TOP):
            counts = jnp.where(row16 == mb * TOP + k, jnp.sum(pair[k], axis=0, keepdims=True), counts)
    s_src[share : share + 16, :] = counts.astype(bf16)

    for k in range(1, ne):
        wire.send(r_dz + 3 * (k - 1) + 2, s_src, s_all.at[me.idx], (d, lax.rem(z + k, ne)))
    s_all[me.idx] = s_src[...]
    g_d = [Chain(wire, me, gd.at[mb]) for mb in range(MICRO)]
    g_x = [Chain(wire, me, gx.at[mb]) for mb in range(MICRO)]
    own_d = [
        pltpu.make_async_copy(cot.at[mb], gd.at[mb, s_me], local_sems.at[3 + mb])
        for mb in range(MICRO)
    ]
    for cp in own_d:
        cp.start()

    for cp in local:
        cp.wait()
    for k in range(1, ne):
        wire.arrive(r_dz + 3 * (k - 1), qkv)
        wire.arrive(r_dz + 3 * (k - 1) + 1, outw)
        wire.arrive(r_dz + 3 * (k - 1) + 2, s_src)

    def column(dd):
        at = pl.ds(pl.multiple_of(dd * (ne * share), 16), ne * share)
        return w_all.at[:, at], s_all.at[pl.ds(dd * ne, ne)]

    chips = nd // 2
    r_dx = wire.roles(2 * (chips - 1))
    r_ds = wire.roles(2 * chips)
    blk, sblk = column(d)
    for k in range(1, chips):
        wire.send(r_dx + 2 * (k - 1), blk, blk, (me.chip(k), z))
        wire.send(r_dx + 2 * (k - 1) + 1, sblk, sblk, (me.chip(k), z))
    wire.send(r_ds, blk, blk, me.sib)
    wire.send(r_ds + 1, sblk, sblk, me.sib)
    send_halo(1)
    g_d[0].own(cot.at[0])
    wire.send(r_us, win.at[1 - c], up_at(d), me.sib)
    wire.send(r_dsib, wout.at[1 - c], down_at(d), me.sib)
    for k in range(1, chips):
        wire.arrive(r_dx + 2 * (k - 1), blk)
        wire.arrive(r_dx + 2 * (k - 1) + 1, sblk)
        b, sb = column(lax.rem(d + nd - 2 * k, nd))
        wire.send(r_ds + 2 * k, b, b, me.sib)
        wire.send(r_ds + 2 * k + 1, sb, sb, me.sib)
    for cc in range(2):
        wire.send(r_dx2 + cc, wout.at[cc], down_at(d), (me.xn - c + cc, z), recv_role=r_dx2 + c)
        wire.send(r_uy + cc, win.at[cc], up_at(d), (me.yn - c + cc, z), recv_role=r_uy + c)
        wire.arrive(r_ux + cc, win.at[0])
        wire.arrive(r_dy + cc, wout.at[0])
    wire.send(r_uf, up_at(me.xn - c, 2), up_at(me.xn - c, 2), (me.yn, z))
    wire.send(r_df, down_at(me.yn - c, 2), down_at(me.yn - c, 2), (me.xn, z))
    for k in range(chips):
        wire.arrive(r_ds + 2 * k, blk)
        wire.arrive(r_ds + 2 * k + 1, sblk)

    o_small[...] = s_all[:, 0:share, :].reshape(D, 128).astype(f32)
    s_rows = o_small[...].T
    all_counts = s_all[:, share : share + 16, :].astype(f32)
    ahead = lax.broadcasted_iota(jnp.int32, all_counts.shape, 0) < me.idx
    before = jnp.sum(jnp.where(ahead, all_counts, 0.0), axis=0)
    total = jnp.sum(all_counts, axis=0)
    gains = [s_rows[experts + k : experts + k + 1, :] for k in range(2)]
    biases = [s_rows[experts + 2 + k : experts + 3 + k, :] for k in range(2)]

    r_rk = wire.roles(2 * ne)

    def send_ranks():
        for mb in range(MICRO):
            one, two = hots[mb]
            rank_one = mm(before_row, one.astype(bf16))
            rank_two = mm(before_row, two.astype(bf16))
            b1, b2 = before[2 * mb : 2 * mb + 1], before[2 * mb + 1 : 2 * mb + 2]
            t1 = total[2 * mb : 2 * mb + 1]
            place_one = jnp.sum(one * (b1 + rank_one), axis=1, keepdims=True)
            place_two = jnp.sum(two * (t1 + b2 + rank_two), axis=1, keepdims=True)
            kept = one * (place_one < capacity).astype(f32) + two * (place_two < capacity).astype(
                f32
            )
            ranks = jnp.where(kept > 0.0, rank_one + rank_two, -1.0)
            rk_src[mb] = ranks.T[0:experts, :]
        for k in range(ne):
            zk = lax.rem(z + k, ne)
            if k > 0:
                wire.send(r_rk + 2 * k, rk_src, rk.at[s_me], (d, zk))
            wire.send(r_rk + 2 * k + 1, rk_src, rk.at[s_me], (me.sib_d, zk))
        rk[s_me] = rk_src[...]

    wire.arrive(r_id, ids)
    wire.arrive(r_id + 1, ids)
    pos = lax.broadcasted_iota(jnp.int32, (1, rows), 1)
    gap = rows - halo
    for mb in range(MICRO):
        here = ids[mb : mb + 1, :].astype(f32)
        below = jnp.where((pos >= gap) & (me.idx > 0), ip[mb : mb + 1, :].astype(f32), -1.0)
        above = jnp.where(
            (pos < halo) & (me.idx < nd * ne - 1), inx[mb : mb + 1, :].astype(f32), -1.0
        )
        o_idr[mb] = jnp.concatenate([below, here, above], axis=1)

    zero_gap = jnp.zeros((gap, D), bf16)
    acts[0:gap, 0:D] = zero_gap
    acts[ext - gap : ext, 0:D] = zero_gap
    scale = 1.0 / math.sqrt(HEAD_DIM)
    given = []

    def give(src, dst):
        given.append(pltpu.make_async_copy(src, dst, give_sems.at[len(given)]))
        given[-1].start()

    give(w_all, g_w)
    saves = [pltpu.make_async_copy(
            acts.at[pl.ds(0, ext), pl.ds(D, 3 * D)], o_qkv.at[mb], local_sems.at[7 + mb]
        )
        for mb in range(MICRO)]

    def attend(mb, hooks):
        wire.arrive(r_h + 2 * mb, hp.at[mb])
        wire.arrive(r_h + 2 * mb + 1, hn.at[mb])

        def put(value, start):
            acts[start : start + value.shape[0], 0:D] = normed(
                value.astype(f32), gains[0], biases[0]
            ).astype(bf16)

        put(hp[mb], gap)
        put(tok[mb], rows)
        put(hn[mb], 2 * rows)
        if mb > 0:
            saves[mb - 1].wait()
        for k in range(3):
            for r in range(3):
                part = slice(r * rows, (r + 1) * rows)
                acts[part, (k + 1) * D : (k + 2) * D] = mm(acts[part, 0:D], w_all[k]).astype(bf16)
        saves[mb].start()
        idr = o_idr[mb]
        idc = jnp.broadcast_to(idr[:, rows : 2 * rows], (128, rows)).T[:, 0:1]
        bias[...] = jnp.where(idc == idr, 0.0, neg_big)
        o_lse[mb] = jnp.zeros((rows, 128), f32)

        @pl.loop(0, HEADS // 2, unroll=True)
        def _(pair):
            at = pl.ds(pl.multiple_of(pair * 128, 128), 128)
            query, key, value = (
                acts[part, pl.ds(pl.multiple_of((k + 1) * D + pair * 128, 128), 128)]
                for k, part in enumerate((slice(rows, 2 * rows), slice(0, ext), slice(0, ext)))
            )
            mixed = jnp.zeros((rows, 128), f32)
            lse = o_lse[mb]
            for half in range(2):
                keep = (lane < 64) if half == 0 else (lane >= 64)
                q = jnp.where(keep, query, jnp.zeros_like(query))
                v = jnp.where(keep, value, jnp.zeros_like(value))
                s = mm_nt(q, key) * scale + bias[...]
                top = jnp.max(s, axis=-1, keepdims=True)
                p = jnp.exp(s - top)
                total_p = jnp.sum(p, axis=-1, keepdims=True)
                mixed = mixed + mm((p * (1.0 / total_p)).astype(bf16), v)
                lse = jnp.where(lane == 2 * pair + half, top + jnp.log(total_p), lse)
            o_lse[mb] = lse
            o_mixed[mb, :, at] = mixed.astype(bf16)
            for when, hook in hooks.items():
                pl.when(pair == when)(hook)

        resid = tok[mb].astype(f32) + mm(o_mixed[mb], w_all[3])
        o_resid[mb] = resid
        n2 = normed(resid, gains[1], biases[1]).astype(bf16)
        gx[mb, s_me] = n2
        g_x[mb].own(gx.at[mb, s_me])
        logits = mm(n2, o_small[...].astype(bf16))
        logits = jnp.where(lane < experts, logits, neg_big)
        p = jnp.exp(logits - jnp.max(logits, axis=-1, keepdims=True))
        o_probs[mb] = p / jnp.sum(p, axis=-1, keepdims=True)
        give(gx.at[mb, s_me], g_n2.at[mb])
        give(o_probs.at[mb], g_probs.at[mb])
        give(o_resid.at[mb], g_resid.at[mb])
        give(o_mixed.at[mb], g_mixed.at[mb])
        give(o_lse.at[mb], g_lse.at[mb])

    def later_halves():
        g_x[0].pump(0)
        g_d[1].own(cot.at[1])

    attend(0, {0: lambda: g_d[0].pump(0), 3: lambda: g_d[0].pump(1)})
    send_ranks()
    attend(1, {0: lambda: g_d[0].pump(2), 2: later_halves})
    g_x[0].pump(1)

    r_cx = wire.roles(2 * MICRO * ne)
    r_up = wire.roles(MICRO * ne)
    r_dn = wire.roles(MICRO * ne)
    r_dg = wire.roles(MICRO * 2 * ne)
    r_far = wire.roles()
    sub = lax.broadcasted_iota(jnp.int32, (slots, rows), 0).astype(f32)
    tile = 2 * slots
    chunk = 512
    like = qo.at[0, 0, 0]

    def target(i):
        swap = jnp.where(i < 2, 1 - i, i)
        return jnp.where(
            z == 0, i, jnp.where(z == 1, swap, jnp.where(z == 2, ne - 1 - swap, ne - 1 - i))
        )

    def pass_up(mb, to):
        wire.send(r_up + mb * ne + to, qo.at[mb, 0, to], ud.at[mb, to], me.up)

    def pass_down(mb, to):
        slot = jnp.where(z - 1 == to, ne, to)
        wire.send(r_dn + mb * ne + to, qo.at[mb, 0, to], ud.at[mb, slot], me.down)

    def settle(mb, zp):
        for t in range(2):
            wire.arrive(r_cx + (mb * 2 + t) * ne + zp, like)
            qo[mb, t, zp] = (qo[mb, t, zp].astype(f32) + cr[mb, t, zp].astype(f32)).astype(bf16)

        straight = (mb > 0) & (z + zp == ne - 1) & ((z == 0) | (zp == 0))

        @pl.when((z == 0) & (zp > 0) & jnp.logical_not(straight))
        def _():
            pass_up(mb, zp)

        @pl.when((z == ne - 1) & (zp < ne - 1) & jnp.logical_not(straight))
        def _():
            pass_down(mb, zp)

        @pl.when(straight)
        def _():
            wire.send(r_far, qo.at[1, 0, zp], ud.at[1, 1], (d, zp))

    def relay(mb, hop, to):
        @pl.when(z == hop)
        def _():
            wire.arrive(r_up + mb * ne + to, like)
            qo[mb, 0, to] = (qo[mb, 0, to].astype(f32) + ud[mb, to].astype(f32)).astype(bf16)
            pass_up(mb, to)

        @pl.when(z == ne - 1 - hop)
        def _():
            low = ne - 1 - to
            wire.arrive(r_dn + mb * ne + low, like)
            qo[mb, 0, low] = (qo[mb, 0, low].astype(f32) + ud[mb, low].astype(f32)).astype(bf16)
            pass_down(mb, low)

    def end_sums(mb):
        acc_eo[...] = qo[mb, 0, z].astype(f32)

        @pl.when(z > 0)
        def _():
            wire.arrive(r_up + mb * ne + z, like)
            acc_eo[...] += ud[mb, z].astype(f32)

        @pl.when(z < ne - 1)
        def _():
            wire.arrive(r_dn + mb * ne + z, like)
            acc_eo[...] += ud[mb, ne].astype(f32)

        if mb > 0:

            @pl.when((z == 0) | (z == ne - 1))
            def _():
                wire.arrive(r_far, like)
                acc_eo[...] += ud[mb, 1].astype(f32)

        o_din[mb] = acc_eo[...]

    def first_tile():
        for cp in own_w + own_d + saves[1:]:
            cp.wait()
        for cc in range(2):
            wire.arrive(r_uy + cc, win.at[0])
            wire.arrive(r_dx2 + cc, wout.at[0])
        wire.arrive(r_us, win.at[0])
        wire.arrive(r_dsib, wout.at[0])
        wire.arrive(r_uf, up_at(0, 2))
        wire.arrive(r_df, down_at(0, 2))
        for k in range(ne):
            if k > 0:
                wire.arrive(r_rk + 2 * k, rk_src)
            wire.arrive(r_rk + 2 * k + 1, rk_src)
        g_d[0].near()
        g_x[0].near()

    def both(mb, what, k):
        for g in (g_d[mb], g_x[mb]):
            getattr(g, what)(k)

    def tile_1():
        both(0, "finish", 0)
        g_x[0].pump(2)

    def tile_2():
        both(0, "finish", 1)

    def tile_3():
        both(0, "finish", 2)
        both(1, "pump", 0)

    def tile_4():
        g_d[1].near()
        g_x[1].near()

    def tile_5():
        both(1, "finish", 0)
        both(1, "pump", 1)
        relay(0, 1, 2)

    def tile_6():
        both(1, "finish", 1)
        both(1, "pump", 2)
        relay(0, 1, 3)

    def tile_7():
        both(1, "finish", 2)
        relay(0, 2, 3)

    before_tile = [first_tile, tile_1, tile_2, tile_3, tile_4, tile_5, tile_6, tile_7]

    @pl.loop(0, MICRO * ne)
    def _(i):
        mb = i // ne
        zp = target(lax.rem(i, ne))

        for when, hook in enumerate(before_tile):
            pl.when(i == when)(hook)

        for cc in range(2):
            s = zp * 2 + cc
            at = slice(cc * slots, (cc + 1) * slots)
            pick = (sub == rk[s, mb, pl.ds(e, 1), :]).astype(bf16)
            pm[cc] = pick
            xs[at, :] = mm(pick, gx[mb, s]).astype(bf16)
            ds[at, :] = mm(pick, gd[mb, s]).astype(bf16)
        x = xs[...]
        logits = mm(x, o_small[...].astype(bf16))
        logits = jnp.where(lane < experts, logits, neg_big)
        p = jnp.exp(logits - jnp.max(logits, axis=-1, keepdims=True))
        p = p / jnp.sum(p, axis=-1, keepdims=True)
        gate = jnp.sum(jnp.where(lane == e, p, 0.0), axis=-1, keepdims=True)
        gt[...] = jnp.broadcast_to(gate, (tile, 128))
        dy = (gate * ds[...].astype(f32)).astype(bf16)
        deo[...] = dy
        across = pl.ds(pl.multiple_of(i * tile, tile), tile)
        xt[:, across] = x.T
        dt[:, across] = dy.T

        @pl.loop(0, FF // 256, unroll=True)
        def _(f):
            at = pl.ds(pl.multiple_of(f * 256, 256), 256)
            pre = mm(xs[...], wu[:, at])
            d_act = mm_nt(deo[...], wd[at, :])
            sq = pre * pre
            k0 = math.sqrt(2.0 / math.pi)
            th = jnp.tanh(pre * (k0 + (k0 * 0.044715) * sq))
            half = 0.5 + 0.5 * th
            slope = half + (0.5 * pre) * (1.0 - th * th) * (k0 + (3.0 * k0 * 0.044715) * sq)
            acts[across, at] = (pre * half).astype(bf16)
            grads[across, at] = (slope * d_act).astype(bf16)

        @pl.when(i > 0)
        def _():
            settle((i - 1) // ne, target(lax.rem(i - 1 + ne, ne)))

        eo = mm(acts[across, :], wd[...]).astype(bf16).astype(f32)
        d_gate = jnp.sum(ds[...].astype(f32) * eo, axis=-1, keepdims=True)
        ys[0] = mm_nt(grads[across, :], wu[...]).astype(bf16)
        ys[1] = (gt[:, 0:1] * eo).astype(bf16)
        box = lax.rem(i, 2)

        @pl.when(i > 1)
        def _():
            old = i - 2
            for t in range(2):
                wire.left(r_cx + ((old // ne) * 2 + t) * ne + target(lax.rem(old, ne)), like)

        for own in range(2):
            cc = c if own else 1 - c
            back = pm[cc].T
            at = pl.ds(pl.multiple_of(cc * slots, slots), slots)
            for t in range(2):
                moved = mm(back, ys[t, at, :]).astype(bf16)
                if own:
                    qo[mb, t, zp] = moved
                else:
                    cs[box, t] = moved
        for t in range(2):
            role = r_cx + (mb * 2 + t) * ne + zp
            wire.send(role, cs.at[box, t], cr.at[mb, t, zp], me.sib)
        for cc in range(2):
            at = slice(cc * slots, (cc + 1) * slots)
            line = jnp.sum(pm[cc].astype(f32) * d_gate[at], axis=0, keepdims=True)
            to = zp * 2 + cc
            dgs[mb, to] = jnp.broadcast_to(line, (8, rows))

            @pl.when(to != s_me)
            def _():
                wire.send(
                    r_dg + mb * 2 * ne + to,
                    dgs.at[mb, to],
                    dg.at[mb, e],
                    (d - c + cc, zp),
                    recv_role=r_dg + mb * 2 * ne + s_me,
                )

            @pl.when(to == s_me)
            def _():
                dg[mb, e] = jnp.broadcast_to(line, (8, rows))

    settle(1, target(ne - 1))

    @pl.when(z == 1)
    def _():
        pass_up(1, ne - 1)

    @pl.when(z == ne - 2)
    def _():
        pass_down(1, 0)


    wide_at = [pl.ds(k * chunk, chunk) for k in range(FF // chunk)]
    outs = []
    hooks = {0: lambda: relay(1, 1, 2), 2: lambda: relay(1, 2, 3)}
    for f, at in enumerate(wide_at):
        for k, (left, right, to) in enumerate(((xt, grads, o_up), (dt, acts, o_down))):
            if f > 1:
                outs[2 * (f - 2) + k].wait()
            stage[f % 2, k] = mm(left[...], right[:, at]).astype(bf16)
            cp = pltpu.make_async_copy(stage.at[f % 2, k], to.at[:, at], local_sems.at[9 + 2 * f + k])
            cp.start()
            outs.append(cp)
        if f in hooks:
            hooks[f]()
    end_sums(0)
    give_y = [pltpu.make_async_copy(qo.at[mb, 1], o_y.at[mb], local_sems.at[mb]) for mb in range(MICRO)]
    for cp in give_y:
        cp.start()
    for mb in range(MICRO):
        for s in range(2 * ne):

            @pl.when(s != s_me)
            def _():
                wire.arrive(r_dg + mb * 2 * ne + s, dgs.at[0, 0])

        groups = []
        sub8 = lax.broadcasted_iota(jnp.int32, (8, rows), 0)
        for base in range(0, experts, 8):
            group = dg[mb, base]
            for j in range(1, 8):
                group = jnp.where(sub8 == j, dg[mb, base + j], group)
            groups.append(group)
        lines = jnp.concatenate(groups + [jnp.zeros((128 - experts, rows), f32)], axis=0)
        o_dprobs[mb] = lines.T
    end_sums(1)
    for cp in outs[-4:] + give_y + given:
        cp.wait()

    for k in range(1, ne):
        wire.left(r_dz + 3 * (k - 1), qkv)
        wire.left(r_dz + 3 * (k - 1) + 1, outw)
        wire.left(r_dz + 3 * (k - 1) + 2, s_src)
    wire.left(r_id, ids)
    wire.left(r_id + 1, ids)
    for k in range(2 * MICRO):
        wire.left(r_h + k, hp.at[0])
    for k in range(1, chips):
        wire.left(r_dx + 2 * (k - 1), blk)
        wire.left(r_dx + 2 * (k - 1) + 1, sblk)
    for k in range(chips):
        wire.left(r_ds + 2 * k, blk)
        wire.left(r_ds + 2 * k + 1, sblk)
    for cc in range(2):
        wire.left(r_ux + cc, win.at[0])
        wire.left(r_uy + cc, win.at[0])
        wire.left(r_dy + cc, wout.at[0])
        wire.left(r_dx2 + cc, wout.at[0])
    wire.left(r_us, win.at[0])
    wire.left(r_dsib, wout.at[0])
    wire.left(r_uf, up_at(0, 2))
    wire.left(r_df, down_at(0, 2))
    for k in range(ne):
        if k > 0:
            wire.left(r_rk + 2 * k, rk_src)
        wire.left(r_rk + 2 * k + 1, rk_src)
    for g in g_d + g_x:
        g.drain()
    for old in (MICRO * ne - 2, MICRO * ne - 1):
        for t in range(2):
            wire.left(r_cx + ((old // ne) * 2 + t) * ne + target(old % ne), like)
    @pl.when((z == 0) | (z == ne - 1))
    def _():
        wire.left(r_far, like)

    for mb in range(MICRO):
        for to in range(ne):
            lowest = 1 if mb > 0 and to == ne - 1 else 0
            highest = ne - 2 if mb > 0 and to == 0 else ne - 1

            @pl.when((z < to) & (z >= lowest))
            def _():
                wire.left(r_up + mb * ne + to, like)

            @pl.when((z > to) & (z <= highest))
            def _():
                wire.left(r_dn + mb * ne + to, like)

        for s in range(2 * ne):

            @pl.when(s != s_me)
            def _():
                wire.left(r_dg + mb * 2 * ne + s, dgs.at[0, 0])

    assert wire.used <= ROLES


ROLES = 192


def front(nd, ne, *args):
    tokens, qkv = args[0], args[3]
    rows, share = tokens.shape[1], qkv.shape[1]
    halo = -(-(IMG - 1) // 16) * 16
    experts = 2 * ne
    slots = 4 * rows // experts
    tile = 2 * slots
    every = MICRO * ne * tile
    shape = jax.ShapeDtypeStruct
    vmem, anywhere = pl.BlockSpec(memory_space=pltpu.VMEM), pl.BlockSpec(memory_space=pl.ANY)
    outs = (
        (vmem, (MICRO, rows, D), f32),
        (anywhere, (MICRO, ne, rows, D), bf16),
        (vmem, (MICRO, rows, 128), f32),
        (anywhere, (D, FF), bf16),
        (anywhere, (D, FF), bf16),
        (anywhere, (MICRO, rows, D), bf16),
        (anywhere, (MICRO, rows, 128), f32),
        (anywhere, (MICRO, rows, D), f32),
        (anywhere, (MICRO, rows, D), bf16),
        (anywhere, (MICRO, 3 * rows, 3 * D), bf16),
        (anywhere, (MICRO, rows, 128), f32),
        (anywhere, (4, D, D), bf16),
        (vmem, (D, 128), f32),
        (vmem, (MICRO, 1, 3 * rows), f32),
    )
    v = pltpu.VMEM
    return pl.pallas_call(
        functools.partial(front_kernel, nd, ne),
        out_shape=[shape(*o[1:]) for o in outs],
        in_specs=[vmem, vmem, vmem, anywhere, anywhere, vmem, vmem, vmem] + [anywhere] * 3,
        out_specs=[o[0] for o in outs],
        scratch_shapes=[
            v((share + 16, 128), bf16),
            v((nd * ne, share + 16, 128), bf16),
            v((MICRO, halo, D), bf16),
            v((MICRO, halo, D), bf16),
            v((MICRO, rows), jnp.int32),
            v((MICRO, rows), jnp.int32),
            v((MICRO, 2 * ne, rows, D), bf16),
            v((MICRO, 2 * ne, rows, D), bf16),
            v((D, FF), bf16),
            v((FF, D), bf16),
            v((MICRO, experts, rows), f32),
            v((2 * ne, MICRO, experts, rows), f32),
            v((rows, 3 * rows), f32),
            v((every, FF), bf16),
            v((every, FF), bf16),
            v((2, slots, rows), bf16),
            v((tile, D), bf16),
            v((tile, D), bf16),
            v((tile, D), bf16),
            v((D, every), bf16),
            v((D, every), bf16),
            v((tile, 128), f32),
            v((rows, D), f32),
            v((2, tile, D), bf16),
            v((MICRO, 2, ne, rows, D), bf16),
            v((2, 2, rows, D), bf16),
            v((MICRO, 2, ne, rows, D), bf16),
            v((MICRO, ne + 1, rows, D), bf16),
            v((MICRO, 2 * ne, 8, rows), f32),
            v((MICRO, experts, 8, rows), f32),
            v((2, 2, D, 512), bf16),
            v((128, 128), f32),
            v((MICRO, rows, 128), f32),
            v((MICRO, rows, D), f32),
            v((MICRO, rows, D), bf16),
            v((MICRO, rows, 128), f32),
            v((4, D, D), bf16),
            pltpu.SemaphoreType.DMA((16,)),
            pltpu.SemaphoreType.DMA((ROLES,)),
            pltpu.SemaphoreType.DMA((ROLES,)),
            pltpu.SemaphoreType.DMA((17,)),
        ],
        compiler_params=pltpu.CompilerParams(
            collective_id=0, has_side_effects=True, vmem_limit_bytes=VMEM_BYTES
        ),
        name="front",
    )(*args)


def mm_exact(a, b):
    return jnp.dot(a, b, preferred_element_type=f32, precision=highest)


def back_kernel(
    nd,
    ne,
    tok,
    cot,
    d_in,
    y,
    d_probs,
    up,
    down,
    n2,
    probs,
    resid,
    mixed,
    qkv_in,
    lse,
    w_in,
    small,
    idr,
    o_block,
    o_input,
    o_dense,
    o_small,
    o_up,
    o_down,
    yq,
    yu,
    gu,
    gd,
    d_res,
    dm,
    stat_src,
    stat_p,
    stat_n,
    hp,
    hn,
    stats,
    bias,
    dp,
    gw,
    gs,
    gwb,
    gsb,
    rc,
    rcs,
    sx,
    sxs,
    rx,
    rxs,
    sz,
    szs,
    rz,
    rzs,
    block,
    qkv,
    w,
    send_sems,
    recv_sems,
    local_sems,
):
    me = Place(nd, ne)
    d, z, c = me.d, me.z, me.c
    rows = tok.shape[1]
    experts = 2 * ne
    halo = hp.shape[1]
    gap = rows - halo
    chips = nd // 2
    wire = Wire(send_sems, recv_sems, me.sib)
    lane = lax.broadcasted_iota(jnp.int32, (1, 128), 1)
    up_rows, down_rows = gu.shape[1], gd.shape[2]
    part = D // nd
    share = part // ne
    me.enter()

    r_g = wire.roles(2 * (nd - 1))

    def up_of(dd):
        return up.at[pl.ds(pl.multiple_of(dd * up_rows, 16), up_rows)]

    def down_of(dd):
        return down.at[:, pl.ds(pl.multiple_of(dd * down_rows, 128), down_rows)]

    own_g = [
        pltpu.make_async_copy(up_of(d), gu.at[d], local_sems.at[0]),
        pltpu.make_async_copy(down_of(d), gd.at[d], local_sems.at[1]),
    ]
    for cp in own_g:
        cp.start()
    for k in range(1, nd):
        dd = lax.rem(d + k, nd)
        wire.send(r_g + 2 * (k - 1), up_of(dd), gu.at[d], (dd, z))
        wire.send(r_g + 2 * (k - 1) + 1, down_of(dd), gd.at[d], (dd, z))

    fetches = [
        pltpu.make_async_copy(w_in.at[3], w.at[3], local_sems.at[2]),
        pltpu.make_async_copy(qkv_in.at[0], qkv.at[0], local_sems.at[3]),
        pltpu.make_async_copy(qkv_in.at[1], qkv.at[1], local_sems.at[4]),
        pltpu.make_async_copy(w_in.at[pl.ds(0, 3)], w.at[pl.ds(0, 3)], local_sems.at[5]),
        pltpu.make_async_copy(y.at[0, z], yq.at[0], local_sems.at[6]),
        pltpu.make_async_copy(y.at[1, z], yq.at[1], local_sems.at[7]),
    ]
    for cp in fetches:
        cp.start()
    r_y = wire.roles(MICRO * ne)
    like = yq.at[0]

    def send_y(mb, distances):
        for k in distances:
            to = lax.rem(z + k, ne)
            wire.send(r_y + mb * ne + k, y.at[mb, to], yu.at[mb, k], (d, to))

    def end_sums(mb):
        block[...] = resid[mb] + yq[mb].astype(f32)
        for k in range(1, ne):
            wire.arrive(r_y + mb * ne + k, like)
            block[...] += yu[mb, k].astype(f32)
        o_block[mb] = block[...].astype(bf16)

    send_y(0, (1,))

    s_rows = small[...].T
    gains = [s_rows[experts + k : experts + k + 1, :] for k in range(2)]
    router = jnp.where(lane < experts, small[...], 0.0)
    head_of = (
        lax.broadcasted_iota(jnp.int32, (D, 128), 0) // HEAD_DIM
        == lax.broadcasted_iota(jnp.int32, (D, 128), 1)
    ).astype(f32)

    def norm_back(values, dn, gain):
        offset = values - jnp.mean(values, axis=-1, keepdims=True)
        inv = lax.rsqrt(jnp.mean(offset * offset, axis=-1, keepdims=True) + norm_eps)
        hat = offset * inv
        q = dn * gain
        dv = inv * (
            q
            - jnp.mean(q, axis=-1, keepdims=True)
            - hat * jnp.mean(q * hat, axis=-1, keepdims=True)
        )
        return dv, jnp.sum(dn * hat, axis=0, keepdims=True), jnp.sum(dn, axis=0, keepdims=True)

    r_h = wire.roles(4 * MICRO)
    norm_sums = [jnp.zeros((1, D), f32) for _ in range(4)]
    zero_gap = jnp.zeros((gap, D), bf16)
    own = slice(rows, 2 * rows)
    for mb in range(MICRO):
        prob, dpr = probs[mb], d_probs[mb]
        d_logits = prob * (dpr - jnp.sum(prob * dpr, axis=-1, keepdims=True))
        dn2 = d_in[mb] + lax.dot_general(
            d_logits,
            router,
            (((1,), (1,)), ((), ())),
            preferred_element_type=f32,
            precision=highest,
        )
        dv, d_gain, d_bias = norm_back(resid[mb], dn2, gains[1])
        norm_sums[1] += d_gain
        norm_sums[3] += d_bias
        d_resid = cot[mb].astype(f32) + dv
        d_res[mb] = d_resid
        d_attn = d_resid.astype(bf16)
        if mb == 0:
            fetches[0].wait()
        d_mixed = mm_nt(d_attn, w[3]).astype(bf16)
        dm[mb, own, :] = d_mixed
        delta = mm_exact(d_mixed.astype(f32) * mixed[mb].astype(f32), head_of)
        stat_src[mb, 0] = lse[mb].T[0:HEADS, :]
        stat_src[mb, 1] = delta.T[0:HEADS, :]
        low, high = pl.ds(rows, halo), pl.ds(2 * rows - halo, halo)
        wire.send(r_h + 4 * mb, dm.at[mb, high], hp.at[mb], me.next)
        wire.send(r_h + 4 * mb + 1, stat_src.at[mb], stat_p.at[mb], me.next)
        wire.send(r_h + 4 * mb + 2, dm.at[mb, low], hn.at[mb], me.prev)
        wire.send(r_h + 4 * mb + 3, stat_src.at[mb], stat_n.at[mb], me.prev)
        g_out = mm(mixed[mb].T, d_attn)
        g_router = mm_exact(n2[mb].astype(f32).T, d_logits)
        if mb == 0:
            gw[3] = g_out
            gs[...] = g_router
        else:
            gw[3] += g_out
            gs[...] += g_router

    scale = 1.0 / math.sqrt(HEAD_DIM)
    for mb in range(MICRO):
        ids = idr[mb]
        fetches[1 + mb].wait()
        if mb == 0:
            fetches[3].wait()
        idc = jnp.broadcast_to(ids[:, own], (128, rows)).T[:, 0:1]
        bias[...] = jnp.where(idc == ids, 0.0, neg_big)
        dst = jnp.zeros((rows, 128), f32)
        delta_cols = jnp.concatenate(
            [stat_src[mb, 1], jnp.zeros((128 - HEADS, rows), f32)], axis=0
        ).T

        @pl.loop(0, HEADS // 2, unroll=True)
        def _(pair):
            at = pl.ds(pl.multiple_of(pair * 128, 128), 128)
            query, key, value = (
                qkv[mb, part, pl.ds(pl.multiple_of(k * D + pair * 128, 128), 128)]
                for k, part in enumerate((own, slice(None), slice(None)))
            )
            grad = dm[mb, own, at]
            dq = jnp.zeros((rows, 128), f32)
            for half in range(2):
                keep = (lane < 64) if half == 0 else (lane >= 64)
                h = 2 * pair + half
                q = jnp.where(keep, query, jnp.zeros_like(query))
                g = jnp.where(keep, grad, jnp.zeros_like(grad))
                k = jnp.where(keep, key, jnp.zeros_like(key))
                lse_col = jnp.sum(jnp.where(lane == h, lse[mb], 0.0), axis=1, keepdims=True)
                delta_col = jnp.sum(jnp.where(lane == h, delta_cols, 0.0), axis=1, keepdims=True)
                p = jnp.exp(mm_nt(q, key) * scale + bias[...] - lse_col)
                ds = (p * (mm_nt(g, value) - delta_col)).astype(bf16)
                dq = dq + mm(ds, k)
            dp[0, :, at] = (dq * scale).astype(bf16)

        wire.arrive(r_h + 4 * mb, hp.at[mb])
        wire.arrive(r_h + 4 * mb + 1, stat_src.at[mb])
        wire.arrive(r_h + 4 * mb + 2, hp.at[mb])
        wire.arrive(r_h + 4 * mb + 3, stat_src.at[mb])
        send_y(mb, range(1 if mb else 2, ne))
        dm[mb, 0:gap, :] = zero_gap
        dm[mb, gap:rows, :] = hp[mb]
        dm[mb, 2 * rows : 2 * rows + halo, :] = hn[mb]
        dm[mb, 2 * rows + halo : 3 * rows, :] = zero_gap
        for k in range(2):
            stats[k, :, 0:rows] = stat_p[mb, k]
            stats[k, :, own] = stat_src[mb, k]
            stats[k, :, 2 * rows : 3 * rows] = stat_n[mb, k]

        @pl.loop(0, HEADS // 2, unroll=True)
        def _(pair):
            at = pl.ds(pl.multiple_of(pair * 128, 128), 128)
            query, key, value = (
                qkv[mb, part, pl.ds(pl.multiple_of(k * D + pair * 128, 128), 128)]
                for k, part in enumerate((slice(None), own, own))
            )
            grad = dm[mb, :, at]
            dk = jnp.zeros((rows, 128), f32)
            dv = jnp.zeros((rows, 128), f32)
            for half in range(2):
                keep = (lane < 64) if half == 0 else (lane >= 64)
                h = 2 * pair + half
                q = jnp.where(keep, query, jnp.zeros_like(query))
                g = jnp.where(keep, grad, jnp.zeros_like(grad))
                k = jnp.where(keep, key, jnp.zeros_like(key))
                v = jnp.where(keep, value, jnp.zeros_like(value))
                p = jnp.exp(mm_nt(k, query) * scale + bias[...] - stats[0, pl.ds(h, 1), :])
                ds = (p * (mm_nt(v, grad) - stats[1, pl.ds(h, 1), :])).astype(bf16)
                dk = dk + mm(ds, q)
                dv = dv + mm(p.astype(bf16), g)
            dp[1, :, at] = (dk * scale).astype(bf16)
            dp[2, :, at] = dv.astype(bf16)

        token = tok[mb].astype(f32)
        n1t = normed(token, gains[0], s_rows[experts + 2 : experts + 3, :]).astype(bf16).T
        dn1 = jnp.zeros((rows, D), f32)
        for k in range(3):
            dn1 = dn1 + mm_nt(dp[k], w[k])
            g_part = mm(n1t, dp[k])
            if mb == 0:
                gw[k] = g_part
            else:
                gw[k] += g_part
        dv, d_gain, d_bias = norm_back(token, dn1, gains[0])
        norm_sums[0] += d_gain
        norm_sums[2] += d_bias
        o_input[mb] = (d_res[mb] + dv).astype(bf16)

    rows128 = lax.broadcasted_iota(jnp.int32, (128, D), 0)
    norm_rows = jnp.zeros((128, D), f32)
    for k in range(4):
        norm_rows = jnp.where(rows128 == experts + k, norm_sums[k], norm_rows)
    gs[...] = jnp.where(lane < experts, gs[...], norm_rows.T)

    def of(dd):
        return pl.ds(pl.multiple_of(dd * part, 16), part)

    r_c = wire.roles(2 * chips)
    r_x = wire.roles(2 * (chips - 1))
    r_z = wire.roles(2 * (ne - 1))
    for k in range(chips):
        dd = 2 * k + 1 - c
        for m in range(4):
            gwb[k, m] = gw[m, of(dd), :].astype(bf16)
        gsb[k] = gs[of(dd), :]
        wire.send(r_c + 2 * k, gwb.at[k], rc.at[k], me.sib)
        wire.send(r_c + 2 * k + 1, gsb.at[k], rcs.at[k], me.sib)
    for k in range(chips):
        wire.arrive(r_c + 2 * k, rc.at[k])
        wire.arrive(r_c + 2 * k + 1, rcs.at[k])
    my_chip = d // 2
    for k in range(1, chips):
        to = lax.rem(my_chip + k, chips)
        dd = 2 * to + c
        for m in range(4):
            sx[k, m] = (gw[m, of(dd), :] + rc[to, m].astype(f32)).astype(bf16)
        sxs[k] = gs[of(dd), :] + rcs[to]
        wire.send(r_x + 2 * (k - 1), sx.at[k], rx.at[k], (dd, z))
        wire.send(r_x + 2 * (k - 1) + 1, sxs.at[k], rxs.at[k], (dd, z))
    total = [gw[m, of(d), :] + rc[my_chip, m].astype(f32) for m in range(4)]
    total_s = gs[of(d), :] + rcs[my_chip]
    for k in range(1, chips):
        wire.arrive(r_x + 2 * (k - 1), rx.at[k])
        wire.arrive(r_x + 2 * (k - 1) + 1, rxs.at[k])
        total = [total[m] + rx[k, m].astype(f32) for m in range(4)]
        total_s = total_s + rxs[k]
    for m in range(4):
        gw[m, 0:part, :] = total[m]
    gs[0:part, :] = total_s
    for k in range(1, ne):
        to = lax.rem(z + k, ne)
        at = pl.ds(pl.multiple_of(to * share, 16), share)
        for m in range(4):
            sz[k, m] = gw[m, at, :].astype(bf16)
        szs[k] = gs[at, :]
        wire.send(r_z + 2 * (k - 1), sz.at[k], rz.at[k], (d, to))
        wire.send(r_z + 2 * (k - 1) + 1, szs.at[k], rzs.at[k], (d, to))

    for cp in own_g:
        cp.wait()
    for k in range(1, nd):
        wire.arrive(r_g + 2 * (k - 1), gu.at[0])
        wire.arrive(r_g + 2 * (k - 1) + 1, gd.at[0])
    for x in range(2):
        o_up[x] = sum(gu[2 * k + x].astype(f32) for k in range(chips))
        o_down[x] = sum(gd[2 * k + x].astype(f32) for k in range(chips)).T

    for cp in fetches[4:]:
        cp.wait()
    for mb in range(MICRO):
        end_sums(mb)
    at = pl.ds(pl.multiple_of(z * share, 16), share)
    for k in range(1, ne):
        wire.arrive(r_z + 2 * (k - 1), rz.at[k])
        wire.arrive(r_z + 2 * (k - 1) + 1, rzs.at[k])
    for m in range(4):
        o_dense[m] = gw[m, at, :] + sum(rz[k, m].astype(f32) for k in range(1, ne))
    o_small[...] = gs[at, :] + sum(rzs[k] for k in range(1, ne))

    for k in range(1, nd):
        wire.left(r_g + 2 * (k - 1), gu.at[0])
        wire.left(r_g + 2 * (k - 1) + 1, gd.at[0])
    for mb in range(MICRO):
        for k in range(1, ne):
            wire.left(r_y + mb * ne + k, like)
        for k in range(2):
            wire.left(r_h + 4 * mb + 2 * k, hp.at[0])
            wire.left(r_h + 4 * mb + 2 * k + 1, stat_src.at[0])
    for k in range(chips):
        wire.left(r_c + 2 * k, rc.at[0])
        wire.left(r_c + 2 * k + 1, rcs.at[0])
    for k in range(1, chips):
        wire.left(r_x + 2 * (k - 1), rx.at[0])
        wire.left(r_x + 2 * (k - 1) + 1, rxs.at[0])
    for k in range(1, ne):
        wire.left(r_z + 2 * (k - 1), rz.at[0])
        wire.left(r_z + 2 * (k - 1) + 1, rzs.at[0])
    assert wire.used <= BACK_ROLES


BACK_ROLES = 80


def back(nd, ne, *args):
    tokens = args[0]
    rows = tokens.shape[1]
    halo = -(-(IMG - 1) // 16) * 16
    chips = nd // 2
    part = D // nd
    share = part // ne
    shape = jax.ShapeDtypeStruct
    outs = (
        shape((MICRO, rows, D), bf16),
        shape((MICRO, rows, D), bf16),
        shape((4, share, D), f32),
        shape((share, 128), f32),
        shape((2, D // nd, FF), f32),
        shape((2, FF // nd, D), f32),
    )
    vmem, anywhere = pl.BlockSpec(memory_space=pltpu.VMEM), pl.BlockSpec(memory_space=pl.ANY)
    v = pltpu.VMEM
    return pl.pallas_call(
        functools.partial(back_kernel, nd, ne),
        out_shape=outs,
        in_specs=[anywhere if k in (3, 5, 6, 11, 13) else vmem for k in range(len(args))],
        out_specs=[vmem] * len(outs),
        scratch_shapes=[
            v((MICRO, rows, D), bf16),
            v((MICRO, ne, rows, D), bf16),
            v((nd, D // nd, FF), bf16),
            v((nd, D, FF // nd), bf16),
            v((MICRO, rows, D), f32),
            v((MICRO, 3 * rows, D), bf16),
            v((MICRO, 2, HEADS, rows), f32),
            v((MICRO, 2, HEADS, rows), f32),
            v((MICRO, 2, HEADS, rows), f32),
            v((MICRO, halo, D), bf16),
            v((MICRO, halo, D), bf16),
            v((2, HEADS, 3 * rows), f32),
            v((rows, 3 * rows), f32),
            v((3, rows, D), bf16),
            v((4, D, D), f32),
            v((D, 128), f32),
            v((chips, 4, part, D), bf16),
            v((chips, part, 128), f32),
            v((chips, 4, part, D), bf16),
            v((chips, part, 128), f32),
            v((chips, 4, part, D), bf16),
            v((chips, part, 128), f32),
            v((chips, 4, part, D), bf16),
            v((chips, part, 128), f32),
            v((ne, 4, share, D), bf16),
            v((ne, share, 128), f32),
            v((ne, 4, share, D), bf16),
            v((ne, share, 128), f32),
            v((rows, D), f32),
            v((MICRO, 3 * rows, 3 * D), bf16),
            v((4, D, D), bf16),
            pltpu.SemaphoreType.DMA((BACK_ROLES,)),
            pltpu.SemaphoreType.DMA((BACK_ROLES,)),
            pltpu.SemaphoreType.DMA((8,)),
        ],
        compiler_params=pltpu.CompilerParams(
            collective_id=1, has_side_effects=True, vmem_limit_bytes=VMEM_BYTES
        ),
        name="back",
    )(*args)


def finish_kernel(block, inputs, dense, small, up, down, *rest):
    o_block, o_input, o_qkv, o_out, o_router, o_gain, o_bias, o_up, o_down = rest[:9]
    bufs, in_sems, out_sems = rest[9:-2], rest[-2], rest[-1]
    moves = (
        (up, o_up),
        (down, o_down),
        (inputs, o_input),
        (block, o_block),
        (dense.at[pl.ds(0, 3)], o_qkv),
        (dense.at[3], o_out),
    )
    ins = [pltpu.make_async_copy(m[0], b, in_sems.at[k]) for k, (m, b) in enumerate(zip(moves, bufs))]
    outs = [pltpu.make_async_copy(b, m[1], out_sems.at[k]) for k, (m, b) in enumerate(zip(moves, bufs))]
    for cp in ins:
        cp.start()
    experts, share = o_router.shape
    turned = jnp.concatenate([small[...], jnp.zeros((128 - share, 128), f32)], axis=0).T
    o_router[...] = turned[0:experts, 0:share]
    o_gain[...] = turned[experts : experts + 2, 0:share]
    o_bias[...] = turned[experts + 2 : experts + 4, 0:share]
    for there, back_again in zip(ins, outs):
        there.wait()
        back_again.start()
    for cp in outs:
        cp.wait()


def finish(experts, *args):
    block, inputs, dense, small, up, down = args
    share = small.shape[0]
    vmem, anywhere = pl.BlockSpec(memory_space=pltpu.VMEM), pl.BlockSpec(memory_space=pl.ANY)
    shape = jax.ShapeDtypeStruct
    outs = (
        (anywhere, block),
        (anywhere, inputs),
        (anywhere, shape((3, share, D), f32)),
        (anywhere, shape((share, D), f32)),
        (vmem, shape((experts, share), f32)),
        (vmem, shape((2, share), f32)),
        (vmem, shape((2, share), f32)),
        (anywhere, up),
        (anywhere, down),
    )
    bufs = (up, down, inputs, block, outs[2][1], outs[3][1])
    return pl.pallas_call(
        finish_kernel,
        out_shape=[shape(o[1].shape, o[1].dtype) for o in outs],
        in_specs=[vmem if k == 3 else anywhere for k in range(len(args))],
        out_specs=[o[0] for o in outs],
        scratch_shapes=[
            *(pltpu.VMEM(b.shape, b.dtype) for b in bufs),
            pltpu.SemaphoreType.DMA((7,)),
            pltpu.SemaphoreType.DMA((7,)),
        ],
        name="finish",
    )(*args)


def kernel_body(
    nd,
    ne,
    tokens,
    image_ids,
    routes,
    qkv_weight,
    out_weight,
    router_weight,
    norm_gains,
    norm_biases,
    expert_in,
    expert_out,
    cotangent,
):
    experts = 2 * ne
    saved = front(
        nd,
        ne,
        tokens,
        image_ids,
        routes.transpose(0, 2, 1),
        qkv_weight,
        out_weight,
        router_weight.T,
        norm_gains,
        norm_biases,
        expert_in,
        expert_out,
        cotangent,
    )
    outs = finish(experts, *back(nd, ne, tokens, cotangent, *saved))
    return (*outs[:4], outs[4].T, *outs[5:])


def chosen_body(nd, ne, tokens, *rest):
    rows, experts = tokens.shape[1], 2 * ne
    whole = D % (16 * nd * ne) == 0 and nd % 2 == 0 and 8 * rows == experts * rows and rows % 128 == 0
    whole = whole and nd == 8 and ne == 4
    if whole and rest[-3].shape[0] == 2:
        return kernel_body(nd, ne, tokens, *rest)
    return body(tokens, *rest)


def solution(mesh):
    return jax.shard_map(
        functools.partial(chosen_body, mesh.shape["dp"], mesh.shape["expert"]),
        mesh=mesh,
        in_specs=(
            P(None, ("dp", "expert"), None),
            P(None, ("dp", "expert")),
            P(None, ("dp", "expert"), None),
            P(None, ("dp", "expert"), None),
            P(("dp", "expert"), None),
            P(("dp", "expert"), None),
            P(None, ("dp", "expert")),
            P(None, ("dp", "expert")),
            P("expert", "dp", None),
            P("expert", "dp", None),
            P(None, ("dp", "expert"), None),
        ),
        out_specs=(
            P(None, ("dp", "expert"), None),
            P(None, ("dp", "expert"), None),
            P(None, ("dp", "expert"), None),
            P(("dp", "expert"), None),
            P(("dp", "expert"), None),
            P(None, ("dp", "expert")),
            P(None, ("dp", "expert")),
            P("expert", "dp", None),
            P("expert", "dp", None),
        ),
        check_vma=False,
    )
```
